32 devices in a mesh: dp: 4 (over z), seq: 8 (over y, x, core).
Axes of the slice: x: 2, y: 2, z: 4, core: 2. Of those that a mesh axis runs over, the one named last changes fastest.
Arguments:
- hidden: bfloat16 [4, 2560, 2048], P('dp', 'seq'), may hold values from -6 to 6
- seg_ids: int32 [4, 2560], P('dp', 'seq'), may hold values from 0 to 1, as said below
- pad_mask: int32 [4, 2560], P('dp', 'seq'), may hold values from 0 to 1, as said below
- attn_gain: bfloat16 [2048], P(('dp', 'seq')), may hold values from 0.25 to 1.75
- gate_gap: bfloat16 [2048], P(('dp', 'seq')), may hold values from 0.0002 to 0.5
- out_gain: bfloat16 [2048], P(('dp', 'seq')), may hold values from 0.25 to 1.75
- w_query: bfloat16 [2048, 2048], P(('dp', 'seq')), may hold values from -0.125 to 0.125
- w_forget: bfloat16 [2048, 2048], P(('dp', 'seq')), may hold values from -0.125 to 0.125
- w_input: bfloat16 [2048, 2048], P(('dp', 'seq')), may hold values from -0.125 to 0.125
- w_output: bfloat16 [2048, 2048], P(('dp', 'seq')), may hold values from -0.125 to 0.125
- ffn_gain: bfloat16 [2048], P(('dp', 'seq')), may hold values from 0.25 to 1.75
- w_gate: bfloat16 [2048, 5632], P(('dp', 'seq')), may hold values from -0.125 to 0.125
- w_up: bfloat16 [2048, 5632], P(('dp', 'seq')), may hold values from -0.125 to 0.125
- w_down: bfloat16 [5632, 2048], P(('dp', 'seq')), may hold values from -0.078125 to 0.078125
- out_grad: bfloat16 [4, 2560, 2048], P('dp', 'seq'), may hold values from -6 to 6
Outputs:
- block_out: bfloat16 [4, 2560, 2048], P('dp', 'seq')
- hidden_grad: bfloat16 [4, 2560, 2048], P('dp', 'seq')
- grad_attn_gain: float32 [2048], P(('dp', 'seq'))
- grad_gate_gap: float32 [2048], P(('dp', 'seq'))
- grad_out_gain: float32 [2048], P(('dp', 'seq'))
- grad_query: float32 [2048, 2048], P(('dp', 'seq'))
- grad_forget: float32 [2048, 2048], P(('dp', 'seq'))
- grad_input: float32 [2048, 2048], P(('dp', 'seq'))
- grad_output: float32 [2048, 2048], P(('dp', 'seq'))
- grad_ffn_gain: float32 [2048], P(('dp', 'seq'))
- grad_gate: float32 [2048, 5632], P(('dp', 'seq'))
- grad_up: float32 [2048, 5632], P(('dp', 'seq'))
- grad_down: float32 [5632, 2048], P(('dp', 'seq'))
The draws below stay inside these ranges and needn't reach their ends.
Inputs may be any that keep to these rules, and one draw needn't show every extreme that they name: `seg_ids`: in each row the numbers start at 0, never fall and rise by at most one from a token to the next; each sequence holds 1024 tokens or more. `pad_mask`: in each row, 1 on a leading run of tokens and 0 on the rest, which may be empty.
All inputs are finite; a program needn't handle non-finite values.
Results may differ from the reference program's by a relative error of at most 0.012.
Values may be sent and summed in bfloat16 or wider, within the bound.
A program may use at most 448 MiB of HBM per device.

```python
import math
import jax
import jax.numpy as jnp
from jax import lax

D = 2048
HEADS = 16
FF = 5632
TOK_DEV = 320
BLOCK = 64
MIN_LEN = 1024
ROW = 2560
ROWS = 4
N_DP = 4
N_SEQ = 8


def draw_gate_gap(key, part):
    uniform_draw = jax.random.uniform(jax.random.fold_in(key, 11), (D,), jnp.float32)
    lowest, highest = (math.log(0.001), math.log(0.5))
    return jnp.exp(lowest + (highest - lowest) * uniform_draw).astype(jnp.bfloat16)


def draw_seg_ids(key, part):
    row_tokens = TOK_DEV * N_SEQ
    most_segments = row_tokens // MIN_LEN
    count_key, cut_key = jax.random.split(jax.random.fold_in(key, 23))
    counts = jax.random.randint(count_key, (N_DP, 1), 1, most_segments + 1)
    first_row = jnp.arange(N_DP)[:, None] == 0
    counts = jnp.where(first_row, most_segments, counts).astype(jnp.int32)
    spare_room = row_tokens - counts * MIN_LEN
    cut_points = jax.random.randint(cut_key, (N_DP, most_segments), 0, spare_room + 1)
    cut_points = jnp.sort(cut_points, axis=1)
    places = jnp.arange(most_segments)[None, :]
    bounds = (places + 1) * MIN_LEN + cut_points
    bounds = jnp.where(places + 1 < counts, bounds, row_tokens + 1)
    tokens_at = jnp.arange(row_tokens)
    return jnp.sum((tokens_at[None, :, None] >= bounds[:, None, :]).astype(jnp.int32), axis=2).astype(jnp.int32)


def draw_pad_mask(key, part):
    row_tokens = TOK_DEV * N_SEQ
    padding = jax.random.randint(jax.random.fold_in(key, 37), (N_DP, 1), 0, MIN_LEN // 2 + 1)
    tokens_at = jnp.arange(row_tokens)[None, :]
    return (tokens_at < row_tokens - padding).astype(jnp.int32)


def with_spikes(values, own_key, source, target, parts, factor):
    def block_of(axis_at):
        return (jnp.arange(values.shape[axis_at]) // (values.shape[axis_at] // parts)).reshape((-1,) + (1,) * (values.ndim - 1 - axis_at))

    near = jax.random.permutation(own_key, parts)[block_of(target)]
    other_side = (block_of(target) + parts // 2) % parts
    return jnp.where((block_of(source) == near) | (block_of(source) == other_side), factor * values, values)


def level_of(rng, dims, pieces, least, high):
    def one(dim, parts):
        draws = jax.random.uniform(jax.random.fold_in(jax.random.fold_in(rng, 6), dim), (parts,), jnp.float32, least / len(pieces), high / len(pieces))
        return jnp.repeat(jnp.exp(draws), dims[dim] // parts).reshape((-1,) + (1,) * (len(dims) - dim - 1))

    level = one(*pieces[0])
    for cut in pieces[1:]:
        level = level * one(*cut)
    return level


def noise(stream_key, dims, spread, reach, shards=(), kind=jnp.bfloat16):
    drawn = spread * jax.random.normal(stream_key, dims, jnp.float32)
    if shards:
        drawn = drawn * level_of(stream_key, dims, shards, -0.22, 0.18)
    return jnp.clip(drawn, -reach, reach).astype(kind)


def bell_draw_with(stream_key, extent, spread, most, pieces, heavy, kind=jnp.bfloat16):
    values = spread * jax.random.normal(stream_key, extent, jnp.float32)
    if pieces:
        values = values * level_of(stream_key, extent, pieces, -0.22, 0.18)
    return jnp.clip(with_spikes(values, jax.random.fold_in(stream_key, 3), *heavy), -most, most).astype(kind)


def setup_inputs(seed: int = 0) -> dict:
    key_list = jax.random.split(jax.random.key(seed), 16)
    return {
        "hidden": bell_draw_with(key_list[0], (ROWS, ROW, D), 1.0, 6.0, ((0, 4), (1, 8)), (1, 2, 8, 2.0)),
        "seg_ids": draw_seg_ids(jax.random.fold_in(key_list[15], 71), 0),
        "pad_mask": draw_pad_mask(jax.random.fold_in(key_list[15], 71), 0),
        "attn_gain": jnp.clip(1.0 + 0.15 * jax.random.normal(key_list[3], (D,), jnp.float32), 0.25, 1.75).astype(jnp.bfloat16),
        "gate_gap": draw_gate_gap(jax.random.fold_in(key_list[15], 71), 0),
        "out_gain": jnp.clip(1.0 + 0.15 * jax.random.normal(key_list[5], (D,), jnp.float32), 0.25, 1.75).astype(jnp.bfloat16),
        "w_query": noise(key_list[6], (D, D), D ** -0.5, 0.125, ((0, 32),)),
        "w_forget": noise(key_list[7], (D, D), D ** -0.5, 0.125, ((0, 32),)),
        "w_input": noise(key_list[8], (D, D), D ** -0.5, 0.125, ((0, 32),)),
        "w_output": noise(key_list[9], (D, D), D ** -0.5, 0.125, ((0, 32),)),
        "ffn_gain": jnp.clip(1.0 + 0.15 * jax.random.normal(key_list[10], (D,), jnp.float32), 0.25, 1.75).astype(jnp.bfloat16),
        "w_gate": noise(key_list[11], (D, FF), D ** -0.5, 0.125, ((0, 32),)),
        "w_up": noise(key_list[12], (D, FF), D ** -0.5, 0.125, ((0, 32),)),
        "w_down": noise(key_list[13], (FF, D), FF ** -0.5, 0.078125, ((0, 32),)),
        "out_grad": bell_draw_with(key_list[14], (ROWS, ROW, D), 1.0, 6.0, ((0, 4), (1, 8)), (1, 2, 8, 2.0)),
    }


EPSILON = 1e-06
STRICT_ARITHMETIC = lax.Precision.HIGHEST

@jax.custom_vjp
def low(v):
    return lax.optimization_barrier(v.astype(jnp.bfloat16)).astype(jnp.float32)

@jax.custom_vjp
def low_back(v):
    return v

def low_keep(v):
    return (low(v), None)

def low_pass(kept, grad):
    return (grad,)

def back_keep(v):
    return (v, None)

def back_low(kept, grad):
    return (low(grad),)
low.defvjp(low_keep, low_pass)
low_back.defvjp(back_keep, back_low)

def rms_scale(value_rows, gain):
    return value_rows * lax.rsqrt(lax.optimization_barrier(jnp.mean(value_rows * value_rows, axis=-1, keepdims=True)) + EPSILON) * gain

def project(left, right):
    return jnp.dot(left, right, precision=STRICT_ARITHMETIC, preferred_element_type=jnp.float32)

def block_step(present_memory, inputs):
    probe_vectors, key_part, log_keep, value_rows, segment, before = inputs
    steps_here = probe_vectors.shape[0]
    prefix_accumulations = jnp.cumsum(log_keep, axis=0)
    centre = prefix_accumulations[steps_here // 2]
    scaled_query = probe_vectors * jnp.exp(prefix_accumulations - centre)
    scaled_key = key_part * jnp.exp(centre - prefix_accumulations)
    scores = jnp.einsum('thk,shk->hts', scaled_query, scaled_key, precision=STRICT_ARITHMETIC)
    places = jnp.arange(steps_here)
    allowed = (places[None, :] <= places[:, None]) & (segment[None, :] == segment[:, None])
    scores = jnp.where(allowed[None], scores, jnp.zeros_like(scores))
    inner_part = jnp.einsum('hts,shv->thv', scores, value_rows, precision=STRICT_ARITHMETIC)
    inherited_flag = (segment == before).astype(probe_vectors.dtype)
    rank_one_update = jnp.einsum('fsl,slu->fsu', probe_vectors * jnp.exp(prefix_accumulations), present_memory, precision=STRICT_ARITHMETIC) * inherited_flag[:, None, None]
    ending = prefix_accumulations[-1]
    tail_ok = (segment == segment[-1]).astype(probe_vectors.dtype)
    segment_ends = key_part * jnp.exp(ending - prefix_accumulations) * tail_ok[:, None, None]
    keep_product = jnp.exp(ending) * (segment[-1] == before).astype(probe_vectors.dtype)
    updated_state = present_memory * keep_product[:, :, None] + jnp.einsum('ufe,ufc->fec', segment_ends, value_rows, precision=STRICT_ARITHMETIC)
    return (updated_state, inner_part + rank_one_update)

def mixer_row(query_pre, forget_pre, input_pre, gate_gap, segment, live_mask):
    row_tokens = query_pre.shape[0]
    head_width = query_pre.shape[1] // HEADS
    probe_vectors = query_pre * jax.nn.sigmoid(query_pre)
    key_part = gate_gap * jax.nn.sigmoid(-forget_pre)
    log_keep = jnp.log1p(-key_part)
    value_rows = input_pre * live_mask[:, None]
    blocks = row_tokens // BLOCK

    def to_blocks(array):
        return array.reshape(blocks, BLOCK, HEADS, head_width)
    earlier = jnp.concatenate([segment[:1], segment[:-1]])
    before = earlier.reshape(blocks, BLOCK)[:, 0]
    initial = jnp.zeros((HEADS, head_width, head_width), probe_vectors.dtype)
    _, mixed_out = lax.scan(jax.checkpoint(block_step), initial, (to_blocks(probe_vectors), to_blocks(key_part), to_blocks(log_keep), to_blocks(value_rows), segment.reshape(blocks, BLOCK), before))
    return mixed_out.reshape(row_tokens, -1)

def row_forward(params, hidden_row, segment, live_mask):
    attn_gain, gate_gap, out_gain, w_query, w_forget, w_input, w_output, ffn_gain, w_gate, w_up, w_down = params
    normed = low(rms_scale(hidden_row, attn_gain))
    query_pre = low_back(project(normed, w_query))
    forget_pre = low_back(project(normed, w_forget))
    input_pre = low_back(project(normed, w_input))
    mixed_out = mixer_row(query_pre, forget_pre, input_pre, gate_gap, segment, live_mask)
    middle = hidden_row + low_back(project(low(rms_scale(mixed_out, out_gain)), w_output))
    second = low(rms_scale(middle, ffn_gain))
    gate_pre = low_back(project(second, w_gate))
    up_pre = low_back(project(second, w_up))
    hidden_units = low(jax.nn.silu(gate_pre) * up_pre)
    return middle + low_back(project(hidden_units, w_down))

def reference(hidden, seg_ids, pad_mask, attn_gain, gate_gap, out_gain, w_query, w_forget, w_input, w_output, ffn_gain, w_gate, w_up, w_down, out_grad):
    params = (attn_gain.astype(jnp.float32), gate_gap.astype(jnp.float32), out_gain.astype(jnp.float32), w_query.astype(jnp.float32), w_forget.astype(jnp.float32), w_input.astype(jnp.float32), w_output.astype(jnp.float32), ffn_gain.astype(jnp.float32), w_gate.astype(jnp.float32), w_up.astype(jnp.float32), w_down.astype(jnp.float32))
    inputs = hidden.astype(jnp.float32)
    live_rows = pad_mask.astype(jnp.float32)

    def whole_block(param_set, input_set):

        def one_row(packed):
            return jax.checkpoint(row_forward)(param_set, packed[0], packed[1], packed[2])
        return lax.map(one_row, (input_set, seg_ids, live_rows))
    outputs, pullback = jax.vjp(whole_block, params, inputs)
    weight_grads, input_grad = pullback(out_grad.astype(jnp.float32))
    return (outputs.astype(jnp.bfloat16), input_grad.astype(jnp.bfloat16), weight_grads[0], weight_grads[1], weight_grads[2], weight_grads[3], weight_grads[4], weight_grads[5], weight_grads[6], weight_grads[7], weight_grads[8], weight_grads[9], weight_grads[10])
```

```python
import functools

import jax
import jax.numpy as jnp
from jax import lax
from jax.experimental import pallas as pl
from jax.experimental.pallas import tpu as pltpu
from jax.sharding import PartitionSpec as P

HEADS = 16
BLOCK = 64
UNROLL = 2
EPSILON = 1e-06
BF = jnp.bfloat16
F32 = jnp.float32


def dot(a, b, dims):
    return lax.dot_general(a, b, (dims, ((), ())), preferred_element_type=F32)


def nn(a, b):
    return dot(a, b, ((1,), (0,)))


def nt(a, b):
    return dot(a, b, ((1,), (1,)))


def tn(a, b):
    return dot(a, b, ((0,), (0,)))


def split_sum(tri, v):
    high = v.astype(BF)
    low = (v - high.astype(F32)).astype(BF)
    return nn(tri, high) + nn(tri, low)


def chunk_prep(qfi, gap, live, width):
    query_pre, forget_pre, input_pre = (
        qfi[:, :width],
        qfi[:, width : 2 * width],
        qfi[:, 2 * width :],
    )
    sig_q = jax.nn.sigmoid(query_pre)
    sig_nf = jax.nn.sigmoid(-forget_pre)
    key = gap * sig_nf
    return query_pre, sig_q, sig_nf, key, input_pre * live


def triangle(lower):
    row = lax.broadcasted_iota(jnp.int32, (BLOCK, BLOCK), 0)
    col = lax.broadcasted_iota(jnp.int32, (BLOCK, BLOCK), 1)
    return (row >= col) if lower else (row <= col)


def chunk_masks(cut):
    row = lax.broadcasted_iota(jnp.int32, (BLOCK, BLOCK), 0)
    col = lax.broadcasted_iota(jnp.int32, (BLOCK, BLOCK), 1)
    allowed = (row >= col) & ((row >= cut) == (col >= cut))
    at = lax.broadcasted_iota(jnp.int32, (BLOCK, 1), 0)
    inherits = (at < cut).astype(F32)
    tail = ((at >= cut) | (cut >= BLOCK)).astype(F32)
    whole = (cut >= BLOCK).astype(F32)
    return allowed, inherits, tail, whole


def mixer_forward_kernel(heads, cut_ref, live_ref, qfi_ref, gap_ref, mixed_ref, square_ref, kept_ref, state):
    step = pl.program_id(0)
    width = heads * 128

    @pl.when(step == 0)
    def _():
        state[...] = jnp.zeros_like(state)

    lower = triangle(True).astype(BF)
    for u in range(UNROLL):
        chunk = step * UNROLL + u
        rows = slice(u * BLOCK, (u + 1) * BLOCK)
        at = lax.broadcasted_iota(jnp.int32, (BLOCK, 1), 0) + chunk * BLOCK
        live = (at < live_ref[0]).astype(F32)
        query_pre, sig_q, sig_nf, key, value = chunk_prep(qfi_ref[rows, :], gap_ref[...], live, width)
        query = query_pre * sig_q
        total = split_sum(lower, jnp.log1p(-key))
        centre = total[BLOCK // 2 : BLOCK // 2 + 1]
        ending = total[BLOCK - 1 :]
        scaled_q = (query * jnp.exp(total - centre)).astype(BF)
        scaled_k = (key * jnp.exp(centre - total)).astype(BF)
        value_low = value.astype(BF)
        allowed, inherits, tail, whole = chunk_masks(cut_ref[chunk])
        value_tail = (value * tail).astype(BF)
        e_centre = jnp.exp(centre)
        e_rest = jnp.exp(ending - centre)
        e_all = jnp.exp(ending) * whole
        square = jnp.zeros((BLOCK, 1), F32)
        for h in range(heads):
            cols = slice(h * 128, (h + 1) * 128)
            before = state[h]
            kept_ref[u, h] = before.astype(BF)
            scores = jnp.where(allowed, nt(scaled_q[:, cols], scaled_k[:, cols]), 0.0)
            inner = nn(scores.astype(BF), value_low[:, cols])
            outer = nt(scaled_q[:, cols], (before * e_centre[:, cols]).astype(BF))
            mixed = inner + outer * inherits
            square = square + jnp.sum(mixed * mixed, axis=1, keepdims=True)
            mixed_ref[rows, cols] = mixed.astype(BF)
            state[h] = before * e_all[:, cols] + tn(value_tail[:, cols], scaled_k[:, cols]) * e_rest[:, cols]
        square_ref[rows, :] = square


def mixer_backward_kernel(heads, cut_ref, live_ref, qfi_ref, gap_ref, kept_ref, grad_ref, out_ref, gap_out_ref, state):
    step = pl.program_id(0)
    last = pl.num_programs(0) - 1
    width = heads * 128

    @pl.when(step == 0)
    def _():
        state[...] = jnp.zeros_like(state)
        gap_out_ref[...] = jnp.zeros_like(gap_out_ref)

    lower = triangle(True).astype(BF)
    upper = triangle(False).astype(BF)
    for u in reversed(range(UNROLL)):
        chunk = (last - step) * UNROLL + u
        rows = slice(u * BLOCK, (u + 1) * BLOCK)
        at = lax.broadcasted_iota(jnp.int32, (BLOCK, 1), 0) + chunk * BLOCK
        live = (at < live_ref[0]).astype(F32)
        gap = gap_ref[...]
        query_pre, sig_q, sig_nf, key, value = chunk_prep(qfi_ref[rows, :], gap, live, width)
        query = query_pre * sig_q
        total = split_sum(lower, jnp.log1p(-key))
        centre = total[BLOCK // 2 : BLOCK // 2 + 1]
        ending = total[BLOCK - 1 :]
        e_q = jnp.exp(total - centre)
        e_k = jnp.exp(centre - total)
        scaled_q = (query * e_q).astype(BF)
        scaled_k = (key * e_k).astype(BF)
        value_low = value.astype(BF)
        allowed, inherits, tail, whole = chunk_masks(cut_ref[chunk])
        value_tail = (value * tail).astype(BF)
        grad = grad_ref[rows, :]
        grad_in = (grad.astype(F32) * inherits).astype(BF)
        e_centre = jnp.exp(centre)
        e_rest = jnp.exp(ending - centre)
        e_all = jnp.exp(ending) * whole
        d_query, d_key, d_value, d_total, d_end = [], [], [], [], []
        for h in range(heads):
            cols = slice(h * 128, (h + 1) * 128)
            before = kept_ref[u, h].astype(F32)
            after = state[h]
            q, k, v, g, gi = scaled_q[:, cols], scaled_k[:, cols], value_low[:, cols], grad[:, cols], grad_in[:, cols]
            vt = value_tail[:, cols]
            scores = jnp.where(allowed, nt(q, k), 0.0).astype(BF)
            d_scores = jnp.where(allowed, nt(g, v), 0.0).astype(BF)
            shifted = (before * e_centre[:, cols]).astype(BF)
            onward = (after * e_rest[:, cols]).astype(BF)
            dq = nn(d_scores, k) + nn(gi, shifted)
            dk_state = nn(vt, onward)
            dk = tn(d_scores, q) + dk_state
            dv = tn(scores, g) + nt(k, onward) * tail
            k32 = k.astype(F32)
            d_total.append(dq * q.astype(F32) - dk * k32)
            d_end.append(
                jnp.sum(after * before, axis=0, keepdims=True) * e_all[:, cols]
                + jnp.sum(dk_state * k32, axis=0, keepdims=True)
            )
            state[h] = after * e_all[:, cols] + tn(gi, q) * e_centre[:, cols]
            d_query.append(dq)
            d_key.append(dk)
            d_value.append(dv)
        d_query = jnp.concatenate(d_query, axis=1) * e_q
        d_key = jnp.concatenate(d_key, axis=1) * e_k
        d_value = jnp.concatenate(d_value, axis=1) * live
        d_log = split_sum(upper, jnp.concatenate(d_total, axis=1)) + jnp.concatenate(d_end, axis=1)
        d_key = d_key - d_log / (1.0 - key)
        gap_out_ref[...] += jnp.sum(d_key * sig_nf, axis=0, keepdims=True)
        out_ref[rows, :width] = (d_query * sig_q * (1.0 + query_pre * (1.0 - sig_q))).astype(BF)
        out_ref[rows, width : 2 * width] = (-d_key * key * (1.0 - sig_nf)).astype(BF)
        out_ref[rows, 2 * width :] = d_value.astype(BF)


def mixer_forward(cut, live, qfi, gap):
    tokens, heads = qfi.shape[0], gap.shape[1] // 128
    width, span = heads * 128, UNROLL * BLOCK
    steps = tokens // span
    return pl.pallas_call(
        functools.partial(mixer_forward_kernel, heads),
        grid_spec=pltpu.PrefetchScalarGridSpec(
            num_scalar_prefetch=2,
            grid=(steps,),
            in_specs=[
                pl.BlockSpec((span, 3 * width), lambda i, *_: (i, 0)),
                pl.BlockSpec((1, width), lambda i, *_: (0, 0)),
            ],
            out_specs=[
                pl.BlockSpec((span, width), lambda i, *_: (i, 0)),
                pl.BlockSpec((span, 1), lambda i, *_: (i, 0)),
                pl.BlockSpec((UNROLL, heads, 128, 128), lambda i, *_: (i, 0, 0, 0)),
            ],
            scratch_shapes=[pltpu.VMEM((heads, 128, 128), F32)],
        ),
        out_shape=[
            jax.ShapeDtypeStruct((tokens, width), BF),
            jax.ShapeDtypeStruct((tokens, 1), F32),
            jax.ShapeDtypeStruct((tokens // BLOCK, heads, 128, 128), BF),
        ],
        cost_estimate=pl.CostEstimate(
            flops=tokens * width * 128 * 10, bytes_accessed=tokens * width * 20, transcendentals=tokens * width * 6
        ),
        name="mixer_forward",
    )(cut, live, qfi, gap)


def mixer_backward(cut, live, qfi, gap, kept, grad):
    tokens, heads = qfi.shape[0], gap.shape[1] // 128
    width, span = heads * 128, UNROLL * BLOCK
    steps = tokens // span
    return pl.pallas_call(
        functools.partial(mixer_backward_kernel, heads),
        grid_spec=pltpu.PrefetchScalarGridSpec(
            num_scalar_prefetch=2,
            grid=(steps,),
            in_specs=[
                pl.BlockSpec((span, 3 * width), lambda i, *_: (steps - 1 - i, 0)),
                pl.BlockSpec((1, width), lambda i, *_: (0, 0)),
                pl.BlockSpec((UNROLL, heads, 128, 128), lambda i, *_: (steps - 1 - i, 0, 0, 0)),
                pl.BlockSpec((span, width), lambda i, *_: (steps - 1 - i, 0)),
            ],
            out_specs=[
                pl.BlockSpec((span, 3 * width), lambda i, *_: (steps - 1 - i, 0)),
                pl.BlockSpec((1, width), lambda i, *_: (0, 0)),
            ],
            scratch_shapes=[pltpu.VMEM((heads, 128, 128), F32)],
        ),
        out_shape=[
            jax.ShapeDtypeStruct((tokens, 3 * width), BF),
            jax.ShapeDtypeStruct((1, width), F32),
        ],
        cost_estimate=pl.CostEstimate(
            flops=tokens * width * 128 * 24, bytes_accessed=tokens * width * 28, transcendentals=tokens * width * 6
        ),
        name="mixer_backward",
    )(cut, live, qfi, gap, kept, grad)


def gather_seq(v):
    return lax.all_gather(v, "seq", axis=0, tiled=True)


def scatter_seq(v):
    return lax.psum_scatter(v, "seq", scatter_dimension=0, tiled=True).astype(F32)


def gather_dp(v):
    return lax.all_gather(v, "dp", axis=0, tiled=True)


def scatter_dp(v):
    return lax.psum_scatter(v, "dp", scatter_dimension=0, tiled=True)


def swap_seq(v):
    return lax.all_to_all(v, "seq", split_axis=0, concat_axis=0, tiled=True)


def inverse_rms(square_mean):
    return lax.rsqrt(square_mean + EPSILON)


def on_device(
    hidden,
    seg_ids,
    pad_mask,
    attn_gain,
    gate_gap,
    out_gain,
    w_query,
    w_forget,
    w_input,
    w_output,
    ffn_gain,
    w_gate,
    w_up,
    w_down,
    out_grad,
):
    planes, ranks = lax.axis_size("dp"), lax.axis_size("seq")
    row_tokens, model = hidden.shape[1:]
    rows = w_query.shape[0]
    units_in = w_down.shape[0]
    head = model // HEADS
    span = head // rows
    per_rank, groups = planes // span, ranks // span
    channels = per_rank * head
    units = planes * units_in
    tokens = ranks * row_tokens
    members = [[a * span + m for m in range(span)] for a in range(groups)]

    def to_heads(w):
        parts = w.reshape(rows, span, per_rank, groups, head)
        return parts.transpose(3, 1, 0, 2, 4).reshape(ranks, rows, channels)

    def from_heads(parts):
        parts = parts.reshape(groups, span, rows, per_rank, head)
        return parts.transpose(2, 1, 3, 0, 4).reshape(rows, model)

    def to_units(w):
        parts = w.reshape(rows, planes, ranks, units_in)
        return parts.transpose(2, 0, 1, 3).reshape(ranks, rows, units)

    def from_units(parts):
        parts = parts.reshape(ranks, rows, planes, units_in)
        return parts.transpose(1, 2, 0, 3).reshape(rows, planes * ranks * units_in)

    def own_rows(v):
        return v.reshape((span, per_rank) + v.shape[1:])

    def swap_group(v):
        return lax.all_to_all(v, "seq", split_axis=0, concat_axis=0, axis_index_groups=members)

    gain_a, gain_o, gain_f = (g.astype(F32)[:, None] for g in (attn_gain, out_gain, ffn_gain))

    def fold(gain, w):
        return (gain * w.astype(F32)).astype(BF)

    qfi_part = jnp.concatenate([to_heads(fold(gain_a, w)) for w in (w_query, w_forget, w_input)], axis=2)
    qfi_full = gather_dp(swap_seq(qfi_part).reshape(ranks * rows, 3 * channels))
    gap_pieces = lax.all_gather(gate_gap, "dp", axis=0)
    gap_own = swap_group(own_rows(gap_pieces)).transpose(1, 0, 2).reshape(1, channels).astype(F32)
    out_pieces = lax.all_gather(fold(gain_o, w_output), "dp", axis=0)
    out_own = swap_group(own_rows(out_pieces)).transpose(1, 0, 2, 3).reshape(channels, model)
    gu_part = jnp.concatenate([to_units(fold(gain_f, w)) for w in (w_gate, w_up)], axis=2)
    gu_full = gather_dp(swap_seq(gu_part).reshape(ranks * rows, 2 * units))
    down_own = gather_dp(w_down)

    ids = lax.all_gather(jnp.concatenate([seg_ids, pad_mask], axis=0), "seq", axis=0)
    segment = ids[:, 0].reshape(tokens // BLOCK, BLOCK)
    live = jnp.sum(ids[:, 1]).reshape(1)
    ends = segment[:, -1]
    before = jnp.concatenate([segment[:1, 0], ends[:-1]])
    cut = jnp.sum((segment == before[:, None]).astype(jnp.int32), axis=1)

    x = hidden[0].astype(F32)
    factor_x = inverse_rms(jnp.mean(x * x, axis=1, keepdims=True))
    normed_x = x * factor_x
    n1 = gather_seq(normed_x.astype(BF))
    qfi = nn(n1, qfi_full)
    mixed, square, kept = mixer_forward(cut, live, qfi, gap_own)
    square_all = lax.psum_scatter(square, "seq", scatter_dimension=0, tiled=True)
    factor_o = inverse_rms(square_all / model)
    attn_out = factor_o * scatter_seq(nn(mixed, out_own).astype(BF))
    middle = x + attn_out
    factor_m = inverse_rms(jnp.mean(middle * middle, axis=1, keepdims=True))
    normed_m = middle * factor_m
    n2 = gather_seq(normed_m.astype(BF))
    gate_up = nn(n2, gu_full)
    gate, up = gate_up[:, :units], gate_up[:, units:]
    sig_g = jax.nn.sigmoid(gate)
    act = gate * sig_g
    hidden_units = (act * up).astype(BF)
    block_out = middle + scatter_seq(nn(hidden_units, down_own).astype(BF))

    grad_all = gather_seq(out_grad[0])
    d_units = nt(grad_all, down_own)
    grad_down = tn(hidden_units, grad_all).astype(BF)
    d_gate = (d_units * up * sig_g * (1.0 + gate * (1.0 - sig_g))).astype(BF)
    d_up = (d_units * act).astype(BF)
    d_gu = jnp.concatenate([d_gate, d_up], axis=1)
    grad_gu = tn(n2, d_gu).astype(BF)
    d_n2 = scatter_seq(nt(d_gu, gu_full).astype(BF))
    d_middle = out_grad[0].astype(F32) + factor_m * (
        d_n2 - normed_m * jnp.mean(d_n2 * normed_m, axis=1, keepdims=True)
    )
    mean_o = jnp.mean(d_middle * attn_out, axis=1, keepdims=True)
    d_attn = gather_seq((factor_o * d_middle).astype(BF))
    beta = gather_seq(factor_o * factor_o * mean_o)
    grad_out = tn(mixed, d_attn).astype(BF)
    d_mixed = (nt(d_attn, out_own) - beta * mixed.astype(F32)).astype(BF)
    d_qfi, gap_grad = mixer_backward(cut, live, qfi, gap_own, kept, d_mixed)
    grad_qfi = tn(n1, d_qfi).astype(BF)
    d_n1 = scatter_seq(nt(d_qfi, qfi_full).astype(BF))
    hidden_grad = d_middle + factor_x * (d_n1 - normed_x * jnp.mean(d_n1 * normed_x, axis=1, keepdims=True))

    g_down = scatter_dp(grad_down).astype(F32)
    gu_rows = swap_seq(scatter_dp(grad_gu)).reshape(ranks, rows, 2 * units).astype(F32)
    gate_rows, up_rows = from_units(gu_rows[:, :, :units]), from_units(gu_rows[:, :, units:])
    out_back = grad_out.reshape(per_rank, span, rows, model).transpose(1, 0, 2, 3)
    out_back = swap_group(out_back).reshape(planes * rows, model)
    out_rows = scatter_dp(out_back).astype(F32)
    gap_back = swap_group(gap_grad.reshape(per_rank, span, rows).transpose(1, 0, 2)).reshape(planes * rows)
    g_gap = scatter_dp(gap_back)
    qfi_rows = swap_seq(scatter_dp(grad_qfi)).reshape(ranks, rows, 3 * channels).astype(F32)
    q_rows, f_rows, i_rows = (from_heads(qfi_rows[:, :, j * channels : (j + 1) * channels]) for j in range(3))

    def rowdot(w, g):
        return jnp.sum(w.astype(F32) * g, axis=1)

    g_attn_gain = rowdot(w_query, q_rows) + rowdot(w_forget, f_rows) + rowdot(w_input, i_rows)
    g_ffn_gain = rowdot(w_gate, gate_rows) + rowdot(w_up, up_rows)
    g_out_gain = rowdot(w_output, out_rows)
    return (
        block_out[None].astype(BF),
        hidden_grad[None].astype(BF),
        g_attn_gain,
        g_gap,
        g_out_gain,
        gain_a * q_rows,
        gain_a * f_rows,
        gain_a * i_rows,
        gain_o * out_rows,
        g_ffn_gain,
        gain_f * gate_rows,
        gain_f * up_rows,
        g_down,
    )


def solution(mesh):
    tok, row, both = P("dp", "seq", None), P("dp", "seq"), P(("dp", "seq"))
    mat = P(("dp", "seq"), None)
    return jax.shard_map(
        on_device,
        mesh=mesh,
        in_specs=(tok, row, row, both, both, both, mat, mat, mat, mat, both, mat, mat, mat, tok),
        out_specs=(tok, tok, both, both, both, mat, mat, mat, mat, both, mat, mat, mat),
        check_vma=False,
    )
```

```python
import functools

import jax
import jax.numpy as jnp
from jax import lax
from jax.experimental import pallas as pl
from jax.experimental.pallas import tpu as pltpu
from jax.sharding import PartitionSpec as P

HEADS = 16
BLOCK = 64
UNROLL = 2
EPSILON = 1e-06
EXTRA = 128
BF = jnp.bfloat16
F32 = jnp.float32


def dot(a, b, dims):
    return lax.dot_general(a, b, (dims, ((), ())), preferred_element_type=F32)


def nn(a, b):
    return dot(a, b, ((1,), (0,)))


def nt(a, b):
    return dot(a, b, ((1,), (1,)))


def tn(a, b):
    return dot(a, b, ((0,), (0,)))


def split_sum(tri, v):
    high = v.astype(BF)
    low = (v - high.astype(F32)).astype(BF)
    return nn(tri, high) + nn(tri, low)


def chunk_prep(qfi, gap, live, width):
    query_pre, forget_pre, input_pre = (
        qfi[:, :width],
        qfi[:, width : 2 * width],
        qfi[:, 2 * width :],
    )
    sig_q = jax.nn.sigmoid(query_pre)
    sig_nf = jax.nn.sigmoid(-forget_pre)
    key = gap * sig_nf
    return query_pre, sig_q, sig_nf, key, input_pre * live


def triangle(lower):
    row = lax.broadcasted_iota(jnp.int32, (BLOCK, BLOCK), 0)
    col = lax.broadcasted_iota(jnp.int32, (BLOCK, BLOCK), 1)
    return (row >= col) if lower else (row <= col)


def chunk_masks(cut):
    row = lax.broadcasted_iota(jnp.int32, (BLOCK, BLOCK), 0)
    col = lax.broadcasted_iota(jnp.int32, (BLOCK, BLOCK), 1)
    allowed = (row >= col) & ((row >= cut) == (col >= cut))
    at = lax.broadcasted_iota(jnp.int32, (BLOCK, 1), 0)
    inherits = (at < cut).astype(F32)
    tail = ((at >= cut) | (cut >= BLOCK)).astype(F32)
    whole = (cut >= BLOCK).astype(F32)
    return allowed, inherits, tail, whole


def mixer_forward_kernel(heads, cut_ref, live_ref, qfi_ref, gap_ref, mixed_ref, kept_ref, state):
    step = pl.program_id(0)
    width = heads * 128

    @pl.when(step == 0)
    def _():
        state[...] = jnp.zeros_like(state)

    lower = triangle(True).astype(BF)
    for u in range(UNROLL):
        chunk = step * UNROLL + u
        rows = slice(u * BLOCK, (u + 1) * BLOCK)
        at = lax.broadcasted_iota(jnp.int32, (BLOCK, 1), 0) + chunk * BLOCK
        live = (at < live_ref[0]).astype(F32)
        query_pre, sig_q, sig_nf, key, value = chunk_prep(qfi_ref[rows, :], gap_ref[...], live, width)
        query = query_pre * sig_q
        total = split_sum(lower, jnp.log1p(-key))
        centre = total[BLOCK // 2 : BLOCK // 2 + 1]
        ending = total[BLOCK - 1 :]
        scaled_q = (query * jnp.exp(total - centre)).astype(BF)
        scaled_k = (key * jnp.exp(centre - total)).astype(BF)
        value_low = value.astype(BF)
        allowed, inherits, tail, whole = chunk_masks(cut_ref[chunk])
        value_tail = (value * tail).astype(BF)
        e_centre = jnp.exp(centre)
        e_rest = jnp.exp(ending - centre)
        e_all = jnp.exp(ending) * whole
        square = jnp.zeros((BLOCK, 1), F32)
        for h in range(heads):
            cols = slice(h * 128, (h + 1) * 128)
            before = state[h]
            kept_ref[u, h] = before.astype(BF)
            scores = jnp.where(allowed, nt(scaled_q[:, cols], scaled_k[:, cols]), 0.0)
            inner = nn(scores.astype(BF), value_low[:, cols])
            outer = nt(scaled_q[:, cols], (before * e_centre[:, cols]).astype(BF))
            mixed = inner + outer * inherits
            square = square + jnp.sum(mixed * mixed, axis=1, keepdims=True)
            mixed_ref[rows, cols] = mixed.astype(BF)
            state[h] = before * e_all[:, cols] + tn(value_tail[:, cols], scaled_k[:, cols]) * e_rest[:, cols]
        lane = lax.broadcasted_iota(jnp.int32, (BLOCK, EXTRA), 1)
        high = square.astype(BF).astype(F32)
        mixed_ref[rows, width:] = jnp.where(lane == 0, high, jnp.where(lane == 1, square - high, 0.0)).astype(BF)


def mixer_backward_kernel(heads, cut_ref, live_ref, qfi_ref, gap_ref, kept_ref, grad_ref, out_ref, gap_out_ref, state):
    step = pl.program_id(0)
    last = pl.num_programs(0) - 1
    width = heads * 128

    @pl.when(step == 0)
    def _():
        state[...] = jnp.zeros_like(state)
        gap_out_ref[...] = jnp.zeros_like(gap_out_ref)

    lower = triangle(True).astype(BF)
    upper = triangle(False).astype(BF)
    for u in reversed(range(UNROLL)):
        chunk = (last - step) * UNROLL + u
        rows = slice(u * BLOCK, (u + 1) * BLOCK)
        at = lax.broadcasted_iota(jnp.int32, (BLOCK, 1), 0) + chunk * BLOCK
        live = (at < live_ref[0]).astype(F32)
        gap = gap_ref[...]
        query_pre, sig_q, sig_nf, key, value = chunk_prep(qfi_ref[rows, :], gap, live, width)
        query = query_pre * sig_q
        total = split_sum(lower, jnp.log1p(-key))
        centre = total[BLOCK // 2 : BLOCK // 2 + 1]
        ending = total[BLOCK - 1 :]
        e_q = jnp.exp(total - centre)
        e_k = jnp.exp(centre - total)
        scaled_q = (query * e_q).astype(BF)
        scaled_k = (key * e_k).astype(BF)
        value_low = value.astype(BF)
        allowed, inherits, tail, whole = chunk_masks(cut_ref[chunk])
        value_tail = (value * tail).astype(BF)
        grad = grad_ref[rows, :]
        grad_in = (grad.astype(F32) * inherits).astype(BF)
        e_centre = jnp.exp(centre)
        e_rest = jnp.exp(ending - centre)
        e_all = jnp.exp(ending) * whole
        d_query, d_key, d_value, d_total, d_end = [], [], [], [], []
        for h in range(heads):
            cols = slice(h * 128, (h + 1) * 128)
            before = kept_ref[u, h].astype(F32)
            after = state[h]
            q, k, v, g, gi = scaled_q[:, cols], scaled_k[:, cols], value_low[:, cols], grad[:, cols], grad_in[:, cols]
            vt = value_tail[:, cols]
            scores = jnp.where(allowed, nt(q, k), 0.0).astype(BF)
            d_scores = jnp.where(allowed, nt(g, v), 0.0).astype(BF)
            shifted = (before * e_centre[:, cols]).astype(BF)
            onward = (after * e_rest[:, cols]).astype(BF)
            dq = nn(d_scores, k) + nn(gi, shifted)
            dk_state = nn(vt, onward)
            dk = tn(d_scores, q) + dk_state
            dv = tn(scores, g) + nt(k, onward) * tail
            k32 = k.astype(F32)
            d_total.append(dq * q.astype(F32) - dk * k32)
            d_end.append(
                jnp.sum(after * before, axis=0, keepdims=True) * e_all[:, cols]
                + jnp.sum(dk_state * k32, axis=0, keepdims=True)
            )
            state[h] = after * e_all[:, cols] + tn(gi, q) * e_centre[:, cols]
            d_query.append(dq)
            d_key.append(dk)
            d_value.append(dv)
        d_query = jnp.concatenate(d_query, axis=1) * e_q
        d_key = jnp.concatenate(d_key, axis=1) * e_k
        d_value = jnp.concatenate(d_value, axis=1) * live
        d_log = split_sum(upper, jnp.concatenate(d_total, axis=1)) + jnp.concatenate(d_end, axis=1)
        d_key = d_key - d_log / (1.0 - key)
        gap_out_ref[...] += jnp.sum(d_key * sig_nf, axis=0, keepdims=True)
        out_ref[rows, :width] = (d_query * sig_q * (1.0 + query_pre * (1.0 - sig_q))).astype(BF)
        out_ref[rows, width : 2 * width] = (-d_key * key * (1.0 - sig_nf)).astype(BF)
        out_ref[rows, 2 * width :] = d_value.astype(BF)


def mixer_forward(cut, live, qfi, gap):
    tokens, heads = qfi.shape[0], gap.shape[1] // 128
    width, span = heads * 128, UNROLL * BLOCK
    steps = tokens // span
    return pl.pallas_call(
        functools.partial(mixer_forward_kernel, heads),
        grid_spec=pltpu.PrefetchScalarGridSpec(
            num_scalar_prefetch=2,
            grid=(steps,),
            in_specs=[
                pl.BlockSpec((span, 3 * width), lambda i, *_: (i, 0)),
                pl.BlockSpec((1, width), lambda i, *_: (0, 0)),
            ],
            out_specs=[
                pl.BlockSpec((span, width + EXTRA), lambda i, *_: (i, 0)),
                pl.BlockSpec((UNROLL, heads, 128, 128), lambda i, *_: (i, 0, 0, 0)),
            ],
            scratch_shapes=[pltpu.VMEM((heads, 128, 128), F32)],
        ),
        out_shape=[
            jax.ShapeDtypeStruct((tokens, width + EXTRA), BF),
            jax.ShapeDtypeStruct((tokens // BLOCK, heads, 128, 128), BF),
        ],
        cost_estimate=pl.CostEstimate(
            flops=tokens * width * 128 * 10, bytes_accessed=tokens * width * 20, transcendentals=tokens * width * 6
        ),
        name="mixer_forward",
    )(cut, live, qfi, gap)


def mixer_backward(cut, live, qfi, gap, kept, grad):
    tokens, heads = qfi.shape[0], gap.shape[1] // 128
    width, span = heads * 128, UNROLL * BLOCK
    steps = tokens // span
    return pl.pallas_call(
        functools.partial(mixer_backward_kernel, heads),
        grid_spec=pltpu.PrefetchScalarGridSpec(
            num_scalar_prefetch=2,
            grid=(steps,),
            in_specs=[
                pl.BlockSpec((span, 3 * width), lambda i, *_: (steps - 1 - i, 0)),
                pl.BlockSpec((1, width), lambda i, *_: (0, 0)),
                pl.BlockSpec((UNROLL, heads, 128, 128), lambda i, *_: (steps - 1 - i, 0, 0, 0)),
                pl.BlockSpec((span, width), lambda i, *_: (steps - 1 - i, 0)),
            ],
            out_specs=[
                pl.BlockSpec((span, 3 * width), lambda i, *_: (steps - 1 - i, 0)),
                pl.BlockSpec((1, width), lambda i, *_: (0, 0)),
            ],
            scratch_shapes=[pltpu.VMEM((heads, 128, 128), F32)],
        ),
        out_shape=[
            jax.ShapeDtypeStruct((tokens, 3 * width), BF),
            jax.ShapeDtypeStruct((1, width), F32),
        ],
        cost_estimate=pl.CostEstimate(
            flops=tokens * width * 128 * 24, bytes_accessed=tokens * width * 28, transcendentals=tokens * width * 6
        ),
        name="mixer_backward",
    )(cut, live, qfi, gap, kept, grad)


MESH = pl.DeviceIdType.MESH
PIECES = 5
VMEM_LIMIT = 60 * 1024 * 1024
(S_X, S_Y, S_CORE, S_DIAG_Y, S_DIAG_X, S_CORE_X, S_CORE_Y, S_CORE_D, R_CORE, R_X, R_Y, R_LAST_Y, R_LAST_X, KINDS) = range(14)


class Place:
    def __init__(self):
        self.plane = lax.axis_index("dp")
        me = lax.axis_index("seq")
        self.me = me
        self.core = me % 2
        self.x = (me // 2) % 2
        self.y = me // 4

    def rank(self, fy=0, fx=0, fc=0):
        y = 1 - self.y if fy else self.y
        x = 1 - self.x if fx else self.x
        core = 1 - self.core if fc else self.core
        return 4 * y + 2 * x + core

    def device(self, fy=0, fx=0, fc=0):
        return (self.plane, self.rank(fy, fx, fc))


def greet(place):
    barrier = pltpu.get_barrier_semaphore()
    for flip in ((0, 0, 1), (0, 1, 0), (1, 0, 0)):
        pl.semaphore_signal(barrier, inc=1, device_id=place.device(*flip), device_id_type=MESH)
    pl.semaphore_wait(barrier, 3)


def remote(src, dst, sems, kind, b, device):
    send, recv = sems
    return pltpu.make_async_remote_copy(
        src_ref=src,
        dst_ref=dst,
        send_sem=send.at[kind, b],
        recv_sem=recv.at[kind, b],
        device_id=device,
        device_id_type=MESH,
    )


class Gather:
    def __init__(self, place, own, full, sems, local_sem):
        self.p, self.own, self.full, self.sems, self.local = place, own, full, sems, local_sem
        self.half = full.shape[2] // 2

    def keep(self, b):
        return pltpu.make_async_copy(self.own.at[b], self.full.at[self.p.me, b], self.local.at[b])

    def first(self, b):
        p, dst = self.p, self.full.at[self.p.me, b]
        return [
            remote(self.own.at[b], dst, self.sems, S_X, b, p.device(0, 1, 0)),
            remote(self.own.at[b], dst, self.sems, S_Y, b, p.device(1, 0, 0)),
            remote(self.own.at[b], dst, self.sems, S_CORE, b, p.device(0, 0, 1)),
        ]

    def second(self, b):
        p, h = self.p, self.half
        from_x, from_y = self.full.at[p.rank(0, 1, 0), b], self.full.at[p.rank(1, 0, 0), b]
        up, down = from_x.at[pl.ds(0, h)], from_y.at[pl.ds(h, h)]
        return [
            remote(up, up, self.sems, S_DIAG_Y, b, p.device(1, 0, 0)),
            remote(down, down, self.sems, S_DIAG_X, b, p.device(0, 1, 0)),
            remote(from_x, from_x, self.sems, S_CORE_X, b, p.device(0, 0, 1)),
            remote(from_y, from_y, self.sems, S_CORE_Y, b, p.device(0, 0, 1)),
        ]

    def third(self, b):
        p = self.p
        block = self.full.at[p.rank(1, 1, 0), b]
        return [remote(block, block, self.sems, S_CORE_D, b, p.device(0, 0, 1))]

    def arrived(self, kind, b, flips, rows=None):
        block = self.full.at[self.p.rank(*flips), b]
        if rows is not None:
            block = block.at[pl.ds(rows * self.half, self.half)]
        remote(block, block, self.sems, kind, b, self.p.device(0, 0, 1)).wait_recv()

    def start(self, b):
        self.keep(b).start()
        for copy in self.first(b):
            copy.start()

    def forward(self, b):
        self.arrived(S_X, b, (0, 1, 0))
        self.arrived(S_Y, b, (1, 0, 0))
        for copy in self.second(b):
            copy.start()

    def forward_last(self, b):
        self.arrived(S_DIAG_Y, b, (1, 1, 0), 0)
        self.arrived(S_DIAG_X, b, (1, 1, 0), 1)
        for copy in self.third(b):
            copy.start()

    def finish(self, b):
        self.arrived(S_CORE, b, (0, 0, 1))
        self.arrived(S_CORE_X, b, (0, 1, 1))
        self.arrived(S_CORE_Y, b, (1, 0, 1))
        self.arrived(S_CORE_D, b, (1, 1, 1))

    def drain(self, b):
        self.keep(b).wait()
        for copy in self.first(b) + self.second(b) + self.third(b):
            copy.wait_send()


def swap_starts(place, parts, outs, send, recv, local):
    copies = []
    for i, (part, out) in enumerate(zip(parts, outs)):
        own = pltpu.make_async_copy(part.at[place.me], out.at[place.me], local.at[i])
        own.start()
        for k, flips in enumerate(((0, 0, 1), (0, 1, 0), (1, 0, 0), (0, 1, 1), (1, 0, 1), (1, 1, 0), (1, 1, 1))):
            copy = pltpu.make_async_remote_copy(
                src_ref=part.at[place.rank(*flips)],
                dst_ref=out.at[place.me],
                send_sem=send.at[i, k],
                recv_sem=recv.at[i, k],
                device_id=place.device(*flips),
                device_id_type=MESH,
            )
            copy.start()
            there = out.at[place.rank(*flips)]
            copies.append((copy, pltpu.make_async_remote_copy(
                src_ref=there, dst_ref=there, send_sem=send.at[i, k], recv_sem=recv.at[i, k],
                device_id=place.device(*flips), device_id_type=MESH)))
        copies.append((own, None))
    return copies


def swap_waits(copies):
    for copy, arrival in copies:
        if arrival is None:
            copy.wait()
        else:
            copy.wait_send()
            arrival.wait_recv()


def greet_all(place):
    barrier = pltpu.get_barrier_semaphore()
    for flips in ((0, 0, 1), (0, 1, 0), (1, 0, 0), (0, 1, 1), (1, 0, 1), (1, 1, 0), (1, 1, 1)):
        pl.semaphore_signal(barrier, inc=1, device_id=place.device(*flips), device_id_type=MESH)
    pl.semaphore_wait(barrier, 7)


def swap_plane(parts, collective_id):
    count = len(parts)

    def kernel(*refs):
        ins, outs, (send, recv, local) = refs[:count], refs[count : 2 * count], refs[2 * count :]
        place = Place()
        greet_all(place)
        swap_waits(swap_starts(place, ins, outs, send, recv, local))

    any_spec = pl.BlockSpec(memory_space=pl.ANY)
    return pl.pallas_call(
        kernel,
        in_specs=[any_spec] * count,
        out_specs=[any_spec] * count,
        out_shape=[jax.ShapeDtypeStruct(p.shape, p.dtype) for p in parts],
        scratch_shapes=[
            pltpu.SemaphoreType.DMA((count, 7)),
            pltpu.SemaphoreType.DMA((count, 7)),
            pltpu.SemaphoreType.DMA((count,)),
        ],
        compiler_params=pltpu.CompilerParams(collective_id=collective_id, has_side_effects=True),
        name="swap_plane",
    )(*parts)


def gather_plane(own, parts, collective_id):
    tokens, width = own.shape
    rows = tokens // PIECES
    own = own.reshape(PIECES, rows, width)
    count = len(parts)

    def kernel(own_ref, *refs):
        ins, full, outs = refs[:count], refs[count], refs[count + 1 : 2 * count + 1]
        send, recv, local, swap_send, swap_recv, swap_local = refs[2 * count + 1 :]
        place = Place()
        greet_all(place)
        gather = Gather(place, own_ref, full, (send, recv), local)
        for b in range(PIECES):
            gather.start(b)
        for b in range(PIECES):
            gather.forward(b)
        copies = swap_starts(place, ins, outs, swap_send, swap_recv, swap_local)
        for b in range(PIECES):
            gather.forward_last(b)
        for b in range(PIECES):
            gather.finish(b)
        swap_waits(copies)
        for b in range(PIECES):
            gather.drain(b)

    any_spec = pl.BlockSpec(memory_space=pl.ANY)
    results = pl.pallas_call(
        kernel,
        in_specs=[any_spec] * (1 + count),
        out_specs=[any_spec] * (1 + count),
        out_shape=[jax.ShapeDtypeStruct((8, PIECES, rows, width), own.dtype)]
        + [jax.ShapeDtypeStruct(p.shape, p.dtype) for p in parts],
        scratch_shapes=[
            pltpu.SemaphoreType.DMA((KINDS, PIECES)),
            pltpu.SemaphoreType.DMA((KINDS, PIECES)),
            pltpu.SemaphoreType.DMA((PIECES,)),
            pltpu.SemaphoreType.DMA((max(count, 1), 7)),
            pltpu.SemaphoreType.DMA((max(count, 1), 7)),
            pltpu.SemaphoreType.DMA((max(count, 1),)),
        ],
        compiler_params=pltpu.CompilerParams(collective_id=collective_id, has_side_effects=True),
        name="gather_plane",
    )(own, *parts)
    return results[0].reshape(8 * tokens, width), results[1:]


def product_scatter(left, weight, transposed, stats, epilogue, owned, outs, gathered, collective_id):
    tokens = left.shape[0] // 8
    rows = tokens // PIECES
    depth = weight.shape[1] if transposed else weight.shape[0]
    width = weight.shape[0] if transposed else weight.shape[1]
    half = width // 2
    extra = EXTRA if stats else 0
    right = half + extra
    columns = left.shape[1]
    left = left.reshape(8, PIECES, rows, columns)
    tile = 256

    def kernel(*refs):
        refs = list(refs)
        left_ref, weight_ref = refs.pop(0), refs.pop(0)
        own_refs = [refs.pop(0) for _ in owned]
        out_refs = [refs.pop(0) for _ in outs]
        full_ref = refs.pop(0) if gathered else None
        (x_buf, w_buf, core_out, core_in, total, x_out, x_in, y_out, y_in, keep_a, keep_b, done_a, done_b, last_y_out, last_y_in,
         last_x_out, last_x_in, send, recv, load_sem, w_sem) = refs[:21]
        refs = refs[21:]
        place = Place()
        sems = (send, recv)

        def loads(b):
            copies = []
            for j in range(4):
                copies.append(pltpu.make_async_copy(left_ref.at[2 * j + 1 - place.core, b], x_buf.at[b, j], load_sem.at[b]))
                copies.append(pltpu.make_async_copy(left_ref.at[2 * j + place.core, b], x_buf.at[b, 4 + j], load_sem.at[b]))
            return copies

        w_copy = pltpu.make_async_copy(weight_ref, w_buf, w_sem.at[0])
        w_copy.start()
        for b in range(PIECES):
            for copy in loads(b):
                copy.start()
        greet(place)
        if gathered:
            n_buf, keep_sem = refs
            gather = Gather(place, n_buf, full_ref, sems, keep_sem)

        def send_core(b):
            return remote(core_out.at[b], core_in.at[b], sems, R_CORE, b, place.device(0, 0, 1))

        def send_x(b):
            return remote(x_out.at[b], x_in.at[b], sems, R_X, b, place.device(0, 1, 0))

        def send_y(b):
            return remote(y_out.at[b], y_in.at[b], sems, R_Y, b, place.device(1, 0, 0))

        def send_last_y(b):
            return remote(last_y_out.at[b], last_y_in.at[b], sems, R_LAST_Y, b, place.device(1, 0, 0))

        def send_last_x(b):
            return remote(last_x_out.at[b], last_x_in.at[b], sems, R_LAST_X, b, place.device(0, 1, 0))

        def produce(b):
            pltpu.make_async_copy(x_buf.at[b], x_buf.at[b], load_sem.at[b]).wait()

            @pl.loop(0, width // tile)
            def _(t):
                at = pl.multiple_of(t * tile, tile)
                lhs = x_buf[b, :, :, :depth].reshape(8 * rows, depth)
                if transposed:
                    out = nt(lhs, w_buf[pl.ds(at, tile), :])
                else:
                    out = nn(lhs, w_buf[:, pl.ds(at, tile)])
                core_out[b, :, :, pl.ds(at, tile)] = out[: 4 * rows].astype(BF).reshape(4, rows, tile)
                total[:, :, pl.ds(at, tile)] = out[4 * rows :].reshape(4, rows, tile)

            if stats:
                core_out[b, :, :, width:] = x_buf[b, :4, :, depth:]
                total[:, :, width:] = x_buf[b, 4:, :, depth:].astype(F32)
            send_core(b).start()

        def stage_one(b):
            send_core(b).wait_recv()
            for i in range(2):
                go, stay = 2 * i + 1 - place.x, 2 * i + place.x
                x_out[b, i] = (total[go, :, :half] + core_in[b, go, :, :half].astype(F32)).astype(BF)
                keep_a[i] = total[stay, :, :half] + core_in[b, stay, :, :half].astype(F32)
            send_x(b).start()
            for i in range(2):
                go, stay = 2 * (1 - place.y) + i, 2 * place.y + i
                y_out[b, i] = (total[go, :, half:] + core_in[b, go, :, half:].astype(F32)).astype(BF)
                keep_b[i] = total[stay, :, half:] + core_in[b, stay, :, half:].astype(F32)
            send_y(b).start()

        def stage_two(b):
            send_x(b).wait_recv()
            go, stay = 1 - place.y, place.y
            last_y_out[b] = (keep_a[go] + x_in[b, go].astype(F32)).astype(BF)
            send_last_y(b).start()
            done_a[...] = keep_a[stay] + x_in[b, stay].astype(F32)
            send_y(b).wait_recv()
            go, stay = 1 - place.x, place.x
            last_x_out[b] = (keep_b[go] + y_in[b, go].astype(F32)).astype(BF)
            send_last_x(b).start()
            done_b[...] = keep_b[stay] + y_in[b, stay].astype(F32)

        def stage_three(b):
            send_last_y(b).wait_recv()
            send_last_x(b).wait_recv()
            low = done_a[...] + last_y_in[b].astype(F32)
            high = done_b[...] + last_x_in[b].astype(F32)
            result = jnp.concatenate([low, high[:, :half]], axis=1)
            stat = high[:, half:] if stats else None
            written, sent = epilogue(result, stat, *[r[b] for r in own_refs])
            for ref, value in zip(out_refs, written):
                ref[b] = value
            if gathered:
                n_buf[b] = sent
                gather.start(b)

        w_copy.wait()

        def guarded(body, b):
            @pl.when((b >= 0) & (b < PIECES))
            def _():
                body(b)

        @pl.loop(0, PIECES + (6 if gathered else 3))
        def _(step):
            guarded(stage_three, step - 3)
            guarded(stage_two, step - 2)
            guarded(stage_one, step - 1)
            guarded(produce, step)
            if gathered:
                guarded(gather.forward, step - 4)
                guarded(gather.forward_last, step - 5)

        @pl.loop(0, PIECES)
        def _(b):
            if gathered:
                gather.finish(b)
                gather.drain(b)
            for copy in (send_core, send_x, send_y, send_last_y, send_last_x):
                copy(b).wait_send()

    any_spec, vmem = pl.BlockSpec(memory_space=pl.ANY), pl.BlockSpec(memory_space=pltpu.VMEM)
    out_shape = [jax.ShapeDtypeStruct((PIECES, rows, c), d) for c, d in outs]
    out_specs = [vmem] * len(outs)
    scratch = [
        pltpu.VMEM((PIECES, 8, rows, columns), BF),
        pltpu.VMEM(weight.shape, BF),
        pltpu.VMEM((PIECES, 4, rows, width + extra), BF),
        pltpu.VMEM((PIECES, 4, rows, width + extra), BF),
        pltpu.VMEM((4, rows, width + extra), F32),
        pltpu.VMEM((PIECES, 2, rows, half), BF),
        pltpu.VMEM((PIECES, 2, rows, half), BF),
        pltpu.VMEM((PIECES, 2, rows, right), BF),
        pltpu.VMEM((PIECES, 2, rows, right), BF),
        pltpu.VMEM((2, rows, half), F32),
        pltpu.VMEM((2, rows, right), F32),
        pltpu.VMEM((rows, half), F32),
        pltpu.VMEM((rows, right), F32),
        pltpu.VMEM((PIECES, rows, half), BF),
        pltpu.VMEM((PIECES, rows, half), BF),
        pltpu.VMEM((PIECES, rows, right), BF),
        pltpu.VMEM((PIECES, rows, right), BF),
        pltpu.SemaphoreType.DMA((KINDS, PIECES)),
        pltpu.SemaphoreType.DMA((KINDS, PIECES)),
        pltpu.SemaphoreType.DMA((PIECES,)),
        pltpu.SemaphoreType.DMA((1,)),
    ]
    if gathered:
        out_shape.append(jax.ShapeDtypeStruct((8, PIECES, rows, gathered), BF))
        out_specs.append(any_spec)
        scratch += [pltpu.VMEM((PIECES, rows, gathered), BF), pltpu.SemaphoreType.DMA((PIECES,))]
    results = pl.pallas_call(
        kernel,
        in_specs=[any_spec, any_spec] + [vmem] * len(owned),
        out_specs=out_specs,
        out_shape=out_shape,
        scratch_shapes=scratch,
        compiler_params=pltpu.CompilerParams(
            collective_id=collective_id, has_side_effects=True, vmem_limit_bytes=VMEM_LIMIT
        ),
        name="product_scatter",
    )(left, weight, *[o.reshape(PIECES, rows, o.shape[1]) for o in owned])
    flat = [r.reshape(tokens, r.shape[2]) for r in results[: len(outs)]]
    if gathered:
        flat.append(results[-1].reshape(8 * tokens, gathered))
    return flat


def gather_dp(v):
    return lax.all_gather(v, "dp", axis=0, tiled=True)


def scatter_dp(v):
    return lax.psum_scatter(v, "dp", scatter_dimension=0, tiled=True)


def swap_seq(v):
    return lax.all_to_all(v, "seq", split_axis=0, concat_axis=0, tiled=True)


def swap_all(parts, collective_id):
    if lax.axis_size("seq") == 8:
        return swap_plane(parts, collective_id)
    return [swap_seq(p) for p in parts]


def gather_all(own, parts, collective_id):
    if lax.axis_size("seq") == 8:
        return gather_plane(own, parts, collective_id)
    return lax.all_gather(own, "seq", axis=0, tiled=True), [swap_seq(p) for p in parts]


def product_all(left, weight, transposed, stats, epilogue, owned, outs, gathered, collective_id):
    if lax.axis_size("seq") == 8:
        return product_scatter(left, weight, transposed, stats, epilogue, owned, outs, gathered, collective_id)
    depth = left.shape[1] - (EXTRA if stats else 0)
    product = (nt if transposed else nn)(left[:, :depth], weight).astype(BF)
    result = lax.psum_scatter(product, "seq", scatter_dimension=0, tiled=True).astype(F32)
    stat = None
    if stats:
        stat = lax.psum_scatter(left[:, depth:].astype(F32), "seq", scatter_dimension=0, tiled=True)
    written, sent = epilogue(result, stat, *owned)
    written = [w.astype(d) for w, (_, d) in zip(written, outs)]
    return written + ([lax.all_gather(sent, "seq", axis=0, tiled=True)] if gathered else [])


def split_lanes(v):
    lane = lax.broadcasted_iota(jnp.int32, (v.shape[0], EXTRA), 1)
    high = v.astype(BF).astype(F32)
    return jnp.where(lane == 0, high, jnp.where(lane == 1, v - high, 0.0)).astype(BF)


def inverse_rms(square_mean):
    return lax.rsqrt(square_mean + EPSILON)


def row_mean(v):
    return jnp.mean(v, axis=1, keepdims=True)


def on_device(
    hidden,
    seg_ids,
    pad_mask,
    attn_gain,
    gate_gap,
    out_gain,
    w_query,
    w_forget,
    w_input,
    w_output,
    ffn_gain,
    w_gate,
    w_up,
    w_down,
    out_grad,
):
    planes, ranks = lax.axis_size("dp"), lax.axis_size("seq")
    row_tokens, model = hidden.shape[1:]
    rows = w_query.shape[0]
    units_in = w_down.shape[0]
    head = model // HEADS
    span = head // rows
    per_rank, groups = planes // span, ranks // span
    channels = per_rank * head
    units = planes * units_in
    tokens = ranks * row_tokens
    members = [[a * span + m for m in range(span)] for a in range(groups)]

    def to_heads(w):
        parts = w.reshape(rows, span, per_rank, groups, head)
        return parts.transpose(3, 1, 0, 2, 4).reshape(ranks, rows, channels)

    def from_heads(parts):
        parts = parts.reshape(groups, span, rows, per_rank, head)
        return parts.transpose(2, 1, 3, 0, 4).reshape(rows, model)

    def to_units(w):
        parts = w.reshape(rows, planes, ranks, units_in)
        return parts.transpose(2, 0, 1, 3).reshape(ranks, rows, units)

    def from_units(parts):
        parts = parts.reshape(ranks, rows, planes, units_in)
        return parts.transpose(1, 2, 0, 3).reshape(rows, planes * ranks * units_in)

    def own_rows(v):
        return v.reshape((span, per_rank) + v.shape[1:])

    def swap_group(v):
        return lax.all_to_all(v, "seq", split_axis=0, concat_axis=0, axis_index_groups=members)

    gain_a, gain_o, gain_f = (g.astype(F32)[:, None] for g in (attn_gain, out_gain, ffn_gain))

    def fold(gain, w):
        return (gain * w.astype(F32)).astype(BF)

    def order(first, *rest):
        return lax.optimization_barrier((first,) + rest)

    qfi_part = jnp.concatenate([to_heads(fold(gain_a, w)) for w in (w_query, w_forget, w_input)], axis=2)
    (qfi_swapped,) = swap_all([qfi_part], 1)
    qfi_full = gather_dp(qfi_swapped.reshape(ranks * rows, 3 * channels))
    out_pieces = lax.all_gather(fold(gain_o, w_output), "dp", axis=0)
    gu_part = jnp.concatenate([to_units(fold(gain_f, w)) for w in (w_gate, w_up)], axis=2)
    x16 = hidden[0]
    x = x16.astype(F32)
    normed = (x * inverse_rms(row_mean(x * x))).astype(BF)
    _, normed, gu_part = order(qfi_swapped, normed, gu_part)
    n1, (gu_swapped,) = gather_all(normed, [gu_part], 2)
    gap_pieces = lax.all_gather(gate_gap, "dp", axis=0)
    gap_own = swap_group(own_rows(gap_pieces)).transpose(1, 0, 2).reshape(1, channels).astype(F32)
    ids = lax.all_gather(jnp.concatenate([seg_ids, pad_mask], axis=0), "seq", axis=0)
    segment = ids[:, 0].reshape(tokens // BLOCK, BLOCK)
    live = jnp.sum(ids[:, 1]).reshape(1)
    ends = segment[:, -1]
    before = jnp.concatenate([segment[:1, 0], ends[:-1]])
    cut = jnp.sum((segment == before[:, None]).astype(jnp.int32), axis=1)
    out_own = swap_group(own_rows(out_pieces)).transpose(1, 0, 2, 3).reshape(channels, model)
    gu_full = gather_dp(gu_swapped.reshape(ranks * rows, 2 * units))
    down_own = gather_dp(w_down)

    qfi = nn(n1, qfi_full)
    mixed, kept = mixer_forward(cut, live, qfi, gap_own)
    og16 = out_grad[0]
    grad_all, _ = gather_all(og16, [], 3)

    def after_output(result, stat, x16):
        x = x16.astype(F32)
        factor_o = inverse_rms(jnp.sum(stat, axis=1, keepdims=True) / model)
        middle = x + factor_o * result
        normed = middle * inverse_rms(row_mean(middle * middle))
        return [middle, jnp.broadcast_to(factor_o, (x.shape[0], EXTRA))], normed.astype(BF)

    middle, factor_o, n2 = product_all(
        mixed, out_own, False, True, after_output, [x16], [(model, F32), (EXTRA, F32)], model, 4
    )
    gate_up = nn(n2, gu_full)
    gate, up = gate_up[:, :units], gate_up[:, units:]
    sig_g = jax.nn.sigmoid(gate)
    act = gate * sig_g
    hidden_units = (act * up).astype(BF)

    d_units = nt(grad_all, down_own)
    d_gate = (d_units * up * sig_g * (1.0 + gate * (1.0 - sig_g))).astype(BF)
    d_up = (d_units * act).astype(BF)
    d_gu = jnp.concatenate([d_gate, d_up], axis=1)
    grad_down = tn(hidden_units, grad_all).astype(BF)
    grad_gu = tn(n2, d_gu).astype(BF)

    def after_ffn(result, stat, middle, og16, x16, factor_o):
        factor_o = factor_o[:, :1]
        factor_m = inverse_rms(row_mean(middle * middle))
        normed = middle * factor_m
        d_middle = og16.astype(F32) + factor_m * (result - normed * row_mean(result * normed))
        mean_o = row_mean(d_middle * (middle - x16.astype(F32)))
        beta = split_lanes(factor_o * factor_o * mean_o)
        return [d_middle], jnp.concatenate([(factor_o * d_middle).astype(BF), beta], axis=1)

    d_middle, d_attn = product_all(
        d_gu, gu_full, True, False, after_ffn, [middle, og16, x16, factor_o], [(model, F32)], model + EXTRA, 5
    )
    beta = jnp.sum(d_attn[:, model:].astype(F32), axis=1, keepdims=True)
    d_attn = d_attn[:, :model]

    def after_down(result, stat, middle):
        return [(middle + result).astype(BF)], None

    (block_out,) = product_all(hidden_units, down_own, False, False, after_down, [middle], [(model, BF)], 0, 6)
    mixed = mixed[:, :channels]
    grad_out = tn(mixed, d_attn).astype(BF)
    d_mixed = (nt(d_attn, out_own) - beta * mixed.astype(F32)).astype(BF)
    d_qfi, gap_grad = mixer_backward(cut, live, qfi, gap_own, kept, d_mixed)
    grad_qfi = tn(n1, d_qfi).astype(BF)

    def after_mixer(result, stat, x16, d_middle):
        x = x16.astype(F32)
        factor_x = inverse_rms(row_mean(x * x))
        normed = x * factor_x
        return [(d_middle + factor_x * (result - normed * row_mean(result * normed))).astype(BF)], None

    (hidden_grad,) = product_all(d_qfi, qfi_full, True, False, after_mixer, [x16, d_middle], [(model, BF)], 0, 7)

    g_down = scatter_dp(grad_down).astype(F32)
    gu_rows = swap_seq(scatter_dp(grad_gu)).reshape(ranks, rows, 2 * units).astype(F32)
    gate_rows, up_rows = from_units(gu_rows[:, :, :units]), from_units(gu_rows[:, :, units:])
    out_back = grad_out.reshape(per_rank, span, rows, model).transpose(1, 0, 2, 3)
    out_back = swap_group(out_back).reshape(planes * rows, model)
    out_rows = scatter_dp(out_back).astype(F32)
    gap_back = swap_group(gap_grad.reshape(per_rank, span, rows).transpose(1, 0, 2)).reshape(planes * rows)
    g_gap = scatter_dp(gap_back)
    qfi_rows = swap_seq(scatter_dp(grad_qfi)).reshape(ranks, rows, 3 * channels).astype(F32)
    q_rows, f_rows, i_rows = (from_heads(qfi_rows[:, :, j * channels : (j + 1) * channels]) for j in range(3))

    def rowdot(w, g):
        return jnp.sum(w.astype(F32) * g, axis=1)

    g_attn_gain = rowdot(w_query, q_rows) + rowdot(w_forget, f_rows) + rowdot(w_input, i_rows)
    g_ffn_gain = rowdot(w_gate, gate_rows) + rowdot(w_up, up_rows)
    g_out_gain = rowdot(w_output, out_rows)
    return (
        block_out[None],
        hidden_grad[None],
        g_attn_gain,
        g_gap,
        g_out_gain,
        gain_a * q_rows,
        gain_a * f_rows,
        gain_a * i_rows,
        gain_o * out_rows,
        g_ffn_gain,
        gain_f * gate_rows,
        gain_f * up_rows,
        g_down,
    )


def solution(mesh):
    tok, row, both = P("dp", "seq", None), P("dp", "seq"), P(("dp", "seq"))
    mat = P(("dp", "seq"), None)
    return jax.shard_map(
        on_device,
        mesh=mesh,
        in_specs=(tok, row, row, both, both, both, mat, mat, mat, mat, both, mat, mat, mat, tok),
        out_specs=(tok, tok, both, both, both, mat, mat, mat, mat, both, mat, mat, mat),
        check_vma=False,
    )
```

```python
import functools

import jax
import jax.numpy as jnp
from jax import lax
from jax.experimental import pallas as pl
from jax.experimental.pallas import tpu as pltpu
from jax.sharding import PartitionSpec as P

HEADS = 16
BLOCK = 64
UNROLL = 2
UNROLL_FORWARD = 4
EPSILON = 1e-06
EXTRA = 128
BF = jnp.bfloat16
F32 = jnp.float32


def dot(a, b, dims):
    return lax.dot_general(a, b, (dims, ((), ())), preferred_element_type=F32)


def nn(a, b):
    return dot(a, b, ((1,), (0,)))


def nt(a, b):
    return dot(a, b, ((1,), (1,)))


def tn(a, b):
    return dot(a, b, ((0,), (0,)))


def inverse_rms(square_mean):
    return lax.rsqrt(square_mean + EPSILON)


def row_mean(v):
    return jnp.mean(v, axis=1, keepdims=True)


def split_sum(tri, v):
    high = v.astype(BF)
    low = (v - high.astype(F32)).astype(BF)
    return nn(tri, high) + nn(tri, low)


def chunk_prep(qfi, gap, live, width):
    query_pre, forget_pre, input_pre = (
        qfi[:, :width],
        qfi[:, width : 2 * width],
        qfi[:, 2 * width :],
    )
    sig_q = jax.nn.sigmoid(query_pre)
    sig_nf = jax.nn.sigmoid(-forget_pre)
    key = gap * sig_nf
    return query_pre, sig_q, sig_nf, key, input_pre * live


def triangle(lower):
    row = lax.broadcasted_iota(jnp.int32, (BLOCK, BLOCK), 0)
    col = lax.broadcasted_iota(jnp.int32, (BLOCK, BLOCK), 1)
    return (row >= col) if lower else (row <= col)


def chunk_masks(cut):
    row = lax.broadcasted_iota(jnp.int32, (BLOCK, BLOCK), 0)
    col = lax.broadcasted_iota(jnp.int32, (BLOCK, BLOCK), 1)
    allowed = (row >= col) & ((row >= cut) == (col >= cut))
    at = lax.broadcasted_iota(jnp.int32, (BLOCK, 1), 0)
    inherits = (at < cut).astype(F32)
    tail = ((at >= cut) | (cut >= BLOCK)).astype(F32)
    whole = (cut >= BLOCK).astype(F32)
    return allowed, inherits, tail, whole


def mixer_forward_kernel(heads, cut_ref, live_ref, n_ref, w_ref, gap_ref, mixed_ref, kept_ref, qfi_ref, state):
    step = pl.program_id(0)
    width = heads * 128

    @pl.when(step == 0)
    def _():
        state[...] = jnp.zeros_like(state)

    qfi_ref[...] = nn(n_ref[...], w_ref[...])
    lower = triangle(True).astype(BF)
    for u in range(UNROLL_FORWARD):
        chunk = step * UNROLL_FORWARD + u
        rows = slice(u * BLOCK, (u + 1) * BLOCK)
        at = lax.broadcasted_iota(jnp.int32, (BLOCK, 1), 0) + chunk * BLOCK
        live = (at < live_ref[0]).astype(F32)
        query_pre, sig_q, sig_nf, key, value = chunk_prep(qfi_ref[rows, :], gap_ref[...], live, width)
        query = query_pre * sig_q
        total = split_sum(lower, jnp.log1p(-key))
        centre = total[BLOCK // 2 : BLOCK // 2 + 1]
        ending = total[BLOCK - 1 :]
        scaled_q = (query * jnp.exp(total - centre)).astype(BF)
        scaled_k = (key * jnp.exp(centre - total)).astype(BF)
        value_low = value.astype(BF)
        allowed, inherits, tail, whole = chunk_masks(cut_ref[chunk])
        value_tail = (value * tail).astype(BF)
        e_centre = jnp.exp(centre)
        e_rest = jnp.exp(ending - centre)
        e_all = jnp.exp(ending) * whole
        square = jnp.zeros((BLOCK, 1), F32)
        for h in range(heads):
            cols = slice(h * 128, (h + 1) * 128)
            before = state[h]
            kept_ref[u, h] = before.astype(BF)
            scores = jnp.where(allowed, nt(scaled_q[:, cols], scaled_k[:, cols]), 0.0)
            inner = nn(scores.astype(BF), value_low[:, cols])
            outer = nt(scaled_q[:, cols], (before * e_centre[:, cols]).astype(BF))
            mixed = inner + outer * inherits
            square = square + jnp.sum(mixed * mixed, axis=1, keepdims=True)
            mixed_ref[rows, cols] = mixed.astype(BF)
            state[h] = before * e_all[:, cols] + tn(value_tail[:, cols], scaled_k[:, cols]) * e_rest[:, cols]
        lane = lax.broadcasted_iota(jnp.int32, (BLOCK, EXTRA), 1)
        high = square.astype(BF).astype(F32)
        mixed_ref[rows, width:] = jnp.where(lane == 0, high, jnp.where(lane == 1, square - high, 0.0)).astype(BF)


def mixer_backward_kernel(heads, cut_ref, live_ref, qfi_ref, gap_ref, kept_ref, grad_ref, out_ref, gap_out_ref, state):
    step = pl.program_id(0)
    last = pl.num_programs(0) - 1
    width = heads * 128

    @pl.when(step == 0)
    def _():
        state[...] = jnp.zeros_like(state)
        gap_out_ref[...] = jnp.zeros_like(gap_out_ref)

    lower = triangle(True).astype(BF)
    upper = triangle(False).astype(BF)
    for u in reversed(range(UNROLL)):
        chunk = (last - step) * UNROLL + u
        rows = slice(u * BLOCK, (u + 1) * BLOCK)
        at = lax.broadcasted_iota(jnp.int32, (BLOCK, 1), 0) + chunk * BLOCK
        live = (at < live_ref[0]).astype(F32)
        gap = gap_ref[...]
        query_pre, sig_q, sig_nf, key, value = chunk_prep(qfi_ref[rows, :], gap, live, width)
        query = query_pre * sig_q
        total = split_sum(lower, jnp.log1p(-key))
        centre = total[BLOCK // 2 : BLOCK // 2 + 1]
        ending = total[BLOCK - 1 :]
        e_q = jnp.exp(total - centre)
        e_k = jnp.exp(centre - total)
        scaled_q = (query * e_q).astype(BF)
        scaled_k = (key * e_k).astype(BF)
        value_low = value.astype(BF)
        allowed, inherits, tail, whole = chunk_masks(cut_ref[chunk])
        value_tail = (value * tail).astype(BF)
        grad = grad_ref[rows, :]
        grad_in = (grad.astype(F32) * inherits).astype(BF)
        e_centre = jnp.exp(centre)
        e_rest = jnp.exp(ending - centre)
        e_all = jnp.exp(ending) * whole
        d_query, d_key, d_value, d_total, d_end = [], [], [], [], []
        for h in range(heads):
            cols = slice(h * 128, (h + 1) * 128)
            before = kept_ref[u, h].astype(F32)
            after = state[h]
            q, k, v, g, gi = scaled_q[:, cols], scaled_k[:, cols], value_low[:, cols], grad[:, cols], grad_in[:, cols]
            vt = value_tail[:, cols]
            scores = jnp.where(allowed, nt(q, k), 0.0).astype(BF)
            d_scores = jnp.where(allowed, nt(g, v), 0.0).astype(BF)
            shifted = (before * e_centre[:, cols]).astype(BF)
            onward = (after * e_rest[:, cols]).astype(BF)
            dq = nn(d_scores, k) + nn(gi, shifted)
            dk_state = nn(vt, onward)
            dk = tn(d_scores, q) + dk_state
            dv = tn(scores, g) + nt(k, onward) * tail
            k32 = k.astype(F32)
            d_total.append(dq * q.astype(F32) - dk * k32)
            d_end.append(
                jnp.sum(after * before, axis=0, keepdims=True) * e_all[:, cols]
                + jnp.sum(dk_state * k32, axis=0, keepdims=True)
            )
            state[h] = after * e_all[:, cols] + tn(gi, q) * e_centre[:, cols]
            d_query.append(dq)
            d_key.append(dk)
            d_value.append(dv)
        d_query = jnp.concatenate(d_query, axis=1) * e_q
        d_key = jnp.concatenate(d_key, axis=1) * e_k
        d_value = jnp.concatenate(d_value, axis=1) * live
        d_log = split_sum(upper, jnp.concatenate(d_total, axis=1)) + jnp.concatenate(d_end, axis=1)
        d_key = d_key - d_log / (1.0 - key)
        gap_out_ref[...] += jnp.sum(d_key * sig_nf, axis=0, keepdims=True)
        out_ref[rows, :width] = (d_query * sig_q * (1.0 + query_pre * (1.0 - sig_q))).astype(BF)
        out_ref[rows, width : 2 * width] = (-d_key * key * (1.0 - sig_nf)).astype(BF)
        out_ref[rows, 2 * width :] = d_value.astype(BF)


MESH = pl.DeviceIdType.MESH
PIECES = 5
VMEM_LIMIT = 60 * 1024 * 1024
(S_X, S_Y, S_CORE, S_DIAG_Y, S_DIAG_X, S_CORE_X, S_CORE_Y, S_CORE_D, R_CORE, R_X, R_Y, R_LAST_Y, R_LAST_X, KINDS) = range(14)


class Place:
    def __init__(self):
        self.plane = lax.axis_index("dp")
        me = lax.axis_index("seq")
        self.me = me
        self.core = me % 2
        self.x = (me // 2) % 2
        self.y = me // 4

    def rank(self, fy=0, fx=0, fc=0):
        y = 1 - self.y if fy else self.y
        x = 1 - self.x if fx else self.x
        core = 1 - self.core if fc else self.core
        return 4 * y + 2 * x + core

    def device(self, fy=0, fx=0, fc=0):
        return (self.plane, self.rank(fy, fx, fc))


def greet(place):
    barrier = pltpu.get_barrier_semaphore()
    for flip in ((0, 0, 1), (0, 1, 0), (1, 0, 0)):
        pl.semaphore_signal(barrier, inc=1, device_id=place.device(*flip), device_id_type=MESH)
    pl.semaphore_wait(barrier, 3)


def remote(src, dst, sems, kind, b, device):
    send, recv = sems
    return pltpu.make_async_remote_copy(
        src_ref=src,
        dst_ref=dst,
        send_sem=send.at[kind, b],
        recv_sem=recv.at[kind, b],
        device_id=device,
        device_id_type=MESH,
    )


class Gather:
    def __init__(self, place, own, full, sems, local_sem):
        self.p, self.own, self.full, self.sems, self.local = place, own, full, sems, local_sem
        self.half = full.shape[2] // 2

    def keep(self, b):
        return pltpu.make_async_copy(self.own.at[b], self.full.at[self.p.me, b], self.local.at[b])

    def first(self, b):
        p, dst = self.p, self.full.at[self.p.me, b]
        return [
            remote(self.own.at[b], dst, self.sems, S_X, b, p.device(0, 1, 0)),
            remote(self.own.at[b], dst, self.sems, S_Y, b, p.device(1, 0, 0)),
            remote(self.own.at[b], dst, self.sems, S_CORE, b, p.device(0, 0, 1)),
        ]

    def second(self, b):
        p, h = self.p, self.half
        from_x, from_y = self.full.at[p.rank(0, 1, 0), b], self.full.at[p.rank(1, 0, 0), b]
        up, down = from_x.at[pl.ds(0, h)], from_y.at[pl.ds(h, h)]
        return [
            remote(up, up, self.sems, S_DIAG_Y, b, p.device(1, 0, 0)),
            remote(down, down, self.sems, S_DIAG_X, b, p.device(0, 1, 0)),
            remote(from_x, from_x, self.sems, S_CORE_X, b, p.device(0, 0, 1)),
            remote(from_y, from_y, self.sems, S_CORE_Y, b, p.device(0, 0, 1)),
        ]

    def third(self, b):
        p = self.p
        block = self.full.at[p.rank(1, 1, 0), b]
        return [remote(block, block, self.sems, S_CORE_D, b, p.device(0, 0, 1))]

    def arrived(self, kind, b, flips, rows=None):
        block = self.full.at[self.p.rank(*flips), b]
        if rows is not None:
            block = block.at[pl.ds(rows * self.half, self.half)]
        remote(block, block, self.sems, kind, b, self.p.device(0, 0, 1)).wait_recv()

    def start(self, b):
        self.keep(b).start()
        for copy in self.first(b):
            copy.start()

    def forward(self, b):
        self.arrived(S_X, b, (0, 1, 0))
        self.arrived(S_Y, b, (1, 0, 0))
        for copy in self.second(b):
            copy.start()

    def forward_last(self, b):
        self.arrived(S_DIAG_Y, b, (1, 1, 0), 0)
        self.arrived(S_DIAG_X, b, (1, 1, 0), 1)
        for copy in self.third(b):
            copy.start()

    def finish(self, b):
        self.arrived(S_CORE, b, (0, 0, 1))
        self.arrived(S_CORE_X, b, (0, 1, 1))
        self.arrived(S_CORE_Y, b, (1, 0, 1))
        self.arrived(S_CORE_D, b, (1, 1, 1))

    def drain(self, b):
        self.keep(b).wait()
        for copy in self.first(b) + self.second(b) + self.third(b):
            copy.wait_send()


def swap_starts(place, parts, outs, send, recv, local):
    copies = []
    for i, (part, out) in enumerate(zip(parts, outs)):
        own = pltpu.make_async_copy(part.at[place.me], out.at[place.me], local.at[i])
        own.start()
        for k, flips in enumerate(((0, 0, 1), (0, 1, 0), (1, 0, 0), (0, 1, 1), (1, 0, 1), (1, 1, 0), (1, 1, 1))):
            copy = pltpu.make_async_remote_copy(
                src_ref=part.at[place.rank(*flips)],
                dst_ref=out.at[place.me],
                send_sem=send.at[i, k],
                recv_sem=recv.at[i, k],
                device_id=place.device(*flips),
                device_id_type=MESH,
            )
            copy.start()
            there = out.at[place.rank(*flips)]
            copies.append((copy, pltpu.make_async_remote_copy(
                src_ref=there, dst_ref=there, send_sem=send.at[i, k], recv_sem=recv.at[i, k],
                device_id=place.device(*flips), device_id_type=MESH)))
        copies.append((own, None))
    return copies


def swap_waits(copies):
    for copy, arrival in copies:
        if arrival is None:
            copy.wait()
        else:
            copy.wait_send()
            arrival.wait_recv()


def greet_all(place):
    barrier = pltpu.get_barrier_semaphore()
    for flips in ((0, 0, 1), (0, 1, 0), (1, 0, 0), (0, 1, 1), (1, 0, 1), (1, 1, 0), (1, 1, 1)):
        pl.semaphore_signal(barrier, inc=1, device_id=place.device(*flips), device_id_type=MESH)
    pl.semaphore_wait(barrier, 7)


def fold(gain, w):
    return (gain * w.astype(F32)).astype(BF)


FLIPS = ((0, 0, 1), (0, 1, 0), (1, 0, 0), (0, 1, 1), (1, 0, 1), (1, 1, 0), (1, 1, 1))
ANY_SPEC = pl.BlockSpec(memory_space=pl.ANY)
VMEM_SPEC = pl.BlockSpec(memory_space=pltpu.VMEM)


def column_peers(place, planes):
    peers = []
    for hop in range(planes):
        for flip in (0, 1):
            if hop or flip:
                plane = lax.rem(place.plane + hop, planes)
                peers.append((plane, place.rank(0, 0, flip)))
    return peers


def column_spread(place, planes, src, dst, send, recv):
    waits = []
    for k, (plane, rank) in enumerate(column_peers(place, planes)):
        mine = dst.at[place.plane, place.core]
        copy = pltpu.make_async_remote_copy(
            src_ref=src, dst_ref=mine, send_sem=send.at[k], recv_sem=recv.at[k],
            device_id=(plane, rank), device_id_type=MESH,
        )
        copy.start()
        back = lax.rem(planes + 2 * place.plane - plane, planes)
        there = dst.at[back, lax.rem(rank, 2)]
        waits.append((copy, pltpu.make_async_remote_copy(
            src_ref=there, dst_ref=there, send_sem=send.at[k], recv_sem=recv.at[k],
            device_id=(plane, rank), device_id_type=MESH,
        )))
    return waits


def greet_column_and_plane(place, planes):
    barrier = pltpu.get_barrier_semaphore()
    devices = [place.device(*flips) for flips in FLIPS]
    devices += [p for p in column_peers(place, planes)[1:]]
    for device in devices:
        pl.semaphore_signal(barrier, inc=1, device_id=device, device_id_type=MESH)
    pl.semaphore_wait(barrier, len(devices))


def enter_plane(weights, gain, ids, gap, per_rank, groups, planes, collective_id):
    rows, model = weights[0].shape
    head = model // (8 * per_rank)
    channels = per_rank * head
    span = 8 // groups

    def kernel(q_ref, f_ref, i_ref, gain_ref, ids_ref, gap_ref, out_ref, ids_out, gap_out, part, *sems):
        send, recv, local, gap_send, gap_recv = sems
        place = Place()
        scale = gain_ref[...]
        for w, ref in enumerate((q_ref, f_ref, i_ref)):
            for a in range(groups):
                for m in range(span):
                    for j in range(per_rank):
                        h = (m * per_rank + j) * groups + a
                        at = w * channels + j * head
                        part[a * span + m, :, at : at + head] = fold(scale, ref[:, h * head : (h + 1) * head])
        greet_column_and_plane(place, planes)
        copies = swap_starts(place, [part], [out_ref], send, recv, local)
        gaps = column_spread(place, planes, gap_ref, gap_out, gap_send, gap_recv)
        own_gap = pltpu.make_async_copy(gap_ref, gap_out.at[place.plane, place.core], local.at[2])
        own_gap.start()
        own_ids = pltpu.make_async_copy(ids_ref, ids_out.at[place.me], local.at[1])
        own_ids.start()
        ids_copies = []
        for k, flips in enumerate(FLIPS):
            there = ids_out.at[place.rank(*flips)]
            made = [
                pltpu.make_async_remote_copy(
                    src_ref=src, dst_ref=dst, send_sem=send.at[1, k], recv_sem=recv.at[1, k],
                    device_id=place.device(*flips), device_id_type=MESH,
                )
                for src, dst in ((ids_ref, ids_out.at[place.me]), (there, there))
            ]
            made[0].start()
            ids_copies.append(made)
        swap_waits(copies)
        for copy, arrival in ids_copies + gaps:
            copy.wait_send()
            arrival.wait_recv()
        own_gap.wait()
        own_ids.wait()

    return pl.pallas_call(
        kernel,
        in_specs=[VMEM_SPEC] * 4 + [ANY_SPEC] * 2,
        out_specs=[ANY_SPEC] * 3,
        out_shape=[
            jax.ShapeDtypeStruct((8, rows, 3 * channels), BF),
            jax.ShapeDtypeStruct((8,) + ids.shape, ids.dtype),
            jax.ShapeDtypeStruct((planes, 2) + gap.shape, gap.dtype),
        ],
        scratch_shapes=[
            pltpu.VMEM((8, rows, 3 * channels), BF),
            pltpu.SemaphoreType.DMA((2, 7)),
            pltpu.SemaphoreType.DMA((2, 7)),
            pltpu.SemaphoreType.DMA((3,)),
            pltpu.SemaphoreType.DMA((2 * planes - 1,)),
            pltpu.SemaphoreType.DMA((2 * planes - 1,)),
        ],
        compiler_params=pltpu.CompilerParams(
            collective_id=collective_id, has_side_effects=True, vmem_limit_bytes=VMEM_LIMIT
        ),
        name="enter_plane",
    )(*weights, gain, ids, gap)


def gather_plane(x, w_gate, w_up, gain, planes, collective_id):
    tokens, width = x.shape
    rows = tokens // PIECES
    w_rows, every_unit = w_gate.shape
    units_in = every_unit // (8 * planes)
    units = units_in * planes
    x = x.reshape(PIECES, rows, width)

    def kernel(x_ref, gate_ref, up_ref, gain_ref, full, out_ref, normed, part, *sems):
        send, recv, local, swap_send, swap_recv, swap_local = sems
        place = Place()
        gather = Gather(place, normed, full, (send, recv), local)
        value = x_ref[0].astype(F32)
        normed[0] = (value * inverse_rms(row_mean(value * value))).astype(BF)
        greet_all(place)
        gather.start(0)
        for b in range(1, PIECES):
            value = x_ref[b].astype(F32)
            normed[b] = (value * inverse_rms(row_mean(value * value))).astype(BF)
            gather.start(b)
        scale = gain_ref[...]
        for side, ref in enumerate((gate_ref, up_ref)):
            for i in range(planes):
                for s in range(8):
                    at = (i * 8 + s) * units_in
                    to = side * units + i * units_in
                    part[s, :, to : to + units_in] = fold(scale, ref[:, at : at + units_in])
        copies = swap_starts(place, [part], [out_ref], swap_send, swap_recv, swap_local)
        for stage in (gather.forward, gather.forward_last, gather.finish):
            pl.loop(0, PIECES)(stage)
        swap_waits(copies)
        pl.loop(0, PIECES)(gather.drain)

    full, swapped = pl.pallas_call(
        kernel,
        in_specs=[VMEM_SPEC] * 4,
        out_specs=[ANY_SPEC] * 2,
        out_shape=[
            jax.ShapeDtypeStruct((8, PIECES, rows, width), BF),
            jax.ShapeDtypeStruct((8, w_rows, 2 * units), BF),
        ],
        scratch_shapes=[
            pltpu.VMEM((PIECES, rows, width), BF),
            pltpu.VMEM((8, w_rows, 2 * units), BF),
            pltpu.SemaphoreType.DMA((KINDS, PIECES)),
            pltpu.SemaphoreType.DMA((KINDS, PIECES)),
            pltpu.SemaphoreType.DMA((PIECES,)),
            pltpu.SemaphoreType.DMA((1, 7)),
            pltpu.SemaphoreType.DMA((1, 7)),
            pltpu.SemaphoreType.DMA((1,)),
        ],
        compiler_params=pltpu.CompilerParams(
            collective_id=collective_id, has_side_effects=True, vmem_limit_bytes=VMEM_LIMIT
        ),
        name="gather_plane",
    )(x, w_gate, w_up, gain)
    return full.reshape(8 * tokens, width), swapped


def finish_units(in_ref, weights, outs, scale, planes):
    ranks, rows, both = in_ref.shape
    units = both // 2
    units_in = units // planes
    total = jnp.zeros((rows, 1), F32)
    for side, (ref, out) in enumerate(zip(weights, outs)):
        for i in range(planes):
            for s in range(ranks):
                at = side * units + i * units_in
                to = (i * ranks + s) * units_in
                grad = in_ref[s, :, at : at + units_in].astype(F32)
                total += jnp.sum(grad * ref[:, to : to + units_in].astype(F32), axis=1, keepdims=True)
                out[:, to : to + units_in] = grad * scale
    return total


def exit_plane(summed, weights, gain, gap_grad, unit_rows, unit_weights, unit_gain, per_rank, groups, planes, collective_id):
    rows, model = weights[0].shape
    head = model // (8 * per_rank)
    channels = per_rank * head
    span = 8 // groups

    def kernel(sum_ref, q_ref, f_ref, i_ref, gain_ref, gap_ref, unit_ref, gate_ref, up_ref, unit_gain_ref,
               q_out, f_out, i_out, gain_out, gap_out, gate_out, up_out, unit_gain_out, landed, *sems):
        send, recv, local, gap_send, gap_recv = sems
        place = Place()
        greet_column_and_plane(place, planes)
        copies = swap_starts(place, [sum_ref], [landed], send, recv, local)
        gaps = column_spread(place, planes, gap_ref, gap_out, gap_send, gap_recv)
        own_gap = pltpu.make_async_copy(gap_ref, gap_out.at[place.plane, place.core], local.at[1])
        own_gap.start()
        unit_gain_out[...] = finish_units(unit_ref, (gate_ref, up_ref), (gate_out, up_out), unit_gain_ref[...], planes)
        swap_waits(copies)
        scale = gain_ref[...]
        total = jnp.zeros((rows, 1), F32)
        for w, (ref, out) in enumerate(((q_ref, q_out), (f_ref, f_out), (i_ref, i_out))):
            for a in range(groups):
                for m in range(span):
                    for j in range(per_rank):
                        h = (m * per_rank + j) * groups + a
                        at = w * channels + j * head
                        grad = landed[a * span + m, :, at : at + head].astype(F32)
                        cols = slice(h * head, (h + 1) * head)
                        total += jnp.sum(grad * ref[:, cols].astype(F32), axis=1, keepdims=True)
                        out[:, cols] = grad * scale
        gain_out[...] = total
        for copy, arrival in gaps:
            copy.wait_send()
            arrival.wait_recv()
        own_gap.wait()

    return pl.pallas_call(
        kernel,
        in_specs=[ANY_SPEC] + [VMEM_SPEC] * 4 + [ANY_SPEC] + [VMEM_SPEC] * 4,
        out_specs=[VMEM_SPEC] * 4 + [ANY_SPEC] + [VMEM_SPEC] * 3,
        out_shape=[jax.ShapeDtypeStruct((rows, model), F32)] * 3
        + [
            jax.ShapeDtypeStruct((rows, 1), F32),
            jax.ShapeDtypeStruct((planes, 2) + gap_grad.shape, gap_grad.dtype),
        ]
        + [jax.ShapeDtypeStruct(unit_weights[0].shape, F32)] * 2
        + [jax.ShapeDtypeStruct((rows, 1), F32)],
        scratch_shapes=[
            pltpu.VMEM((8, rows, 3 * channels), BF),
            pltpu.SemaphoreType.DMA((1, 7)),
            pltpu.SemaphoreType.DMA((1, 7)),
            pltpu.SemaphoreType.DMA((2,)),
            pltpu.SemaphoreType.DMA((2 * planes - 1,)),
            pltpu.SemaphoreType.DMA((2 * planes - 1,)),
        ],
        compiler_params=pltpu.CompilerParams(
            collective_id=collective_id, has_side_effects=True, vmem_limit_bytes=VMEM_LIMIT
        ),
        name="exit_plane",
    )(summed, *weights, gain, gap_grad, unit_rows, *unit_weights, unit_gain)


class Scatter:
    def __init__(self, left, weight, transposed, stats):
        self.rows, self.columns = left[2], left[3]
        self.transposed, self.stats = transposed, stats
        self.weight = weight
        self.depth = weight[1] if transposed else weight[0]
        self.width = weight[0] if transposed else weight[1]
        self.half = self.width // 2
        self.extra = EXTRA if stats else 0

    def scratch(self):
        rows, half, full = self.rows, self.half, self.width + self.extra
        right = half + self.extra
        return [
            pltpu.VMEM((PIECES, 8, rows, self.columns), BF),
            pltpu.VMEM(self.weight, BF),
            pltpu.VMEM((PIECES, 4, rows, full), BF),
            pltpu.VMEM((PIECES, 4, rows, full), BF),
            pltpu.VMEM((4, rows, full), F32),
            pltpu.VMEM((PIECES, 2, rows, half), BF),
            pltpu.VMEM((PIECES, 2, rows, half), BF),
            pltpu.VMEM((PIECES, 2, rows, right), BF),
            pltpu.VMEM((PIECES, 2, rows, right), BF),
            pltpu.VMEM((PIECES, 2, rows, half), F32),
            pltpu.VMEM((PIECES, 2, rows, right), F32),
            pltpu.VMEM((PIECES, rows, half), BF),
            pltpu.VMEM((PIECES, rows, half), BF),
            pltpu.VMEM((PIECES, rows, right), BF),
            pltpu.VMEM((PIECES, rows, right), BF),
            pltpu.SemaphoreType.DMA((PIECES,)),
            pltpu.SemaphoreType.DMA((1,)),
        ]

    def bind(self, place, sems, left_ref, weight_ref, refs):
        self.place, self.sems, self.left_ref, self.weight_ref = place, sems, left_ref, weight_ref
        (self.x_buf, self.w_buf, self.core_out, self.core_in, self.total, self.x_out, self.x_in, self.y_out, self.y_in,
         self.keep_a, self.keep_b, self.last_y_out, self.last_y_in, self.last_x_out,
         self.last_x_in, self.load_sem, self.w_sem) = refs

    def weight_copy(self):
        return pltpu.make_async_copy(self.weight_ref, self.w_buf, self.w_sem.at[0])

    def start_loads(self):
        core = self.place.core
        self.weight_copy().start()
        for b in range(PIECES):
            for j in range(4):
                for side, at in ((0, 2 * j + 1 - core), (4, 2 * j + core)):
                    pltpu.make_async_copy(
                        self.left_ref.at[at, b], self.x_buf.at[b, side + j], self.load_sem.at[b]
                    ).start()

    def send_core(self, b):
        return remote(self.core_out.at[b], self.core_in.at[b], self.sems, R_CORE, b, self.place.device(0, 0, 1))

    def send_x(self, b):
        return remote(self.x_out.at[b], self.x_in.at[b], self.sems, R_X, b, self.place.device(0, 1, 0))

    def send_y(self, b):
        return remote(self.y_out.at[b], self.y_in.at[b], self.sems, R_Y, b, self.place.device(1, 0, 0))

    def send_last_y(self, b):
        return remote(self.last_y_out.at[b], self.last_y_in.at[b], self.sems, R_LAST_Y, b, self.place.device(1, 0, 0))

    def send_last_x(self, b):
        return remote(self.last_x_out.at[b], self.last_x_in.at[b], self.sems, R_LAST_X, b, self.place.device(0, 1, 0))

    def produce(self, b):
        rows, depth, width, tile = self.rows, self.depth, self.width, 256
        pltpu.make_async_copy(self.x_buf.at[b], self.x_buf.at[b], self.load_sem.at[b]).wait()

        @pl.loop(0, width // tile)
        def _(t):
            at = pl.multiple_of(t * tile, tile)
            lhs = self.x_buf[b, :, :, :depth].reshape(8 * rows, depth)
            if self.transposed:
                out = nt(lhs, self.w_buf[pl.ds(at, tile), :])
            else:
                out = nn(lhs, self.w_buf[:, pl.ds(at, tile)])
            self.core_out[b, :, :, pl.ds(at, tile)] = out[: 4 * rows].astype(BF).reshape(4, rows, tile)
            self.total[:, :, pl.ds(at, tile)] = out[4 * rows :].reshape(4, rows, tile)

        if self.stats:
            self.core_out[b, :, :, width:] = self.x_buf[b, :4, :, depth:]
            self.total[:, :, width:] = self.x_buf[b, 4:, :, depth:].astype(F32)
        self.send_core(b).start()

    def stage_one(self, b):
        place, half, total, core_in = self.place, self.half, self.total, self.core_in
        self.send_core(b).wait_recv()
        for i in range(2):
            go, stay = 2 * i + 1 - place.x, 2 * i + place.x
            self.x_out[b, i] = (total[go, :, :half] + core_in[b, go, :, :half].astype(F32)).astype(BF)
            self.keep_a[b, i] = total[stay, :, :half] + core_in[b, stay, :, :half].astype(F32)
        self.send_x(b).start()
        for i in range(2):
            go, stay = 2 * (1 - place.y) + i, 2 * place.y + i
            self.y_out[b, i] = (total[go, :, half:] + core_in[b, go, :, half:].astype(F32)).astype(BF)
            self.keep_b[b, i] = total[stay, :, half:] + core_in[b, stay, :, half:].astype(F32)
        self.send_y(b).start()

    def stage_two(self, b):
        self.send_x(b).wait_recv()
        go = 1 - self.place.y
        self.last_y_out[b] = (self.keep_a[b, go] + self.x_in[b, go].astype(F32)).astype(BF)
        self.send_last_y(b).start()
        self.send_y(b).wait_recv()
        go = 1 - self.place.x
        self.last_x_out[b] = (self.keep_b[b, go] + self.y_in[b, go].astype(F32)).astype(BF)
        self.send_last_x(b).start()

    def stage_three(self, b):
        self.send_last_y(b).wait_recv()
        self.send_last_x(b).wait_recv()
        y, x = self.place.y, self.place.x
        low = self.keep_a[b, y] + self.x_in[b, y].astype(F32) + self.last_y_in[b].astype(F32)
        high = self.keep_b[b, x] + self.y_in[b, x].astype(F32) + self.last_x_in[b].astype(F32)
        result = jnp.concatenate([low, high[:, : self.half]], axis=1)
        return result, (high[:, self.half :] if self.stats else None)

    def drain(self, b):
        for copy in (self.send_core, self.send_x, self.send_y, self.send_last_y, self.send_last_x):
            copy(b).wait_send()


def guarded(body, b):
    @pl.when((b >= 0) & (b < PIECES))
    def _():
        body(b)


def plane_sems():
    return [pltpu.SemaphoreType.DMA((KINDS, PIECES)), pltpu.SemaphoreType.DMA((KINDS, PIECES))]


def product_scatter(left, weight, transposed, stats, epilogue, owned, outs, gathered, collective_id):
    tokens = left.shape[0] // 8
    rows = tokens // PIECES
    left = left.reshape(8, PIECES, rows, left.shape[1])
    scatter = Scatter(left.shape, weight.shape, transposed, stats)
    count = len(scatter.scratch())

    def kernel(*refs):
        refs = list(refs)
        left_ref, weight_ref = refs.pop(0), refs.pop(0)
        own_refs = [refs.pop(0) for _ in owned]
        out_refs = [refs.pop(0) for _ in outs]
        full_ref = refs.pop(0) if gathered else None
        place = Place()
        sems = (refs.pop(0), refs.pop(0))
        scatter.bind(place, sems, left_ref, weight_ref, refs[:count])
        scatter.start_loads()
        greet(place)
        if gathered:
            n_buf, keep_sem = refs[count:]
            gather = Gather(place, n_buf, full_ref, sems, keep_sem)

        def end(b):
            result, stat = scatter.stage_three(b)
            written, sent = epilogue(result, stat, *[r[b] for r in own_refs])
            for ref, value in zip(out_refs, written):
                ref[b] = value
            if gathered:
                n_buf[b] = sent
                gather.start(b)

        scatter.weight_copy().wait()

        @pl.loop(0, PIECES + (9 if gathered else 5))
        def _(step):
            guarded(scatter.stage_one, step - 1)
            guarded(scatter.produce, step)
            guarded(scatter.stage_two, step - 3)
            guarded(end, step - 5)
            if gathered:
                guarded(gather.forward, step - 7)
                guarded(gather.forward_last, step - 9)

        @pl.loop(0, PIECES)
        def _(b):
            if gathered:
                gather.finish(b)
                gather.drain(b)
            scatter.drain(b)

    any_spec, vmem = pl.BlockSpec(memory_space=pl.ANY), pl.BlockSpec(memory_space=pltpu.VMEM)
    out_shape = [jax.ShapeDtypeStruct((PIECES, rows, c), d) for c, d in outs]
    out_specs = [vmem] * len(outs)
    scratch = plane_sems() + scatter.scratch()
    if gathered:
        out_shape.append(jax.ShapeDtypeStruct((8, PIECES, rows, gathered), BF))
        out_specs.append(any_spec)
        scratch += [pltpu.VMEM((PIECES, rows, gathered), BF), pltpu.SemaphoreType.DMA((PIECES,))]
    results = pl.pallas_call(
        kernel,
        in_specs=[any_spec, any_spec] + [vmem] * len(owned),
        out_specs=out_specs,
        out_shape=out_shape,
        scratch_shapes=scratch,
        compiler_params=pltpu.CompilerParams(
            collective_id=collective_id, has_side_effects=True, vmem_limit_bytes=VMEM_LIMIT
        ),
        cost_estimate=pl.CostEstimate(
            flops=16 * tokens * scatter.depth * scatter.width,
            bytes_accessed=(240 if gathered else 140) * tokens * scatter.width * 2,
            transcendentals=0,
        ),
        name="product_scatter",
    )(left, weight, *[o.reshape(PIECES, rows, o.shape[1]) for o in owned])
    flat = [r.reshape(tokens, r.shape[2]) for r in results[: len(outs)]]
    if gathered:
        flat.append(results[-1].reshape(8 * tokens, gathered))
    return flat


def mixer_specs(tokens, heads, reverse):
    width, unroll = heads * 128, UNROLL if reverse else UNROLL_FORWARD
    span = unroll * BLOCK
    steps = tokens // span

    def at(i):
        return steps - 1 - i if reverse else i

    return (
        steps,
        pl.BlockSpec((span, 3 * width), lambda i, *_: (at(i), 0)),
        pl.BlockSpec((1, width), lambda i, *_: (0, 0)),
        pl.BlockSpec((unroll, heads, 128, 128), lambda i, *_: (at(i), 0, 0, 0)),
        lambda columns: pl.BlockSpec((span, columns), lambda i, *_: (at(i), 0)),
    )


def mixer_forward(cut, live, n1, weight, gap, own, out_pieces, per_rank, collective_id):
    tokens, heads = n1.shape[0], gap.shape[1] // 128
    width = heads * 128
    steps, qfi_spec, gap_spec, kept_spec, block = mixer_specs(tokens, heads, False)
    together = lax.axis_size("seq") == 8

    def kernel(cut_ref, live_ref, n_ref, w_ref, gap_ref, *refs):
        if not together:
            return mixer_forward_kernel(heads, cut_ref, live_ref, n_ref, w_ref, gap_ref, *refs)
        own_ref, pieces_ref, mixed_ref, kept_ref, qfi_ref, full_ref, rows_ref, state, send, recv, local, w_send, w_recv, w_local = refs
        place = Place()
        gather = Gather(place, own_ref, full_ref, (send, recv), local)

        def exchange(j):
            core = place.core
            here = pltpu.make_async_copy(
                pieces_ref.at[core * per_rank + j], rows_ref.at[j, core], w_local.at[j]
            )
            there = pltpu.make_async_remote_copy(
                src_ref=pieces_ref.at[(1 - core) * per_rank + j], dst_ref=rows_ref.at[j, core],
                send_sem=w_send.at[j], recv_sem=w_recv.at[j], device_id=place.device(0, 0, 1), device_id_type=MESH,
            )
            back = rows_ref.at[j, 1 - core]
            arrival = pltpu.make_async_remote_copy(
                src_ref=back, dst_ref=back, send_sem=w_send.at[j], recv_sem=w_recv.at[j],
                device_id=place.device(0, 0, 1), device_id_type=MESH,
            )
            return here, there, arrival

        @pl.when(pl.program_id(0) == 0)
        def _():
            greet(place)
            pl.loop(0, PIECES)(gather.start)
            for j in range(per_rank):
                here, there, _ = exchange(j)
                here.start()
                there.start()

        mixer_forward_kernel(
            heads, cut_ref, live_ref, n_ref, w_ref, gap_ref, mixed_ref, kept_ref, qfi_ref, state
        )

        @pl.when(pl.program_id(0) == steps - 1)
        def _():
            for stage in (gather.forward, gather.forward_last, gather.finish, gather.drain):
                pl.loop(0, PIECES)(stage)
            for j in range(per_rank):
                here, there, arrival = exchange(j)
                here.wait()
                there.wait_send()
                arrival.wait_recv()

    fixed = pl.BlockSpec(weight.shape, lambda i, *_: (0, 0), pipeline_mode=pl.Buffered(1))
    in_specs, args = [block(n1.shape[1]), fixed, gap_spec], [n1, weight, gap]
    out_specs = [block(width + EXTRA), kept_spec, qfi_spec]
    out_shape = [
        jax.ShapeDtypeStruct((tokens, width + EXTRA), BF),
        jax.ShapeDtypeStruct((tokens // BLOCK, heads, 128, 128), BF),
        jax.ShapeDtypeStruct((tokens, 3 * width), F32),
    ]
    scratch = [pltpu.VMEM((heads, 128, 128), F32)]
    params = pltpu.CompilerParams(vmem_limit_bytes=VMEM_LIMIT)
    if together:
        rows = own.shape[0] // PIECES
        own = own.reshape(PIECES, rows, own.shape[1])
        w_rows, model = out_pieces.shape[1:]
        in_specs, args = in_specs + [ANY_SPEC] * 2, args + [own, out_pieces]
        out_specs = out_specs + [ANY_SPEC] * 2
        out_shape = out_shape + [
            jax.ShapeDtypeStruct((8,) + own.shape, own.dtype),
            jax.ShapeDtypeStruct((per_rank, 2, w_rows, model), BF),
        ]
        scratch = scratch + plane_sems() + [pltpu.SemaphoreType.DMA((PIECES,))]
        scratch = scratch + [pltpu.SemaphoreType.DMA((per_rank,))] * 3
        params = pltpu.CompilerParams(
            vmem_limit_bytes=VMEM_LIMIT, collective_id=collective_id, has_side_effects=True
        )
    results = pl.pallas_call(
        kernel,
        grid_spec=pltpu.PrefetchScalarGridSpec(
            num_scalar_prefetch=2, grid=(steps,), in_specs=in_specs, out_specs=out_specs, scratch_shapes=scratch
        ),
        out_shape=out_shape,
        compiler_params=params,
        cost_estimate=pl.CostEstimate(
            flops=tokens * width * (128 * 10 + 6 * n1.shape[1]),
            bytes_accessed=60 * tokens * n1.shape[1],
            transcendentals=tokens * width * 6,
        ),
        name="mixer_forward",
    )(cut, live, *args)
    mixed, kept, qfi = results[:3]
    if together:
        return mixed, kept, qfi, results[3].reshape(tokens, own.shape[2]), results[4].reshape(width, model)
    return mixed, kept, qfi, lax.all_gather(own, "seq", axis=0, tiled=True), None


def mixer_backward(cut, live, qfi, gap, kept, grad, left, weight, epilogue, owned, collective_id):
    tokens, heads = qfi.shape[0], gap.shape[1] // 128
    width = heads * 128
    steps, qfi_spec, gap_spec, kept_spec, block = mixer_specs(tokens, heads, True)
    together = lax.axis_size("seq") == 8
    in_specs = [qfi_spec, gap_spec, kept_spec, block(width)]
    out_specs = [block(3 * width), gap_spec]
    out_shape = [jax.ShapeDtypeStruct((tokens, 3 * width), BF), jax.ShapeDtypeStruct((1, width), F32)]
    scratch = [pltpu.VMEM((heads, 128, 128), F32)]
    args = [qfi, gap, kept, grad]
    params = pltpu.CompilerParams(vmem_limit_bytes=VMEM_LIMIT)
    if together:
        rows = tokens // 8 // PIECES
        left = left.reshape(8, PIECES, rows, left.shape[1])
        scatter = Scatter(left.shape, weight.shape, False, False)
        model = weight.shape[1]
        stride = max(1, (steps - 2) // PIECES)
        any_spec = pl.BlockSpec(memory_space=pl.ANY)
        whole = pl.BlockSpec((PIECES, rows, model), lambda i, *_: (0, 0, 0), pipeline_mode=pl.Buffered(1))
        in_specs = in_specs + [any_spec, any_spec, whole]
        args = args + [left, weight, owned.reshape(PIECES, rows, model)]
        out_specs = out_specs + [whole]
        out_shape = out_shape + [jax.ShapeDtypeStruct((PIECES, rows, model), BF)]
        scratch = scratch + plane_sems() + scatter.scratch()
        params = pltpu.CompilerParams(
            vmem_limit_bytes=VMEM_LIMIT, collective_id=collective_id, has_side_effects=True
        )

    def kernel(cut_ref, live_ref, qfi_ref, gap_ref, kept_ref, grad_ref, *refs):
        if not together:
            out_ref, gap_out_ref, state = refs
            mixer_backward_kernel(
                heads, cut_ref, live_ref, qfi_ref, gap_ref, kept_ref, grad_ref, out_ref, gap_out_ref, state
            )
            return
        left_ref, weight_ref, owned_ref, out_ref, gap_out_ref, sum_ref, state, send, recv = refs[:9]
        place, step = Place(), pl.program_id(0)
        scatter.bind(place, (send, recv), left_ref, weight_ref, refs[9:])

        @pl.when(step == 0)
        def _():
            scatter.start_loads()
            greet(place)
            scatter.weight_copy().wait()

        def end(b):
            result, _ = scatter.stage_three(b)
            sum_ref[b] = epilogue(result, None, owned_ref[b])[0][0]

        def phases(at):
            for body, first in ((scatter.stage_one, 2), (scatter.produce, 0), (scatter.stage_two, 8), (end, 12)):
                @pl.when((at >= first) & (lax.rem(at - first, stride) == 0) & (at < first + stride * PIECES))
                def _():
                    body((at - first) // stride)

        phases(step)
        mixer_backward_kernel(
            heads, cut_ref, live_ref, qfi_ref, gap_ref, kept_ref, grad_ref, out_ref, gap_out_ref, state
        )

        @pl.when(step == steps - 1)
        def _():
            @pl.loop(steps, stride * (PIECES - 1) + 13)
            def _(late):
                phases(late)

            pl.loop(0, PIECES)(scatter.drain)

    results = pl.pallas_call(
        kernel,
        grid_spec=pltpu.PrefetchScalarGridSpec(
            num_scalar_prefetch=2, grid=(steps,), in_specs=in_specs, out_specs=out_specs, scratch_shapes=scratch
        ),
        out_shape=out_shape,
        compiler_params=params,
        cost_estimate=pl.CostEstimate(
            flops=tokens * width * 128 * 24, bytes_accessed=tokens * width * 28, transcendentals=tokens * width * 6
        ),
        name="mixer_backward",
    )(cut, live, *args)
    if together:
        return results[0], results[1], results[2].reshape(tokens // 8, model)
    (summed,) = product_all(left, weight, False, False, epilogue, [owned], [(weight.shape[1], BF)], 0, collective_id)
    return results[0], results[1], summed


def feed_forward_kernel(units, n_ref, g_ref, gu_ref, down_ref, units_ref, grad_ref, gate_w, up_w):
    @pl.when(pl.program_id(0) == 0)
    def _():
        gate_w[...] = gu_ref[:, :units]
        up_w[...] = gu_ref[:, units:]

    n = n_ref[...]
    gate, up = nn(n, gate_w[...]), nn(n, up_w[...])
    d_units = nt(g_ref[...], down_ref[...])
    sig = jax.nn.sigmoid(gate)
    act = gate * sig
    units_ref[...] = (act * up).astype(BF)
    grad_ref[:, :units] = (d_units * up * sig * (1.0 + gate * (1.0 - sig))).astype(BF)
    grad_ref[:, units:] = (d_units * act).astype(BF)


def feed_forward(n2, grad, gu, down):
    tokens, model = n2.shape
    units = down.shape[0]
    span = 512
    fixed = lambda shape: pl.BlockSpec(shape, lambda i: (0, 0), pipeline_mode=pl.Buffered(1))
    block = lambda columns: pl.BlockSpec((span, columns), lambda i: (i, 0))
    return pl.pallas_call(
        functools.partial(feed_forward_kernel, units),
        grid=(tokens // span,),
        in_specs=[block(model), block(model), fixed(gu.shape), fixed(down.shape)],
        out_specs=[block(units), block(2 * units)],
        out_shape=[jax.ShapeDtypeStruct((tokens, units), BF), jax.ShapeDtypeStruct((tokens, 2 * units), BF)],
        scratch_shapes=[pltpu.VMEM((model, units), BF), pltpu.VMEM((model, units), BF)],
        compiler_params=pltpu.CompilerParams(vmem_limit_bytes=VMEM_LIMIT),
        cost_estimate=pl.CostEstimate(
            flops=6 * tokens * model * units, bytes_accessed=4 * tokens * model, transcendentals=tokens * units
        ),
        name="feed_forward",
    )(n2, grad, gu, down)


def gather_dp(v):
    return lax.all_gather(v, "dp", axis=0, tiled=True)


def scatter_dp(v):
    return lax.psum_scatter(v, "dp", scatter_dimension=0, tiled=True)


def swap_seq(v):
    return lax.all_to_all(v, "seq", split_axis=0, concat_axis=0, tiled=True)


def product_all(left, weight, transposed, stats, epilogue, owned, outs, gathered, collective_id):
    if lax.axis_size("seq") == 8:
        return product_scatter(left, weight, transposed, stats, epilogue, owned, outs, gathered, collective_id)
    depth = left.shape[1] - (EXTRA if stats else 0)
    product = (nt if transposed else nn)(left[:, :depth], weight).astype(BF)
    result = lax.psum_scatter(product, "seq", scatter_dimension=0, tiled=True).astype(F32)
    stat = None
    if stats:
        stat = lax.psum_scatter(left[:, depth:].astype(F32), "seq", scatter_dimension=0, tiled=True)
    written, sent = epilogue(result, stat, *owned)
    written = [w.astype(d) for w, (_, d) in zip(written, outs)]
    return written + ([lax.all_gather(sent, "seq", axis=0, tiled=True)] if gathered else [])


def split_lanes(v):
    lane = lax.broadcasted_iota(jnp.int32, (v.shape[0], EXTRA), 1)
    high = v.astype(BF).astype(F32)
    return jnp.where(lane == 0, high, jnp.where(lane == 1, v - high, 0.0)).astype(BF)


def on_device(
    hidden,
    seg_ids,
    pad_mask,
    attn_gain,
    gate_gap,
    out_gain,
    w_query,
    w_forget,
    w_input,
    w_output,
    ffn_gain,
    w_gate,
    w_up,
    w_down,
    out_grad,
):
    planes, ranks = lax.axis_size("dp"), lax.axis_size("seq")
    row_tokens, model = hidden.shape[1:]
    rows = w_query.shape[0]
    units_in = w_down.shape[0]
    head = model // HEADS
    span = head // rows
    per_rank, groups = planes // span, ranks // span
    channels = per_rank * head
    units = planes * units_in
    tokens = ranks * row_tokens
    members = [[a * span + m for m in range(span)] for a in range(groups)]

    def to_heads(w):
        parts = w.reshape(rows, span, per_rank, groups, head)
        return parts.transpose(3, 1, 0, 2, 4).reshape(ranks, rows, channels)

    def from_heads(parts):
        parts = parts.reshape(groups, span, rows, per_rank, head)
        return parts.transpose(2, 1, 3, 0, 4).reshape(rows, model)

    def to_units(w):
        parts = w.reshape(rows, planes, ranks, units_in)
        return parts.transpose(2, 0, 1, 3).reshape(ranks, rows, units)

    def from_units(parts):
        parts = parts.reshape(ranks, rows, planes, units_in)
        return parts.transpose(1, 2, 0, 3).reshape(rows, planes * ranks * units_in)

    def own_rows(v):
        return v.reshape((span, per_rank) + v.shape[1:])

    def swap_group(v):
        return lax.all_to_all(v, "seq", split_axis=0, concat_axis=0, axis_index_groups=members)

    gain_a, gain_o, gain_f = (g.astype(F32)[:, None] for g in (attn_gain, out_gain, ffn_gain))

    plain = ranks != 8

    def order(first, *rest):
        return lax.optimization_barrier((first,) + rest)

    x16 = hidden[0]
    ids = jnp.concatenate([seg_ids, pad_mask], axis=0)
    mixer_weights = (w_query, w_forget, w_input)
    out_pieces = lax.all_gather(fold(gain_o, w_output), "dp", axis=0)
    if plain:
        qfi_part = jnp.concatenate([to_heads(fold(gain_a, w)) for w in mixer_weights], axis=2)
        qfi_swapped = swap_seq(qfi_part)
        gu_part = jnp.concatenate([to_units(fold(gain_f, w)) for w in (w_gate, w_up)], axis=2)
        gu_swapped = swap_seq(gu_part)
        x = x16.astype(F32)
        normed = (x * inverse_rms(row_mean(x * x))).astype(BF)
        n1 = lax.all_gather(normed, "seq", axis=0, tiled=True)
        gap_pieces = lax.all_gather(gate_gap, "dp", axis=0)
        gap_own = swap_group(own_rows(gap_pieces)).transpose(1, 0, 2)
        ids = lax.all_gather(ids, "seq", axis=0)
    else:
        wide = -(-row_tokens // 128) * 128
        ids = jnp.pad(ids, ((0, 6), (0, wide - row_tokens)))
        gap_tile = jnp.pad(gate_gap[None], ((0, 15), (0, 128 - rows)))
        qfi_swapped, ids, gap_all = enter_plane(
            mixer_weights, gain_a, ids, gap_tile, per_rank, groups, planes, 1
        )
        ids = ids[:, :2, :row_tokens]
        mine = lax.rem(lax.axis_index("seq"), 2) * per_rank
        gap_own = lax.dynamic_slice_in_dim(gap_all[:, :, 0, :rows], mine, per_rank, axis=0)
        x16, qfi_swapped = order(x16, qfi_swapped)
        n1, gu_swapped = gather_plane(x16, w_gate, w_up, gain_f, planes, 2)
    qfi_full = gather_dp(qfi_swapped.reshape(ranks * rows, 3 * channels))
    gu_full = gather_dp(gu_swapped.reshape(ranks * rows, 2 * units))
    down_own = gather_dp(w_down)
    gap_own = gap_own.reshape(1, channels).astype(F32)
    segment = ids[:, 0].reshape(tokens // BLOCK, BLOCK)
    live = jnp.sum(ids[:, 1]).reshape(1)
    ends = segment[:, -1]
    before = jnp.concatenate([segment[:1, 0], ends[:-1]])
    cut = jnp.sum((segment == before[:, None]).astype(jnp.int32), axis=1)

    og16 = out_grad[0]
    mixed, kept, qfi, grad_all, out_own = mixer_forward(
        cut, live, n1, qfi_full, gap_own, og16, out_pieces, per_rank, 3
    )
    if plain:
        out_own = swap_group(own_rows(out_pieces)).transpose(1, 0, 2, 3).reshape(channels, model)

    def after_output(result, stat, x16):
        x = x16.astype(F32)
        factor_o = inverse_rms(jnp.sum(stat, axis=1, keepdims=True) / model)
        middle = x + factor_o * result
        normed = middle * inverse_rms(row_mean(middle * middle))
        return [middle, jnp.broadcast_to(factor_o, (x.shape[0], EXTRA))], normed.astype(BF)

    middle, factor_o, n2 = product_all(
        mixed, out_own, False, True, after_output, [x16], [(model, F32), (EXTRA, F32)], model, 4
    )
    hidden_units, d_gu = feed_forward(n2, grad_all, gu_full, down_own)
    grad_down = tn(hidden_units, grad_all).astype(BF)
    down_sum = scatter_dp(grad_down)
    n2, _ = order(n2, grad_down)
    grad_gu = tn(n2, d_gu).astype(BF)
    gu_sum = scatter_dp(grad_gu)
    d_gu, _ = order(d_gu, grad_gu)

    def after_ffn(result, stat, middle, og16, x16, factor_o):
        factor_o = factor_o[:, :1]
        factor_m = inverse_rms(row_mean(middle * middle))
        normed = middle * factor_m
        d_middle = og16.astype(F32) + factor_m * (result - normed * row_mean(result * normed))
        mean_o = row_mean(d_middle * (middle - x16.astype(F32)))
        beta = split_lanes(factor_o * factor_o * mean_o)
        return [d_middle], jnp.concatenate([(factor_o * d_middle).astype(BF), beta], axis=1)

    d_middle, d_attn = product_all(
        d_gu, gu_full, True, False, after_ffn, [middle, og16, x16, factor_o], [(model, F32)], model + EXTRA, 5
    )
    d_attn, down_sum = order(d_attn, down_sum)
    beta = jnp.sum(d_attn[:, model:].astype(F32), axis=1, keepdims=True)
    d_attn = d_attn[:, :model]

    def after_down(result, stat, middle):
        return [(middle + result).astype(BF)], None

    mixed = mixed[:, :channels]
    grad_out = tn(mixed, d_attn).astype(BF)
    d_mixed = (nt(d_attn, out_own) - beta * mixed.astype(F32)).astype(BF)
    grad_out, d_mixed = order(grad_out, d_mixed)
    out_back = grad_out.reshape(per_rank, span, rows, model).transpose(1, 0, 2, 3)
    out_sum = scatter_dp(swap_group(out_back).reshape(planes * rows, model))
    d_qfi, gap_grad, block_out = mixer_backward(
        cut, live, qfi, gap_own, kept, d_mixed, hidden_units, down_own, after_down, middle, 6
    )
    grad_qfi = tn(n1, d_qfi).astype(BF)
    grad_qfi, d_qfi, gu_sum = order(grad_qfi, d_qfi, gu_sum)
    qfi_sum = scatter_dp(grad_qfi)
    gu_rows = swap_seq(gu_sum).reshape(ranks, rows, 2 * units)

    def after_mixer(result, stat, x16, d_middle):
        x = x16.astype(F32)
        factor_x = inverse_rms(row_mean(x * x))
        normed = x * factor_x
        return [(d_middle + factor_x * (result - normed * row_mean(result * normed))).astype(BF)], None

    (hidden_grad,) = product_all(d_qfi, qfi_full, True, False, after_mixer, [x16, d_middle], [(model, BF)], 0, 7)

    hidden_grad, qfi_sum, gap_grad = order(hidden_grad, qfi_sum, gap_grad)

    def rowdot(w, g):
        return jnp.sum(w.astype(F32) * g, axis=1)

    out_rows = out_sum.astype(F32)
    g_out_gain = rowdot(w_output, out_rows)
    if plain:
        gu_rows = gu_rows.astype(F32)
        gate_rows, up_rows = from_units(gu_rows[:, :, :units]), from_units(gu_rows[:, :, units:])
        g_ffn_gain = rowdot(w_gate, gate_rows) + rowdot(w_up, up_rows)
        g_gate, g_up = gain_f * gate_rows, gain_f * up_rows
        gap_back = swap_group(gap_grad.reshape(per_rank, span, rows).transpose(1, 0, 2)).reshape(planes * rows)
        g_gap = scatter_dp(gap_back)
        qfi_rows = swap_seq(qfi_sum).reshape(ranks, rows, 3 * channels).astype(F32)
        parts = [from_heads(qfi_rows[:, :, j * channels : (j + 1) * channels]) for j in range(3)]
        g_attn_gain = sum(rowdot(w, g) for w, g in zip(mixer_weights, parts))
        g_query, g_forget, g_input = [gain_a * g for g in parts]
    else:
        gap_tile = jnp.broadcast_to(gap_grad, (8, channels))
        g_query, g_forget, g_input, g_attn_gain, gap_all, g_gate, g_up, g_ffn_gain = exit_plane(
            qfi_sum.reshape(ranks, rows, 3 * channels), mixer_weights, gain_a, gap_tile,
            gu_rows, (w_gate, w_up), gain_f, per_rank, groups, planes, 8,
        )
        g_attn_gain, g_ffn_gain = g_attn_gain[:, 0], g_ffn_gain[:, 0]
        plane, me = lax.axis_index("dp"), lax.axis_index("seq")
        at = lax.rem(plane, per_rank) * head + lax.rem(me, 2) * rows
        from_core = jnp.sum(gap_all[:, :, 0], axis=0)
        g_gap = lax.dynamic_slice(from_core, (plane // per_rank, at), (1, rows))[0]
    return (
        block_out[None],
        hidden_grad[None],
        g_attn_gain,
        g_gap,
        g_out_gain,
        g_query,
        g_forget,
        g_input,
        gain_o * out_rows,
        g_ffn_gain,
        g_gate,
        g_up,
        down_sum.astype(F32),
    )


def solution(mesh):
    tok, row, both = P("dp", "seq", None), P("dp", "seq"), P(("dp", "seq"))
    mat = P(("dp", "seq"), None)
    return jax.shard_map(
        on_device,
        mesh=mesh,
        in_specs=(tok, row, row, both, both, both, mat, mat, mat, mat, both, mat, mat, mat, tok),
        out_specs=(tok, tok, both, both, both, mat, mat, mat, mat, both, mat, mat, mat),
        check_vma=False,
    )
```

```python
import functools

import jax
import jax.numpy as jnp
from jax import lax
from jax.experimental import pallas as pl
from jax.experimental.pallas import tpu as pltpu
from jax.sharding import PartitionSpec as P

HEADS = 16
BLOCK = 64
UNROLL = 4
EPSILON = 1e-06
EXTRA = 128
BF = jnp.bfloat16
F32 = jnp.float32


def dot(a, b, dims):
    return lax.dot_general(a, b, (dims, ((), ())), preferred_element_type=F32)


def nn(a, b):
    return dot(a, b, ((1,), (0,)))


def nt(a, b):
    return dot(a, b, ((1,), (1,)))


def tn(a, b):
    return dot(a, b, ((0,), (0,)))


def inverse_rms(square_mean):
    return lax.rsqrt(square_mean + EPSILON)


def row_mean(v):
    return jnp.mean(v, axis=1, keepdims=True)


def split_sum(tri, v):
    high = v.astype(BF)
    low = (v - high.astype(F32)).astype(BF)
    return nn(tri, high) + nn(tri, low)


def chunk_prep(qfi, gap, live, width):
    query_pre, forget_pre, input_pre = (
        qfi[:, :width],
        qfi[:, width : 2 * width],
        qfi[:, 2 * width :],
    )
    sig_q = jax.nn.sigmoid(query_pre)
    sig_nf = jax.nn.sigmoid(-forget_pre)
    key = gap * sig_nf
    return query_pre, sig_q, sig_nf, key, input_pre * live


def triangle(lower):
    row = lax.broadcasted_iota(jnp.int32, (BLOCK, BLOCK), 0)
    col = lax.broadcasted_iota(jnp.int32, (BLOCK, BLOCK), 1)
    return (row >= col) if lower else (row <= col)


def chunk_masks(cut):
    row = lax.broadcasted_iota(jnp.int32, (BLOCK, BLOCK), 0)
    col = lax.broadcasted_iota(jnp.int32, (BLOCK, BLOCK), 1)
    allowed = (row >= col) & ((row >= cut) == (col >= cut))
    at = lax.broadcasted_iota(jnp.int32, (BLOCK, 1), 0)
    inherits = (at < cut).astype(F32)
    tail = ((at >= cut) | (cut >= BLOCK)).astype(F32)
    whole = (cut >= BLOCK).astype(F32)
    return allowed, inherits, tail, whole


def mixer_forward_kernel(heads, cut_ref, live_ref, n_ref, w_ref, gap_ref, mixed_ref, kept_ref, qfi_ref, state):
    step = pl.program_id(0)
    width = heads * 128

    @pl.when(step == 0)
    def _():
        state[...] = jnp.zeros_like(state)

    qfi_ref[...] = nn(n_ref[...], w_ref[...])
    lower = triangle(True).astype(BF)
    for u in range(UNROLL):
        chunk = step * UNROLL + u
        rows = slice(u * BLOCK, (u + 1) * BLOCK)
        at = lax.broadcasted_iota(jnp.int32, (BLOCK, 1), 0) + chunk * BLOCK
        live = (at < live_ref[0]).astype(F32)
        query_pre, sig_q, sig_nf, key, value = chunk_prep(qfi_ref[rows, :], gap_ref[...], live, width)
        query = query_pre * sig_q
        total = split_sum(lower, jnp.log1p(-key))
        centre = total[BLOCK // 2 : BLOCK // 2 + 1]
        ending = total[BLOCK - 1 :]
        scaled_q = (query * jnp.exp(total - centre)).astype(BF)
        scaled_k = (key * jnp.exp(centre - total)).astype(BF)
        value_low = value.astype(BF)
        allowed, inherits, tail, whole = chunk_masks(cut_ref[chunk])
        value_tail = (value * tail).astype(BF)
        e_centre = jnp.exp(centre)
        e_rest = jnp.exp(ending - centre)
        e_all = jnp.exp(ending) * whole
        square = jnp.zeros((BLOCK, 1), F32)
        for h in range(heads):
            cols = slice(h * 128, (h + 1) * 128)
            before = state[h]
            kept_ref[u, h] = before.astype(BF)
            scores = jnp.where(allowed, nt(scaled_q[:, cols], scaled_k[:, cols]), 0.0)
            inner = nn(scores.astype(BF), value_low[:, cols])
            outer = nt(scaled_q[:, cols], (before * e_centre[:, cols]).astype(BF))
            mixed = inner + outer * inherits
            square = square + jnp.sum(mixed * mixed, axis=1, keepdims=True)
            mixed_ref[rows, cols] = mixed.astype(BF)
            state[h] = before * e_all[:, cols] + tn(value_tail[:, cols], scaled_k[:, cols]) * e_rest[:, cols]
        lane = lax.broadcasted_iota(jnp.int32, (BLOCK, EXTRA), 1)
        high = square.astype(BF).astype(F32)
        mixed_ref[rows, width:] = jnp.where(lane == 0, high, jnp.where(lane == 1, square - high, 0.0)).astype(BF)


def mixer_backward_kernel(heads, cut_ref, live_ref, qfi_ref, gap_ref, kept_ref, grad_ref, out_ref, gap_out_ref, state):
    step = pl.program_id(0)
    last = pl.num_programs(0) - 1
    width = heads * 128

    @pl.when(step == 0)
    def _():
        state[...] = jnp.zeros_like(state)
        gap_out_ref[...] = jnp.zeros_like(gap_out_ref)

    lower = triangle(True).astype(BF)
    upper = triangle(False).astype(BF)
    for u in reversed(range(UNROLL)):
        chunk = (last - step) * UNROLL + u
        rows = slice(u * BLOCK, (u + 1) * BLOCK)
        at = lax.broadcasted_iota(jnp.int32, (BLOCK, 1), 0) + chunk * BLOCK
        live = (at < live_ref[0]).astype(F32)
        gap = gap_ref[...]
        query_pre, sig_q, sig_nf, key, value = chunk_prep(qfi_ref[rows, :], gap, live, width)
        query = query_pre * sig_q
        total = split_sum(lower, jnp.log1p(-key))
        centre = total[BLOCK // 2 : BLOCK // 2 + 1]
        ending = total[BLOCK - 1 :]
        e_q = jnp.exp(total - centre)
        e_k = jnp.exp(centre - total)
        scaled_q = (query * e_q).astype(BF)
        scaled_k = (key * e_k).astype(BF)
        value_low = value.astype(BF)
        allowed, inherits, tail, whole = chunk_masks(cut_ref[chunk])
        value_tail = (value * tail).astype(BF)
        grad = grad_ref[rows, :]
        grad_in = (grad.astype(F32) * inherits).astype(BF)
        e_centre = jnp.exp(centre)
        e_rest = jnp.exp(ending - centre)
        e_all = jnp.exp(ending) * whole
        d_query, d_key, d_value, d_total, d_end = [], [], [], [], []
        for h in range(heads):
            cols = slice(h * 128, (h + 1) * 128)
            before = kept_ref[u, h].astype(F32)
            after = state[h]
            q, k, v, g, gi = scaled_q[:, cols], scaled_k[:, cols], value_low[:, cols], grad[:, cols], grad_in[:, cols]
            vt = value_tail[:, cols]
            scores = jnp.where(allowed, nt(q, k), 0.0).astype(BF)
            d_scores = jnp.where(allowed, nt(g, v), 0.0).astype(BF)
            shifted = (before * e_centre[:, cols]).astype(BF)
            onward = (after * e_rest[:, cols]).astype(BF)
            dq = nn(d_scores, k) + nn(gi, shifted)
            dk_state = nn(vt, onward)
            dk = tn(d_scores, q) + dk_state
            dv = tn(scores, g) + nt(k, onward) * tail
            k32 = k.astype(F32)
            d_total.append(dq * q.astype(F32) - dk * k32)
            d_end.append(
                jnp.sum(after * before, axis=0, keepdims=True) * e_all[:, cols]
                + jnp.sum(dk_state * k32, axis=0, keepdims=True)
            )
            state[h] = after * e_all[:, cols] + tn(gi, q) * e_centre[:, cols]
            d_query.append(dq)
            d_key.append(dk)
            d_value.append(dv)
        d_query = jnp.concatenate(d_query, axis=1) * e_q
        d_key = jnp.concatenate(d_key, axis=1) * e_k
        d_value = jnp.concatenate(d_value, axis=1) * live
        d_log = split_sum(upper, jnp.concatenate(d_total, axis=1)) + jnp.concatenate(d_end, axis=1)
        d_key = d_key - d_log / (1.0 - key)
        gap_out_ref[...] += jnp.sum(d_key * sig_nf, axis=0, keepdims=True)
        out_ref[rows, :width] = (d_query * sig_q * (1.0 + query_pre * (1.0 - sig_q))).astype(BF)
        out_ref[rows, width : 2 * width] = (-d_key * key * (1.0 - sig_nf)).astype(BF)
        out_ref[rows, 2 * width :] = d_value.astype(BF)


MESH = pl.DeviceIdType.MESH
PIECES = 5
EARLY = 3
TILE = 1024
VMEM_LIMIT = 60 * 1024 * 1024
(S_X, S_Y, S_CORE, S_DIAG_Y, S_DIAG_X, S_CORE_X, S_CORE_Y, S_CORE_D, R_CORE, R_X, R_Y, R_LAST_Y, R_LAST_X, KINDS) = range(14)


class Place:
    def __init__(self):
        self.plane = lax.axis_index("dp")
        me = lax.axis_index("seq")
        self.me = me
        self.core = me % 2
        self.x = (me // 2) % 2
        self.y = me // 4

    def rank(self, fy=0, fx=0, fc=0):
        y = 1 - self.y if fy else self.y
        x = 1 - self.x if fx else self.x
        core = 1 - self.core if fc else self.core
        return 4 * y + 2 * x + core

    def device(self, fy=0, fx=0, fc=0):
        return (self.plane, self.rank(fy, fx, fc))


def greet(place):
    barrier = pltpu.get_barrier_semaphore()
    for flip in ((0, 0, 1), (0, 1, 0), (1, 0, 0)):
        pl.semaphore_signal(barrier, inc=1, device_id=place.device(*flip), device_id_type=MESH)
    pl.semaphore_wait(barrier, 3)


def remote(src, dst, sems, kind, b, device):
    send, recv = sems
    return pltpu.make_async_remote_copy(
        src_ref=src,
        dst_ref=dst,
        send_sem=send.at[kind, b],
        recv_sem=recv.at[kind, b],
        device_id=device,
        device_id_type=MESH,
    )


class Gather:
    def __init__(self, place, own, full, sems, local_sem):
        self.p, self.own, self.full, self.sems, self.local = place, own, full, sems, local_sem
        self.half = full.shape[2] // 2

    def keep(self, b):
        return pltpu.make_async_copy(self.own.at[b], self.full.at[self.p.me, b], self.local.at[b])

    def first(self, b):
        p, dst = self.p, self.full.at[self.p.me, b]
        return [
            remote(self.own.at[b], dst, self.sems, S_X, b, p.device(0, 1, 0)),
            remote(self.own.at[b], dst, self.sems, S_Y, b, p.device(1, 0, 0)),
            remote(self.own.at[b], dst, self.sems, S_CORE, b, p.device(0, 0, 1)),
        ]

    def second(self, b):
        p, h = self.p, self.half
        from_x, from_y = self.full.at[p.rank(0, 1, 0), b], self.full.at[p.rank(1, 0, 0), b]
        up, down = from_x.at[pl.ds(0, h)], from_y.at[pl.ds(h, h)]
        return [
            remote(up, up, self.sems, S_DIAG_Y, b, p.device(1, 0, 0)),
            remote(down, down, self.sems, S_DIAG_X, b, p.device(0, 1, 0)),
            remote(from_x, from_x, self.sems, S_CORE_X, b, p.device(0, 0, 1)),
            remote(from_y, from_y, self.sems, S_CORE_Y, b, p.device(0, 0, 1)),
        ]

    def third(self, b):
        p = self.p
        block = self.full.at[p.rank(1, 1, 0), b]
        return [remote(block, block, self.sems, S_CORE_D, b, p.device(0, 0, 1))]

    def arrived(self, kind, b, flips, rows=None):
        block = self.full.at[self.p.rank(*flips), b]
        if rows is not None:
            block = block.at[pl.ds(rows * self.half, self.half)]
        remote(block, block, self.sems, kind, b, self.p.device(0, 0, 1)).wait_recv()

    def start(self, b):
        self.keep(b).start()
        for copy in self.first(b):
            copy.start()

    def forward(self, b):
        self.arrived(S_X, b, (0, 1, 0))
        self.arrived(S_Y, b, (1, 0, 0))
        for copy in self.second(b):
            copy.start()

    def forward_last(self, b):
        self.arrived(S_DIAG_Y, b, (1, 1, 0), 0)
        self.arrived(S_DIAG_X, b, (1, 1, 0), 1)
        for copy in self.third(b):
            copy.start()

    def finish(self, b):
        self.arrived(S_CORE, b, (0, 0, 1))
        self.arrived(S_CORE_X, b, (0, 1, 1))
        self.arrived(S_CORE_Y, b, (1, 0, 1))
        self.arrived(S_CORE_D, b, (1, 1, 1))

    def drain(self, b):
        self.keep(b).wait()
        for copy in self.first(b) + self.second(b) + self.third(b):
            copy.wait_send()


def swap_pairs(place, parts, outs, send, recv, local):
    pairs = []
    for i, (part, out) in enumerate(zip(parts, outs)):
        pairs.append((pltpu.make_async_copy(part.at[place.me], out.at[place.me], local.at[i]), None))
        for k, flips in enumerate(FLIPS):
            there = out.at[place.rank(*flips)]
            pairs.append(tuple(
                pltpu.make_async_remote_copy(
                    src_ref=src, dst_ref=dst, send_sem=send.at[i, k], recv_sem=recv.at[i, k],
                    device_id=place.device(*flips), device_id_type=MESH,
                )
                for src, dst in ((part.at[place.rank(*flips)], out.at[place.me]), (there, there))
            ))
    return pairs


def swap_starts(place, parts, outs, send, recv, local):
    pairs = swap_pairs(place, parts, outs, send, recv, local)
    for copy, _ in pairs:
        copy.start()
    return pairs


def swap_waits(pairs):
    for copy, arrival in pairs:
        if arrival is None:
            copy.wait()
        else:
            copy.wait_send()
            arrival.wait_recv()


def greet_all(place):
    barrier = pltpu.get_barrier_semaphore()
    for flips in ((0, 0, 1), (0, 1, 0), (1, 0, 0), (0, 1, 1), (1, 0, 1), (1, 1, 0), (1, 1, 1)):
        pl.semaphore_signal(barrier, inc=1, device_id=place.device(*flips), device_id_type=MESH)
    pl.semaphore_wait(barrier, 7)


def fold(gain, w):
    return (gain * w.astype(F32)).astype(BF)


FLIPS = ((0, 0, 1), (0, 1, 0), (1, 0, 0), (0, 1, 1), (1, 0, 1), (1, 1, 0), (1, 1, 1))
ANY_SPEC = pl.BlockSpec(memory_space=pl.ANY)
VMEM_SPEC = pl.BlockSpec(memory_space=pltpu.VMEM)


def column_peers(place, planes):
    peers = []
    for hop in range(planes):
        for flip in (0, 1):
            if hop or flip:
                plane = lax.rem(place.plane + hop, planes)
                peers.append((plane, place.rank(0, 0, flip)))
    return peers


def column_spread(place, planes, src, dst, send, recv):
    waits = []
    for k, (plane, rank) in enumerate(column_peers(place, planes)):
        mine = dst.at[place.plane, place.core]
        copy = pltpu.make_async_remote_copy(
            src_ref=src, dst_ref=mine, send_sem=send.at[k], recv_sem=recv.at[k],
            device_id=(plane, rank), device_id_type=MESH,
        )
        copy.start()
        back = lax.rem(planes + 2 * place.plane - plane, planes)
        there = dst.at[back, lax.rem(rank, 2)]
        waits.append((copy, pltpu.make_async_remote_copy(
            src_ref=there, dst_ref=there, send_sem=send.at[k], recv_sem=recv.at[k],
            device_id=(plane, rank), device_id_type=MESH,
        )))
    return waits


def greet_column_and_plane(place, planes):
    barrier = pltpu.get_barrier_semaphore()
    devices = [place.device(*flips) for flips in FLIPS]
    devices += [p for p in column_peers(place, planes)[1:]]
    for device in devices:
        pl.semaphore_signal(barrier, inc=1, device_id=device, device_id_type=MESH)
    pl.semaphore_wait(barrier, len(devices))


def enter_plane(weights, gain, ids, gap, per_rank, groups, planes, collective_id):
    rows, model = weights[0].shape
    head = model // (8 * per_rank)
    channels = per_rank * head
    span = 8 // groups

    def kernel(q_ref, f_ref, i_ref, gain_ref, ids_ref, gap_ref, out_ref, ids_out, gap_out, part, *sems):
        send, recv, local, gap_send, gap_recv = sems
        place = Place()
        scale = gain_ref[...]
        for w, ref in enumerate((q_ref, f_ref, i_ref)):
            for a in range(groups):
                for m in range(span):
                    for j in range(per_rank):
                        h = (m * per_rank + j) * groups + a
                        at = w * channels + j * head
                        part[a * span + m, :, at : at + head] = fold(scale, ref[:, h * head : (h + 1) * head])
        greet_column_and_plane(place, planes)
        copies = swap_starts(place, [part], [out_ref], send, recv, local)
        gaps = column_spread(place, planes, gap_ref, gap_out, gap_send, gap_recv)
        own_gap = pltpu.make_async_copy(gap_ref, gap_out.at[place.plane, place.core], local.at[2])
        own_gap.start()
        own_ids = pltpu.make_async_copy(ids_ref, ids_out.at[place.me], local.at[1])
        own_ids.start()
        ids_copies = []
        for k, flips in enumerate(FLIPS):
            there = ids_out.at[place.rank(*flips)]
            made = [
                pltpu.make_async_remote_copy(
                    src_ref=src, dst_ref=dst, send_sem=send.at[1, k], recv_sem=recv.at[1, k],
                    device_id=place.device(*flips), device_id_type=MESH,
                )
                for src, dst in ((ids_ref, ids_out.at[place.me]), (there, there))
            ]
            made[0].start()
            ids_copies.append(made)
        swap_waits(copies)
        for copy, arrival in ids_copies + gaps:
            copy.wait_send()
            arrival.wait_recv()
        own_gap.wait()
        own_ids.wait()

    return pl.pallas_call(
        kernel,
        in_specs=[VMEM_SPEC] * 4 + [ANY_SPEC] * 2,
        out_specs=[ANY_SPEC] * 3,
        out_shape=[
            jax.ShapeDtypeStruct((8, rows, 3 * channels), BF),
            jax.ShapeDtypeStruct((8,) + ids.shape, ids.dtype),
            jax.ShapeDtypeStruct((planes, 2) + gap.shape, gap.dtype),
        ],
        scratch_shapes=[
            pltpu.VMEM((8, rows, 3 * channels), BF),
            pltpu.SemaphoreType.DMA((2, 7)),
            pltpu.SemaphoreType.DMA((2, 7)),
            pltpu.SemaphoreType.DMA((3,)),
            pltpu.SemaphoreType.DMA((2 * planes - 1,)),
            pltpu.SemaphoreType.DMA((2 * planes - 1,)),
        ],
        compiler_params=pltpu.CompilerParams(
            collective_id=collective_id, has_side_effects=True, vmem_limit_bytes=VMEM_LIMIT
        ),
        name="enter_plane",
    )(*weights, gain, ids, gap)


def gather_plane(x, w_gate, w_up, gain, planes, collective_id):
    tokens, width = x.shape
    rows = tokens // PIECES
    w_rows, every_unit = w_gate.shape
    units_in = every_unit // (8 * planes)
    units = units_in * planes
    x = x.reshape(PIECES, rows, width)

    def kernel(x_ref, gate_ref, up_ref, gain_ref, full, out_ref, normed, part, *sems):
        send, recv, local, swap_send, swap_recv, swap_local = sems
        place = Place()
        gather = Gather(place, normed, full, (send, recv), local)
        value = x_ref[0].astype(F32)
        normed[0] = (value * inverse_rms(row_mean(value * value))).astype(BF)
        greet_all(place)
        gather.start(0)
        for b in range(1, PIECES):
            value = x_ref[b].astype(F32)
            normed[b] = (value * inverse_rms(row_mean(value * value))).astype(BF)
            gather.start(b)
        scale = gain_ref[...]
        for side, ref in enumerate((gate_ref, up_ref)):
            for i in range(planes):
                for s in range(8):
                    at = (i * 8 + s) * units_in
                    to = side * units + i * units_in
                    part[s, :, to : to + units_in] = fold(scale, ref[:, at : at + units_in])
        copies = swap_starts(place, [part], [out_ref], swap_send, swap_recv, swap_local)
        for stage in (gather.forward, gather.forward_last, gather.finish):
            pl.loop(0, PIECES)(stage)
        swap_waits(copies)
        pl.loop(0, PIECES)(gather.drain)

    full, swapped = pl.pallas_call(
        kernel,
        in_specs=[VMEM_SPEC] * 4,
        out_specs=[ANY_SPEC] * 2,
        out_shape=[
            jax.ShapeDtypeStruct((8, PIECES, rows, width), BF),
            jax.ShapeDtypeStruct((8, w_rows, 2 * units), BF),
        ],
        scratch_shapes=[
            pltpu.VMEM((PIECES, rows, width), BF),
            pltpu.VMEM((8, w_rows, 2 * units), BF),
            pltpu.SemaphoreType.DMA((KINDS, PIECES)),
            pltpu.SemaphoreType.DMA((KINDS, PIECES)),
            pltpu.SemaphoreType.DMA((PIECES,)),
            pltpu.SemaphoreType.DMA((1, 7)),
            pltpu.SemaphoreType.DMA((1, 7)),
            pltpu.SemaphoreType.DMA((1,)),
        ],
        compiler_params=pltpu.CompilerParams(
            collective_id=collective_id, has_side_effects=True, vmem_limit_bytes=VMEM_LIMIT
        ),
        name="gather_plane",
    )(x, w_gate, w_up, gain)
    return full.reshape(8 * tokens, width), swapped


def exit_plane(summed, gap_grad, planes, collective_id):
    def kernel(sum_ref, gap_ref, landed, gap_out, *sems):
        send, recv, local, gap_send, gap_recv = sems
        place = Place()
        greet_column_and_plane(place, planes)
        copies = swap_starts(place, [sum_ref], [landed], send, recv, local)
        gaps = column_spread(place, planes, gap_ref, gap_out, gap_send, gap_recv)
        own_gap = pltpu.make_async_copy(gap_ref, gap_out.at[place.plane, place.core], local.at[1])
        own_gap.start()
        swap_waits(copies)
        for copy, arrival in gaps:
            copy.wait_send()
            arrival.wait_recv()
        own_gap.wait()

    return pl.pallas_call(
        kernel,
        in_specs=[ANY_SPEC] * 2,
        out_specs=[ANY_SPEC] * 2,
        out_shape=[
            jax.ShapeDtypeStruct(summed.shape, summed.dtype),
            jax.ShapeDtypeStruct((planes, 2) + gap_grad.shape, gap_grad.dtype),
        ],
        scratch_shapes=[
            pltpu.SemaphoreType.DMA((1, 7)),
            pltpu.SemaphoreType.DMA((1, 7)),
            pltpu.SemaphoreType.DMA((2,)),
            pltpu.SemaphoreType.DMA((2 * planes - 1,)),
            pltpu.SemaphoreType.DMA((2 * planes - 1,)),
        ],
        compiler_params=pltpu.CompilerParams(collective_id=collective_id, has_side_effects=True),
        name="exit_plane",
    )(summed, gap_grad)


def finish(weights, gain, swapped, moves):
    rows, width = weights[0].shape
    tile = 512

    def kernel(*refs):
        in_ref, gain_ref = refs[0], refs[1]
        w_refs = refs[2 : 2 + len(weights)]
        outs, gain_out = refs[2 + len(weights) : -1], refs[-1]
        for w, rank, source, target in moves:
            outs[w][:, target] = in_ref[rank, :, source].astype(F32)
        scale = gain_ref[...]
        total = jnp.zeros((rows, tile), F32)
        for ref, out in zip(w_refs, outs):
            for at in range(0, width, tile):
                grad = out[:, at : at + tile]
                total += grad * ref[:, at : at + tile].astype(F32)
                out[:, at : at + tile] = grad * scale
        column = jnp.sum(total, axis=1, keepdims=True)
        diagonal = lax.broadcasted_iota(jnp.int32, (rows, rows), 0) == lax.broadcasted_iota(jnp.int32, (rows, rows), 1)
        gain_out[...] = jnp.sum(jnp.where(diagonal, column, 0.0), axis=0, keepdims=True)

    results = pl.pallas_call(
        kernel,
        in_specs=[VMEM_SPEC] * (2 + len(weights)),
        out_specs=[VMEM_SPEC] * (len(weights) + 1),
        out_shape=[jax.ShapeDtypeStruct((rows, width), F32)] * len(weights) + [jax.ShapeDtypeStruct((1, rows), F32)],
        compiler_params=pltpu.CompilerParams(vmem_limit_bytes=VMEM_LIMIT),
        name="finish",
    )(swapped, gain, *weights)
    return results[:-1], results[-1].reshape(rows)


def unit_moves(units, planes, ranks):
    units_in = units // planes
    return [
        (
            side,
            s,
            slice(side * units + i * units_in, side * units + (i + 1) * units_in),
            slice((i * ranks + s) * units_in, (i * ranks + s + 1) * units_in),
        )
        for side in range(2)
        for i in range(planes)
        for s in range(ranks)
    ]


def head_moves(head, per_rank, groups, span):
    moves = []
    for w in range(3):
        for a in range(groups):
            for m in range(span):
                for j in range(per_rank):
                    h = (m * per_rank + j) * groups + a
                    at = (w * per_rank + j) * head
                    moves.append((w, a * span + m, slice(at, at + head), slice(h * head, (h + 1) * head)))
    return moves


class Scatter:
    def __init__(self, left, weight, transposed, stats):
        self.rows, self.columns = left[2], left[3]
        self.transposed, self.stats = transposed, stats
        self.weight = weight
        self.depth = weight[1] if transposed else weight[0]
        self.width = weight[0] if transposed else weight[1]
        self.half = self.width // 2
        self.extra = EXTRA if stats else 0

    def scratch(self):
        rows, half, full = self.rows, self.half, self.width + self.extra
        right = half + self.extra
        return [
            pltpu.VMEM((PIECES, 8, rows, self.columns), BF),
            pltpu.VMEM(self.weight, BF),
            pltpu.VMEM((PIECES, 4, rows, full), BF),
            pltpu.VMEM((PIECES, 4, rows, full), BF),
            pltpu.VMEM((4, rows, full), F32),
            pltpu.VMEM((PIECES, 2, rows, half), BF),
            pltpu.VMEM((PIECES, 2, rows, half), BF),
            pltpu.VMEM((PIECES, 2, rows, right), BF),
            pltpu.VMEM((PIECES, 2, rows, right), BF),
            pltpu.VMEM((PIECES, 2, rows, half), F32),
            pltpu.VMEM((PIECES, 2, rows, right), F32),
            pltpu.VMEM((PIECES, rows, half), BF),
            pltpu.VMEM((PIECES, rows, half), BF),
            pltpu.VMEM((PIECES, rows, right), BF),
            pltpu.VMEM((PIECES, rows, right), BF),
            pltpu.SemaphoreType.DMA((PIECES,)),
            pltpu.SemaphoreType.DMA((1,)),
        ]

    def bind(self, place, sems, left_ref, weight_ref, refs):
        self.place, self.sems, self.left_ref, self.weight_ref = place, sems, left_ref, weight_ref
        (self.x_buf, self.w_buf, self.core_out, self.core_in, self.total, self.x_out, self.x_in, self.y_out, self.y_in,
         self.keep_a, self.keep_b, self.last_y_out, self.last_y_in, self.last_x_out,
         self.last_x_in, self.load_sem, self.w_sem) = refs

    def weight_copy(self):
        return pltpu.make_async_copy(self.weight_ref, self.w_buf, self.w_sem.at[0])

    def start_loads(self):
        core = self.place.core
        for b in range(PIECES):
            for j in range(4):
                for side, at in ((0, 2 * j + 1 - core), (4, 2 * j + core)):
                    pltpu.make_async_copy(
                        self.left_ref.at[at, b], self.x_buf.at[b, side + j], self.load_sem.at[b]
                    ).start()
            if b == 0:
                self.weight_copy().start()

    def send_core(self, b):
        return remote(self.core_out.at[b], self.core_in.at[b], self.sems, R_CORE, b, self.place.device(0, 0, 1))

    def send_x(self, b):
        return remote(self.x_out.at[b], self.x_in.at[b], self.sems, R_X, b, self.place.device(0, 1, 0))

    def send_y(self, b):
        return remote(self.y_out.at[b], self.y_in.at[b], self.sems, R_Y, b, self.place.device(1, 0, 0))

    def send_last_y(self, b):
        return remote(self.last_y_out.at[b], self.last_y_in.at[b], self.sems, R_LAST_Y, b, self.place.device(1, 0, 0))

    def send_last_x(self, b):
        return remote(self.last_x_out.at[b], self.last_x_in.at[b], self.sems, R_LAST_X, b, self.place.device(0, 1, 0))

    def produce(self, b):
        rows, depth, width, tile = self.rows, self.depth, self.width, min(TILE, self.width)
        pltpu.make_async_copy(self.x_buf.at[b], self.x_buf.at[b], self.load_sem.at[b]).wait()

        def product(side, t):
            lhs = self.x_buf[b, 4 * side : 4 * side + 4, :, :depth].reshape(4 * rows, depth)
            at = slice(t * tile, (t + 1) * tile)
            out = nt(lhs, self.w_buf[at, :]) if self.transposed else nn(lhs, self.w_buf[:, at])
            return out.reshape(4, rows, tile), at

        for t in range(width // tile):
            out, at = product(0, t)
            self.core_out[b, :, :, at] = out.astype(BF)
        if self.stats:
            self.core_out[b, :, :, width:] = self.x_buf[b, :4, :, depth:]
        self.send_core(b).start()
        for t in range(width // tile):
            out, at = product(1, t)
            self.total[:, :, at] = out
        if self.stats:
            self.total[:, :, width:] = self.x_buf[b, 4:, :, depth:].astype(F32)

    def stage_one(self, b):
        place, half, total, core_in = self.place, self.half, self.total, self.core_in
        self.send_core(b).wait_recv()
        for i in range(2):
            go, stay = 2 * i + 1 - place.x, 2 * i + place.x
            self.x_out[b, i] = (total[go, :, :half] + core_in[b, go, :, :half].astype(F32)).astype(BF)
            self.keep_a[b, i] = total[stay, :, :half] + core_in[b, stay, :, :half].astype(F32)
        self.send_x(b).start()
        for i in range(2):
            go, stay = 2 * (1 - place.y) + i, 2 * place.y + i
            self.y_out[b, i] = (total[go, :, half:] + core_in[b, go, :, half:].astype(F32)).astype(BF)
            self.keep_b[b, i] = total[stay, :, half:] + core_in[b, stay, :, half:].astype(F32)
        self.send_y(b).start()

    def stage_two(self, b):
        self.send_x(b).wait_recv()
        go = 1 - self.place.y
        self.last_y_out[b] = (self.keep_a[b, go] + self.x_in[b, go].astype(F32)).astype(BF)
        self.send_last_y(b).start()
        self.send_y(b).wait_recv()
        go = 1 - self.place.x
        self.last_x_out[b] = (self.keep_b[b, go] + self.y_in[b, go].astype(F32)).astype(BF)
        self.send_last_x(b).start()

    def stage_three(self, b):
        self.send_last_y(b).wait_recv()
        self.send_last_x(b).wait_recv()
        y, x = self.place.y, self.place.x
        low = self.keep_a[b, y] + self.x_in[b, y].astype(F32) + self.last_y_in[b].astype(F32)
        high = self.keep_b[b, x] + self.y_in[b, x].astype(F32) + self.last_x_in[b].astype(F32)
        result = jnp.concatenate([low, high[:, : self.half]], axis=1)
        return result, (high[:, self.half :] if self.stats else None)

    def drain(self, b):
        for copy in (self.send_core, self.send_x, self.send_y, self.send_last_y, self.send_last_x):
            copy(b).wait_send()


def guarded(body, b):
    @pl.when((b >= 0) & (b < PIECES))
    def _():
        body(b)


def plane_sems():
    return [pltpu.SemaphoreType.DMA((KINDS, PIECES)), pltpu.SemaphoreType.DMA((KINDS, PIECES))]


def product_scatter(left, weight, transposed, stats, epilogue, owned, outs, gathered, collective_id, fillers=()):
    tokens = left.shape[0] // 8
    rows = tokens // PIECES
    left = left.reshape(8, PIECES, rows, left.shape[1])
    scatter = Scatter(left.shape, weight.shape, transposed, stats)
    count = len(scatter.scratch())

    def kernel(*refs):
        refs = list(refs)
        left_ref, weight_ref = refs.pop(0), refs.pop(0)
        own_refs = [refs.pop(0) for _ in owned]
        extra_in = [[refs.pop(0) for _ in f.arrays] for f in fillers]
        out_refs = [refs.pop(0) for _ in outs]
        full_ref = refs.pop(0) if gathered else None
        extra_out = [refs.pop(0) for _ in fillers]
        place = Place()
        sems = (refs.pop(0), refs.pop(0))
        scatter.bind(place, sems, left_ref, weight_ref, refs[:count])
        refs = refs[count:]
        own_bufs = [refs.pop(0) for _ in owned]
        out_bufs = [refs.pop(0) for _ in outs]
        own_sem, out_sem = refs.pop(0), refs.pop(0)
        own_copies = [
            pltpu.make_async_copy(ref, buf, own_sem.at[i]) for i, (ref, buf) in enumerate(zip(own_refs, own_bufs))
        ]

        def out_copies(b):
            return [
                pltpu.make_async_copy(buf.at[b], ref.at[b], out_sem.at[i, b])
                for i, (buf, ref) in enumerate(zip(out_bufs, out_refs))
            ]

        scatter.start_loads()
        for copy in own_copies:
            copy.start()
        for f, ins, out in zip(fillers, extra_in, extra_out):
            f.bind(ins, out, refs[: len(f.scratch)])
            refs = refs[len(f.scratch) :]
            f.start()
        greet(place)
        if gathered:
            n_buf, keep_sem = refs
            gather = Gather(place, n_buf, full_ref, sems, keep_sem)

        def end(b):
            result, stat = scatter.stage_three(b)
            written, sent = epilogue(result, stat, *[r[b] for r in own_bufs])
            for buf, value in zip(out_bufs, written):
                buf[b] = value
            for copy in out_copies(b):
                copy.start()
            if gathered:
                n_buf[b] = sent
                gather.start(b)

        scatter.weight_copy().wait()

        @pl.loop(0, PIECES + (9 if gathered else 5))
        def _(step):
            guarded(scatter.stage_one, step - 1)
            guarded(scatter.produce, step)
            guarded(scatter.stage_two, step - 3)
            for f in fillers:
                f.step(step)

            @pl.when(step == 5)
            def _():
                for copy in own_copies:
                    copy.wait()

            guarded(end, step - 5)
            if gathered:
                guarded(gather.forward, step - 7)
                guarded(gather.forward_last, step - 9)

        @pl.loop(0, PIECES)
        def _(b):
            if gathered:
                gather.finish(b)
                gather.drain(b)
            scatter.drain(b)
            for copy in out_copies(b):
                copy.wait()

        for f in fillers:
            f.end()

    any_spec = ANY_SPEC
    out_shape = [jax.ShapeDtypeStruct((PIECES, rows, c), d) for c, d in outs]
    out_specs = [any_spec] * len(outs)
    scratch = plane_sems() + scatter.scratch()
    scratch += [pltpu.VMEM((PIECES, rows, o.shape[1]), o.dtype) for o in owned]
    scratch += [pltpu.VMEM(o.shape, o.dtype) for o in out_shape]
    scratch += [pltpu.SemaphoreType.DMA((len(owned),)), pltpu.SemaphoreType.DMA((len(outs), PIECES))]
    if gathered:
        out_shape.append(jax.ShapeDtypeStruct((8, PIECES, rows, gathered), BF))
        out_specs.append(any_spec)
    args = [left, weight] + [o.reshape(PIECES, rows, o.shape[1]) for o in owned]
    in_specs = [any_spec, any_spec] + [any_spec] * len(owned)
    for f in fillers:
        args, in_specs = args + f.arrays, in_specs + [any_spec] * len(f.arrays)
        out_shape.append(f.out_shape)
        out_specs.append(any_spec)
        scratch += f.scratch
    if gathered:
        scratch += [pltpu.VMEM((PIECES, rows, gathered), BF), pltpu.SemaphoreType.DMA((PIECES,))]
    results = pl.pallas_call(
        kernel,
        in_specs=in_specs,
        out_specs=out_specs,
        out_shape=out_shape,
        scratch_shapes=scratch,
        compiler_params=pltpu.CompilerParams(
            collective_id=collective_id, has_side_effects=True, vmem_limit_bytes=VMEM_LIMIT
        ),
        cost_estimate=pl.CostEstimate(
            flops=16 * tokens * scatter.depth * scatter.width,
            bytes_accessed=(240 if gathered else 140) * tokens * scatter.width * 2,
            transcendentals=0,
        ),
        name="product_scatter",
    )(*args)
    flat = [r.reshape(tokens, r.shape[2]) for r in results[: len(outs)]]
    if gathered:
        flat.append(results[len(outs)].reshape(8 * tokens, gathered))
    return flat + list(results[len(outs) + (1 if gathered else 0) :])


class GradProduct:
    BLOCK = 256

    def __init__(self, left, right, by_right, first):
        self.left, self.right, self.by_right, self.first = left, right, by_right, first
        whole, streamed = (left, right) if by_right else (right, left)
        self.tokens, self.blocks = left.shape[0], streamed.shape[1] // self.BLOCK
        depth, width = left.shape[1], right.shape[1]
        block = (depth, self.BLOCK) if by_right else (self.BLOCK, width)
        self.arrays = [whole, streamed]
        self.out_shape = jax.ShapeDtypeStruct((depth, width), BF)
        self.scratch = [
            pltpu.VMEM(whole.shape, BF),
            pltpu.VMEM((2, self.tokens, self.BLOCK), BF),
            pltpu.VMEM((2,) + block, BF),
            pltpu.SemaphoreType.DMA((1,)),
            pltpu.SemaphoreType.DMA((2,)),
            pltpu.SemaphoreType.DMA((2,)),
        ]

    def plain(self):
        return tn(self.left, self.right).astype(BF)

    def bind(self, ins, out, refs):
        self.whole_ref, self.streamed_ref = ins
        self.out = out
        self.w_buf, self.s_buf, self.o_buf, self.w_sem, self.s_sem, self.o_sem = refs

    def columns(self, b):
        return pl.ds(pl.multiple_of(b * self.BLOCK, self.BLOCK), self.BLOCK)

    def load(self, b):
        return pltpu.make_async_copy(self.streamed_ref.at[:, self.columns(b)], self.s_buf.at[b % 2], self.s_sem.at[b % 2])

    def store(self, b):
        to = self.out.at[:, self.columns(b)] if self.by_right else self.out.at[self.columns(b)]
        return pltpu.make_async_copy(self.o_buf.at[b % 2], to, self.o_sem.at[b % 2])

    def whole_copy(self):
        return pltpu.make_async_copy(self.whole_ref, self.w_buf, self.w_sem.at[0])

    def start(self):
        self.whole_copy().start(priority=1)
        self.load(0).start(priority=1)
        self.load(1).start(priority=1)

    def step(self, step):
        b = step - self.first

        @pl.when(b == 0)
        def _():
            self.whole_copy().wait()

        @pl.when((b >= 0) & (b < self.blocks))
        def _():
            self.load(b).wait()

            @pl.when(b >= 2)
            def _():
                self.store(b - 2).wait()

            streamed, whole = self.s_buf[b % 2], self.w_buf[...]
            product = tn(whole, streamed) if self.by_right else tn(streamed, whole)
            self.o_buf[b % 2] = product.astype(BF)
            self.store(b).start(priority=1)

        @pl.when((b >= 0) & (b + 2 < self.blocks))
        def _():
            self.load(b + 2).start(priority=1)

    def end(self):
        self.store(self.blocks - 2).wait()
        self.store(self.blocks - 1).wait()


def mixer_specs(tokens, heads, reverse):
    width, span = heads * 128, UNROLL * BLOCK
    steps = tokens // span

    def at(i):
        return steps - 1 - i if reverse else i

    return (
        steps,
        pl.BlockSpec((span, 3 * width), lambda i, *_: (at(i), 0)),
        pl.BlockSpec((1, width), lambda i, *_: (0, 0)),
        pl.BlockSpec((UNROLL, heads, 128, 128), lambda i, *_: (at(i), 0, 0, 0)),
        lambda columns: pl.BlockSpec((span, columns), lambda i, *_: (at(i), 0)),
    )


def mixer_forward(cut, live, n1, weight, gap, own, out_pieces, per_rank, collective_id):
    tokens, heads = n1.shape[0], gap.shape[1] // 128
    width = heads * 128
    steps, qfi_spec, gap_spec, kept_spec, block = mixer_specs(tokens, heads, False)
    together = lax.axis_size("seq") == 8

    def kernel(cut_ref, live_ref, n_ref, w_ref, gap_ref, *refs):
        if not together:
            return mixer_forward_kernel(heads, cut_ref, live_ref, n_ref, w_ref, gap_ref, *refs)
        (own_ref, pieces_ref, mixed_ref, kept_ref, qfi_ref, full_ref, rows_ref, state, own_buf, pieces_buf, send, recv, local,
         w_send, w_recv, w_local) = refs
        place = Place()
        gather = Gather(place, own_buf, full_ref, (send, recv), local)
        loads = [
            pltpu.make_async_copy(own_ref, own_buf, local.at[0]),
            pltpu.make_async_copy(pieces_ref, pieces_buf, w_local.at[0]),
        ]

        def exchange(j):
            core = place.core
            here = pltpu.make_async_copy(
                pieces_buf.at[core * per_rank + j], rows_ref.at[j, core], w_local.at[j]
            )
            there = pltpu.make_async_remote_copy(
                src_ref=pieces_buf.at[(1 - core) * per_rank + j], dst_ref=rows_ref.at[j, core],
                send_sem=w_send.at[j], recv_sem=w_recv.at[j], device_id=place.device(0, 0, 1), device_id_type=MESH,
            )
            back = rows_ref.at[j, 1 - core]
            arrival = pltpu.make_async_remote_copy(
                src_ref=back, dst_ref=back, send_sem=w_send.at[j], recv_sem=w_recv.at[j],
                device_id=place.device(0, 0, 1), device_id_type=MESH,
            )
            return here, there, arrival

        @pl.when(pl.program_id(0) == 0)
        def _():
            for load in loads:
                load.start()
            greet(place)
            for load in loads:
                load.wait()
            pl.loop(0, EARLY)(gather.start)
            for j in range(per_rank):
                here, there, _ = exchange(j)
                here.start()
                there.start()

        mixer_forward_kernel(
            heads, cut_ref, live_ref, n_ref, w_ref, gap_ref, mixed_ref, kept_ref, qfi_ref, state
        )

        for b in range(EARLY):
            @pl.when(pl.program_id(0) == min(steps - 1, (8 + 7 * b) // 4))
            def _():
                gather.forward(b)

        @pl.when(pl.program_id(0) == steps - 1)
        def _():
            for stage in (gather.forward_last, gather.finish, gather.drain):
                pl.loop(0, EARLY)(stage)
            for j in range(per_rank):
                here, there, arrival = exchange(j)
                here.wait()
                there.wait_send()
                arrival.wait_recv()

    fixed = pl.BlockSpec(weight.shape, lambda i, *_: (0, 0), pipeline_mode=pl.Buffered(1))
    in_specs, args = [block(n1.shape[1]), fixed, gap_spec], [n1, weight, gap]
    out_specs = [block(width + EXTRA), kept_spec, qfi_spec]
    out_shape = [
        jax.ShapeDtypeStruct((tokens, width + EXTRA), BF),
        jax.ShapeDtypeStruct((tokens // BLOCK, heads, 128, 128), BF),
        jax.ShapeDtypeStruct((tokens, 3 * width), F32),
    ]
    scratch = [pltpu.VMEM((heads, 128, 128), F32)]
    params = pltpu.CompilerParams(vmem_limit_bytes=VMEM_LIMIT)
    if together:
        rows = own.shape[0] // PIECES
        own = own.reshape(PIECES, rows, own.shape[1])
        w_rows, model = out_pieces.shape[1:]
        in_specs, args = in_specs + [ANY_SPEC] * 2, args + [own, out_pieces]
        out_specs = out_specs + [ANY_SPEC] * 2
        out_shape = out_shape + [
            jax.ShapeDtypeStruct((8,) + own.shape, own.dtype),
            jax.ShapeDtypeStruct((per_rank, 2, w_rows, model), BF),
        ]
        scratch = scratch + [pltpu.VMEM(own.shape, BF), pltpu.VMEM(out_pieces.shape, BF)]
        scratch = scratch + plane_sems() + [pltpu.SemaphoreType.DMA((PIECES,))]
        scratch = scratch + [pltpu.SemaphoreType.DMA((per_rank,))] * 3
        params = pltpu.CompilerParams(
            vmem_limit_bytes=VMEM_LIMIT, collective_id=collective_id, has_side_effects=True
        )
    results = pl.pallas_call(
        kernel,
        grid_spec=pltpu.PrefetchScalarGridSpec(
            num_scalar_prefetch=2, grid=(steps,), in_specs=in_specs, out_specs=out_specs, scratch_shapes=scratch
        ),
        out_shape=out_shape,
        compiler_params=params,
        cost_estimate=pl.CostEstimate(
            flops=tokens * width * (128 * 10 + 6 * n1.shape[1]),
            bytes_accessed=60 * tokens * n1.shape[1],
            transcendentals=tokens * width * 6,
        ),
        name="mixer_forward",
    )(cut, live, *args)
    mixed, kept, qfi = results[:3]
    if together:
        return mixed, kept, qfi, results[3], results[4].reshape(width, model)
    return mixed, kept, qfi, lax.all_gather(own, "seq", axis=0, tiled=True), None


def mixer_backward(cut, live, qfi, gap, kept, grad, parts, grad_out, per_rank, collective_id):
    tokens, heads = qfi.shape[0], gap.shape[1] // 128
    width = heads * 128
    steps, qfi_spec, gap_spec, kept_spec, block = mixer_specs(tokens, heads, True)
    together = lax.axis_size("seq") == 8
    planes = lax.axis_size("dp")

    def kernel(cut_ref, live_ref, qfi_ref, gap_ref, kept_ref, grad_ref, *refs):
        if not together:
            return mixer_backward_kernel(heads, cut_ref, live_ref, qfi_ref, gap_ref, kept_ref, grad_ref, *refs)
        (parts_ref, og_ref, out_ref, gap_out_ref, swapped_ref, sum_ref, state, parts_buf, og_buf, by_plane, landed,
         send, recv, local, c_send, c_recv, z_send, z_recv, load_sem) = refs
        place, step = Place(), pl.program_id(0)
        core = place.core
        loads = [
            pltpu.make_async_copy(parts_ref, parts_buf, load_sem.at[0]),
            pltpu.make_async_copy(og_ref, og_buf, load_sem.at[1]),
        ]

        def over_core(j):
            there = by_plane.at[core * per_rank + j]
            back = by_plane.at[(1 - core) * per_rank + j]
            return [
                pltpu.make_async_remote_copy(
                    src_ref=src, dst_ref=dst, send_sem=c_send.at[j], recv_sem=c_recv.at[j],
                    device_id=place.device(0, 0, 1), device_id_type=MESH,
                )
                for src, dst in ((og_buf.at[j, 1 - core], there), (back, back))
            ]

        def over_planes(hop):
            plane = lax.rem(place.plane + hop, planes)
            back = landed.at[planes - hop - 1]
            return [
                pltpu.make_async_remote_copy(
                    src_ref=src, dst_ref=dst, send_sem=z_send.at[hop - 1], recv_sem=z_recv.at[hop - 1],
                    device_id=(plane, place.me), device_id_type=MESH,
                )
                for src, dst in ((by_plane.at[plane], landed.at[planes - hop - 1]), (back, back))
            ]

        swaps = functools.partial(swap_pairs, place, [parts_buf], [swapped_ref], send, recv, local)

        @pl.when(step == 0)
        def _():
            for load in loads:
                load.start()
            greet_column_and_plane(place, planes)
            for load in loads:
                load.wait()
            for j in range(per_rank):
                over_core(j)[0].start()
                by_plane[core * per_rank + j] = og_buf[j, core]
            for copy, _ in swaps():
                copy.start()

        @pl.when(step == 1)
        def _():
            for j in range(per_rank):
                there, arrival = over_core(j)
                there.wait_send()
                arrival.wait_recv()
            for hop in range(1, planes):
                over_planes(hop)[0].start()

        mixer_backward_kernel(
            heads, cut_ref, live_ref, qfi_ref, gap_ref, kept_ref, grad_ref, out_ref, gap_out_ref, state
        )

        @pl.when(step == steps - 1)
        def _():
            swap_waits(swaps())
            total = by_plane[place.plane].astype(F32)
            for hop in range(1, planes):
                there, arrival = over_planes(hop)
                there.wait_send()
                arrival.wait_recv()
                total += landed[planes - hop - 1].astype(F32)
            sum_ref[...] = total

    in_specs = [qfi_spec, gap_spec, kept_spec, block(width)]
    out_specs = [block(3 * width), gap_spec]
    out_shape = [jax.ShapeDtypeStruct((tokens, 3 * width), BF), jax.ShapeDtypeStruct((1, width), F32)]
    scratch = [pltpu.VMEM((heads, 128, 128), F32)]
    args = [qfi, gap, kept, grad]
    params = pltpu.CompilerParams(vmem_limit_bytes=VMEM_LIMIT)
    if together:
        rows, model = grad_out.shape[2:]
        in_specs, args = in_specs + [ANY_SPEC] * 2, args + [parts, grad_out]
        out_specs = out_specs + [ANY_SPEC, pl.BlockSpec((rows, model), lambda i, *_: (0, 0))]
        out_shape = out_shape + [
            jax.ShapeDtypeStruct(parts.shape, BF),
            jax.ShapeDtypeStruct((rows, model), F32),
        ]
        scratch = scratch + [
            pltpu.VMEM(parts.shape, BF),
            pltpu.VMEM(grad_out.shape, BF),
            pltpu.VMEM((planes, rows, model), BF),
            pltpu.VMEM((planes - 1, rows, model), BF),
            pltpu.SemaphoreType.DMA((1, 7)),
            pltpu.SemaphoreType.DMA((1, 7)),
            pltpu.SemaphoreType.DMA((1,)),
            pltpu.SemaphoreType.DMA((per_rank,)),
            pltpu.SemaphoreType.DMA((per_rank,)),
            pltpu.SemaphoreType.DMA((planes - 1,)),
            pltpu.SemaphoreType.DMA((planes - 1,)),
            pltpu.SemaphoreType.DMA((2,)),
        ]
        params = pltpu.CompilerParams(
            vmem_limit_bytes=VMEM_LIMIT, collective_id=collective_id, has_side_effects=True
        )
    return pl.pallas_call(
        kernel,
        grid_spec=pltpu.PrefetchScalarGridSpec(
            num_scalar_prefetch=2, grid=(steps,), in_specs=in_specs, out_specs=out_specs, scratch_shapes=scratch
        ),
        out_shape=out_shape,
        compiler_params=params,
        cost_estimate=pl.CostEstimate(
            flops=tokens * width * 128 * 24, bytes_accessed=tokens * width * 28, transcendentals=tokens * width * 6
        ),
        name="mixer_backward",
    )(cut, live, *args)


def feed_forward_kernel(units, n_ref, gu_ref, units_ref, act_ref, slope_ref, gate_w, up_w):
    @pl.when(pl.program_id(0) == 0)
    def _():
        gate_w[...] = gu_ref[:, :units]
        up_w[...] = gu_ref[:, units:]

    n = n_ref[...]
    gate, up = nn(n, gate_w[...]), nn(n, up_w[...])
    sig = jax.nn.sigmoid(gate)
    act = gate * sig
    units_ref[...] = (act * up).astype(BF)
    act_ref[...] = act.astype(BF)
    slope_ref[...] = (up * sig * (1.0 + gate * (1.0 - sig))).astype(BF)


def feed_backward_kernel(units, g_ref, down_ref, act_ref, slope_ref, grad_ref):
    d_units = nt(g_ref[...], down_ref[...])
    grad_ref[:, :units] = (d_units * slope_ref[...].astype(F32)).astype(BF)
    grad_ref[:, units:] = (d_units * act_ref[...].astype(F32)).astype(BF)


def fixed_block(shape):
    return pl.BlockSpec(shape, lambda i: (0, 0), pipeline_mode=pl.Buffered(1))


def row_block(columns):
    return pl.BlockSpec((512, columns), lambda i: (i, 0))


def feed_forward(n2, gu, own, full, collective_id):
    tokens, model = n2.shape
    units = gu.shape[1] // 2
    steps = tokens // 512
    together = lax.axis_size("seq") == 8

    def kernel(n_ref, gu_ref, *refs):
        if not together:
            return feed_forward_kernel(units, n_ref, gu_ref, *refs)
        own_ref, _, units_ref, act_ref, slope_ref, full_ref, gate_w, up_w, own_buf, send, recv, local = refs
        place, step = Place(), pl.program_id(0)
        gather = Gather(place, own_buf, full_ref, (send, recv), local)

        @pl.when(step == 0)
        def _():
            load = pltpu.make_async_copy(own_ref, own_buf, local.at[0])
            load.start()
            greet(place)
            load.wait()
            pl.loop(EARLY, PIECES)(gather.start)

        feed_forward_kernel(units, n_ref, gu_ref, units_ref, act_ref, slope_ref, gate_w, up_w)

        @pl.when(step == min(3, steps - 1))
        def _():
            pl.loop(EARLY, PIECES)(gather.forward)

        @pl.when(step == steps - 1)
        def _():
            for stage in (gather.forward_last, gather.finish, gather.drain):
                pl.loop(EARLY, PIECES)(stage)

    in_specs, args = [row_block(model), fixed_block(gu.shape)], [n2, gu]
    out_specs = [row_block(units)] * 3
    out_shape = [jax.ShapeDtypeStruct((tokens, units), d) for d in (BF, BF, BF)]
    scratch = [pltpu.VMEM((model, units), BF), pltpu.VMEM((model, units), BF)]
    params, aliases = pltpu.CompilerParams(vmem_limit_bytes=VMEM_LIMIT), {}
    if together:
        own = own.reshape(PIECES, own.shape[0] // PIECES, own.shape[1])
        in_specs, args = in_specs + [ANY_SPEC] * 2, args + [own, full]
        out_specs = out_specs + [ANY_SPEC]
        out_shape = out_shape + [jax.ShapeDtypeStruct(full.shape, full.dtype)]
        scratch = scratch + [pltpu.VMEM(own.shape, BF)] + plane_sems() + [pltpu.SemaphoreType.DMA((PIECES,))]
        params = pltpu.CompilerParams(
            vmem_limit_bytes=VMEM_LIMIT, collective_id=collective_id, has_side_effects=True
        )
        aliases = {3: 3}
    results = pl.pallas_call(
        kernel,
        grid=(steps,),
        in_specs=in_specs,
        out_specs=out_specs,
        out_shape=out_shape,
        scratch_shapes=scratch,
        compiler_params=params,
        input_output_aliases=aliases,
        cost_estimate=pl.CostEstimate(
            flops=4 * tokens * model * units, bytes_accessed=4 * tokens * model, transcendentals=tokens * units
        ),
        name="feed_forward",
    )(*args)
    if together:
        return results[0], results[1], results[2], results[3].reshape(tokens, model)
    return results[0], results[1], results[2], full


def feed_backward(grad, down, act, slope):
    tokens, model = grad.shape
    units = down.shape[0]
    return pl.pallas_call(
        functools.partial(feed_backward_kernel, units),
        grid=(tokens // 512,),
        in_specs=[row_block(model), fixed_block(down.shape), row_block(units), row_block(units)],
        out_specs=row_block(2 * units),
        out_shape=jax.ShapeDtypeStruct((tokens, 2 * units), BF),
        compiler_params=pltpu.CompilerParams(vmem_limit_bytes=VMEM_LIMIT),
        cost_estimate=pl.CostEstimate(
            flops=2 * tokens * model * units, bytes_accessed=8 * tokens * model, transcendentals=0
        ),
        name="feed_backward",
    )(grad, down, act, slope)


def gather_dp(v):
    return lax.all_gather(v, "dp", axis=0, tiled=True)


def scatter_dp(v):
    return lax.psum_scatter(v, "dp", scatter_dimension=0, tiled=True)


def swap_seq(v):
    return lax.all_to_all(v, "seq", split_axis=0, concat_axis=0, tiled=True)


def product_all(left, weight, transposed, stats, epilogue, owned, outs, gathered, collective_id, fillers=()):
    if lax.axis_size("seq") == 8:
        return product_scatter(left, weight, transposed, stats, epilogue, owned, outs, gathered, collective_id, fillers)
    depth = left.shape[1] - (EXTRA if stats else 0)
    product = (nt if transposed else nn)(left[:, :depth], weight).astype(BF)
    result = lax.psum_scatter(product, "seq", scatter_dimension=0, tiled=True).astype(F32)
    stat = None
    if stats:
        stat = lax.psum_scatter(left[:, depth:].astype(F32), "seq", scatter_dimension=0, tiled=True)
    written, sent = epilogue(result, stat, *owned)
    written = [w.astype(d) for w, (_, d) in zip(written, outs)]
    written += [lax.all_gather(sent, "seq", axis=0, tiled=True)] if gathered else []
    return written + [f.plain() for f in fillers]


def split_lanes(v):
    lane = lax.broadcasted_iota(jnp.int32, (v.shape[0], EXTRA), 1)
    high = v.astype(BF).astype(F32)
    return jnp.where(lane == 0, high, jnp.where(lane == 1, v - high, 0.0)).astype(BF)


def on_device(
    hidden,
    seg_ids,
    pad_mask,
    attn_gain,
    gate_gap,
    out_gain,
    w_query,
    w_forget,
    w_input,
    w_output,
    ffn_gain,
    w_gate,
    w_up,
    w_down,
    out_grad,
):
    planes, ranks = lax.axis_size("dp"), lax.axis_size("seq")
    row_tokens, model = hidden.shape[1:]
    rows = w_query.shape[0]
    units_in = w_down.shape[0]
    head = model // HEADS
    span = head // rows
    per_rank, groups = planes // span, ranks // span
    channels = per_rank * head
    units = planes * units_in
    tokens = ranks * row_tokens
    members = [[a * span + m for m in range(span)] for a in range(groups)]

    def to_heads(w):
        parts = w.reshape(rows, span, per_rank, groups, head)
        return parts.transpose(3, 1, 0, 2, 4).reshape(ranks, rows, channels)

    def from_heads(parts):
        parts = parts.reshape(groups, span, rows, per_rank, head)
        return parts.transpose(2, 1, 3, 0, 4).reshape(rows, model)

    def to_units(w):
        parts = w.reshape(rows, planes, ranks, units_in)
        return parts.transpose(2, 0, 1, 3).reshape(ranks, rows, units)

    def from_units(parts):
        parts = parts.reshape(ranks, rows, planes, units_in)
        return parts.transpose(1, 2, 0, 3).reshape(rows, planes * ranks * units_in)

    def own_rows(v):
        return v.reshape((span, per_rank) + v.shape[1:])

    def swap_group(v):
        return lax.all_to_all(v, "seq", split_axis=0, concat_axis=0, axis_index_groups=members)

    gain_a, gain_o, gain_f = (g.astype(F32)[:, None] for g in (attn_gain, out_gain, ffn_gain))

    plain = ranks != 8

    def order(first, *rest):
        return lax.optimization_barrier((first,) + rest)

    x16 = hidden[0]
    ids = jnp.concatenate([seg_ids, pad_mask], axis=0)
    mixer_weights = (w_query, w_forget, w_input)
    out_pieces = lax.all_gather(fold(gain_o, w_output), "dp", axis=0)
    if plain:
        qfi_part = jnp.concatenate([to_heads(fold(gain_a, w)) for w in mixer_weights], axis=2)
        qfi_swapped = swap_seq(qfi_part)
        gu_part = jnp.concatenate([to_units(fold(gain_f, w)) for w in (w_gate, w_up)], axis=2)
        gu_swapped = swap_seq(gu_part)
        x = x16.astype(F32)
        normed = (x * inverse_rms(row_mean(x * x))).astype(BF)
        n1 = lax.all_gather(normed, "seq", axis=0, tiled=True)
        gap_pieces = lax.all_gather(gate_gap, "dp", axis=0)
        gap_own = swap_group(own_rows(gap_pieces)).transpose(1, 0, 2)
        ids = lax.all_gather(ids, "seq", axis=0)
    else:
        wide = -(-row_tokens // 128) * 128
        ids = jnp.pad(ids, ((0, 6), (0, wide - row_tokens)))
        gap_tile = jnp.pad(gate_gap[None], ((0, 15), (0, 128 - rows)))
        qfi_swapped, ids, gap_all = enter_plane(
            mixer_weights, gain_a, ids, gap_tile, per_rank, groups, planes, 1
        )
        ids = ids[:, :2, :row_tokens]
        mine = lax.rem(lax.axis_index("seq"), 2) * per_rank
        gap_own = lax.dynamic_slice_in_dim(gap_all[:, :, 0, :rows], mine, per_rank, axis=0)
        x16, qfi_swapped = order(x16, qfi_swapped)
        n1, gu_swapped = gather_plane(x16, w_gate, w_up, gain_f, planes, 2)
    qfi_full = gather_dp(qfi_swapped.reshape(ranks * rows, 3 * channels))
    gu_full = gather_dp(gu_swapped.reshape(ranks * rows, 2 * units))
    gap_own = gap_own.reshape(1, channels).astype(F32)
    segment = ids[:, 0].reshape(tokens // BLOCK, BLOCK)
    live = jnp.sum(ids[:, 1]).reshape(1)
    ends = segment[:, -1]
    before = jnp.concatenate([segment[:1, 0], ends[:-1]])
    cut = jnp.sum((segment == before[:, None]).astype(jnp.int32), axis=1)

    og16 = out_grad[0]
    mixed, kept, qfi, grad_all, out_own = mixer_forward(
        cut, live, n1, qfi_full, gap_own, og16, out_pieces, per_rank, 3
    )
    if plain:
        out_own = swap_group(own_rows(out_pieces)).transpose(1, 0, 2, 3).reshape(channels, model)

    def after_output(result, stat, x16):
        x = x16.astype(F32)
        factor_o = inverse_rms(jnp.sum(stat, axis=1, keepdims=True) / model)
        middle = x + factor_o * result
        normed = middle * inverse_rms(row_mean(middle * middle))
        return [middle, jnp.broadcast_to(factor_o, (x.shape[0], EXTRA))], normed.astype(BF)

    mixed, w_down_late = order(mixed, w_down)
    down_own = gather_dp(w_down_late)
    middle, factor_o, n2 = product_all(
        mixed, out_own, False, True, after_output, [x16], [(model, F32), (EXTRA, F32)], model, 4
    )
    hidden_units, act, slope, grad_all = feed_forward(n2, gu_full, og16, grad_all, 10)
    def after_down(result, stat, middle):
        return [(middle + result).astype(BF)], None

    grad_down = tn(hidden_units, grad_all).astype(BF)
    down_sum = scatter_dp(grad_down)
    act, _ = order(act, grad_down)
    d_gu = feed_backward(grad_all, down_own, act, slope)
    block_out, grad_gu = product_all(
        hidden_units, down_own, False, False, after_down, [middle], [(model, BF)], 0, 6,
        (GradProduct(n2, d_gu, False, 0),),
    )
    gu_sum = scatter_dp(grad_gu)
    d_gu, grad_gu = order(d_gu, grad_gu)

    def after_ffn(result, stat, middle, og16, x16, factor_o):
        factor_o = factor_o[:, :1]
        factor_m = inverse_rms(row_mean(middle * middle))
        normed = middle * factor_m
        d_middle = og16.astype(F32) + factor_m * (result - normed * row_mean(result * normed))
        mean_o = row_mean(d_middle * (middle - x16.astype(F32)))
        beta = split_lanes(factor_o * factor_o * mean_o)
        return [d_middle], jnp.concatenate([(factor_o * d_middle).astype(BF), beta], axis=1)

    d_middle, d_attn = product_all(
        d_gu, gu_full, True, False, after_ffn, [middle, og16, x16, factor_o], [(model, F32)], model + EXTRA, 5
    )
    d_attn, down_sum = order(d_attn, down_sum)
    beta = jnp.sum(d_attn[:, model:].astype(F32), axis=1, keepdims=True)
    d_attn = d_attn[:, :model]

    mixed = mixed[:, :channels]
    grad_out = tn(mixed, d_attn).astype(BF)
    d_mixed = (nt(d_attn, out_own) - beta * mixed.astype(F32)).astype(BF)
    grad_out, d_mixed = order(grad_out, d_mixed)
    if plain:
        d_qfi, gap_grad = mixer_backward(cut, live, qfi, gap_own, kept, d_mixed, None, None, per_rank, 6)
        out_back = grad_out.reshape(per_rank, span, rows, model).transpose(1, 0, 2, 3)
        out_rows = scatter_dp(swap_group(out_back).reshape(planes * rows, model)).astype(F32)
        gu_rows = swap_seq(gu_sum).reshape(ranks, rows, 2 * units)
    else:
        d_qfi, gap_grad, gu_rows, out_rows = mixer_backward(
            cut, live, qfi, gap_own, kept, d_mixed, gu_sum.reshape(ranks, rows, 2 * units),
            grad_out.reshape(per_rank, span, rows, model), per_rank, 9,
        )
    grad_qfi = tn(n1, d_qfi).astype(BF)
    grad_qfi, d_qfi = order(grad_qfi, d_qfi)
    qfi_sum = scatter_dp(grad_qfi)

    def after_mixer(result, stat, x16, d_middle):
        x = x16.astype(F32)
        factor_x = inverse_rms(row_mean(x * x))
        normed = x * factor_x
        return [(d_middle + factor_x * (result - normed * row_mean(result * normed))).astype(BF)], None

    (hidden_grad,) = product_all(d_qfi, qfi_full, True, False, after_mixer, [x16, d_middle], [(model, BF)], 0, 7)

    hidden_grad, gu_rows, down_sum, out_rows, gap_grad = order(hidden_grad, gu_rows, down_sum, out_rows, gap_grad)

    def rowdot(w, g):
        return jnp.sum(w.astype(F32) * g, axis=1)

    g_out_gain = rowdot(w_output, out_rows)
    if plain:
        gu_rows = gu_rows.astype(F32)
        gate_rows, up_rows = from_units(gu_rows[:, :, :units]), from_units(gu_rows[:, :, units:])
        g_ffn_gain = rowdot(w_gate, gate_rows) + rowdot(w_up, up_rows)
        g_gate, g_up = gain_f * gate_rows, gain_f * up_rows
        gap_back = swap_group(gap_grad.reshape(per_rank, span, rows).transpose(1, 0, 2)).reshape(planes * rows)
        g_gap = scatter_dp(gap_back)
        qfi_rows = swap_seq(qfi_sum).reshape(ranks, rows, 3 * channels).astype(F32)
        parts = [from_heads(qfi_rows[:, :, j * channels : (j + 1) * channels]) for j in range(3)]
        g_attn_gain = sum(rowdot(w, g) for w, g in zip(mixer_weights, parts))
        g_query, g_forget, g_input = [gain_a * g for g in parts]
    else:
        (g_gate, g_up), g_ffn_gain = finish((w_gate, w_up), gain_f, gu_rows, unit_moves(units, planes, ranks))
        gap_tile = jnp.broadcast_to(gap_grad, (8, channels))
        qfi_rows, gap_all = exit_plane(qfi_sum.reshape(ranks, rows, 3 * channels), gap_tile, planes, 8)
        (g_query, g_forget, g_input), g_attn_gain = finish(
            mixer_weights, gain_a, qfi_rows, head_moves(head, per_rank, groups, span)
        )
        plane, me = lax.axis_index("dp"), lax.axis_index("seq")
        at = lax.rem(plane, per_rank) * head + lax.rem(me, 2) * rows
        from_core = jnp.sum(gap_all[:, :, 0], axis=0)
        g_gap = lax.dynamic_slice(from_core, (plane // per_rank, at), (1, rows))[0]
    return (
        block_out[None],
        hidden_grad[None],
        g_attn_gain,
        g_gap,
        g_out_gain,
        g_query,
        g_forget,
        g_input,
        gain_o * out_rows,
        g_ffn_gain,
        g_gate,
        g_up,
        down_sum.astype(F32),
    )


def solution(mesh):
    tok, row, both = P("dp", "seq", None), P("dp", "seq"), P(("dp", "seq"))
    mat = P(("dp", "seq"), None)
    return jax.shard_map(
        on_device,
        mesh=mesh,
        in_specs=(tok, row, row, both, both, both, mat, mat, mat, mat, both, mat, mat, mat, tok),
        out_specs=(tok, tok, both, both, both, mat, mat, mat, mat, both, mat, mat, mat),
        check_vma=False,
    )
```

```python
import functools

import jax
import jax.numpy as jnp
from jax import lax
from jax.experimental import pallas as pl
from jax.experimental.pallas import tpu as pltpu
from jax.sharding import PartitionSpec as P

HEADS = 16
BLOCK = 64
UNROLL = 4
EPSILON = 1e-06
EXTRA = 128
BF = jnp.bfloat16
F32 = jnp.float32


def dot(a, b, dims):
    return lax.dot_general(a, b, (dims, ((), ())), preferred_element_type=F32)


def nn(a, b):
    return dot(a, b, ((1,), (0,)))


def nt(a, b):
    return dot(a, b, ((1,), (1,)))


def tn(a, b):
    return dot(a, b, ((0,), (0,)))


def inverse_rms(square_mean):
    return lax.rsqrt(square_mean + EPSILON)


def row_mean(v):
    return jnp.mean(v, axis=1, keepdims=True)


def split_sum(tri, v):
    high = v.astype(BF)
    low = (v - high.astype(F32)).astype(BF)
    return nn(tri, high) + nn(tri, low)


def chunk_prep(qfi, gap, live, width):
    query_pre, forget_pre, input_pre = (
        qfi[:, :width],
        qfi[:, width : 2 * width],
        qfi[:, 2 * width :],
    )
    sig_q = jax.nn.sigmoid(query_pre)
    sig_nf = jax.nn.sigmoid(-forget_pre)
    key = gap * sig_nf
    return query_pre, sig_q, sig_nf, key, input_pre * live


def triangle(lower):
    row = lax.broadcasted_iota(jnp.int32, (BLOCK, BLOCK), 0)
    col = lax.broadcasted_iota(jnp.int32, (BLOCK, BLOCK), 1)
    return (row >= col) if lower else (row <= col)


def chunk_masks(cut):
    row = lax.broadcasted_iota(jnp.int32, (BLOCK, BLOCK), 0)
    col = lax.broadcasted_iota(jnp.int32, (BLOCK, BLOCK), 1)
    allowed = (row >= col) & ((row >= cut) == (col >= cut))
    at = lax.broadcasted_iota(jnp.int32, (BLOCK, 1), 0)
    inherits = (at < cut).astype(F32)
    tail = ((at >= cut) | (cut >= BLOCK)).astype(F32)
    whole = (cut >= BLOCK).astype(F32)
    return allowed, inherits, tail, whole


def mixer_forward_kernel(heads, blocks, cut_ref, n_ref, w_ref, gap_ref, mixed_ref, kept_ref, qfi_ref, state):
    step = pl.program_id(0)
    width = heads * 128

    @pl.when(step == 0)
    def _():
        state[...] = jnp.zeros_like(state)

    qfi_ref[...] = nn(n_ref[...], w_ref[...])
    lower = triangle(True).astype(BF)
    for u in range(UNROLL):
        chunk = step * UNROLL + u
        rows = slice(u * BLOCK, (u + 1) * BLOCK)
        at = lax.broadcasted_iota(jnp.int32, (BLOCK, 1), 0) + chunk * BLOCK
        live = (at < cut_ref[0, blocks]).astype(F32)
        query_pre, sig_q, sig_nf, key, value = chunk_prep(qfi_ref[rows, :], gap_ref[...], live, width)
        query = query_pre * sig_q
        total = split_sum(lower, jnp.log1p(-key))
        centre = total[BLOCK // 2 : BLOCK // 2 + 1]
        ending = total[BLOCK - 1 :]
        scaled_q = (query * jnp.exp(total - centre)).astype(BF)
        scaled_k = (key * jnp.exp(centre - total)).astype(BF)
        value_low = value.astype(BF)
        allowed, inherits, tail, whole = chunk_masks(cut_ref[chunk // blocks, lax.rem(chunk, blocks)])
        value_tail = (value * tail).astype(BF)
        e_centre = jnp.exp(centre)
        e_rest = jnp.exp(ending - centre)
        e_all = jnp.exp(ending) * whole
        square = jnp.zeros((BLOCK, 1), F32)
        for h in range(heads):
            cols = slice(h * 128, (h + 1) * 128)
            before = state[h]
            kept_ref[u, h] = before.astype(BF)
            scores = jnp.where(allowed, nt(scaled_q[:, cols], scaled_k[:, cols]), 0.0)
            inner = nn(scores.astype(BF), value_low[:, cols])
            outer = nt(scaled_q[:, cols], (before * e_centre[:, cols]).astype(BF))
            mixed = inner + outer * inherits
            square = square + jnp.sum(mixed * mixed, axis=1, keepdims=True)
            mixed_ref[rows, cols] = mixed.astype(BF)
            state[h] = before * e_all[:, cols] + tn(value_tail[:, cols], scaled_k[:, cols]) * e_rest[:, cols]
        lane = lax.broadcasted_iota(jnp.int32, (BLOCK, EXTRA), 1)
        high = square.astype(BF).astype(F32)
        mixed_ref[rows, width:] = jnp.where(lane == 0, high, jnp.where(lane == 1, square - high, 0.0)).astype(BF)


def mixer_backward_kernel(heads, blocks, cut_ref, qfi_ref, gap_ref, kept_ref, grad_ref, out_ref, gap_out_ref, state):
    step = pl.program_id(0)
    last = pl.num_programs(0) - 1
    width = heads * 128

    @pl.when(step == 0)
    def _():
        state[...] = jnp.zeros_like(state)
        gap_out_ref[...] = jnp.zeros_like(gap_out_ref)

    lower = triangle(True).astype(BF)
    upper = triangle(False).astype(BF)
    for u in reversed(range(UNROLL)):
        chunk = (last - step) * UNROLL + u
        rows = slice(u * BLOCK, (u + 1) * BLOCK)
        at = lax.broadcasted_iota(jnp.int32, (BLOCK, 1), 0) + chunk * BLOCK
        live = (at < cut_ref[0, blocks]).astype(F32)
        gap = gap_ref[...]
        query_pre, sig_q, sig_nf, key, value = chunk_prep(qfi_ref[rows, :], gap, live, width)
        query = query_pre * sig_q
        total = split_sum(lower, jnp.log1p(-key))
        centre = total[BLOCK // 2 : BLOCK // 2 + 1]
        ending = total[BLOCK - 1 :]
        e_q = jnp.exp(total - centre)
        e_k = jnp.exp(centre - total)
        scaled_q = (query * e_q).astype(BF)
        scaled_k = (key * e_k).astype(BF)
        value_low = value.astype(BF)
        allowed, inherits, tail, whole = chunk_masks(cut_ref[chunk // blocks, lax.rem(chunk, blocks)])
        value_tail = (value * tail).astype(BF)
        grad = grad_ref[rows, :]
        grad_in = (grad.astype(F32) * inherits).astype(BF)
        e_centre = jnp.exp(centre)
        e_rest = jnp.exp(ending - centre)
        e_all = jnp.exp(ending) * whole
        d_query, d_key, d_value, d_total, d_end = [], [], [], [], []
        for h in range(heads):
            cols = slice(h * 128, (h + 1) * 128)
            before = kept_ref[u, h].astype(F32)
            after = state[h]
            q, k, v, g, gi = scaled_q[:, cols], scaled_k[:, cols], value_low[:, cols], grad[:, cols], grad_in[:, cols]
            vt = value_tail[:, cols]
            scores = jnp.where(allowed, nt(q, k), 0.0).astype(BF)
            d_scores = jnp.where(allowed, nt(g, v), 0.0).astype(BF)
            shifted = (before * e_centre[:, cols]).astype(BF)
            onward = (after * e_rest[:, cols]).astype(BF)
            dq = nn(d_scores, k) + nn(gi, shifted)
            dk_state = nn(vt, onward)
            dk = tn(d_scores, q) + dk_state
            dv = tn(scores, g) + nt(k, onward) * tail
            k32 = k.astype(F32)
            d_total.append(dq * q.astype(F32) - dk * k32)
            d_end.append(
                jnp.sum(after * before, axis=0, keepdims=True) * e_all[:, cols]
                + jnp.sum(dk_state * k32, axis=0, keepdims=True)
            )
            state[h] = after * e_all[:, cols] + tn(gi, q) * e_centre[:, cols]
            d_query.append(dq)
            d_key.append(dk)
            d_value.append(dv)
        d_query = jnp.concatenate(d_query, axis=1) * e_q
        d_key = jnp.concatenate(d_key, axis=1) * e_k
        d_value = jnp.concatenate(d_value, axis=1) * live
        d_log = split_sum(upper, jnp.concatenate(d_total, axis=1)) + jnp.concatenate(d_end, axis=1)
        d_key = d_key - d_log / (1.0 - key)
        gap_out_ref[...] += jnp.sum(d_key * sig_nf, axis=0, keepdims=True)
        out_ref[rows, :width] = (d_query * sig_q * (1.0 + query_pre * (1.0 - sig_q))).astype(BF)
        out_ref[rows, width : 2 * width] = (-d_key * key * (1.0 - sig_nf)).astype(BF)
        out_ref[rows, 2 * width :] = d_value.astype(BF)


MESH = pl.DeviceIdType.MESH
PIECES = 5
EARLY = 4
TILE = 1024
CHUNK = 32
VMEM_LIMIT = 60 * 1024 * 1024
(S_X, S_Y, S_CORE, S_DIAG_Y, S_DIAG_X, S_CORE_X, S_CORE_Y, S_CORE_D, R_CORE, R_X, R_Y, R_LAST_Y, R_LAST_X, KINDS) = range(14)


class Place:
    def __init__(self):
        self.plane = lax.axis_index("dp")
        me = lax.axis_index("seq")
        self.me = me
        self.core = me % 2
        self.x = (me // 2) % 2
        self.y = me // 4

    def rank(self, fy=0, fx=0, fc=0):
        y = 1 - self.y if fy else self.y
        x = 1 - self.x if fx else self.x
        core = 1 - self.core if fc else self.core
        return 4 * y + 2 * x + core

    def device(self, fy=0, fx=0, fc=0):
        return (self.plane, self.rank(fy, fx, fc))


def greet(place):
    barrier = pltpu.get_barrier_semaphore()
    for flip in ((0, 0, 1), (0, 1, 0), (1, 0, 0)):
        pl.semaphore_signal(barrier, inc=1, device_id=place.device(*flip), device_id_type=MESH)
    pl.semaphore_wait(barrier, 3)


def remote(src, dst, sems, kind, b, device):
    send, recv = sems
    return pltpu.make_async_remote_copy(
        src_ref=src,
        dst_ref=dst,
        send_sem=send.at[kind, b],
        recv_sem=recv.at[kind, b],
        device_id=device,
        device_id_type=MESH,
    )


class Gather:
    def __init__(self, place, own, full, sems, local_sem):
        self.p, self.own, self.full, self.sems, self.local = place, own, full, sems, local_sem
        self.half = full.shape[2] // 2

    def keep(self, b):
        return pltpu.make_async_copy(self.own.at[b], self.full.at[self.p.me, b], self.local.at[b])

    def first(self, b):
        p, dst = self.p, self.full.at[self.p.me, b]
        return [
            remote(self.own.at[b], dst, self.sems, S_X, b, p.device(0, 1, 0)),
            remote(self.own.at[b], dst, self.sems, S_Y, b, p.device(1, 0, 0)),
            remote(self.own.at[b], dst, self.sems, S_CORE, b, p.device(0, 0, 1)),
        ]

    def second(self, b):
        p, h = self.p, self.half
        from_x, from_y = self.full.at[p.rank(0, 1, 0), b], self.full.at[p.rank(1, 0, 0), b]
        up, down = from_x.at[pl.ds(0, h)], from_y.at[pl.ds(h, h)]
        return [
            remote(up, up, self.sems, S_DIAG_Y, b, p.device(1, 0, 0)),
            remote(down, down, self.sems, S_DIAG_X, b, p.device(0, 1, 0)),
            remote(from_x, from_x, self.sems, S_CORE_X, b, p.device(0, 0, 1)),
            remote(from_y, from_y, self.sems, S_CORE_Y, b, p.device(0, 0, 1)),
        ]

    def third(self, b):
        p = self.p
        block = self.full.at[p.rank(1, 1, 0), b]
        return [remote(block, block, self.sems, S_CORE_D, b, p.device(0, 0, 1))]

    def arrived(self, kind, b, flips, rows=None):
        block = self.full.at[self.p.rank(*flips), b]
        if rows is not None:
            block = block.at[pl.ds(rows * self.half, self.half)]
        remote(block, block, self.sems, kind, b, self.p.device(0, 0, 1)).wait_recv()

    def start(self, b):
        self.keep(b).start()
        for copy in self.first(b):
            copy.start()

    def forward(self, b):
        self.arrived(S_X, b, (0, 1, 0))
        self.arrived(S_Y, b, (1, 0, 0))
        for copy in self.second(b):
            copy.start()

    def forward_last(self, b):
        self.arrived(S_DIAG_Y, b, (1, 1, 0), 0)
        self.arrived(S_DIAG_X, b, (1, 1, 0), 1)
        for copy in self.third(b):
            copy.start()

    def finish(self, b):
        self.arrived(S_CORE, b, (0, 0, 1))
        self.arrived(S_CORE_X, b, (0, 1, 1))
        self.arrived(S_CORE_Y, b, (1, 0, 1))
        self.arrived(S_CORE_D, b, (1, 1, 1))

    def drain(self, b):
        self.keep(b).wait()
        for copy in self.first(b) + self.second(b) + self.third(b):
            copy.wait_send()


def swap_pairs(place, parts, outs, send, recv, local):
    pairs = []
    for i, (part, out) in enumerate(zip(parts, outs)):
        pairs.append((pltpu.make_async_copy(part.at[place.me], out.at[place.me], local.at[i]), None))
        for k, flips in enumerate(FLIPS):
            there = out.at[place.rank(*flips)]
            pairs.append(tuple(
                pltpu.make_async_remote_copy(
                    src_ref=src, dst_ref=dst, send_sem=send.at[i, k], recv_sem=recv.at[i, k],
                    device_id=place.device(*flips), device_id_type=MESH,
                )
                for src, dst in ((part.at[place.rank(*flips)], out.at[place.me]), (there, there))
            ))
    return pairs


def swap_starts(place, parts, outs, send, recv, local):
    pairs = swap_pairs(place, parts, outs, send, recv, local)
    for copy, _ in pairs:
        copy.start()
    return pairs


def swap_waits(pairs):
    for copy, arrival in pairs:
        if arrival is None:
            copy.wait()
        else:
            copy.wait_send()
            arrival.wait_recv()


def greet_all(place):
    barrier = pltpu.get_barrier_semaphore()
    for flips in ((0, 0, 1), (0, 1, 0), (1, 0, 0), (0, 1, 1), (1, 0, 1), (1, 1, 0), (1, 1, 1)):
        pl.semaphore_signal(barrier, inc=1, device_id=place.device(*flips), device_id_type=MESH)
    pl.semaphore_wait(barrier, 7)


def fold(gain, w):
    return (gain * w.astype(F32)).astype(BF)


FLIPS = ((0, 0, 1), (0, 1, 0), (1, 0, 0), (0, 1, 1), (1, 0, 1), (1, 1, 0), (1, 1, 1))
ANY_SPEC = pl.BlockSpec(memory_space=pl.ANY)
VMEM_SPEC = pl.BlockSpec(memory_space=pltpu.VMEM)


def column_peers(place, planes):
    peers = []
    for hop in range(planes):
        for flip in (0, 1):
            if hop or flip:
                plane = lax.rem(place.plane + hop, planes)
                peers.append((plane, place.rank(0, 0, flip)))
    return peers


def column_spread(place, planes, src, dst, send, recv):
    waits = []
    for k, (plane, rank) in enumerate(column_peers(place, planes)):
        mine = dst.at[place.plane, place.core]
        copy = pltpu.make_async_remote_copy(
            src_ref=src, dst_ref=mine, send_sem=send.at[k], recv_sem=recv.at[k],
            device_id=(plane, rank), device_id_type=MESH,
        )
        copy.start()
        back = lax.rem(planes + 2 * place.plane - plane, planes)
        there = dst.at[back, lax.rem(rank, 2)]
        waits.append((copy, pltpu.make_async_remote_copy(
            src_ref=there, dst_ref=there, send_sem=send.at[k], recv_sem=recv.at[k],
            device_id=(plane, rank), device_id_type=MESH,
        )))
    return waits


def greet_column_and_plane(place, planes):
    barrier = pltpu.get_barrier_semaphore()
    devices = [place.device(*flips) for flips in FLIPS]
    devices += [p for p in column_peers(place, planes)[1:]]
    for device in devices:
        pl.semaphore_signal(barrier, inc=1, device_id=device, device_id_type=MESH)
    pl.semaphore_wait(barrier, len(devices))


class Line:
    def __init__(self, place, planes, full, sems):
        self.p, self.planes, self.full, self.sems = place, planes, full, sems

    def copy(self, way, plane, to, hop):
        send, recv = self.sems
        block = self.full.at[plane]
        return pltpu.make_async_remote_copy(
            src_ref=block, dst_ref=block, send_sem=send.at[way, hop], recv_sem=recv.at[way, hop],
            device_id=(to, self.p.me), device_id_type=MESH,
        )

    def each(self, hop, arriving, body):
        plane, last = self.p.plane, self.planes - 1
        if arriving:
            conditions = (plane - hop >= 0, plane + hop <= last)
        else:
            conditions = ((plane - hop >= 0) & (plane + 1 <= last), (plane + hop <= last) & (plane >= 1))
        for way, condition in enumerate(conditions):
            @pl.when(condition)
            def _():
                block = plane - hop if way == 0 else plane + hop
                to = lax.rem(plane + (1 if way == 0 else last), self.planes)
                body(self.copy(way, block, to, hop - 1 if arriving else hop))

    def start(self, hop):
        self.each(hop, False, lambda copy: copy.start())

    def arrive(self, hop):
        self.each(hop, True, lambda copy: copy.wait_recv())

    def drain(self):
        for hop in range(self.planes - 1):
            self.each(hop, False, lambda copy: copy.wait_send())


def enter_plane(weights, gain, x, unit_weights, unit_gain, ids, gap, per_rank, groups, planes, collective_id):
    rows, model = weights[0].shape
    head = model // (8 * per_rank)
    channels = per_rank * head
    span = 8 // groups
    tokens = x.shape[0]
    x_rows = tokens // PIECES
    every_unit = unit_weights[0].shape[1]
    units_in = every_unit // (8 * planes)
    units = units_in * planes
    x = x.reshape(PIECES, x_rows, model)
    blocks = tokens // BLOCK

    def kernel(q_ref, f_ref, i_ref, gain_ref, x_ref, gate_ref, up_ref, unit_gain_ref, ids_ref, gap_ref,
               qfi_out, full, unit_out, cut_out, gap_out,
               part, normed, unit_part, ids_in, gap_in, *sems):
        (swap_send, swap_recv, swap_local, send, recv, local, gap_send, gap_recv, z_send, z_recv) = sems
        place = Place()
        scale = gain_ref[...]
        for w, ref in enumerate((q_ref, f_ref, i_ref)):
            for rank, source, target in ((r, t, c) for v, r, c, t in head_moves(head, per_rank, groups, span) if v == w):
                part[rank, :, target] = fold(scale, ref[:, source])
        greet_column_and_plane(place, planes)
        first = swap_starts(
            place, [part], [qfi_out.at[place.plane]],
            swap_send.at[pl.ds(0, 1)], swap_recv.at[pl.ds(0, 1)], swap_local.at[pl.ds(0, 1)],
        )
        gaps = column_spread(place, planes, gap_ref, gap_in, gap_send, gap_recv)
        gap_in[place.plane, place.core] = gap_ref[...]
        ids_in[place.me] = ids_ref[...]
        id_pairs = []
        for k, flips in enumerate(FLIPS):
            there = ids_in.at[place.rank(*flips)]
            id_pairs.append(tuple(
                pltpu.make_async_remote_copy(
                    src_ref=src, dst_ref=dst, send_sem=swap_send.at[1, k], recv_sem=swap_recv.at[1, k],
                    device_id=place.device(*flips), device_id_type=MESH,
                )
                for src, dst in ((ids_ref, ids_in.at[place.me]), (there, there))
            ))
            id_pairs[-1][0].start()

        gather = Gather(place, normed, full, (send, recv), local)

        @pl.loop(0, PIECES)
        def _(b):
            value = x_ref[b].astype(F32)
            normed[b] = (value * inverse_rms(row_mean(value * value))).astype(BF)
            gather.start(b)

        line = Line(place, planes, qfi_out, (z_send, z_recv))
        swap_waits(first)
        line.start(0)
        unit_scale = unit_gain_ref[...]
        for side, ref in enumerate((gate_ref, up_ref)):
            for _, rank, target, source in (move for move in unit_moves(units, planes, 8) if move[0] == side):
                unit_part[rank, :, target] = fold(unit_scale, ref[:, source])
        for copy, arrival in id_pairs + gaps:
            copy.wait_send()
            arrival.wait_recv()
        segment = ids_in[:, 0, :].astype(F32)
        live = jnp.sum(ids_in[:, 1, :tokens].astype(F32))
        lane = lax.broadcasted_iota(jnp.int32, (8, EXTRA), 1)
        parts = [segment[:, c * BLOCK : (c + 1) * BLOCK] for c in range(blocks)]
        ends = [jnp.max(p, axis=1, keepdims=True) for p in parts]
        begin = jnp.min(parts[0], axis=1, keepdims=True)
        before = jnp.concatenate([begin[:1], ends[-1][:-1]], axis=0)
        result = jnp.where(lane == blocks, live, 0.0)
        for c in range(blocks):
            stay = jnp.sum((parts[c] == before).astype(F32), axis=1, keepdims=True)
            result = jnp.where(lane == c, stay, result)
            before = ends[c]
        cut_out[...] = result.astype(jnp.int32)
        for j in range(per_rank):
            for c in range(span):
                at = (j * span + c) * rows
                gap_out[:, at : at + rows] = gap_in[place.core * per_rank + j, c, :1, :rows].astype(F32)
        unit_copies = []

        def rest():
            pl.loop(3, PIECES)(gather.forward)
            unit_copies.extend(swap_starts(
                place, [unit_part], [unit_out],
                swap_send.at[pl.ds(2, 1)], swap_recv.at[pl.ds(2, 1)], swap_local.at[pl.ds(1, 1)],
            ))

        stages = [lambda: pl.loop(0, 3)(gather.forward), rest, lambda: pl.loop(0, PIECES)(gather.forward_last)]
        for hop in range(1, planes):
            if hop <= len(stages):
                stages[hop - 1]()
            line.arrive(hop)
            if hop < planes - 1:
                line.start(hop)
        for stage in stages[planes - 1 :]:
            stage()
        pl.loop(0, PIECES)(gather.finish)
        swap_waits(unit_copies)
        line.drain()
        pl.loop(0, PIECES)(gather.drain)

    qfi, full, unit_rows, cut, gap = pl.pallas_call(
        kernel,
        in_specs=[VMEM_SPEC] * 10,
        out_specs=[ANY_SPEC] * 3 + [VMEM_SPEC] * 2,
        out_shape=[
            jax.ShapeDtypeStruct((planes, 8, rows, 3 * channels), BF),
            jax.ShapeDtypeStruct((8, PIECES, x_rows, model), BF),
            jax.ShapeDtypeStruct((8, rows, 2 * units), BF),
            jax.ShapeDtypeStruct((8, EXTRA), jnp.int32),
            jax.ShapeDtypeStruct((1, channels), F32),
        ],
        scratch_shapes=[
            pltpu.VMEM((8, rows, 3 * channels), BF),
            pltpu.VMEM((PIECES, x_rows, model), BF),
            pltpu.VMEM((8, rows, 2 * units), BF),
            pltpu.VMEM((8,) + ids.shape, ids.dtype),
            pltpu.VMEM((planes, 2) + gap.shape, gap.dtype),
            pltpu.SemaphoreType.DMA((3, 7)),
            pltpu.SemaphoreType.DMA((3, 7)),
            pltpu.SemaphoreType.DMA((2,)),
            pltpu.SemaphoreType.DMA((KINDS, PIECES)),
            pltpu.SemaphoreType.DMA((KINDS, PIECES)),
            pltpu.SemaphoreType.DMA((PIECES,)),
            pltpu.SemaphoreType.DMA((2 * planes - 1,)),
            pltpu.SemaphoreType.DMA((2 * planes - 1,)),
            pltpu.SemaphoreType.DMA((2, planes)),
            pltpu.SemaphoreType.DMA((2, planes)),
        ],
        compiler_params=pltpu.CompilerParams(
            collective_id=collective_id, has_side_effects=True, vmem_limit_bytes=VMEM_LIMIT
        ),
        cost_estimate=pl.CostEstimate(flops=0, bytes_accessed=200 * tokens * model, transcendentals=0),
        name="enter_plane",
    )(*weights, gain, x, *unit_weights, unit_gain, ids, gap)
    return (
        qfi.reshape(model, 3 * channels),
        full.reshape(8 * tokens, model),
        unit_rows,
        cut,
        gap,
    )


def exit_plane(summed, gap_grad, planes, collective_id):
    def kernel(sum_ref, gap_ref, landed, gap_out, *sems):
        send, recv, local, gap_send, gap_recv = sems
        place = Place()
        greet_column_and_plane(place, planes)
        copies = swap_starts(place, [sum_ref], [landed], send, recv, local)
        gaps = column_spread(place, planes, gap_ref, gap_out, gap_send, gap_recv)
        own_gap = pltpu.make_async_copy(gap_ref, gap_out.at[place.plane, place.core], local.at[1])
        own_gap.start()
        swap_waits(copies)
        for copy, arrival in gaps:
            copy.wait_send()
            arrival.wait_recv()
        own_gap.wait()

    return pl.pallas_call(
        kernel,
        in_specs=[ANY_SPEC] * 2,
        out_specs=[ANY_SPEC] * 2,
        out_shape=[
            jax.ShapeDtypeStruct(summed.shape, summed.dtype),
            jax.ShapeDtypeStruct((planes, 2) + gap_grad.shape, gap_grad.dtype),
        ],
        scratch_shapes=[
            pltpu.SemaphoreType.DMA((1, 7)),
            pltpu.SemaphoreType.DMA((1, 7)),
            pltpu.SemaphoreType.DMA((2,)),
            pltpu.SemaphoreType.DMA((2 * planes - 1,)),
            pltpu.SemaphoreType.DMA((2 * planes - 1,)),
        ],
        compiler_params=pltpu.CompilerParams(collective_id=collective_id, has_side_effects=True),
        name="exit_plane",
    )(summed, gap_grad)


def finish(weights, gain, swapped, moves):
    rows, width = weights[0].shape
    tile = 512

    def kernel(*refs):
        in_ref, gain_ref = refs[0], refs[1]
        w_refs = refs[2 : 2 + len(weights)]
        outs, gain_out = refs[2 + len(weights) : -1], refs[-1]
        for w, rank, source, target in moves:
            outs[w][:, target] = in_ref[rank, :, source].astype(F32)
        scale = gain_ref[...]
        total = jnp.zeros((rows, tile), F32)
        for ref, out in zip(w_refs, outs):
            for at in range(0, width, tile):
                grad = out[:, at : at + tile]
                total += grad * ref[:, at : at + tile].astype(F32)
                out[:, at : at + tile] = grad * scale
        column = jnp.sum(total, axis=1, keepdims=True)
        diagonal = lax.broadcasted_iota(jnp.int32, (rows, rows), 0) == lax.broadcasted_iota(jnp.int32, (rows, rows), 1)
        gain_out[...] = jnp.sum(jnp.where(diagonal, column, 0.0), axis=0, keepdims=True)

    results = pl.pallas_call(
        kernel,
        in_specs=[VMEM_SPEC] * (2 + len(weights)),
        out_specs=[VMEM_SPEC] * (len(weights) + 1),
        out_shape=[jax.ShapeDtypeStruct((rows, width), F32)] * len(weights) + [jax.ShapeDtypeStruct((1, rows), F32)],
        compiler_params=pltpu.CompilerParams(vmem_limit_bytes=VMEM_LIMIT),
        name="finish",
    )(swapped, gain, *weights)
    return results[:-1], results[-1].reshape(rows)


def unit_moves(units, planes, ranks):
    units_in = units // planes
    return [
        (
            side,
            s,
            slice(side * units + i * units_in, side * units + (i + 1) * units_in),
            slice((i * ranks + s) * units_in, (i * ranks + s + 1) * units_in),
        )
        for side in range(2)
        for i in range(planes)
        for s in range(ranks)
    ]


def head_moves(head, per_rank, groups, span):
    moves = []
    for w in range(3):
        for a in range(groups):
            for m in range(span):
                for j in range(per_rank):
                    h = (m * per_rank + j) * groups + a
                    at = (w * per_rank + j) * head
                    moves.append((w, a * span + m, slice(at, at + head), slice(h * head, (h + 1) * head)))
    return moves


class Scatter:
    def __init__(self, left, weight, transposed, stats):
        self.rows, self.columns = left[2], left[3]
        self.transposed, self.stats = transposed, stats
        self.weight = weight
        self.depth = weight[1] if transposed else weight[0]
        self.width = weight[0] if transposed else weight[1]
        self.half = self.width // 2
        self.extra = EXTRA if stats else 0

    def scratch(self):
        rows, half, full = self.rows, self.half, self.width + self.extra
        right = half + self.extra
        return [
            pltpu.VMEM((PIECES, 8, rows, self.columns), BF),
            pltpu.VMEM(self.weight, BF),
            pltpu.VMEM((PIECES, 4, rows, full), BF),
            pltpu.VMEM((PIECES, 4, rows, full), BF),
            pltpu.VMEM((4, rows, full), F32),
            pltpu.VMEM((PIECES, 2, rows, half), BF),
            pltpu.VMEM((PIECES, 2, rows, half), BF),
            pltpu.VMEM((PIECES, 2, rows, right), BF),
            pltpu.VMEM((PIECES, 2, rows, right), BF),
            pltpu.VMEM((PIECES, 2, rows, half), F32),
            pltpu.VMEM((PIECES, 2, rows, right), F32),
            pltpu.VMEM((PIECES, rows, half), BF),
            pltpu.VMEM((PIECES, rows, half), BF),
            pltpu.VMEM((PIECES, rows, right), BF),
            pltpu.VMEM((PIECES, rows, right), BF),
            pltpu.SemaphoreType.DMA((PIECES,)),
            pltpu.SemaphoreType.DMA((2,)),
        ]

    def bind(self, place, sems, left_ref, weight_ref, refs):
        self.place, self.sems, self.left_ref, self.weight_ref = place, sems, left_ref, weight_ref
        (self.x_buf, self.w_buf, self.core_out, self.core_in, self.total, self.x_out, self.x_in, self.y_out, self.y_in,
         self.keep_a, self.keep_b, self.last_y_out, self.last_y_in, self.last_x_out,
         self.last_x_in, self.load_sem, self.w_sem) = refs

    def weight_copy(self, t):
        tile = min(TILE, self.width)
        at = pl.ds(t * tile, tile)
        if self.transposed:
            return pltpu.make_async_copy(self.weight_ref.at[at], self.w_buf.at[at], self.w_sem.at[t])
        return pltpu.make_async_copy(self.weight_ref.at[:, at], self.w_buf.at[:, at], self.w_sem.at[t])

    def start_loads(self):
        core = self.place.core
        for b in range(PIECES):
            for j in range(4):
                for side, at in ((0, 2 * j + 1 - core), (4, 2 * j + core)):
                    pltpu.make_async_copy(
                        self.left_ref.at[at, b], self.x_buf.at[b, side + j], self.load_sem.at[b]
                    ).start()
            if b == 0:
                for t in range(self.width // min(TILE, self.width)):
                    self.weight_copy(t).start()

    def send_core(self, b):
        return remote(self.core_out.at[b], self.core_in.at[b], self.sems, R_CORE, b, self.place.device(0, 0, 1))

    def send_x(self, b):
        return remote(self.x_out.at[b], self.x_in.at[b], self.sems, R_X, b, self.place.device(0, 1, 0))

    def send_y(self, b):
        return remote(self.y_out.at[b], self.y_in.at[b], self.sems, R_Y, b, self.place.device(1, 0, 0))

    def send_last_y(self, b):
        return remote(self.last_y_out.at[b], self.last_y_in.at[b], self.sems, R_LAST_Y, b, self.place.device(1, 0, 0))

    def send_last_x(self, b):
        return remote(self.last_x_out.at[b], self.last_x_in.at[b], self.sems, R_LAST_X, b, self.place.device(0, 1, 0))

    def produce(self, b):
        rows, depth, width, tile = self.rows, self.depth, self.width, min(TILE, self.width)
        pltpu.make_async_copy(self.x_buf.at[b], self.x_buf.at[b], self.load_sem.at[b]).wait()

        def product(side, t):
            lhs = self.x_buf[b, 4 * side : 4 * side + 4, :, :depth].reshape(4 * rows, depth)
            at = slice(t * tile, (t + 1) * tile)
            out = nt(lhs, self.w_buf[at, :]) if self.transposed else nn(lhs, self.w_buf[:, at])
            return out.reshape(4, rows, tile), at

        for t in range(width // tile):
            @pl.when(b == 0)
            def _():
                self.weight_copy(t).wait()

            out, at = product(0, t)
            self.core_out[b, :, :, at] = out.astype(BF)
        if self.stats:
            self.core_out[b, :, :, width:] = self.x_buf[b, :4, :, depth:]
        self.send_core(b).start()
        for t in range(width // tile):
            out, at = product(1, t)
            self.total[:, :, at] = out
        if self.stats:
            self.total[:, :, width:] = self.x_buf[b, 4:, :, depth:].astype(F32)

    def by_chunks(self, body):
        @pl.loop(0, self.rows // CHUNK)
        def _(r):
            body(pl.ds(pl.multiple_of(r * CHUNK, CHUNK), CHUNK))

    def stage_one(self, b):
        place, half, total, core_in = self.place, self.half, self.total, self.core_in
        self.send_core(b).wait_recv()

        def for_x(r):
            for i in range(2):
                go, stay = 2 * i + 1 - place.x, 2 * i + place.x
                self.x_out[b, i, r] = (total[go, r, :half] + core_in[b, go, r, :half].astype(F32)).astype(BF)
                self.keep_a[b, i, r] = total[stay, r, :half] + core_in[b, stay, r, :half].astype(F32)

        def for_y(r):
            for i in range(2):
                go, stay = 2 * (1 - place.y) + i, 2 * place.y + i
                self.y_out[b, i, r] = (total[go, r, half:] + core_in[b, go, r, half:].astype(F32)).astype(BF)
                self.keep_b[b, i, r] = total[stay, r, half:] + core_in[b, stay, r, half:].astype(F32)

        self.by_chunks(for_x)
        self.send_x(b).start()
        self.by_chunks(for_y)
        self.send_y(b).start()

    def stage_two(self, b):
        go_y, go_x = 1 - self.place.y, 1 - self.place.x

        def low(r):
            self.last_y_out[b, r] = (self.keep_a[b, go_y, r] + self.x_in[b, go_y, r].astype(F32)).astype(BF)

        def high(r):
            self.last_x_out[b, r] = (self.keep_b[b, go_x, r] + self.y_in[b, go_x, r].astype(F32)).astype(BF)

        self.send_x(b).wait_recv()
        self.by_chunks(low)
        self.send_last_y(b).start()
        self.send_y(b).wait_recv()
        self.by_chunks(high)
        self.send_last_x(b).start()

    def stage_three(self, b, body):
        self.send_last_y(b).wait_recv()
        self.send_last_x(b).wait_recv()
        y, x = self.place.y, self.place.x

        def end(r):
            low = self.keep_a[b, y, r] + self.x_in[b, y, r].astype(F32) + self.last_y_in[b, r].astype(F32)
            high = self.keep_b[b, x, r] + self.y_in[b, x, r].astype(F32) + self.last_x_in[b, r].astype(F32)
            result = jnp.concatenate([low, high[:, : self.half]], axis=1)
            body(r, result, high[:, self.half :] if self.stats else None)

        self.by_chunks(end)

    def drain(self, b):
        for copy in (self.send_core, self.send_x, self.send_y, self.send_last_y, self.send_last_x):
            copy(b).wait_send()


def guarded(body, b):
    @pl.when((b >= 0) & (b < PIECES))
    def _():
        body(b)


def plane_sems():
    return [pltpu.SemaphoreType.DMA((KINDS, PIECES)), pltpu.SemaphoreType.DMA((KINDS, PIECES))]


def product_scatter(left, weight, transposed, stats, epilogue, owned, outs, gathered, collective_id, fillers=()):
    tokens = left.shape[0] // 8
    rows = tokens // PIECES
    left = left.reshape(8, PIECES, rows, left.shape[1])
    scatter = Scatter(left.shape, weight.shape, transposed, stats)
    count = len(scatter.scratch())

    def kernel(*refs):
        refs = list(refs)
        left_ref, weight_ref = refs.pop(0), refs.pop(0)
        own_refs = [refs.pop(0) for _ in owned]
        extra_in = [[refs.pop(0) for _ in f.arrays] for f in fillers]
        out_refs = [refs.pop(0) for _ in outs]
        full_ref = refs.pop(0) if gathered else None
        extra_out = [refs.pop(0) for _ in fillers]
        place = Place()
        sems = (refs.pop(0), refs.pop(0))
        scatter.bind(place, sems, left_ref, weight_ref, refs[:count])
        refs = refs[count:]
        own_bufs = [refs.pop(0) for _ in owned]
        out_bufs = [refs.pop(0) for _ in outs]
        own_sem, out_sem = refs.pop(0), refs.pop(0)
        own_copies = [
            pltpu.make_async_copy(ref, buf, own_sem.at[i]) for i, (ref, buf) in enumerate(zip(own_refs, own_bufs))
        ]

        def out_copies(b):
            return [
                pltpu.make_async_copy(buf.at[b], ref.at[b], out_sem.at[i, b])
                for i, (buf, ref) in enumerate(zip(out_bufs, out_refs))
            ]

        scatter.start_loads()
        for copy in own_copies:
            copy.start()
        for f, ins, out in zip(fillers, extra_in, extra_out):
            f.bind(ins, out, refs[: len(f.scratch)])
            refs = refs[len(f.scratch) :]
            f.start()
        greet(place)
        if gathered:
            n_buf, keep_sem = refs
            gather = Gather(place, n_buf, full_ref, sems, keep_sem)

        def end(b):
            def rows_done(r, result, stat):
                written, sent = epilogue(result, stat, *[o[b, r] for o in own_bufs])
                for buf, value in zip(out_bufs, written):
                    buf[b, r] = value
                if gathered:
                    n_buf[b, r] = sent

            scatter.stage_three(b, rows_done)
            for copy in out_copies(b):
                copy.start()
            if gathered:
                gather.start(b)
        @pl.loop(0, PIECES + (9 if gathered else 5))
        def _(step):
            guarded(scatter.stage_one, step - 1)
            guarded(scatter.produce, step)
            guarded(scatter.stage_two, step - 3)
            for f in fillers:
                f.step(step)

            @pl.when(step == 5)
            def _():
                for copy in own_copies:
                    copy.wait()

            guarded(end, step - 5)
            if gathered:
                guarded(gather.forward, step - 7)
                guarded(gather.forward_last, step - 9)

        @pl.loop(0, PIECES)
        def _(b):
            if gathered:
                gather.finish(b)
                gather.drain(b)
            scatter.drain(b)
            for copy in out_copies(b):
                copy.wait()

        for f in fillers:
            f.end()

    any_spec = ANY_SPEC
    out_shape = [jax.ShapeDtypeStruct((PIECES, rows, c), d) for c, d in outs]
    out_specs = [any_spec] * len(outs)
    scratch = plane_sems() + scatter.scratch()
    scratch += [pltpu.VMEM((PIECES, rows, o.shape[1]), o.dtype) for o in owned]
    scratch += [pltpu.VMEM(o.shape, o.dtype) for o in out_shape]
    scratch += [pltpu.SemaphoreType.DMA((len(owned),)), pltpu.SemaphoreType.DMA((len(outs), PIECES))]
    if gathered:
        out_shape.append(jax.ShapeDtypeStruct((8, PIECES, rows, gathered), BF))
        out_specs.append(any_spec)
    args = [left, weight] + [o.reshape(PIECES, rows, o.shape[1]) for o in owned]
    in_specs = [any_spec, any_spec] + [any_spec] * len(owned)
    for f in fillers:
        args, in_specs = args + f.arrays, in_specs + [any_spec] * len(f.arrays)
        out_shape.append(f.out_shape)
        out_specs.append(any_spec)
        scratch += f.scratch
    if gathered:
        scratch += [pltpu.VMEM((PIECES, rows, gathered), BF), pltpu.SemaphoreType.DMA((PIECES,))]
    results = pl.pallas_call(
        kernel,
        in_specs=in_specs,
        out_specs=out_specs,
        out_shape=out_shape,
        scratch_shapes=scratch,
        compiler_params=pltpu.CompilerParams(
            collective_id=collective_id, has_side_effects=True, vmem_limit_bytes=VMEM_LIMIT
        ),
        cost_estimate=pl.CostEstimate(
            flops=16 * tokens * scatter.depth * scatter.width,
            bytes_accessed=(240 if gathered else 140) * tokens * scatter.width * 2,
            transcendentals=0,
        ),
        name="product_scatter",
    )(*args)
    flat = [r.reshape(tokens, r.shape[2]) for r in results[: len(outs)]]
    if gathered:
        flat.append(results[len(outs)].reshape(8 * tokens, gathered))
    return flat + list(results[len(outs) + (1 if gathered else 0) :])


class GradProduct:
    BLOCK = 256

    def __init__(self, left, right, by_right, first):
        self.left, self.right, self.by_right, self.first = left, right, by_right, first
        whole, streamed = (left, right) if by_right else (right, left)
        self.tokens, self.blocks = left.shape[0], streamed.shape[1] // self.BLOCK
        depth, width = left.shape[1], right.shape[1]
        block = (depth, self.BLOCK) if by_right else (self.BLOCK, width)
        self.arrays = [whole, streamed]
        self.out_shape = jax.ShapeDtypeStruct((depth, width), BF)
        self.scratch = [
            pltpu.VMEM(whole.shape, BF),
            pltpu.VMEM((2, self.tokens, self.BLOCK), BF),
            pltpu.VMEM((2,) + block, BF),
            pltpu.SemaphoreType.DMA((1,)),
            pltpu.SemaphoreType.DMA((2,)),
            pltpu.SemaphoreType.DMA((2,)),
        ]

    def plain(self):
        return tn(self.left, self.right).astype(BF)

    def bind(self, ins, out, refs):
        self.whole_ref, self.streamed_ref = ins
        self.out = out
        self.w_buf, self.s_buf, self.o_buf, self.w_sem, self.s_sem, self.o_sem = refs

    def columns(self, b):
        return pl.ds(pl.multiple_of(b * self.BLOCK, self.BLOCK), self.BLOCK)

    def load(self, b):
        return pltpu.make_async_copy(self.streamed_ref.at[:, self.columns(b)], self.s_buf.at[b % 2], self.s_sem.at[b % 2])

    def store(self, b):
        to = self.out.at[:, self.columns(b)] if self.by_right else self.out.at[self.columns(b)]
        return pltpu.make_async_copy(self.o_buf.at[b % 2], to, self.o_sem.at[b % 2])

    def whole_copy(self):
        return pltpu.make_async_copy(self.whole_ref, self.w_buf, self.w_sem.at[0])

    def start(self):
        self.whole_copy().start(priority=1)
        self.load(0).start(priority=1)
        self.load(1).start(priority=1)

    def step(self, step):
        b = step - self.first

        @pl.when(b == 0)
        def _():
            self.whole_copy().wait()

        @pl.when((b >= 0) & (b < self.blocks))
        def _():
            self.load(b).wait()

            @pl.when(b >= 2)
            def _():
                self.store(b - 2).wait()

            streamed, whole = self.s_buf[b % 2], self.w_buf[...]
            product = tn(whole, streamed) if self.by_right else tn(streamed, whole)
            self.o_buf[b % 2] = product.astype(BF)
            self.store(b).start(priority=1)

        @pl.when((b >= 0) & (b + 2 < self.blocks))
        def _():
            self.load(b + 2).start(priority=1)

    def end(self):
        self.store(self.blocks - 2).wait()
        self.store(self.blocks - 1).wait()


def mixer_specs(tokens, heads, reverse):
    width, span = heads * 128, UNROLL * BLOCK
    steps = tokens // span

    def at(i):
        return steps - 1 - i if reverse else i

    return (
        steps,
        pl.BlockSpec((span, 3 * width), lambda i, *_: (at(i), 0)),
        pl.BlockSpec((1, width), lambda i, *_: (0, 0)),
        pl.BlockSpec((UNROLL, heads, 128, 128), lambda i, *_: (at(i), 0, 0, 0)),
        lambda columns: pl.BlockSpec((span, columns), lambda i, *_: (at(i), 0)),
    )


def mixer_forward(cut, n1, weight, gap, own, out_pieces, per_rank, collective_id):
    tokens, heads = n1.shape[0], gap.shape[1] // 128
    width = heads * 128
    blocks = tokens // BLOCK // lax.axis_size("seq")
    steps, qfi_spec, gap_spec, kept_spec, block = mixer_specs(tokens, heads, False)
    together = lax.axis_size("seq") == 8

    def kernel(cut_ref, n_ref, w_ref, gap_ref, *refs):
        if not together:
            return mixer_forward_kernel(heads, blocks, cut_ref, n_ref, w_ref, gap_ref, *refs)
        (own_ref, pieces_ref, mixed_ref, kept_ref, qfi_ref, full_ref, rows_ref, state, own_buf, pieces_buf, send, recv, local,
         w_send, w_recv, w_local) = refs
        place = Place()
        gather = Gather(place, own_buf, full_ref, (send, recv), local)
        loads = [
            pltpu.make_async_copy(own_ref, own_buf, local.at[0]),
            pltpu.make_async_copy(pieces_ref, pieces_buf, w_local.at[0]),
        ]

        def exchange(j):
            core = place.core
            here = pltpu.make_async_copy(
                pieces_buf.at[core * per_rank + j], rows_ref.at[j, core], w_local.at[j]
            )
            there = pltpu.make_async_remote_copy(
                src_ref=pieces_buf.at[(1 - core) * per_rank + j], dst_ref=rows_ref.at[j, core],
                send_sem=w_send.at[j], recv_sem=w_recv.at[j], device_id=place.device(0, 0, 1), device_id_type=MESH,
            )
            back = rows_ref.at[j, 1 - core]
            arrival = pltpu.make_async_remote_copy(
                src_ref=back, dst_ref=back, send_sem=w_send.at[j], recv_sem=w_recv.at[j],
                device_id=place.device(0, 0, 1), device_id_type=MESH,
            )
            return here, there, arrival

        @pl.when(pl.program_id(0) == 0)
        def _():
            for load in loads:
                load.start()
            greet(place)
            for load in loads:
                load.wait()
            pl.loop(0, EARLY)(gather.start)
            for j in range(per_rank):
                here, there, _ = exchange(j)
                here.start()
                there.start()

        @pl.when(pl.program_id(0) == steps - 1)
        def _():
            pl.loop(0, EARLY)(gather.forward_last)

        mixer_forward_kernel(
            heads, blocks, cut_ref, n_ref, w_ref, gap_ref, mixed_ref, kept_ref, qfi_ref, state
        )

        for b in range(EARLY):
            @pl.when(pl.program_id(0) == min(steps - 1, (8 + 7 * b) // 4))
            def _():
                gather.forward(b)

        @pl.when(pl.program_id(0) == steps - 1)
        def _():
            for stage in (gather.finish, gather.drain):
                pl.loop(0, EARLY)(stage)
            for j in range(per_rank):
                here, there, arrival = exchange(j)
                here.wait()
                there.wait_send()
                arrival.wait_recv()

    fixed = pl.BlockSpec(weight.shape, lambda i, *_: (0, 0), pipeline_mode=pl.Buffered(1))
    in_specs, args = [block(n1.shape[1]), fixed, gap_spec], [n1, weight, gap]
    out_specs = [block(width + EXTRA), kept_spec, qfi_spec]
    out_shape = [
        jax.ShapeDtypeStruct((tokens, width + EXTRA), BF),
        jax.ShapeDtypeStruct((tokens // BLOCK, heads, 128, 128), BF),
        jax.ShapeDtypeStruct((tokens, 3 * width), F32),
    ]
    scratch = [pltpu.VMEM((heads, 128, 128), F32)]
    params = pltpu.CompilerParams(vmem_limit_bytes=VMEM_LIMIT)
    if together:
        rows = own.shape[0] // PIECES
        own = own.reshape(PIECES, rows, own.shape[1])
        w_rows, model = out_pieces.shape[1:]
        in_specs, args = in_specs + [ANY_SPEC] * 2, args + [own, out_pieces]
        out_specs = out_specs + [ANY_SPEC] * 2
        out_shape = out_shape + [
            jax.ShapeDtypeStruct((8,) + own.shape, own.dtype),
            jax.ShapeDtypeStruct((per_rank, 2, w_rows, model), BF),
        ]
        scratch = scratch + [pltpu.VMEM(own.shape, BF), pltpu.VMEM(out_pieces.shape, BF)]
        scratch = scratch + plane_sems() + [pltpu.SemaphoreType.DMA((PIECES,))]
        scratch = scratch + [pltpu.SemaphoreType.DMA((per_rank,))] * 3
        params = pltpu.CompilerParams(
            vmem_limit_bytes=VMEM_LIMIT, collective_id=collective_id, has_side_effects=True
        )
    results = pl.pallas_call(
        kernel,
        grid_spec=pltpu.PrefetchScalarGridSpec(
            num_scalar_prefetch=1, grid=(steps,), in_specs=in_specs, out_specs=out_specs, scratch_shapes=scratch
        ),
        out_shape=out_shape,
        compiler_params=params,
        cost_estimate=pl.CostEstimate(
            flops=tokens * width * (128 * 10 + 6 * n1.shape[1]),
            bytes_accessed=60 * tokens * n1.shape[1],
            transcendentals=tokens * width * 6,
        ),
        name="mixer_forward",
    )(cut, *args)
    mixed, kept, qfi = results[:3]
    if together:
        return mixed, kept, qfi, results[3], results[4].reshape(width, model)
    return mixed, kept, qfi, lax.all_gather(own, "seq", axis=0, tiled=True), None


def mixer_backward(cut, qfi, gap, kept, grad, parts, grad_out, per_rank, collective_id):
    tokens, heads = qfi.shape[0], gap.shape[1] // 128
    width = heads * 128
    blocks = tokens // BLOCK // lax.axis_size("seq")
    steps, qfi_spec, gap_spec, kept_spec, block = mixer_specs(tokens, heads, True)
    together = lax.axis_size("seq") == 8
    planes = lax.axis_size("dp")

    def kernel(cut_ref, qfi_ref, gap_ref, kept_ref, grad_ref, *refs):
        if not together:
            return mixer_backward_kernel(heads, blocks, cut_ref, qfi_ref, gap_ref, kept_ref, grad_ref, *refs)
        (parts_ref, og_ref, out_ref, gap_out_ref, swapped_ref, sum_ref, state, parts_buf, og_buf, by_plane, landed,
         send, recv, local, c_send, c_recv, z_send, z_recv, load_sem) = refs
        place, step = Place(), pl.program_id(0)
        core = place.core
        loads = [
            pltpu.make_async_copy(parts_ref, parts_buf, load_sem.at[0]),
            pltpu.make_async_copy(og_ref, og_buf, load_sem.at[1]),
        ]

        def over_core(j):
            there = by_plane.at[core * per_rank + j]
            back = by_plane.at[(1 - core) * per_rank + j]
            return [
                pltpu.make_async_remote_copy(
                    src_ref=src, dst_ref=dst, send_sem=c_send.at[j], recv_sem=c_recv.at[j],
                    device_id=place.device(0, 0, 1), device_id_type=MESH,
                )
                for src, dst in ((og_buf.at[j, 1 - core], there), (back, back))
            ]

        def over_planes(hop):
            plane = lax.rem(place.plane + hop, planes)
            back = landed.at[planes - hop - 1]
            return [
                pltpu.make_async_remote_copy(
                    src_ref=src, dst_ref=dst, send_sem=z_send.at[hop - 1], recv_sem=z_recv.at[hop - 1],
                    device_id=(plane, place.me), device_id_type=MESH,
                )
                for src, dst in ((by_plane.at[plane], landed.at[planes - hop - 1]), (back, back))
            ]

        swaps = functools.partial(swap_pairs, place, [parts_buf], [swapped_ref], send, recv, local)

        @pl.when(step == 0)
        def _():
            for load in loads:
                load.start()
            greet_column_and_plane(place, planes)
            for load in loads:
                load.wait()
            for j in range(per_rank):
                over_core(j)[0].start()
                by_plane[core * per_rank + j] = og_buf[j, core]
            for copy, _ in swaps():
                copy.start()

        @pl.when(step == 1)
        def _():
            for j in range(per_rank):
                there, arrival = over_core(j)
                there.wait_send()
                arrival.wait_recv()
            for hop in range(1, planes):
                over_planes(hop)[0].start()

        mixer_backward_kernel(
            heads, blocks, cut_ref, qfi_ref, gap_ref, kept_ref, grad_ref, out_ref, gap_out_ref, state
        )

        @pl.when(step == steps - 1)
        def _():
            swap_waits(swaps())
            total = by_plane[place.plane].astype(F32)
            for hop in range(1, planes):
                there, arrival = over_planes(hop)
                there.wait_send()
                arrival.wait_recv()
                total += landed[planes - hop - 1].astype(F32)
            sum_ref[...] = total

    in_specs = [qfi_spec, gap_spec, kept_spec, block(width)]
    out_specs = [block(3 * width), gap_spec]
    out_shape = [jax.ShapeDtypeStruct((tokens, 3 * width), BF), jax.ShapeDtypeStruct((1, width), F32)]
    scratch = [pltpu.VMEM((heads, 128, 128), F32)]
    args = [qfi, gap, kept, grad]
    params = pltpu.CompilerParams(vmem_limit_bytes=VMEM_LIMIT)
    if together:
        rows, model = grad_out.shape[2:]
        in_specs, args = in_specs + [ANY_SPEC] * 2, args + [parts, grad_out]
        out_specs = out_specs + [ANY_SPEC, pl.BlockSpec((rows, model), lambda i, *_: (0, 0))]
        out_shape = out_shape + [
            jax.ShapeDtypeStruct(parts.shape, BF),
            jax.ShapeDtypeStruct((rows, model), F32),
        ]
        scratch = scratch + [
            pltpu.VMEM(parts.shape, BF),
            pltpu.VMEM(grad_out.shape, BF),
            pltpu.VMEM((planes, rows, model), BF),
            pltpu.VMEM((planes - 1, rows, model), BF),
            pltpu.SemaphoreType.DMA((1, 7)),
            pltpu.SemaphoreType.DMA((1, 7)),
            pltpu.SemaphoreType.DMA((1,)),
            pltpu.SemaphoreType.DMA((per_rank,)),
            pltpu.SemaphoreType.DMA((per_rank,)),
            pltpu.SemaphoreType.DMA((planes - 1,)),
            pltpu.SemaphoreType.DMA((planes - 1,)),
            pltpu.SemaphoreType.DMA((2,)),
        ]
        params = pltpu.CompilerParams(
            vmem_limit_bytes=VMEM_LIMIT, collective_id=collective_id, has_side_effects=True
        )
    return pl.pallas_call(
        kernel,
        grid_spec=pltpu.PrefetchScalarGridSpec(
            num_scalar_prefetch=1, grid=(steps,), in_specs=in_specs, out_specs=out_specs, scratch_shapes=scratch
        ),
        out_shape=out_shape,
        compiler_params=params,
        cost_estimate=pl.CostEstimate(
            flops=tokens * width * 128 * 24, bytes_accessed=tokens * width * 28, transcendentals=tokens * width * 6
        ),
        name="mixer_backward",
    )(cut, *args)


def feed_forward_kernel(units, n_ref, gu_ref, units_ref, act_ref, slope_ref, gate_w, up_w):
    @pl.when(pl.program_id(0) == 0)
    def _():
        gate_w[...] = gu_ref[:, :units]
        up_w[...] = gu_ref[:, units:]

    n = n_ref[...]
    gate, up = nn(n, gate_w[...]), nn(n, up_w[...])
    sig = jax.nn.sigmoid(gate)
    act = gate * sig
    units_ref[...] = (act * up).astype(BF)
    act_ref[...] = act.astype(BF)
    slope_ref[...] = (up * sig * (1.0 + gate * (1.0 - sig))).astype(BF)


def add_up(total, product, out_ref):
    step = pl.program_id(0)

    @pl.when(step == 0)
    def _():
        total[...] = product

    @pl.when(step > 0)
    def _():
        total[...] += product

    @pl.when(step == pl.num_programs(0) - 1)
    def _():
        out_ref[...] = total[...].astype(BF)


def feed_backward_kernel(units, g_ref, units_ref, down_ref, act_ref, slope_ref, grad_ref, down_grad_ref, g_all, u_all, sem, u_sem):
    step, steps = pl.program_id(0), pl.num_programs(0)
    blocks, rows, model = g_all.shape
    u_copy = pltpu.make_async_copy(units_ref, u_all, u_sem.at[0])

    def load(b):
        return pltpu.make_async_copy(g_ref.at[b], g_all.at[b], sem.at[b])

    @pl.when(step == 0)
    def _():
        for b in range(blocks):
            load(b).start()
        u_copy.start()

    load(step).wait()
    d_units = nt(g_all[step], down_ref[...])
    grad_ref[:, :units] = (d_units * slope_ref[...].astype(F32)).astype(BF)
    grad_ref[:, units:] = (d_units * act_ref[...].astype(F32)).astype(BF)

    @pl.when(step == steps - 1)
    def _():
        u_copy.wait()
        for at in range(0, model, 1024):
            cols = slice(at, at + 1024)
            down_grad_ref[:, cols] = tn(u_all[...], g_all[:, :, cols].reshape(blocks * rows, 1024)).astype(BF)


def output_backward_kernel(model, width, d_ref, mixed_ref, out_ref, d_mixed_ref, grad_ref, total):
    d_attn = d_ref[:, :model]
    mixed = mixed_ref[:, :width]
    beta = jnp.sum(d_ref[:, model:].astype(F32), axis=1, keepdims=True)
    d_mixed_ref[...] = (nt(d_attn, out_ref[...]) - beta * mixed.astype(F32)).astype(BF)
    add_up(total, tn(mixed, d_attn), grad_ref)


def fixed_block(shape):
    return pl.BlockSpec(shape, lambda i: (0, 0), pipeline_mode=pl.Buffered(1))


def row_block(columns):
    return pl.BlockSpec((512, columns), lambda i: (i, 0))


def feed_forward(n2, gu, own, full, collective_id):
    tokens, model = n2.shape
    units = gu.shape[1] // 2
    steps = tokens // 512
    together = lax.axis_size("seq") == 8

    def kernel(n_ref, gu_ref, *refs):
        if not together:
            return feed_forward_kernel(units, n_ref, gu_ref, *refs)
        own_ref, _, units_ref, act_ref, slope_ref, full_ref, gate_w, up_w, own_buf, send, recv, local = refs
        place, step = Place(), pl.program_id(0)
        gather = Gather(place, own_buf, full_ref, (send, recv), local)

        @pl.when(step == 0)
        def _():
            load = pltpu.make_async_copy(own_ref, own_buf, local.at[0])
            load.start()
            greet(place)
            load.wait()
            pl.loop(EARLY, PIECES)(gather.start)

        @pl.when(step == min(2, steps - 1))
        def _():
            pl.loop(EARLY, PIECES)(gather.forward)

        @pl.when(step == steps - 1)
        def _():
            pl.loop(EARLY, PIECES)(gather.forward_last)

        feed_forward_kernel(units, n_ref, gu_ref, units_ref, act_ref, slope_ref, gate_w, up_w)

        @pl.when(step == steps - 1)
        def _():
            for stage in (gather.finish, gather.drain):
                pl.loop(EARLY, PIECES)(stage)

    in_specs, args = [row_block(model), fixed_block(gu.shape)], [n2, gu]
    out_specs = [row_block(units)] * 3
    out_shape = [jax.ShapeDtypeStruct((tokens, units), d) for d in (BF, BF, BF)]
    scratch = [pltpu.VMEM((model, units), BF), pltpu.VMEM((model, units), BF)]
    params, aliases = pltpu.CompilerParams(vmem_limit_bytes=VMEM_LIMIT), {}
    if together:
        own = own.reshape(PIECES, own.shape[0] // PIECES, own.shape[1])
        in_specs, args = in_specs + [ANY_SPEC] * 2, args + [own, full]
        out_specs = out_specs + [ANY_SPEC]
        out_shape = out_shape + [jax.ShapeDtypeStruct(full.shape, full.dtype)]
        scratch = scratch + [pltpu.VMEM(own.shape, BF)] + plane_sems() + [pltpu.SemaphoreType.DMA((PIECES,))]
        params = pltpu.CompilerParams(
            vmem_limit_bytes=VMEM_LIMIT, collective_id=collective_id, has_side_effects=True
        )
        aliases = {3: 3}
    results = pl.pallas_call(
        kernel,
        grid=(steps,),
        in_specs=in_specs,
        out_specs=out_specs,
        out_shape=out_shape,
        scratch_shapes=scratch,
        compiler_params=params,
        input_output_aliases=aliases,
        cost_estimate=pl.CostEstimate(
            flops=4 * tokens * model * units, bytes_accessed=4 * tokens * model, transcendentals=tokens * units
        ),
        name="feed_forward",
    )(*args)
    if together:
        return results[0], results[1], results[2], results[3].reshape(tokens, model)
    return results[0], results[1], results[2], full


def feed_backward(grad, down, hidden_units, act, slope):
    tokens, model = grad.shape
    units = down.shape[0]
    blocks = tokens // 512
    return pl.pallas_call(
        functools.partial(feed_backward_kernel, units),
        grid=(blocks,),
        in_specs=[ANY_SPEC, ANY_SPEC, fixed_block(down.shape)] + [row_block(units)] * 2,
        out_specs=[row_block(2 * units), fixed_block(down.shape)],
        out_shape=[jax.ShapeDtypeStruct((tokens, 2 * units), BF), jax.ShapeDtypeStruct(down.shape, BF)],
        scratch_shapes=[
            pltpu.VMEM((blocks, 512, model), BF),
            pltpu.VMEM((tokens, units), BF),
            pltpu.SemaphoreType.DMA((blocks,)),
            pltpu.SemaphoreType.DMA((1,)),
        ],
        compiler_params=pltpu.CompilerParams(vmem_limit_bytes=VMEM_LIMIT),
        cost_estimate=pl.CostEstimate(
            flops=4 * tokens * model * units, bytes_accessed=8 * tokens * model, transcendentals=0
        ),
        name="feed_backward",
    )(grad.reshape(blocks, 512, model), hidden_units, down, act, slope)


def output_backward(d_attn, mixed, weight):
    tokens, (width, model) = mixed.shape[0], weight.shape
    return pl.pallas_call(
        functools.partial(output_backward_kernel, model, width),
        grid=(tokens // 512,),
        in_specs=[row_block(d_attn.shape[1]), row_block(mixed.shape[1]), fixed_block(weight.shape)],
        out_specs=[row_block(width), fixed_block(weight.shape)],
        out_shape=[jax.ShapeDtypeStruct((tokens, width), BF), jax.ShapeDtypeStruct(weight.shape, BF)],
        scratch_shapes=[pltpu.VMEM(weight.shape, F32)],
        compiler_params=pltpu.CompilerParams(vmem_limit_bytes=VMEM_LIMIT),
        cost_estimate=pl.CostEstimate(
            flops=4 * tokens * model * width, bytes_accessed=3 * tokens * model, transcendentals=0
        ),
        name="output_backward",
    )(d_attn, mixed, weight)


def gather_dp(v):
    return lax.all_gather(v, "dp", axis=0, tiled=True)


def scatter_dp(v):
    return lax.psum_scatter(v, "dp", scatter_dimension=0, tiled=True)


def swap_seq(v):
    return lax.all_to_all(v, "seq", split_axis=0, concat_axis=0, tiled=True)


def product_all(left, weight, transposed, stats, epilogue, owned, outs, gathered, collective_id, fillers=()):
    if lax.axis_size("seq") == 8:
        return product_scatter(left, weight, transposed, stats, epilogue, owned, outs, gathered, collective_id, fillers)
    depth = left.shape[1] - (EXTRA if stats else 0)
    product = (nt if transposed else nn)(left[:, :depth], weight).astype(BF)
    result = lax.psum_scatter(product, "seq", scatter_dimension=0, tiled=True).astype(F32)
    stat = None
    if stats:
        stat = lax.psum_scatter(left[:, depth:].astype(F32), "seq", scatter_dimension=0, tiled=True)
    written, sent = epilogue(result, stat, *owned)
    written = [w.astype(d) for w, (_, d) in zip(written, outs)]
    written += [lax.all_gather(sent, "seq", axis=0, tiled=True)] if gathered else []
    return written + [f.plain() for f in fillers]


def split_lanes(v):
    lane = lax.broadcasted_iota(jnp.int32, (v.shape[0], EXTRA), 1)
    high = v.astype(BF).astype(F32)
    return jnp.where(lane == 0, high, jnp.where(lane == 1, v - high, 0.0)).astype(BF)


def on_device(
    hidden,
    seg_ids,
    pad_mask,
    attn_gain,
    gate_gap,
    out_gain,
    w_query,
    w_forget,
    w_input,
    w_output,
    ffn_gain,
    w_gate,
    w_up,
    w_down,
    out_grad,
):
    planes, ranks = lax.axis_size("dp"), lax.axis_size("seq")
    row_tokens, model = hidden.shape[1:]
    rows = w_query.shape[0]
    units_in = w_down.shape[0]
    head = model // HEADS
    span = head // rows
    per_rank, groups = planes // span, ranks // span
    channels = per_rank * head
    units = planes * units_in
    tokens = ranks * row_tokens
    members = [[a * span + m for m in range(span)] for a in range(groups)]

    def to_heads(w):
        parts = w.reshape(rows, span, per_rank, groups, head)
        return parts.transpose(3, 1, 0, 2, 4).reshape(ranks, rows, channels)

    def from_heads(parts):
        parts = parts.reshape(groups, span, rows, per_rank, head)
        return parts.transpose(2, 1, 3, 0, 4).reshape(rows, model)

    def to_units(w):
        parts = w.reshape(rows, planes, ranks, units_in)
        return parts.transpose(2, 0, 1, 3).reshape(ranks, rows, units)

    def from_units(parts):
        parts = parts.reshape(ranks, rows, planes, units_in)
        return parts.transpose(1, 2, 0, 3).reshape(rows, planes * ranks * units_in)

    def own_rows(v):
        return v.reshape((span, per_rank) + v.shape[1:])

    def swap_group(v):
        return lax.all_to_all(v, "seq", split_axis=0, concat_axis=0, axis_index_groups=members)

    gain_a, gain_o, gain_f = (g.astype(F32)[:, None] for g in (attn_gain, out_gain, ffn_gain))

    plain = ranks != 8

    def order(first, *rest):
        return lax.optimization_barrier((first,) + rest)

    x16 = hidden[0]
    ids = jnp.concatenate([seg_ids, pad_mask], axis=0)
    mixer_weights = (w_query, w_forget, w_input)
    out_pieces = lax.all_gather(fold(gain_o, w_output), "dp", axis=0)
    if plain:
        qfi_part = jnp.concatenate([to_heads(fold(gain_a, w)) for w in mixer_weights], axis=2)
        qfi_full = gather_dp(swap_seq(qfi_part).reshape(ranks * rows, 3 * channels))
        gu_part = jnp.concatenate([to_units(fold(gain_f, w)) for w in (w_gate, w_up)], axis=2)
        gu_swapped = swap_seq(gu_part)
        x = x16.astype(F32)
        normed = (x * inverse_rms(row_mean(x * x))).astype(BF)
        n1 = lax.all_gather(normed, "seq", axis=0, tiled=True)
        gap_pieces = lax.all_gather(gate_gap, "dp", axis=0)
        gap_own = swap_group(own_rows(gap_pieces)).transpose(1, 0, 2).reshape(1, channels).astype(F32)
        ids = lax.all_gather(ids, "seq", axis=0)
        segment = ids[:, 0].reshape(tokens // BLOCK, BLOCK)
        live = jnp.sum(ids[:, 1]).reshape(1)
        ends = segment[:, -1]
        before = jnp.concatenate([segment[:1, 0], ends[:-1]])
        cut = jnp.sum((segment == before[:, None]).astype(jnp.int32), axis=1).reshape(ranks, -1)
        cut = jnp.concatenate([cut, jnp.broadcast_to(live, (ranks, 1))], axis=1)
        cut = jnp.pad(cut, ((0, 0), (0, EXTRA - cut.shape[1])))
    else:
        wide = -(-row_tokens // 128) * 128
        ids = jnp.pad(ids, ((0, 6), (0, wide - row_tokens)))
        gap_tile = jnp.pad(gate_gap[None], ((0, 15), (0, 128 - rows)))
        qfi_full, n1, gu_swapped, cut, gap_own = enter_plane(
            mixer_weights, gain_a, x16, (w_gate, w_up), gain_f, ids, gap_tile, per_rank, groups, planes, 1
        )
    gu_full = gather_dp(gu_swapped.reshape(ranks * rows, 2 * units))

    og16 = out_grad[0]
    mixed, kept, qfi, grad_all, out_own = mixer_forward(
        cut, n1, qfi_full, gap_own, og16, out_pieces, per_rank, 3
    )
    if plain:
        out_own = swap_group(own_rows(out_pieces)).transpose(1, 0, 2, 3).reshape(channels, model)

    def after_output(result, stat, x16):
        x = x16.astype(F32)
        factor_o = inverse_rms(jnp.sum(stat, axis=1, keepdims=True) / model)
        middle = x + factor_o * result
        normed = middle * inverse_rms(row_mean(middle * middle))
        return [middle, jnp.broadcast_to(factor_o, (x.shape[0], EXTRA))], normed.astype(BF)

    mixed, w_down_late = order(mixed, w_down)
    down_own = gather_dp(w_down_late)
    middle, factor_o, n2 = product_all(
        mixed, out_own, False, True, after_output, [x16], [(model, F32), (EXTRA, F32)], model, 4
    )
    hidden_units, act, slope, grad_all = feed_forward(n2, gu_full, og16, grad_all, 10)
    def after_down(result, stat, middle):
        return [(middle + result).astype(BF)], None

    d_gu, grad_down = feed_backward(grad_all, down_own, hidden_units, act, slope)
    down_sum = scatter_dp(grad_down)
    block_out, grad_gu = product_all(
        hidden_units, down_own, False, False, after_down, [middle], [(model, BF)], 0, 6,
        (GradProduct(n2, d_gu, False, 0),),
    )
    gu_sum = scatter_dp(grad_gu)
    d_gu, grad_gu = order(d_gu, grad_gu)

    def after_ffn(result, stat, middle, og16, x16, factor_o):
        factor_o = factor_o[:, :1]
        factor_m = inverse_rms(row_mean(middle * middle))
        normed = middle * factor_m
        d_middle = og16.astype(F32) + factor_m * (result - normed * row_mean(result * normed))
        mean_o = row_mean(d_middle * (middle - x16.astype(F32)))
        beta = split_lanes(factor_o * factor_o * mean_o)
        return [d_middle], jnp.concatenate([(factor_o * d_middle).astype(BF), beta], axis=1)

    d_middle, d_attn = product_all(
        d_gu, gu_full, True, False, after_ffn, [middle, og16, x16, factor_o], [(model, F32)], model + EXTRA, 5
    )
    d_attn, down_sum = order(d_attn, down_sum)
    d_mixed, grad_out = output_backward(d_attn, mixed, out_own)
    grad_out, d_mixed = order(grad_out, d_mixed)
    if plain:
        d_qfi, gap_grad = mixer_backward(cut, qfi, gap_own, kept, d_mixed, None, None, per_rank, 6)
        out_back = grad_out.reshape(per_rank, span, rows, model).transpose(1, 0, 2, 3)
        out_rows = scatter_dp(swap_group(out_back).reshape(planes * rows, model)).astype(F32)
        gu_rows = swap_seq(gu_sum).reshape(ranks, rows, 2 * units)
    else:
        d_qfi, gap_grad, gu_rows, out_rows = mixer_backward(
            cut, qfi, gap_own, kept, d_mixed, gu_sum.reshape(ranks, rows, 2 * units),
            grad_out.reshape(per_rank, span, rows, model), per_rank, 9,
        )
    grad_qfi = tn(n1, d_qfi).astype(BF)
    grad_qfi, d_qfi = order(grad_qfi, d_qfi)
    qfi_sum = scatter_dp(grad_qfi)

    def after_mixer(result, stat, x16, d_middle):
        x = x16.astype(F32)
        factor_x = inverse_rms(row_mean(x * x))
        normed = x * factor_x
        return [(d_middle + factor_x * (result - normed * row_mean(result * normed))).astype(BF)], None

    (hidden_grad,) = product_all(d_qfi, qfi_full, True, False, after_mixer, [x16, d_middle], [(model, BF)], 0, 7)

    hidden_grad, gu_rows, down_sum, out_rows, gap_grad = order(hidden_grad, gu_rows, down_sum, out_rows, gap_grad)

    def rowdot(w, g):
        return jnp.sum(w.astype(F32) * g, axis=1)

    g_out_gain = rowdot(w_output, out_rows)
    if plain:
        gu_rows = gu_rows.astype(F32)
        gate_rows, up_rows = from_units(gu_rows[:, :, :units]), from_units(gu_rows[:, :, units:])
        g_ffn_gain = rowdot(w_gate, gate_rows) + rowdot(w_up, up_rows)
        g_gate, g_up = gain_f * gate_rows, gain_f * up_rows
        gap_back = swap_group(gap_grad.reshape(per_rank, span, rows).transpose(1, 0, 2)).reshape(planes * rows)
        g_gap = scatter_dp(gap_back)
        qfi_rows = swap_seq(qfi_sum).reshape(ranks, rows, 3 * channels).astype(F32)
        parts = [from_heads(qfi_rows[:, :, j * channels : (j + 1) * channels]) for j in range(3)]
        g_attn_gain = sum(rowdot(w, g) for w, g in zip(mixer_weights, parts))
        g_query, g_forget, g_input = [gain_a * g for g in parts]
    else:
        (g_gate, g_up), g_ffn_gain = finish((w_gate, w_up), gain_f, gu_rows, unit_moves(units, planes, ranks))
        gap_tile = jnp.broadcast_to(gap_grad, (8, channels))
        qfi_rows, gap_all = exit_plane(qfi_sum.reshape(ranks, rows, 3 * channels), gap_tile, planes, 8)
        (g_query, g_forget, g_input), g_attn_gain = finish(
            mixer_weights, gain_a, qfi_rows, head_moves(head, per_rank, groups, span)
        )
        plane, me = lax.axis_index("dp"), lax.axis_index("seq")
        at = lax.rem(plane, per_rank) * head + lax.rem(me, 2) * rows
        from_core = jnp.sum(gap_all[:, :, 0], axis=0)
        g_gap = lax.dynamic_slice(from_core, (plane // per_rank, at), (1, rows))[0]
    return (
        block_out[None],
        hidden_grad[None],
        g_attn_gain,
        g_gap,
        g_out_gain,
        g_query,
        g_forget,
        g_input,
        gain_o * out_rows,
        g_ffn_gain,
        g_gate,
        g_up,
        down_sum.astype(F32),
    )


def solution(mesh):
    tok, row, both = P("dp", "seq", None), P("dp", "seq"), P(("dp", "seq"))
    mat = P(("dp", "seq"), None)
    return jax.shard_map(
        on_device,
        mesh=mesh,
        in_specs=(tok, row, row, both, both, both, mat, mat, mat, mat, both, mat, mat, mat, tok),
        out_specs=(tok, tok, both, both, both, mat, mat, mat, mat, both, mat, mat, mat),
        check_vma=False,
    )
```

```python
import functools

import jax
import jax.numpy as jnp
from jax import lax
from jax.experimental import pallas as pl
from jax.experimental.pallas import tpu as pltpu
from jax.sharding import PartitionSpec as P

HEADS = 16
BLOCK = 64
UNROLL = 4
EPSILON = 1e-06
EXTRA = 128
BF = jnp.bfloat16
F32 = jnp.float32


def dot(a, b, dims):
    return lax.dot_general(a, b, (dims, ((), ())), preferred_element_type=F32)


def nn(a, b):
    return dot(a, b, ((1,), (0,)))


def nt(a, b):
    return dot(a, b, ((1,), (1,)))


def tn(a, b):
    return dot(a, b, ((0,), (0,)))


def inverse_rms(square_mean):
    return lax.rsqrt(square_mean + EPSILON)


def row_mean(v):
    return jnp.mean(v, axis=1, keepdims=True)


def split_sum(tri, v):
    high = v.astype(BF)
    low = (v - high.astype(F32)).astype(BF)
    return nn(tri, high) + nn(tri, low)


def chunk_prep(qfi, gap, live, width):
    query_pre, forget_pre, input_pre = (
        qfi[:, :width],
        qfi[:, width : 2 * width],
        qfi[:, 2 * width :],
    )
    sig_q = jax.nn.sigmoid(query_pre)
    sig_nf = jax.nn.sigmoid(-forget_pre)
    key = gap * sig_nf
    return query_pre, sig_q, sig_nf, key, input_pre * live


def triangle(lower):
    row = lax.broadcasted_iota(jnp.int32, (BLOCK, BLOCK), 0)
    col = lax.broadcasted_iota(jnp.int32, (BLOCK, BLOCK), 1)
    return (row >= col) if lower else (row <= col)


def chunk_masks(cut):
    row = lax.broadcasted_iota(jnp.int32, (BLOCK, BLOCK), 0)
    col = lax.broadcasted_iota(jnp.int32, (BLOCK, BLOCK), 1)
    allowed = (row >= col) & ((row >= cut) == (col >= cut))
    at = lax.broadcasted_iota(jnp.int32, (BLOCK, 1), 0)
    inherits = (at < cut).astype(F32)
    tail = ((at >= cut) | (cut >= BLOCK)).astype(F32)
    whole = (cut >= BLOCK).astype(F32)
    return allowed, inherits, tail, whole


def mixer_forward_kernel(heads, blocks, cut_ref, n_ref, w_ref, gap_ref, mixed_ref, kept_ref, qfi_ref, state):
    step = pl.program_id(0)
    width = heads * 128

    @pl.when(step == 0)
    def _():
        state[...] = jnp.zeros_like(state)

    qfi_ref[...] = nn(n_ref[...], w_ref[...])
    lower = triangle(True).astype(BF)
    for u in range(UNROLL):
        chunk = step * UNROLL + u
        rows = slice(u * BLOCK, (u + 1) * BLOCK)
        at = lax.broadcasted_iota(jnp.int32, (BLOCK, 1), 0) + chunk * BLOCK
        live = (at < cut_ref[0, blocks]).astype(F32)
        query_pre, sig_q, sig_nf, key, value = chunk_prep(qfi_ref[rows, :], gap_ref[...], live, width)
        query = query_pre * sig_q
        total = split_sum(lower, jnp.log1p(-key))
        centre = total[BLOCK // 2 : BLOCK // 2 + 1]
        ending = total[BLOCK - 1 :]
        scaled_q = (query * jnp.exp(total - centre)).astype(BF)
        scaled_k = (key * jnp.exp(centre - total)).astype(BF)
        value_low = value.astype(BF)
        allowed, inherits, tail, whole = chunk_masks(cut_ref[chunk // blocks, lax.rem(chunk, blocks)])
        value_tail = (value * tail).astype(BF)
        e_centre = jnp.exp(centre)
        e_rest = jnp.exp(ending - centre)
        e_all = jnp.exp(ending) * whole
        square = jnp.zeros((BLOCK, 1), F32)
        for h in range(heads):
            cols = slice(h * 128, (h + 1) * 128)
            before = state[h]
            kept_ref[u, h] = before.astype(BF)
            scores = jnp.where(allowed, nt(scaled_q[:, cols], scaled_k[:, cols]), 0.0)
            inner = nn(scores.astype(BF), value_low[:, cols])
            outer = nt(scaled_q[:, cols], (before * e_centre[:, cols]).astype(BF))
            mixed = inner + outer * inherits
            square = square + jnp.sum(mixed * mixed, axis=1, keepdims=True)
            mixed_ref[rows, cols] = mixed.astype(BF)
            state[h] = before * e_all[:, cols] + tn(value_tail[:, cols], scaled_k[:, cols]) * e_rest[:, cols]
        lane = lax.broadcasted_iota(jnp.int32, (BLOCK, EXTRA), 1)
        high = square.astype(BF).astype(F32)
        mixed_ref[rows, width:] = jnp.where(lane == 0, high, jnp.where(lane == 1, square - high, 0.0)).astype(BF)


def mixer_backward_kernel(heads, blocks, cut_ref, qfi_ref, gap_ref, kept_ref, grad_ref, out_ref, gap_out_ref, state):
    step = pl.program_id(0)
    last = pl.num_programs(0) - 1
    width = heads * 128

    @pl.when(step == 0)
    def _():
        state[...] = jnp.zeros_like(state)
        gap_out_ref[...] = jnp.zeros_like(gap_out_ref)

    lower = triangle(True).astype(BF)
    upper = triangle(False).astype(BF)
    for u in reversed(range(UNROLL)):
        chunk = (last - step) * UNROLL + u
        rows = slice(u * BLOCK, (u + 1) * BLOCK)
        at = lax.broadcasted_iota(jnp.int32, (BLOCK, 1), 0) + chunk * BLOCK
        live = (at < cut_ref[0, blocks]).astype(F32)
        gap = gap_ref[...]
        query_pre, sig_q, sig_nf, key, value = chunk_prep(qfi_ref[rows, :], gap, live, width)
        query = query_pre * sig_q
        total = split_sum(lower, jnp.log1p(-key))
        centre = total[BLOCK // 2 : BLOCK // 2 + 1]
        ending = total[BLOCK - 1 :]
        e_q = jnp.exp(total - centre)
        e_k = jnp.exp(centre - total)
        scaled_q = (query * e_q).astype(BF)
        scaled_k = (key * e_k).astype(BF)
        value_low = value.astype(BF)
        allowed, inherits, tail, whole = chunk_masks(cut_ref[chunk // blocks, lax.rem(chunk, blocks)])
        value_tail = (value * tail).astype(BF)
        grad = grad_ref[rows, :]
        grad_in = (grad.astype(F32) * inherits).astype(BF)
        e_centre = jnp.exp(centre)
        e_rest = jnp.exp(ending - centre)
        e_all = jnp.exp(ending) * whole
        d_query, d_key, d_value, d_total, d_end = [], [], [], [], []
        for h in range(heads):
            cols = slice(h * 128, (h + 1) * 128)
            before = kept_ref[u, h].astype(F32)
            after = state[h]
            q, k, v, g, gi = scaled_q[:, cols], scaled_k[:, cols], value_low[:, cols], grad[:, cols], grad_in[:, cols]
            vt = value_tail[:, cols]
            scores = jnp.where(allowed, nt(q, k), 0.0).astype(BF)
            d_scores = jnp.where(allowed, nt(g, v), 0.0).astype(BF)
            shifted = (before * e_centre[:, cols]).astype(BF)
            onward = (after * e_rest[:, cols]).astype(BF)
            dq = nn(d_scores, k) + nn(gi, shifted)
            dk_state = nn(vt, onward)
            dk = tn(d_scores, q) + dk_state
            dv = tn(scores, g) + nt(k, onward) * tail
            k32 = k.astype(F32)
            d_total.append(dq * q.astype(F32) - dk * k32)
            d_end.append(
                jnp.sum(after * before, axis=0, keepdims=True) * e_all[:, cols]
                + jnp.sum(dk_state * k32, axis=0, keepdims=True)
            )
            state[h] = after * e_all[:, cols] + tn(gi, q) * e_centre[:, cols]
            d_query.append(dq)
            d_key.append(dk)
            d_value.append(dv)
        d_query = jnp.concatenate(d_query, axis=1) * e_q
        d_key = jnp.concatenate(d_key, axis=1) * e_k
        d_value = jnp.concatenate(d_value, axis=1) * live
        d_log = split_sum(upper, jnp.concatenate(d_total, axis=1)) + jnp.concatenate(d_end, axis=1)
        d_key = d_key - d_log / (1.0 - key)
        gap_out_ref[...] += jnp.sum(d_key * sig_nf, axis=0, keepdims=True)
        out_ref[rows, :width] = (d_query * sig_q * (1.0 + query_pre * (1.0 - sig_q))).astype(BF)
        out_ref[rows, width : 2 * width] = (-d_key * key * (1.0 - sig_nf)).astype(BF)
        out_ref[rows, 2 * width :] = d_value.astype(BF)


MESH = pl.DeviceIdType.MESH
PIECES = 5
EARLY = 4
TILE = 1024
CHUNK = 32
VMEM_LIMIT = 60 * 1024 * 1024
(S_X, S_Y, S_CORE, S_DIAG_Y, S_DIAG_X, S_CORE_X, S_CORE_Y, S_CORE_D, R_CORE, R_X, R_Y, R_LAST_Y, R_LAST_X, KINDS) = range(14)


class Place:
    def __init__(self):
        self.plane = lax.axis_index("dp")
        me = lax.axis_index("seq")
        self.me = me
        self.core = me % 2
        self.x = (me // 2) % 2
        self.y = me // 4

    def rank(self, fy=0, fx=0, fc=0):
        y = 1 - self.y if fy else self.y
        x = 1 - self.x if fx else self.x
        core = 1 - self.core if fc else self.core
        return 4 * y + 2 * x + core

    def device(self, fy=0, fx=0, fc=0):
        return (self.plane, self.rank(fy, fx, fc))


def greet(place):
    barrier = pltpu.get_barrier_semaphore()
    for flip in ((0, 0, 1), (0, 1, 0), (1, 0, 0)):
        pl.semaphore_signal(barrier, inc=1, device_id=place.device(*flip), device_id_type=MESH)
    pl.semaphore_wait(barrier, 3)


def remote(src, dst, sems, kind, b, device):
    send, recv = sems
    return pltpu.make_async_remote_copy(
        src_ref=src,
        dst_ref=dst,
        send_sem=send.at[kind, b],
        recv_sem=recv.at[kind, b],
        device_id=device,
        device_id_type=MESH,
    )


class Gather:
    def __init__(self, place, own, full, sems, local_sem):
        self.p, self.own, self.full, self.sems, self.local = place, own, full, sems, local_sem
        self.half = full.shape[2] // 2

    def keep(self, b):
        return pltpu.make_async_copy(self.own.at[b], self.full.at[self.p.me, b], self.local.at[b])

    def first(self, b):
        p, dst = self.p, self.full.at[self.p.me, b]
        return [
            remote(self.own.at[b], dst, self.sems, S_X, b, p.device(0, 1, 0)),
            remote(self.own.at[b], dst, self.sems, S_Y, b, p.device(1, 0, 0)),
            remote(self.own.at[b], dst, self.sems, S_CORE, b, p.device(0, 0, 1)),
        ]

    def second(self, b):
        p, h = self.p, self.half
        from_x, from_y = self.full.at[p.rank(0, 1, 0), b], self.full.at[p.rank(1, 0, 0), b]
        up, down = from_x.at[pl.ds(0, h)], from_y.at[pl.ds(h, h)]
        return [
            remote(up, up, self.sems, S_DIAG_Y, b, p.device(1, 0, 0)),
            remote(down, down, self.sems, S_DIAG_X, b, p.device(0, 1, 0)),
            remote(from_x, from_x, self.sems, S_CORE_X, b, p.device(0, 0, 1)),
            remote(from_y, from_y, self.sems, S_CORE_Y, b, p.device(0, 0, 1)),
        ]

    def third(self, b):
        p = self.p
        block = self.full.at[p.rank(1, 1, 0), b]
        return [remote(block, block, self.sems, S_CORE_D, b, p.device(0, 0, 1))]

    def arrived(self, kind, b, flips, rows=None):
        block = self.full.at[self.p.rank(*flips), b]
        if rows is not None:
            block = block.at[pl.ds(rows * self.half, self.half)]
        remote(block, block, self.sems, kind, b, self.p.device(0, 0, 1)).wait_recv()

    def start(self, b):
        self.keep(b).start()
        for copy in self.first(b):
            copy.start()

    def forward(self, b):
        self.arrived(S_X, b, (0, 1, 0))
        self.arrived(S_Y, b, (1, 0, 0))
        for copy in self.second(b):
            copy.start()

    def forward_last(self, b):
        self.arrived(S_DIAG_Y, b, (1, 1, 0), 0)
        self.arrived(S_DIAG_X, b, (1, 1, 0), 1)
        for copy in self.third(b):
            copy.start()

    def finish(self, b):
        self.arrived(S_CORE, b, (0, 0, 1))
        self.arrived(S_CORE_X, b, (0, 1, 1))
        self.arrived(S_CORE_Y, b, (1, 0, 1))
        self.arrived(S_CORE_D, b, (1, 1, 1))

    def drain(self, b):
        self.keep(b).wait()
        for copy in self.first(b) + self.second(b) + self.third(b):
            copy.wait_send()


def swap_pairs(place, parts, outs, send, recv, local):
    pairs = []
    for i, (part, out) in enumerate(zip(parts, outs)):
        pairs.append((pltpu.make_async_copy(part.at[place.me], out.at[place.me], local.at[i]), None))
        for k, flips in enumerate(FLIPS):
            there = out.at[place.rank(*flips)]
            pairs.append(tuple(
                pltpu.make_async_remote_copy(
                    src_ref=src, dst_ref=dst, send_sem=send.at[i, k], recv_sem=recv.at[i, k],
                    device_id=place.device(*flips), device_id_type=MESH,
                )
                for src, dst in ((part.at[place.rank(*flips)], out.at[place.me]), (there, there))
            ))
    return pairs


def swap_starts(place, parts, outs, send, recv, local):
    pairs = swap_pairs(place, parts, outs, send, recv, local)
    for copy, _ in pairs:
        copy.start()
    return pairs


def swap_waits(pairs):
    for copy, arrival in pairs:
        if arrival is None:
            copy.wait()
        else:
            copy.wait_send()
            arrival.wait_recv()


def greet_all(place):
    barrier = pltpu.get_barrier_semaphore()
    for flips in ((0, 0, 1), (0, 1, 0), (1, 0, 0), (0, 1, 1), (1, 0, 1), (1, 1, 0), (1, 1, 1)):
        pl.semaphore_signal(barrier, inc=1, device_id=place.device(*flips), device_id_type=MESH)
    pl.semaphore_wait(barrier, 7)


def fold(gain, w):
    return (gain * w.astype(F32)).astype(BF)


FLIPS = ((0, 0, 1), (0, 1, 0), (1, 0, 0), (0, 1, 1), (1, 0, 1), (1, 1, 0), (1, 1, 1))
ANY_SPEC = pl.BlockSpec(memory_space=pl.ANY)
VMEM_SPEC = pl.BlockSpec(memory_space=pltpu.VMEM)


def column_peers(place, planes):
    peers = []
    for hop in range(planes):
        for flip in (0, 1):
            if hop or flip:
                plane = lax.rem(place.plane + hop, planes)
                peers.append((plane, place.rank(0, 0, flip)))
    return peers


def column_spread(place, planes, src, dst, send, recv):
    waits = []
    for k, (plane, rank) in enumerate(column_peers(place, planes)):
        mine = dst.at[place.plane, place.core]
        copy = pltpu.make_async_remote_copy(
            src_ref=src, dst_ref=mine, send_sem=send.at[k], recv_sem=recv.at[k],
            device_id=(plane, rank), device_id_type=MESH,
        )
        copy.start()
        back = lax.rem(planes + 2 * place.plane - plane, planes)
        there = dst.at[back, lax.rem(rank, 2)]
        waits.append((copy, pltpu.make_async_remote_copy(
            src_ref=there, dst_ref=there, send_sem=send.at[k], recv_sem=recv.at[k],
            device_id=(plane, rank), device_id_type=MESH,
        )))
    return waits


def greet_column_and_plane(place, planes):
    barrier = pltpu.get_barrier_semaphore()
    devices = [place.device(*flips) for flips in FLIPS]
    devices += [p for p in column_peers(place, planes)[1:]]
    for device in devices:
        pl.semaphore_signal(barrier, inc=1, device_id=device, device_id_type=MESH)
    pl.semaphore_wait(barrier, len(devices))


class Line:
    def __init__(self, place, planes, full, sems):
        self.p, self.planes, self.full, self.sems = place, planes, full, sems

    def copy(self, way, plane, to, hop):
        send, recv = self.sems
        block = self.full.at[plane]
        return pltpu.make_async_remote_copy(
            src_ref=block, dst_ref=block, send_sem=send.at[way, hop], recv_sem=recv.at[way, hop],
            device_id=(to, self.p.me), device_id_type=MESH,
        )

    def each(self, hop, arriving, body):
        plane, last = self.p.plane, self.planes - 1
        if arriving:
            conditions = (plane - hop >= 0, plane + hop <= last)
        else:
            conditions = ((plane - hop >= 0) & (plane + 1 <= last), (plane + hop <= last) & (plane >= 1))
        for way, condition in enumerate(conditions):
            @pl.when(condition)
            def _():
                block = plane - hop if way == 0 else plane + hop
                to = lax.rem(plane + (1 if way == 0 else last), self.planes)
                body(self.copy(way, block, to, hop - 1 if arriving else hop))

    def start(self, hop):
        self.each(hop, False, lambda copy: copy.start())

    def arrive(self, hop):
        self.each(hop, True, lambda copy: copy.wait_recv())

    def drain(self):
        for hop in range(self.planes - 1):
            self.each(hop, False, lambda copy: copy.wait_send())


def enter_plane(weights, gain, x, unit_weights, unit_gain, ids, gap, per_rank, groups, planes, collective_id):
    rows, model = weights[0].shape
    head = model // (8 * per_rank)
    channels = per_rank * head
    span = 8 // groups
    tokens = x.shape[0]
    x_rows = tokens // PIECES
    every_unit = unit_weights[0].shape[1]
    units_in = every_unit // (8 * planes)
    units = units_in * planes
    x = x.reshape(PIECES, x_rows, model)
    blocks = tokens // BLOCK

    def kernel(q_ref, f_ref, i_ref, gain_ref, x_ref, gate_ref, up_ref, unit_gain_ref, ids_ref, gap_ref,
               qfi_out, full, unit_out, cut_out, gap_out,
               part, normed, unit_part, ids_in, gap_in, *sems):
        (swap_send, swap_recv, swap_local, send, recv, local, gap_send, gap_recv, z_send, z_recv) = sems
        place = Place()
        scale = gain_ref[...]
        for w, ref in enumerate((q_ref, f_ref, i_ref)):
            for rank, source, target in ((r, t, c) for v, r, c, t in head_moves(head, per_rank, groups, span) if v == w):
                part[rank, :, target] = fold(scale, ref[:, source])
        greet_column_and_plane(place, planes)
        first = swap_starts(
            place, [part], [qfi_out.at[place.plane]],
            swap_send.at[pl.ds(0, 1)], swap_recv.at[pl.ds(0, 1)], swap_local.at[pl.ds(0, 1)],
        )
        gaps = column_spread(place, planes, gap_ref, gap_in, gap_send, gap_recv)
        gap_in[place.plane, place.core] = gap_ref[...]
        ids_in[place.me] = ids_ref[...]
        id_pairs = []
        for k, flips in enumerate(FLIPS):
            there = ids_in.at[place.rank(*flips)]
            id_pairs.append(tuple(
                pltpu.make_async_remote_copy(
                    src_ref=src, dst_ref=dst, send_sem=swap_send.at[1, k], recv_sem=swap_recv.at[1, k],
                    device_id=place.device(*flips), device_id_type=MESH,
                )
                for src, dst in ((ids_ref, ids_in.at[place.me]), (there, there))
            ))
            id_pairs[-1][0].start()

        gather = Gather(place, normed, full, (send, recv), local)

        @pl.loop(0, PIECES)
        def _(b):
            value = x_ref[b].astype(F32)
            normed[b] = (value * inverse_rms(row_mean(value * value))).astype(BF)
            gather.start(b)

        line = Line(place, planes, qfi_out, (z_send, z_recv))
        swap_waits(first)
        line.start(0)
        unit_scale = unit_gain_ref[...]
        for side, ref in enumerate((gate_ref, up_ref)):
            for _, rank, target, source in (move for move in unit_moves(units, planes, 8) if move[0] == side):
                unit_part[rank, :, target] = fold(unit_scale, ref[:, source])
        unit_copies = swap_starts(
            place, [unit_part], [unit_out],
            swap_send.at[pl.ds(2, 1)], swap_recv.at[pl.ds(2, 1)], swap_local.at[pl.ds(1, 1)],
        )
        for copy, arrival in id_pairs + gaps:
            copy.wait_send()
            arrival.wait_recv()
        segment = ids_in[:, 0, :].astype(F32)
        live = jnp.sum(ids_in[:, 1, :tokens].astype(F32))
        lane = lax.broadcasted_iota(jnp.int32, (8, EXTRA), 1)
        parts = [segment[:, c * BLOCK : (c + 1) * BLOCK] for c in range(blocks)]
        ends = [jnp.max(p, axis=1, keepdims=True) for p in parts]
        begin = jnp.min(parts[0], axis=1, keepdims=True)
        before = jnp.concatenate([begin[:1], ends[-1][:-1]], axis=0)
        result = jnp.where(lane == blocks, live, 0.0)
        for c in range(blocks):
            stay = jnp.sum((parts[c] == before).astype(F32), axis=1, keepdims=True)
            result = jnp.where(lane == c, stay, result)
            before = ends[c]
        cut_out[...] = result.astype(jnp.int32)
        for j in range(per_rank):
            for c in range(span):
                at = (j * span + c) * rows
                gap_out[:, at : at + rows] = gap_in[place.core * per_rank + j, c, :1, :rows].astype(F32)
        stages = [lambda: pl.loop(0, 3)(gather.forward), lambda: pl.loop(3, PIECES)(gather.forward)]
        stages += [lambda: pl.loop(0, PIECES)(gather.forward_last)]
        for hop in range(1, planes):
            if hop <= len(stages):
                stages[hop - 1]()
            line.arrive(hop)
            if hop < planes - 1:
                line.start(hop)
        for stage in stages[planes - 1 :]:
            stage()
        pl.loop(0, PIECES)(gather.finish)
        swap_waits(unit_copies)
        line.drain()
        pl.loop(0, PIECES)(gather.drain)

    qfi, full, unit_rows, cut, gap = pl.pallas_call(
        kernel,
        in_specs=[VMEM_SPEC] * 10,
        out_specs=[ANY_SPEC] * 3 + [VMEM_SPEC] * 2,
        out_shape=[
            jax.ShapeDtypeStruct((planes, 8, rows, 3 * channels), BF),
            jax.ShapeDtypeStruct((8, PIECES, x_rows, model), BF),
            jax.ShapeDtypeStruct((8, rows, 2 * units), BF),
            jax.ShapeDtypeStruct((8, EXTRA), jnp.int32),
            jax.ShapeDtypeStruct((1, channels), F32),
        ],
        scratch_shapes=[
            pltpu.VMEM((8, rows, 3 * channels), BF),
            pltpu.VMEM((PIECES, x_rows, model), BF),
            pltpu.VMEM((8, rows, 2 * units), BF),
            pltpu.VMEM((8,) + ids.shape, ids.dtype),
            pltpu.VMEM((planes, 2) + gap.shape, gap.dtype),
            pltpu.SemaphoreType.DMA((3, 7)),
            pltpu.SemaphoreType.DMA((3, 7)),
            pltpu.SemaphoreType.DMA((2,)),
            pltpu.SemaphoreType.DMA((KINDS, PIECES)),
            pltpu.SemaphoreType.DMA((KINDS, PIECES)),
            pltpu.SemaphoreType.DMA((PIECES,)),
            pltpu.SemaphoreType.DMA((2 * planes - 1,)),
            pltpu.SemaphoreType.DMA((2 * planes - 1,)),
            pltpu.SemaphoreType.DMA((2, planes)),
            pltpu.SemaphoreType.DMA((2, planes)),
        ],
        compiler_params=pltpu.CompilerParams(
            collective_id=collective_id, has_side_effects=True, vmem_limit_bytes=VMEM_LIMIT
        ),
        cost_estimate=pl.CostEstimate(flops=0, bytes_accessed=200 * tokens * model, transcendentals=0),
        name="enter_plane",
    )(*weights, gain, x, *unit_weights, unit_gain, ids, gap)
    return (
        qfi.reshape(model, 3 * channels),
        full.reshape(8 * tokens, model),
        unit_rows,
        cut,
        gap,
    )


def exit_plane(summed, gap_grad, planes, collective_id):
    def kernel(sum_ref, gap_ref, landed, gap_out, *sems):
        send, recv, local, gap_send, gap_recv = sems
        place = Place()
        greet_column_and_plane(place, planes)
        copies = swap_starts(place, [sum_ref], [landed], send, recv, local)
        gaps = column_spread(place, planes, gap_ref, gap_out, gap_send, gap_recv)
        own_gap = pltpu.make_async_copy(gap_ref, gap_out.at[place.plane, place.core], local.at[1])
        own_gap.start()
        swap_waits(copies)
        for copy, arrival in gaps:
            copy.wait_send()
            arrival.wait_recv()
        own_gap.wait()

    return pl.pallas_call(
        kernel,
        in_specs=[ANY_SPEC] * 2,
        out_specs=[ANY_SPEC] * 2,
        out_shape=[
            jax.ShapeDtypeStruct(summed.shape, summed.dtype),
            jax.ShapeDtypeStruct((planes, 2) + gap_grad.shape, gap_grad.dtype),
        ],
        scratch_shapes=[
            pltpu.SemaphoreType.DMA((1, 7)),
            pltpu.SemaphoreType.DMA((1, 7)),
            pltpu.SemaphoreType.DMA((2,)),
            pltpu.SemaphoreType.DMA((2 * planes - 1,)),
            pltpu.SemaphoreType.DMA((2 * planes - 1,)),
        ],
        compiler_params=pltpu.CompilerParams(collective_id=collective_id, has_side_effects=True),
        name="exit_plane",
    )(summed, gap_grad)


def finish(weights, gain, swapped, moves):
    rows, width = weights[0].shape
    tile = 512

    def kernel(*refs):
        in_ref, gain_ref = refs[0], refs[1]
        w_refs = refs[2 : 2 + len(weights)]
        outs, gain_out = refs[2 + len(weights) : -1], refs[-1]
        for w, rank, source, target in moves:
            outs[w][:, target] = in_ref[rank, :, source].astype(F32)
        scale = gain_ref[...]
        total = jnp.zeros((rows, tile), F32)
        for ref, out in zip(w_refs, outs):
            for at in range(0, width, tile):
                grad = out[:, at : at + tile]
                total += grad * ref[:, at : at + tile].astype(F32)
                out[:, at : at + tile] = grad * scale
        column = jnp.sum(total, axis=1, keepdims=True)
        diagonal = lax.broadcasted_iota(jnp.int32, (rows, rows), 0) == lax.broadcasted_iota(jnp.int32, (rows, rows), 1)
        gain_out[...] = jnp.sum(jnp.where(diagonal, column, 0.0), axis=0, keepdims=True)

    results = pl.pallas_call(
        kernel,
        in_specs=[VMEM_SPEC] * (2 + len(weights)),
        out_specs=[VMEM_SPEC] * (len(weights) + 1),
        out_shape=[jax.ShapeDtypeStruct((rows, width), F32)] * len(weights) + [jax.ShapeDtypeStruct((1, rows), F32)],
        compiler_params=pltpu.CompilerParams(vmem_limit_bytes=VMEM_LIMIT),
        name="finish",
    )(swapped, gain, *weights)
    return results[:-1], results[-1].reshape(rows)


def unit_moves(units, planes, ranks):
    units_in = units // planes
    return [
        (
            side,
            s,
            slice(side * units + i * units_in, side * units + (i + 1) * units_in),
            slice((i * ranks + s) * units_in, (i * ranks + s + 1) * units_in),
        )
        for side in range(2)
        for i in range(planes)
        for s in range(ranks)
    ]


def head_moves(head, per_rank, groups, span):
    moves = []
    for w in range(3):
        for a in range(groups):
            for m in range(span):
                for j in range(per_rank):
                    h = (m * per_rank + j) * groups + a
                    at = (w * per_rank + j) * head
                    moves.append((w, a * span + m, slice(at, at + head), slice(h * head, (h + 1) * head)))
    return moves


class Scatter:
    def __init__(self, left, weight, transposed, stats):
        self.rows, self.columns = left[2], left[3]
        self.transposed, self.stats = transposed, stats
        self.weight = weight
        self.depth = weight[1] if transposed else weight[0]
        self.width = weight[0] if transposed else weight[1]
        self.half = self.width // 2
        self.extra = EXTRA if stats else 0

    def scratch(self):
        rows, half, full = self.rows, self.half, self.width + self.extra
        right = half + self.extra
        return [
            pltpu.VMEM((PIECES, 8, rows, self.columns), BF),
            pltpu.VMEM(self.weight, BF),
            pltpu.VMEM((PIECES, 4, rows, full), BF),
            pltpu.VMEM((PIECES, 4, rows, full), BF),
            pltpu.VMEM((4, rows, full), F32),
            pltpu.VMEM((PIECES, 2, rows, half), BF),
            pltpu.VMEM((PIECES, 2, rows, half), BF),
            pltpu.VMEM((PIECES, 2, rows, right), BF),
            pltpu.VMEM((PIECES, 2, rows, right), BF),
            pltpu.VMEM((PIECES, 2, rows, half), F32),
            pltpu.VMEM((PIECES, 2, rows, right), F32),
            pltpu.VMEM((PIECES, rows, half), BF),
            pltpu.VMEM((PIECES, rows, half), BF),
            pltpu.VMEM((PIECES, rows, right), BF),
            pltpu.VMEM((PIECES, rows, right), BF),
            pltpu.SemaphoreType.DMA((PIECES,)),
            pltpu.SemaphoreType.DMA((1,)),
        ]

    def bind(self, place, sems, left_ref, weight_ref, refs):
        self.place, self.sems, self.left_ref, self.weight_ref = place, sems, left_ref, weight_ref
        (self.x_buf, self.w_buf, self.core_out, self.core_in, self.total, self.x_out, self.x_in, self.y_out, self.y_in,
         self.keep_a, self.keep_b, self.last_y_out, self.last_y_in, self.last_x_out,
         self.last_x_in, self.load_sem, self.w_sem) = refs

    def weight_copy(self):
        return pltpu.make_async_copy(self.weight_ref, self.w_buf, self.w_sem.at[0])

    def start_loads(self):
        core = self.place.core
        for b in range(PIECES):
            for j in range(4):
                for side, at in ((0, 2 * j + 1 - core), (4, 2 * j + core)):
                    pltpu.make_async_copy(
                        self.left_ref.at[at, b], self.x_buf.at[b, side + j], self.load_sem.at[b]
                    ).start()
            if b == 0:
                self.weight_copy().start()

    def send_core(self, b):
        return remote(self.core_out.at[b], self.core_in.at[b], self.sems, R_CORE, b, self.place.device(0, 0, 1))

    def send_x(self, b):
        return remote(self.x_out.at[b], self.x_in.at[b], self.sems, R_X, b, self.place.device(0, 1, 0))

    def send_y(self, b):
        return remote(self.y_out.at[b], self.y_in.at[b], self.sems, R_Y, b, self.place.device(1, 0, 0))

    def send_last_y(self, b):
        return remote(self.last_y_out.at[b], self.last_y_in.at[b], self.sems, R_LAST_Y, b, self.place.device(1, 0, 0))

    def send_last_x(self, b):
        return remote(self.last_x_out.at[b], self.last_x_in.at[b], self.sems, R_LAST_X, b, self.place.device(0, 1, 0))

    def produce(self, b):
        rows, depth, width, tile = self.rows, self.depth, self.width, min(TILE, self.width)
        pltpu.make_async_copy(self.x_buf.at[b], self.x_buf.at[b], self.load_sem.at[b]).wait()

        def product(side, t):
            lhs = self.x_buf[b, 4 * side : 4 * side + 4, :, :depth].reshape(4 * rows, depth)
            at = slice(t * tile, (t + 1) * tile)
            out = nt(lhs, self.w_buf[at, :]) if self.transposed else nn(lhs, self.w_buf[:, at])
            return out.reshape(4, rows, tile), at

        for t in range(width // tile):
            out, at = product(0, t)
            self.core_out[b, :, :, at] = out.astype(BF)
        if self.stats:
            self.core_out[b, :, :, width:] = self.x_buf[b, :4, :, depth:]
        self.send_core(b).start()
        for t in range(width // tile):
            out, at = product(1, t)
            self.total[:, :, at] = out
        if self.stats:
            self.total[:, :, width:] = self.x_buf[b, 4:, :, depth:].astype(F32)

    def by_chunks(self, body):
        @pl.loop(0, self.rows // CHUNK)
        def _(r):
            body(pl.ds(pl.multiple_of(r * CHUNK, CHUNK), CHUNK))

    def stage_one(self, b):
        place, half, total, core_in = self.place, self.half, self.total, self.core_in
        self.send_core(b).wait_recv()

        def for_x(r):
            for i in range(2):
                go, stay = 2 * i + 1 - place.x, 2 * i + place.x
                self.x_out[b, i, r] = (total[go, r, :half] + core_in[b, go, r, :half].astype(F32)).astype(BF)
                self.keep_a[b, i, r] = total[stay, r, :half] + core_in[b, stay, r, :half].astype(F32)

        def for_y(r):
            for i in range(2):
                go, stay = 2 * (1 - place.y) + i, 2 * place.y + i
                self.y_out[b, i, r] = (total[go, r, half:] + core_in[b, go, r, half:].astype(F32)).astype(BF)
                self.keep_b[b, i, r] = total[stay, r, half:] + core_in[b, stay, r, half:].astype(F32)

        self.by_chunks(for_x)
        self.send_x(b).start()
        self.by_chunks(for_y)
        self.send_y(b).start()

    def stage_two(self, b):
        go_y, go_x = 1 - self.place.y, 1 - self.place.x

        def low(r):
            self.last_y_out[b, r] = (self.keep_a[b, go_y, r] + self.x_in[b, go_y, r].astype(F32)).astype(BF)

        def high(r):
            self.last_x_out[b, r] = (self.keep_b[b, go_x, r] + self.y_in[b, go_x, r].astype(F32)).astype(BF)

        self.send_x(b).wait_recv()
        self.by_chunks(low)
        self.send_last_y(b).start()
        self.send_y(b).wait_recv()
        self.by_chunks(high)
        self.send_last_x(b).start()

    def stage_three(self, b, body):
        self.send_last_y(b).wait_recv()
        self.send_last_x(b).wait_recv()
        y, x = self.place.y, self.place.x

        def end(r):
            low = self.keep_a[b, y, r] + self.x_in[b, y, r].astype(F32) + self.last_y_in[b, r].astype(F32)
            high = self.keep_b[b, x, r] + self.y_in[b, x, r].astype(F32) + self.last_x_in[b, r].astype(F32)
            result = jnp.concatenate([low, high[:, : self.half]], axis=1)
            body(r, result, high[:, self.half :] if self.stats else None)

        self.by_chunks(end)

    def drain(self, b):
        for copy in (self.send_core, self.send_x, self.send_y, self.send_last_y, self.send_last_x):
            copy(b).wait_send()


def guarded(body, b):
    @pl.when((b >= 0) & (b < PIECES))
    def _():
        body(b)


def plane_sems():
    return [pltpu.SemaphoreType.DMA((KINDS, PIECES)), pltpu.SemaphoreType.DMA((KINDS, PIECES))]


def product_scatter(left, weight, transposed, stats, epilogue, owned, outs, gathered, collective_id, fillers=()):
    tokens = left.shape[0] // 8
    rows = tokens // PIECES
    left = left.reshape(8, PIECES, rows, left.shape[1])
    scatter = Scatter(left.shape, weight.shape, transposed, stats)
    count = len(scatter.scratch())

    def kernel(*refs):
        refs = list(refs)
        left_ref, weight_ref = refs.pop(0), refs.pop(0)
        own_refs = [refs.pop(0) for _ in owned]
        extra_in = [[refs.pop(0) for _ in f.arrays] for f in fillers]
        out_refs = [refs.pop(0) for _ in outs]
        full_ref = refs.pop(0) if gathered else None
        extra_out = [refs.pop(0) for _ in fillers]
        place = Place()
        sems = (refs.pop(0), refs.pop(0))
        scatter.bind(place, sems, left_ref, weight_ref, refs[:count])
        refs = refs[count:]
        own_bufs = [refs.pop(0) for _ in owned]
        out_bufs = [refs.pop(0) for _ in outs]
        own_sem, out_sem = refs.pop(0), refs.pop(0)
        own_copies = [
            pltpu.make_async_copy(ref, buf, own_sem.at[i]) for i, (ref, buf) in enumerate(zip(own_refs, own_bufs))
        ]

        def out_copies(b):
            return [
                pltpu.make_async_copy(buf.at[b], ref.at[b], out_sem.at[i, b])
                for i, (buf, ref) in enumerate(zip(out_bufs, out_refs))
            ]

        scatter.start_loads()
        for copy in own_copies:
            copy.start()
        for f, ins, out in zip(fillers, extra_in, extra_out):
            f.bind(ins, out, refs[: len(f.scratch)])
            refs = refs[len(f.scratch) :]
            f.start()
        greet(place)
        if gathered:
            n_buf, keep_sem = refs
            gather = Gather(place, n_buf, full_ref, sems, keep_sem)

        def end(b):
            def rows_done(r, result, stat):
                written, sent = epilogue(result, stat, *[o[b, r] for o in own_bufs])
                for buf, value in zip(out_bufs, written):
                    buf[b, r] = value
                if gathered:
                    n_buf[b, r] = sent

            scatter.stage_three(b, rows_done)
            for copy in out_copies(b):
                copy.start()
            if gathered:
                gather.start(b)
        scatter.weight_copy().wait()

        @pl.loop(0, PIECES + (9 if gathered else 5))
        def _(step):
            guarded(scatter.stage_one, step - 1)
            guarded(scatter.produce, step)
            guarded(scatter.stage_two, step - 3)
            for f in fillers:
                f.step(step)

            @pl.when(step == 5)
            def _():
                for copy in own_copies:
                    copy.wait()

            guarded(end, step - 5)
            if gathered:
                guarded(gather.forward, step - 7)
                guarded(gather.forward_last, step - 9)

        @pl.loop(0, PIECES)
        def _(b):
            if gathered:
                gather.finish(b)
                gather.drain(b)
            scatter.drain(b)
            for copy in out_copies(b):
                copy.wait()

        for f in fillers:
            f.end()

    any_spec = ANY_SPEC
    out_shape = [jax.ShapeDtypeStruct((PIECES, rows, c), d) for c, d in outs]
    out_specs = [any_spec] * len(outs)
    scratch = plane_sems() + scatter.scratch()
    scratch += [pltpu.VMEM((PIECES, rows, o.shape[1]), o.dtype) for o in owned]
    scratch += [pltpu.VMEM(o.shape, o.dtype) for o in out_shape]
    scratch += [pltpu.SemaphoreType.DMA((len(owned),)), pltpu.SemaphoreType.DMA((len(outs), PIECES))]
    if gathered:
        out_shape.append(jax.ShapeDtypeStruct((8, PIECES, rows, gathered), BF))
        out_specs.append(any_spec)
    args = [left, weight] + [o.reshape(PIECES, rows, o.shape[1]) for o in owned]
    in_specs = [any_spec, any_spec] + [any_spec] * len(owned)
    for f in fillers:
        args, in_specs = args + f.arrays, in_specs + [any_spec] * len(f.arrays)
        out_shape.append(f.out_shape)
        out_specs.append(any_spec)
        scratch += f.scratch
    if gathered:
        scratch += [pltpu.VMEM((PIECES, rows, gathered), BF), pltpu.SemaphoreType.DMA((PIECES,))]
    results = pl.pallas_call(
        kernel,
        in_specs=in_specs,
        out_specs=out_specs,
        out_shape=out_shape,
        scratch_shapes=scratch,
        compiler_params=pltpu.CompilerParams(
            collective_id=collective_id, has_side_effects=True, vmem_limit_bytes=VMEM_LIMIT
        ),
        cost_estimate=pl.CostEstimate(
            flops=16 * tokens * scatter.depth * scatter.width,
            bytes_accessed=(240 if gathered else 140) * tokens * scatter.width * 2,
            transcendentals=0,
        ),
        name="product_scatter",
    )(*args)
    flat = [r.reshape(tokens, r.shape[2]) for r in results[: len(outs)]]
    if gathered:
        flat.append(results[len(outs)].reshape(8 * tokens, gathered))
    return flat + list(results[len(outs) + (1 if gathered else 0) :])


class GradProduct:
    BLOCK = 256

    def __init__(self, left, right, by_right, first):
        self.left, self.right, self.by_right, self.first = left, right, by_right, first
        whole, streamed = (left, right) if by_right else (right, left)
        self.tokens, self.blocks = left.shape[0], streamed.shape[1] // self.BLOCK
        depth, width = left.shape[1], right.shape[1]
        block = (depth, self.BLOCK) if by_right else (self.BLOCK, width)
        self.arrays = [whole, streamed]
        self.out_shape = jax.ShapeDtypeStruct((depth, width), BF)
        self.scratch = [
            pltpu.VMEM(whole.shape, BF),
            pltpu.VMEM((2, self.tokens, self.BLOCK), BF),
            pltpu.VMEM((2,) + block, BF),
            pltpu.SemaphoreType.DMA((1,)),
            pltpu.SemaphoreType.DMA((2,)),
            pltpu.SemaphoreType.DMA((2,)),
        ]

    def plain(self):
        return tn(self.left, self.right).astype(BF)

    def bind(self, ins, out, refs):
        self.whole_ref, self.streamed_ref = ins
        self.out = out
        self.w_buf, self.s_buf, self.o_buf, self.w_sem, self.s_sem, self.o_sem = refs

    def columns(self, b):
        return pl.ds(pl.multiple_of(b * self.BLOCK, self.BLOCK), self.BLOCK)

    def load(self, b):
        return pltpu.make_async_copy(self.streamed_ref.at[:, self.columns(b)], self.s_buf.at[b % 2], self.s_sem.at[b % 2])

    def store(self, b):
        to = self.out.at[:, self.columns(b)] if self.by_right else self.out.at[self.columns(b)]
        return pltpu.make_async_copy(self.o_buf.at[b % 2], to, self.o_sem.at[b % 2])

    def whole_copy(self):
        return pltpu.make_async_copy(self.whole_ref, self.w_buf, self.w_sem.at[0])

    def start(self):
        self.whole_copy().start(priority=1)
        self.load(0).start(priority=1)
        self.load(1).start(priority=1)

    def step(self, step):
        b = step - self.first

        @pl.when(b == 0)
        def _():
            self.whole_copy().wait()

        @pl.when((b >= 0) & (b < self.blocks))
        def _():
            self.load(b).wait()

            @pl.when(b >= 2)
            def _():
                self.store(b - 2).wait()

            streamed, whole = self.s_buf[b % 2], self.w_buf[...]
            product = tn(whole, streamed) if self.by_right else tn(streamed, whole)
            self.o_buf[b % 2] = product.astype(BF)
            self.store(b).start(priority=1)

        @pl.when((b >= 0) & (b + 2 < self.blocks))
        def _():
            self.load(b + 2).start(priority=1)

    def end(self):
        self.store(self.blocks - 2).wait()
        self.store(self.blocks - 1).wait()


def mixer_specs(tokens, heads, reverse):
    width, span = heads * 128, UNROLL * BLOCK
    steps = tokens // span

    def at(i):
        return steps - 1 - i if reverse else i

    return (
        steps,
        pl.BlockSpec((span, 3 * width), lambda i, *_: (at(i), 0)),
        pl.BlockSpec((1, width), lambda i, *_: (0, 0)),
        pl.BlockSpec((UNROLL, heads, 128, 128), lambda i, *_: (at(i), 0, 0, 0)),
        lambda columns: pl.BlockSpec((span, columns), lambda i, *_: (at(i), 0)),
    )


def mixer_forward(cut, n1, weight, gap, own, out_pieces, per_rank, collective_id):
    tokens, heads = n1.shape[0], gap.shape[1] // 128
    width = heads * 128
    blocks = tokens // BLOCK // lax.axis_size("seq")
    steps, qfi_spec, gap_spec, kept_spec, block = mixer_specs(tokens, heads, False)
    together = lax.axis_size("seq") == 8

    def kernel(cut_ref, n_ref, w_ref, gap_ref, *refs):
        if not together:
            return mixer_forward_kernel(heads, blocks, cut_ref, n_ref, w_ref, gap_ref, *refs)
        (own_ref, pieces_ref, mixed_ref, kept_ref, qfi_ref, full_ref, rows_ref, state, own_buf, pieces_buf, send, recv, local,
         w_send, w_recv, w_local) = refs
        place = Place()
        gather = Gather(place, own_buf, full_ref, (send, recv), local)
        loads = [
            pltpu.make_async_copy(own_ref, own_buf, local.at[0]),
            pltpu.make_async_copy(pieces_ref, pieces_buf, w_local.at[0]),
        ]

        def exchange(j):
            core = place.core
            here = pltpu.make_async_copy(
                pieces_buf.at[core * per_rank + j], rows_ref.at[j, core], w_local.at[j]
            )
            there = pltpu.make_async_remote_copy(
                src_ref=pieces_buf.at[(1 - core) * per_rank + j], dst_ref=rows_ref.at[j, core],
                send_sem=w_send.at[j], recv_sem=w_recv.at[j], device_id=place.device(0, 0, 1), device_id_type=MESH,
            )
            back = rows_ref.at[j, 1 - core]
            arrival = pltpu.make_async_remote_copy(
                src_ref=back, dst_ref=back, send_sem=w_send.at[j], recv_sem=w_recv.at[j],
                device_id=place.device(0, 0, 1), device_id_type=MESH,
            )
            return here, there, arrival

        @pl.when(pl.program_id(0) == 0)
        def _():
            for load in loads:
                load.start()
            greet(place)
            for load in loads:
                load.wait()
            pl.loop(0, EARLY)(gather.start)
            for j in range(per_rank):
                here, there, _ = exchange(j)
                here.start()
                there.start()

        @pl.when(pl.program_id(0) == steps - 1)
        def _():
            pl.loop(0, EARLY)(gather.forward_last)

        mixer_forward_kernel(
            heads, blocks, cut_ref, n_ref, w_ref, gap_ref, mixed_ref, kept_ref, qfi_ref, state
        )

        for b in range(EARLY):
            @pl.when(pl.program_id(0) == min(steps - 1, (8 + 7 * b) // 4))
            def _():
                gather.forward(b)

        @pl.when(pl.program_id(0) == steps - 1)
        def _():
            for stage in (gather.finish, gather.drain):
                pl.loop(0, EARLY)(stage)
            for j in range(per_rank):
                here, there, arrival = exchange(j)
                here.wait()
                there.wait_send()
                arrival.wait_recv()

    fixed = pl.BlockSpec(weight.shape, lambda i, *_: (0, 0), pipeline_mode=pl.Buffered(1))
    in_specs, args = [block(n1.shape[1]), fixed, gap_spec], [n1, weight, gap]
    out_specs = [block(width + EXTRA), kept_spec, qfi_spec]
    out_shape = [
        jax.ShapeDtypeStruct((tokens, width + EXTRA), BF),
        jax.ShapeDtypeStruct((tokens // BLOCK, heads, 128, 128), BF),
        jax.ShapeDtypeStruct((tokens, 3 * width), F32),
    ]
    scratch = [pltpu.VMEM((heads, 128, 128), F32)]
    params = pltpu.CompilerParams(vmem_limit_bytes=VMEM_LIMIT)
    if together:
        rows = own.shape[0] // PIECES
        own = own.reshape(PIECES, rows, own.shape[1])
        w_rows, model = out_pieces.shape[1:]
        in_specs, args = in_specs + [ANY_SPEC] * 2, args + [own, out_pieces]
        out_specs = out_specs + [ANY_SPEC] * 2
        out_shape = out_shape + [
            jax.ShapeDtypeStruct((8,) + own.shape, own.dtype),
            jax.ShapeDtypeStruct((per_rank, 2, w_rows, model), BF),
        ]
        scratch = scratch + [pltpu.VMEM(own.shape, BF), pltpu.VMEM(out_pieces.shape, BF)]
        scratch = scratch + plane_sems() + [pltpu.SemaphoreType.DMA((PIECES,))]
        scratch = scratch + [pltpu.SemaphoreType.DMA((per_rank,))] * 3
        params = pltpu.CompilerParams(
            vmem_limit_bytes=VMEM_LIMIT, collective_id=collective_id, has_side_effects=True
        )
    results = pl.pallas_call(
        kernel,
        grid_spec=pltpu.PrefetchScalarGridSpec(
            num_scalar_prefetch=1, grid=(steps,), in_specs=in_specs, out_specs=out_specs, scratch_shapes=scratch
        ),
        out_shape=out_shape,
        compiler_params=params,
        cost_estimate=pl.CostEstimate(
            flops=tokens * width * (128 * 10 + 6 * n1.shape[1]),
            bytes_accessed=60 * tokens * n1.shape[1],
            transcendentals=tokens * width * 6,
        ),
        name="mixer_forward",
    )(cut, *args)
    mixed, kept, qfi = results[:3]
    if together:
        return mixed, kept, qfi, results[3], results[4].reshape(width, model)
    return mixed, kept, qfi, lax.all_gather(own, "seq", axis=0, tiled=True), None


def mixer_backward(cut, qfi, gap, kept, grad, parts, grad_out, per_rank, collective_id):
    tokens, heads = qfi.shape[0], gap.shape[1] // 128
    width = heads * 128
    blocks = tokens // BLOCK // lax.axis_size("seq")
    steps, qfi_spec, gap_spec, kept_spec, block = mixer_specs(tokens, heads, True)
    together = lax.axis_size("seq") == 8
    planes = lax.axis_size("dp")

    def kernel(cut_ref, qfi_ref, gap_ref, kept_ref, grad_ref, *refs):
        if not together:
            return mixer_backward_kernel(heads, blocks, cut_ref, qfi_ref, gap_ref, kept_ref, grad_ref, *refs)
        (parts_ref, og_ref, out_ref, gap_out_ref, swapped_ref, sum_ref, state, parts_buf, og_buf, by_plane, landed,
         send, recv, local, c_send, c_recv, z_send, z_recv, load_sem) = refs
        place, step = Place(), pl.program_id(0)
        core = place.core
        loads = [
            pltpu.make_async_copy(parts_ref, parts_buf, load_sem.at[0]),
            pltpu.make_async_copy(og_ref, og_buf, load_sem.at[1]),
        ]

        def over_core(j):
            there = by_plane.at[core * per_rank + j]
            back = by_plane.at[(1 - core) * per_rank + j]
            return [
                pltpu.make_async_remote_copy(
                    src_ref=src, dst_ref=dst, send_sem=c_send.at[j], recv_sem=c_recv.at[j],
                    device_id=place.device(0, 0, 1), device_id_type=MESH,
                )
                for src, dst in ((og_buf.at[j, 1 - core], there), (back, back))
            ]

        def over_planes(hop):
            plane = lax.rem(place.plane + hop, planes)
            back = landed.at[planes - hop - 1]
            return [
                pltpu.make_async_remote_copy(
                    src_ref=src, dst_ref=dst, send_sem=z_send.at[hop - 1], recv_sem=z_recv.at[hop - 1],
                    device_id=(plane, place.me), device_id_type=MESH,
                )
                for src, dst in ((by_plane.at[plane], landed.at[planes - hop - 1]), (back, back))
            ]

        swaps = functools.partial(swap_pairs, place, [parts_buf], [swapped_ref], send, recv, local)

        @pl.when(step == 0)
        def _():
            for load in loads:
                load.start()
            greet_column_and_plane(place, planes)
            for load in loads:
                load.wait()
            for j in range(per_rank):
                over_core(j)[0].start()
                by_plane[core * per_rank + j] = og_buf[j, core]
            for copy, _ in swaps():
                copy.start()

        @pl.when(step == 1)
        def _():
            for j in range(per_rank):
                there, arrival = over_core(j)
                there.wait_send()
                arrival.wait_recv()
            for hop in range(1, planes):
                over_planes(hop)[0].start()

        mixer_backward_kernel(
            heads, blocks, cut_ref, qfi_ref, gap_ref, kept_ref, grad_ref, out_ref, gap_out_ref, state
        )

        @pl.when(step == steps - 1)
        def _():
            swap_waits(swaps())
            total = by_plane[place.plane].astype(F32)
            for hop in range(1, planes):
                there, arrival = over_planes(hop)
                there.wait_send()
                arrival.wait_recv()
                total += landed[planes - hop - 1].astype(F32)
            sum_ref[...] = total

    in_specs = [qfi_spec, gap_spec, kept_spec, block(width)]
    out_specs = [block(3 * width), gap_spec]
    out_shape = [jax.ShapeDtypeStruct((tokens, 3 * width), BF), jax.ShapeDtypeStruct((1, width), F32)]
    scratch = [pltpu.VMEM((heads, 128, 128), F32)]
    args = [qfi, gap, kept, grad]
    params = pltpu.CompilerParams(vmem_limit_bytes=VMEM_LIMIT)
    if together:
        rows, model = grad_out.shape[2:]
        in_specs, args = in_specs + [ANY_SPEC] * 2, args + [parts, grad_out]
        out_specs = out_specs + [ANY_SPEC, pl.BlockSpec((rows, model), lambda i, *_: (0, 0))]
        out_shape = out_shape + [
            jax.ShapeDtypeStruct(parts.shape, BF),
            jax.ShapeDtypeStruct((rows, model), F32),
        ]
        scratch = scratch + [
            pltpu.VMEM(parts.shape, BF),
            pltpu.VMEM(grad_out.shape, BF),
            pltpu.VMEM((planes, rows, model), BF),
            pltpu.VMEM((planes - 1, rows, model), BF),
            pltpu.SemaphoreType.DMA((1, 7)),
            pltpu.SemaphoreType.DMA((1, 7)),
            pltpu.SemaphoreType.DMA((1,)),
            pltpu.SemaphoreType.DMA((per_rank,)),
            pltpu.SemaphoreType.DMA((per_rank,)),
            pltpu.SemaphoreType.DMA((planes - 1,)),
            pltpu.SemaphoreType.DMA((planes - 1,)),
            pltpu.SemaphoreType.DMA((2,)),
        ]
        params = pltpu.CompilerParams(
            vmem_limit_bytes=VMEM_LIMIT, collective_id=collective_id, has_side_effects=True
        )
    return pl.pallas_call(
        kernel,
        grid_spec=pltpu.PrefetchScalarGridSpec(
            num_scalar_prefetch=1, grid=(steps,), in_specs=in_specs, out_specs=out_specs, scratch_shapes=scratch
        ),
        out_shape=out_shape,
        compiler_params=params,
        cost_estimate=pl.CostEstimate(
            flops=tokens * width * 128 * 24, bytes_accessed=tokens * width * 28, transcendentals=tokens * width * 6
        ),
        name="mixer_backward",
    )(cut, *args)


def feed_forward_kernel(units, n_ref, gu_ref, units_ref, act_ref, slope_ref, gate_w, up_w):
    @pl.when(pl.program_id(0) == 0)
    def _():
        gate_w[...] = gu_ref[:, :units]
        up_w[...] = gu_ref[:, units:]

    n = n_ref[...]
    gate, up = nn(n, gate_w[...]), nn(n, up_w[...])
    sig = jax.nn.sigmoid(gate)
    act = gate * sig
    units_ref[...] = (act * up).astype(BF)
    act_ref[...] = act.astype(BF)
    slope_ref[...] = (up * sig * (1.0 + gate * (1.0 - sig))).astype(BF)


def add_up(total, product, out_ref):
    step = pl.program_id(0)

    @pl.when(step == 0)
    def _():
        total[...] = product

    @pl.when(step > 0)
    def _():
        total[...] += product

    @pl.when(step == pl.num_programs(0) - 1)
    def _():
        out_ref[...] = total[...].astype(BF)


def feed_backward_kernel(units, g_ref, down_ref, units_ref, act_ref, slope_ref, grad_ref, down_grad_ref, total):
    grad = g_ref[...]
    d_units = nt(grad, down_ref[...])
    grad_ref[:, :units] = (d_units * slope_ref[...].astype(F32)).astype(BF)
    grad_ref[:, units:] = (d_units * act_ref[...].astype(F32)).astype(BF)
    add_up(total, tn(units_ref[...], grad), down_grad_ref)


def output_backward_kernel(model, width, d_ref, mixed_ref, out_ref, d_mixed_ref, grad_ref, total):
    d_attn = d_ref[:, :model]
    mixed = mixed_ref[:, :width]
    beta = jnp.sum(d_ref[:, model:].astype(F32), axis=1, keepdims=True)
    d_mixed_ref[...] = (nt(d_attn, out_ref[...]) - beta * mixed.astype(F32)).astype(BF)
    add_up(total, tn(mixed, d_attn), grad_ref)


def fixed_block(shape):
    return pl.BlockSpec(shape, lambda i: (0, 0), pipeline_mode=pl.Buffered(1))


def row_block(columns):
    return pl.BlockSpec((512, columns), lambda i: (i, 0))


def feed_forward(n2, gu, own, full, collective_id):
    tokens, model = n2.shape
    units = gu.shape[1] // 2
    steps = tokens // 512
    together = lax.axis_size("seq") == 8

    def kernel(n_ref, gu_ref, *refs):
        if not together:
            return feed_forward_kernel(units, n_ref, gu_ref, *refs)
        own_ref, _, units_ref, act_ref, slope_ref, full_ref, gate_w, up_w, own_buf, send, recv, local = refs
        place, step = Place(), pl.program_id(0)
        gather = Gather(place, own_buf, full_ref, (send, recv), local)

        @pl.when(step == 0)
        def _():
            load = pltpu.make_async_copy(own_ref, own_buf, local.at[0])
            load.start()
            greet(place)
            load.wait()
            pl.loop(EARLY, PIECES)(gather.start)

        @pl.when(step == min(2, steps - 1))
        def _():
            pl.loop(EARLY, PIECES)(gather.forward)

        @pl.when(step == steps - 1)
        def _():
            pl.loop(EARLY, PIECES)(gather.forward_last)

        feed_forward_kernel(units, n_ref, gu_ref, units_ref, act_ref, slope_ref, gate_w, up_w)

        @pl.when(step == steps - 1)
        def _():
            for stage in (gather.finish, gather.drain):
                pl.loop(EARLY, PIECES)(stage)

    in_specs, args = [row_block(model), fixed_block(gu.shape)], [n2, gu]
    out_specs = [row_block(units)] * 3
    out_shape = [jax.ShapeDtypeStruct((tokens, units), d) for d in (BF, BF, BF)]
    scratch = [pltpu.VMEM((model, units), BF), pltpu.VMEM((model, units), BF)]
    params, aliases = pltpu.CompilerParams(vmem_limit_bytes=VMEM_LIMIT), {}
    if together:
        own = own.reshape(PIECES, own.shape[0] // PIECES, own.shape[1])
        in_specs, args = in_specs + [ANY_SPEC] * 2, args + [own, full]
        out_specs = out_specs + [ANY_SPEC]
        out_shape = out_shape + [jax.ShapeDtypeStruct(full.shape, full.dtype)]
        scratch = scratch + [pltpu.VMEM(own.shape, BF)] + plane_sems() + [pltpu.SemaphoreType.DMA((PIECES,))]
        params = pltpu.CompilerParams(
            vmem_limit_bytes=VMEM_LIMIT, collective_id=collective_id, has_side_effects=True
        )
        aliases = {3: 3}
    results = pl.pallas_call(
        kernel,
        grid=(steps,),
        in_specs=in_specs,
        out_specs=out_specs,
        out_shape=out_shape,
        scratch_shapes=scratch,
        compiler_params=params,
        input_output_aliases=aliases,
        cost_estimate=pl.CostEstimate(
            flops=4 * tokens * model * units, bytes_accessed=4 * tokens * model, transcendentals=tokens * units
        ),
        name="feed_forward",
    )(*args)
    if together:
        return results[0], results[1], results[2], results[3].reshape(tokens, model)
    return results[0], results[1], results[2], full


def feed_backward(grad, down, hidden_units, act, slope):
    tokens, model = grad.shape
    units = down.shape[0]
    return pl.pallas_call(
        functools.partial(feed_backward_kernel, units),
        grid=(tokens // 512,),
        in_specs=[row_block(model), fixed_block(down.shape)] + [row_block(units)] * 3,
        out_specs=[row_block(2 * units), fixed_block(down.shape)],
        out_shape=[jax.ShapeDtypeStruct((tokens, 2 * units), BF), jax.ShapeDtypeStruct(down.shape, BF)],
        scratch_shapes=[pltpu.VMEM(down.shape, F32)],
        compiler_params=pltpu.CompilerParams(vmem_limit_bytes=VMEM_LIMIT),
        cost_estimate=pl.CostEstimate(
            flops=4 * tokens * model * units, bytes_accessed=8 * tokens * model, transcendentals=0
        ),
        name="feed_backward",
    )(grad, down, hidden_units, act, slope)


def output_backward(d_attn, mixed, weight):
    tokens, (width, model) = mixed.shape[0], weight.shape
    return pl.pallas_call(
        functools.partial(output_backward_kernel, model, width),
        grid=(tokens // 512,),
        in_specs=[row_block(d_attn.shape[1]), row_block(mixed.shape[1]), fixed_block(weight.shape)],
        out_specs=[row_block(width), fixed_block(weight.shape)],
        out_shape=[jax.ShapeDtypeStruct((tokens, width), BF), jax.ShapeDtypeStruct(weight.shape, BF)],
        scratch_shapes=[pltpu.VMEM(weight.shape, F32)],
        compiler_params=pltpu.CompilerParams(vmem_limit_bytes=VMEM_LIMIT),
        cost_estimate=pl.CostEstimate(
            flops=4 * tokens * model * width, bytes_accessed=3 * tokens * model, transcendentals=0
        ),
        name="output_backward",
    )(d_attn, mixed, weight)


def gather_dp(v):
    return lax.all_gather(v, "dp", axis=0, tiled=True)


def scatter_dp(v):
    return lax.psum_scatter(v, "dp", scatter_dimension=0, tiled=True)


def swap_seq(v):
    return lax.all_to_all(v, "seq", split_axis=0, concat_axis=0, tiled=True)


def product_all(left, weight, transposed, stats, epilogue, owned, outs, gathered, collective_id, fillers=()):
    if lax.axis_size("seq") == 8:
        return product_scatter(left, weight, transposed, stats, epilogue, owned, outs, gathered, collective_id, fillers)
    depth = left.shape[1] - (EXTRA if stats else 0)
    product = (nt if transposed else nn)(left[:, :depth], weight).astype(BF)
    result = lax.psum_scatter(product, "seq", scatter_dimension=0, tiled=True).astype(F32)
    stat = None
    if stats:
        stat = lax.psum_scatter(left[:, depth:].astype(F32), "seq", scatter_dimension=0, tiled=True)
    written, sent = epilogue(result, stat, *owned)
    written = [w.astype(d) for w, (_, d) in zip(written, outs)]
    written += [lax.all_gather(sent, "seq", axis=0, tiled=True)] if gathered else []
    return written + [f.plain() for f in fillers]


def split_lanes(v):
    lane = lax.broadcasted_iota(jnp.int32, (v.shape[0], EXTRA), 1)
    high = v.astype(BF).astype(F32)
    return jnp.where(lane == 0, high, jnp.where(lane == 1, v - high, 0.0)).astype(BF)


def on_device(
    hidden,
    seg_ids,
    pad_mask,
    attn_gain,
    gate_gap,
    out_gain,
    w_query,
    w_forget,
    w_input,
    w_output,
    ffn_gain,
    w_gate,
    w_up,
    w_down,
    out_grad,
):
    planes, ranks = lax.axis_size("dp"), lax.axis_size("seq")
    row_tokens, model = hidden.shape[1:]
    rows = w_query.shape[0]
    units_in = w_down.shape[0]
    head = model // HEADS
    span = head // rows
    per_rank, groups = planes // span, ranks // span
    channels = per_rank * head
    units = planes * units_in
    tokens = ranks * row_tokens
    members = [[a * span + m for m in range(span)] for a in range(groups)]

    def to_heads(w):
        parts = w.reshape(rows, span, per_rank, groups, head)
        return parts.transpose(3, 1, 0, 2, 4).reshape(ranks, rows, channels)

    def from_heads(parts):
        parts = parts.reshape(groups, span, rows, per_rank, head)
        return parts.transpose(2, 1, 3, 0, 4).reshape(rows, model)

    def to_units(w):
        parts = w.reshape(rows, planes, ranks, units_in)
        return parts.transpose(2, 0, 1, 3).reshape(ranks, rows, units)

    def from_units(parts):
        parts = parts.reshape(ranks, rows, planes, units_in)
        return parts.transpose(1, 2, 0, 3).reshape(rows, planes * ranks * units_in)

    def own_rows(v):
        return v.reshape((span, per_rank) + v.shape[1:])

    def swap_group(v):
        return lax.all_to_all(v, "seq", split_axis=0, concat_axis=0, axis_index_groups=members)

    gain_a, gain_o, gain_f = (g.astype(F32)[:, None] for g in (attn_gain, out_gain, ffn_gain))

    plain = ranks != 8

    def order(first, *rest):
        return lax.optimization_barrier((first,) + rest)

    x16 = hidden[0]
    ids = jnp.concatenate([seg_ids, pad_mask], axis=0)
    mixer_weights = (w_query, w_forget, w_input)
    out_pieces = lax.all_gather(fold(gain_o, w_output), "dp", axis=0)
    if plain:
        qfi_part = jnp.concatenate([to_heads(fold(gain_a, w)) for w in mixer_weights], axis=2)
        qfi_full = gather_dp(swap_seq(qfi_part).reshape(ranks * rows, 3 * channels))
        gu_part = jnp.concatenate([to_units(fold(gain_f, w)) for w in (w_gate, w_up)], axis=2)
        gu_swapped = swap_seq(gu_part)
        x = x16.astype(F32)
        normed = (x * inverse_rms(row_mean(x * x))).astype(BF)
        n1 = lax.all_gather(normed, "seq", axis=0, tiled=True)
        gap_pieces = lax.all_gather(gate_gap, "dp", axis=0)
        gap_own = swap_group(own_rows(gap_pieces)).transpose(1, 0, 2).reshape(1, channels).astype(F32)
        ids = lax.all_gather(ids, "seq", axis=0)
        segment = ids[:, 0].reshape(tokens // BLOCK, BLOCK)
        live = jnp.sum(ids[:, 1]).reshape(1)
        ends = segment[:, -1]
        before = jnp.concatenate([segment[:1, 0], ends[:-1]])
        cut = jnp.sum((segment == before[:, None]).astype(jnp.int32), axis=1).reshape(ranks, -1)
        cut = jnp.concatenate([cut, jnp.broadcast_to(live, (ranks, 1))], axis=1)
        cut = jnp.pad(cut, ((0, 0), (0, EXTRA - cut.shape[1])))
    else:
        wide = -(-row_tokens // 128) * 128
        ids = jnp.pad(ids, ((0, 6), (0, wide - row_tokens)))
        gap_tile = jnp.pad(gate_gap[None], ((0, 15), (0, 128 - rows)))
        qfi_full, n1, gu_swapped, cut, gap_own = enter_plane(
            mixer_weights, gain_a, x16, (w_gate, w_up), gain_f, ids, gap_tile, per_rank, groups, planes, 1
        )
    gu_full = gather_dp(gu_swapped.reshape(ranks * rows, 2 * units))

    og16 = out_grad[0]
    mixed, kept, qfi, grad_all, out_own = mixer_forward(
        cut, n1, qfi_full, gap_own, og16, out_pieces, per_rank, 3
    )
    if plain:
        out_own = swap_group(own_rows(out_pieces)).transpose(1, 0, 2, 3).reshape(channels, model)

    def after_output(result, stat, x16):
        x = x16.astype(F32)
        factor_o = inverse_rms(jnp.sum(stat, axis=1, keepdims=True) / model)
        middle = x + factor_o * result
        normed = middle * inverse_rms(row_mean(middle * middle))
        return [middle, jnp.broadcast_to(factor_o, (x.shape[0], EXTRA))], normed.astype(BF)

    mixed, w_down_late = order(mixed, w_down)
    down_own = gather_dp(w_down_late)
    middle, factor_o, n2 = product_all(
        mixed, out_own, False, True, after_output, [x16], [(model, F32), (EXTRA, F32)], model, 4
    )
    hidden_units, act, slope, grad_all = feed_forward(n2, gu_full, og16, grad_all, 10)
    def after_down(result, stat, middle):
        return [(middle + result).astype(BF)], None

    d_gu, grad_down = feed_backward(grad_all, down_own, hidden_units, act, slope)
    down_sum = scatter_dp(grad_down)
    block_out, grad_gu = product_all(
        hidden_units, down_own, False, False, after_down, [middle], [(model, BF)], 0, 6,
        (GradProduct(n2, d_gu, False, 0),),
    )
    gu_sum = scatter_dp(grad_gu)
    d_gu, grad_gu = order(d_gu, grad_gu)

    def after_ffn(result, stat, middle, og16, x16, factor_o):
        factor_o = factor_o[:, :1]
        factor_m = inverse_rms(row_mean(middle * middle))
        normed = middle * factor_m
        d_middle = og16.astype(F32) + factor_m * (result - normed * row_mean(result * normed))
        mean_o = row_mean(d_middle * (middle - x16.astype(F32)))
        beta = split_lanes(factor_o * factor_o * mean_o)
        return [d_middle], jnp.concatenate([(factor_o * d_middle).astype(BF), beta], axis=1)

    d_middle, d_attn = product_all(
        d_gu, gu_full, True, False, after_ffn, [middle, og16, x16, factor_o], [(model, F32)], model + EXTRA, 5
    )
    d_attn, down_sum = order(d_attn, down_sum)
    d_mixed, grad_out = output_backward(d_attn, mixed, out_own)
    grad_out, d_mixed = order(grad_out, d_mixed)
    if plain:
        d_qfi, gap_grad = mixer_backward(cut, qfi, gap_own, kept, d_mixed, None, None, per_rank, 6)
        out_back = grad_out.reshape(per_rank, span, rows, model).transpose(1, 0, 2, 3)
        out_rows = scatter_dp(swap_group(out_back).reshape(planes * rows, model)).astype(F32)
        gu_rows = swap_seq(gu_sum).reshape(ranks, rows, 2 * units)
    else:
        d_qfi, gap_grad, gu_rows, out_rows = mixer_backward(
            cut, qfi, gap_own, kept, d_mixed, gu_sum.reshape(ranks, rows, 2 * units),
            grad_out.reshape(per_rank, span, rows, model), per_rank, 9,
        )
    grad_qfi = tn(n1, d_qfi).astype(BF)
    grad_qfi, d_qfi = order(grad_qfi, d_qfi)
    qfi_sum = scatter_dp(grad_qfi)

    def after_mixer(result, stat, x16, d_middle):
        x = x16.astype(F32)
        factor_x = inverse_rms(row_mean(x * x))
        normed = x * factor_x
        return [(d_middle + factor_x * (result - normed * row_mean(result * normed))).astype(BF)], None

    (hidden_grad,) = product_all(d_qfi, qfi_full, True, False, after_mixer, [x16, d_middle], [(model, BF)], 0, 7)

    hidden_grad, gu_rows, down_sum, out_rows, gap_grad = order(hidden_grad, gu_rows, down_sum, out_rows, gap_grad)

    def rowdot(w, g):
        return jnp.sum(w.astype(F32) * g, axis=1)

    g_out_gain = rowdot(w_output, out_rows)
    if plain:
        gu_rows = gu_rows.astype(F32)
        gate_rows, up_rows = from_units(gu_rows[:, :, :units]), from_units(gu_rows[:, :, units:])
        g_ffn_gain = rowdot(w_gate, gate_rows) + rowdot(w_up, up_rows)
        g_gate, g_up = gain_f * gate_rows, gain_f * up_rows
        gap_back = swap_group(gap_grad.reshape(per_rank, span, rows).transpose(1, 0, 2)).reshape(planes * rows)
        g_gap = scatter_dp(gap_back)
        qfi_rows = swap_seq(qfi_sum).reshape(ranks, rows, 3 * channels).astype(F32)
        parts = [from_heads(qfi_rows[:, :, j * channels : (j + 1) * channels]) for j in range(3)]
        g_attn_gain = sum(rowdot(w, g) for w, g in zip(mixer_weights, parts))
        g_query, g_forget, g_input = [gain_a * g for g in parts]
    else:
        (g_gate, g_up), g_ffn_gain = finish((w_gate, w_up), gain_f, gu_rows, unit_moves(units, planes, ranks))
        gap_tile = jnp.broadcast_to(gap_grad, (8, channels))
        qfi_rows, gap_all = exit_plane(qfi_sum.reshape(ranks, rows, 3 * channels), gap_tile, planes, 8)
        (g_query, g_forget, g_input), g_attn_gain = finish(
            mixer_weights, gain_a, qfi_rows, head_moves(head, per_rank, groups, span)
        )
        plane, me = lax.axis_index("dp"), lax.axis_index("seq")
        at = lax.rem(plane, per_rank) * head + lax.rem(me, 2) * rows
        from_core = jnp.sum(gap_all[:, :, 0], axis=0)
        g_gap = lax.dynamic_slice(from_core, (plane // per_rank, at), (1, rows))[0]
    return (
        block_out[None],
        hidden_grad[None],
        g_attn_gain,
        g_gap,
        g_out_gain,
        g_query,
        g_forget,
        g_input,
        gain_o * out_rows,
        g_ffn_gain,
        g_gate,
        g_up,
        down_sum.astype(F32),
    )


def solution(mesh):
    tok, row, both = P("dp", "seq", None), P("dp", "seq"), P(("dp", "seq"))
    mat = P(("dp", "seq"), None)
    return jax.shard_map(
        on_device,
        mesh=mesh,
        in_specs=(tok, row, row, both, both, both, mat, mat, mat, mat, both, mat, mat, mat, tok),
        out_specs=(tok, tok, both, both, both, mat, mat, mat, mat, both, mat, mat, mat),
        check_vma=False,
    )
```

```python
import functools

import jax
import jax.numpy as jnp
from jax import lax
from jax.experimental import pallas as pl
from jax.experimental.pallas import tpu as pltpu
from jax.sharding import PartitionSpec as P

HEADS = 16
BLOCK = 64
UNROLL = 4
EPSILON = 1e-06
EXTRA = 128
BF = jnp.bfloat16
F32 = jnp.float32


def dot(a, b, dims):
    return lax.dot_general(a, b, (dims, ((), ())), preferred_element_type=F32)


def nn(a, b):
    return dot(a, b, ((1,), (0,)))


def nt(a, b):
    return dot(a, b, ((1,), (1,)))


def tn(a, b):
    return dot(a, b, ((0,), (0,)))


def inverse_rms(square_mean):
    return lax.rsqrt(square_mean + EPSILON)


def row_mean(v):
    return jnp.mean(v, axis=1, keepdims=True)


def split_sum(tri, v):
    high = v.astype(BF)
    low = (v - high.astype(F32)).astype(BF)
    return nn(tri, high) + nn(tri, low)


def chunk_prep(qfi, gap, live, width):
    query_pre, forget_pre, input_pre = (
        qfi[:, :width],
        qfi[:, width : 2 * width],
        qfi[:, 2 * width :],
    )
    sig_q = jax.nn.sigmoid(query_pre)
    sig_nf = jax.nn.sigmoid(-forget_pre)
    key = gap * sig_nf
    return query_pre, sig_q, sig_nf, key, input_pre * live


def triangle(lower):
    row = lax.broadcasted_iota(jnp.int32, (BLOCK, BLOCK), 0)
    col = lax.broadcasted_iota(jnp.int32, (BLOCK, BLOCK), 1)
    return (row >= col) if lower else (row <= col)


def chunk_masks(cut):
    row = lax.broadcasted_iota(jnp.int32, (BLOCK, BLOCK), 0)
    col = lax.broadcasted_iota(jnp.int32, (BLOCK, BLOCK), 1)
    allowed = (row >= col) & ((row >= cut) == (col >= cut))
    at = lax.broadcasted_iota(jnp.int32, (BLOCK, 1), 0)
    inherits = (at < cut).astype(F32)
    tail = ((at >= cut) | (cut >= BLOCK)).astype(F32)
    whole = (cut >= BLOCK).astype(F32)
    return allowed, inherits, tail, whole


def mixer_forward_kernel(heads, blocks, cut_ref, n_ref, w_ref, gap_ref, mixed_ref, kept_ref, qfi_ref, state):
    step = pl.program_id(0)
    width = heads * 128

    @pl.when(step == 0)
    def _():
        state[...] = jnp.zeros_like(state)

    qfi_ref[...] = nn(n_ref[...], w_ref[...])
    lower = triangle(True).astype(BF)
    for u in range(UNROLL):
        chunk = step * UNROLL + u
        rows = slice(u * BLOCK, (u + 1) * BLOCK)
        at = lax.broadcasted_iota(jnp.int32, (BLOCK, 1), 0) + chunk * BLOCK
        live = (at < cut_ref[0, blocks]).astype(F32)
        query_pre, sig_q, sig_nf, key, value = chunk_prep(qfi_ref[rows, :], gap_ref[...], live, width)
        query = query_pre * sig_q
        total = split_sum(lower, jnp.log1p(-key))
        centre = total[BLOCK // 2 : BLOCK // 2 + 1]
        ending = total[BLOCK - 1 :]
        scaled_q = (query * jnp.exp(total - centre)).astype(BF)
        scaled_k = (key * jnp.exp(centre - total)).astype(BF)
        value_low = value.astype(BF)
        allowed, inherits, tail, whole = chunk_masks(cut_ref[chunk // blocks, lax.rem(chunk, blocks)])
        value_tail = (value * tail).astype(BF)
        e_centre = jnp.exp(centre)
        e_rest = jnp.exp(ending - centre)
        e_all = jnp.exp(ending) * whole
        square = jnp.zeros((BLOCK, 1), F32)
        for h in range(heads):
            cols = slice(h * 128, (h + 1) * 128)
            before = state[h]
            kept_ref[u, h] = before.astype(BF)
            scores = jnp.where(allowed, nt(scaled_q[:, cols], scaled_k[:, cols]), 0.0)
            inner = nn(scores.astype(BF), value_low[:, cols])
            outer = nt(scaled_q[:, cols], (before * e_centre[:, cols]).astype(BF))
            mixed = inner + outer * inherits
            square = square + jnp.sum(mixed * mixed, axis=1, keepdims=True)
            mixed_ref[rows, cols] = mixed.astype(BF)
            state[h] = before * e_all[:, cols] + tn(value_tail[:, cols], scaled_k[:, cols]) * e_rest[:, cols]
        lane = lax.broadcasted_iota(jnp.int32, (BLOCK, EXTRA), 1)
        high = square.astype(BF).astype(F32)
        mixed_ref[rows, width:] = jnp.where(lane == 0, high, jnp.where(lane == 1, square - high, 0.0)).astype(BF)


def mixer_backward_kernel(heads, blocks, cut_ref, qfi_ref, gap_ref, kept_ref, grad_ref, out_ref, gap_out_ref, state):
    step = pl.program_id(0)
    last = pl.num_programs(0) - 1
    width = heads * 128

    @pl.when(step == 0)
    def _():
        state[...] = jnp.zeros_like(state)
        gap_out_ref[...] = jnp.zeros_like(gap_out_ref)

    lower = triangle(True).astype(BF)
    upper = triangle(False).astype(BF)
    for u in reversed(range(UNROLL)):
        chunk = (last - step) * UNROLL + u
        rows = slice(u * BLOCK, (u + 1) * BLOCK)
        at = lax.broadcasted_iota(jnp.int32, (BLOCK, 1), 0) + chunk * BLOCK
        live = (at < cut_ref[0, blocks]).astype(F32)
        gap = gap_ref[...]
        query_pre, sig_q, sig_nf, key, value = chunk_prep(qfi_ref[rows, :], gap, live, width)
        query = query_pre * sig_q
        total = split_sum(lower, jnp.log1p(-key))
        centre = total[BLOCK // 2 : BLOCK // 2 + 1]
        ending = total[BLOCK - 1 :]
        e_q = jnp.exp(total - centre)
        e_k = jnp.exp(centre - total)
        scaled_q = (query * e_q).astype(BF)
        scaled_k = (key * e_k).astype(BF)
        value_low = value.astype(BF)
        allowed, inherits, tail, whole = chunk_masks(cut_ref[chunk // blocks, lax.rem(chunk, blocks)])
        value_tail = (value * tail).astype(BF)
        grad = grad_ref[rows, :]
        grad_in = (grad.astype(F32) * inherits).astype(BF)
        e_centre = jnp.exp(centre)
        e_rest = jnp.exp(ending - centre)
        e_all = jnp.exp(ending) * whole
        d_query, d_key, d_value, d_total, d_end = [], [], [], [], []
        for h in range(heads):
            cols = slice(h * 128, (h + 1) * 128)
            before = kept_ref[u, h].astype(F32)
            after = state[h]
            q, k, v, g, gi = scaled_q[:, cols], scaled_k[:, cols], value_low[:, cols], grad[:, cols], grad_in[:, cols]
            vt = value_tail[:, cols]
            scores = jnp.where(allowed, nt(q, k), 0.0).astype(BF)
            d_scores = jnp.where(allowed, nt(g, v), 0.0).astype(BF)
            shifted = (before * e_centre[:, cols]).astype(BF)
            onward = (after * e_rest[:, cols]).astype(BF)
            dq = nn(d_scores, k) + nn(gi, shifted)
            dk_state = nn(vt, onward)
            dk = tn(d_scores, q) + dk_state
            dv = tn(scores, g) + nt(k, onward) * tail
            k32 = k.astype(F32)
            d_total.append(dq * q.astype(F32) - dk * k32)
            d_end.append(
                jnp.sum(after * before, axis=0, keepdims=True) * e_all[:, cols]
                + jnp.sum(dk_state * k32, axis=0, keepdims=True)
            )
            state[h] = after * e_all[:, cols] + tn(gi, q) * e_centre[:, cols]
            d_query.append(dq)
            d_key.append(dk)
            d_value.append(dv)
        d_query = jnp.concatenate(d_query, axis=1) * e_q
        d_key = jnp.concatenate(d_key, axis=1) * e_k
        d_value = jnp.concatenate(d_value, axis=1) * live
        d_log = split_sum(upper, jnp.concatenate(d_total, axis=1)) + jnp.concatenate(d_end, axis=1)
        d_key = d_key - d_log / (1.0 - key)
        gap_out_ref[...] += jnp.sum(d_key * sig_nf, axis=0, keepdims=True)
        out_ref[rows, :width] = (d_query * sig_q * (1.0 + query_pre * (1.0 - sig_q))).astype(BF)
        out_ref[rows, width : 2 * width] = (-d_key * key * (1.0 - sig_nf)).astype(BF)
        out_ref[rows, 2 * width :] = d_value.astype(BF)


MESH = pl.DeviceIdType.MESH
PIECES = 5
EARLY = 4
TILE = 1024
CHUNK = 32
VMEM_LIMIT = 60 * 1024 * 1024
(S_X, S_Y, S_CORE, S_DIAG_Y, S_DIAG_X, S_CORE_X, S_CORE_Y, S_CORE_D, R_CORE, R_X, R_Y, R_LAST_Y, R_LAST_X, KINDS) = range(14)


class Place:
    def __init__(self):
        self.plane = lax.axis_index("dp")
        me = lax.axis_index("seq")
        self.me = me
        self.core = me % 2
        self.x = (me // 2) % 2
        self.y = me // 4

    def rank(self, fy=0, fx=0, fc=0):
        y = 1 - self.y if fy else self.y
        x = 1 - self.x if fx else self.x
        core = 1 - self.core if fc else self.core
        return 4 * y + 2 * x + core

    def device(self, fy=0, fx=0, fc=0):
        return (self.plane, self.rank(fy, fx, fc))


def greet(place):
    barrier = pltpu.get_barrier_semaphore()
    for flip in ((0, 0, 1), (0, 1, 0), (1, 0, 0)):
        pl.semaphore_signal(barrier, inc=1, device_id=place.device(*flip), device_id_type=MESH)
    pl.semaphore_wait(barrier, 3)


def remote(src, dst, sems, kind, b, device):
    send, recv = sems
    return pltpu.make_async_remote_copy(
        src_ref=src,
        dst_ref=dst,
        send_sem=send.at[kind, b],
        recv_sem=recv.at[kind, b],
        device_id=device,
        device_id_type=MESH,
    )


class Gather:
    def __init__(self, place, own, full, sems, local_sem):
        self.p, self.own, self.full, self.sems, self.local = place, own, full, sems, local_sem
        self.half = full.shape[2] // 2

    def keep(self, b):
        return pltpu.make_async_copy(self.own.at[b], self.full.at[self.p.me, b], self.local.at[b])

    def first(self, b):
        p, dst = self.p, self.full.at[self.p.me, b]
        return [
            remote(self.own.at[b], dst, self.sems, S_X, b, p.device(0, 1, 0)),
            remote(self.own.at[b], dst, self.sems, S_Y, b, p.device(1, 0, 0)),
            remote(self.own.at[b], dst, self.sems, S_CORE, b, p.device(0, 0, 1)),
        ]

    def second(self, b):
        p, h = self.p, self.half
        from_x, from_y = self.full.at[p.rank(0, 1, 0), b], self.full.at[p.rank(1, 0, 0), b]
        up, down = from_x.at[pl.ds(0, h)], from_y.at[pl.ds(h, h)]
        return [
            remote(up, up, self.sems, S_DIAG_Y, b, p.device(1, 0, 0)),
            remote(down, down, self.sems, S_DIAG_X, b, p.device(0, 1, 0)),
            remote(from_x, from_x, self.sems, S_CORE_X, b, p.device(0, 0, 1)),
            remote(from_y, from_y, self.sems, S_CORE_Y, b, p.device(0, 0, 1)),
        ]

    def third(self, b):
        p = self.p
        block = self.full.at[p.rank(1, 1, 0), b]
        return [remote(block, block, self.sems, S_CORE_D, b, p.device(0, 0, 1))]

    def arrived(self, kind, b, flips, rows=None):
        block = self.full.at[self.p.rank(*flips), b]
        if rows is not None:
            block = block.at[pl.ds(rows * self.half, self.half)]
        remote(block, block, self.sems, kind, b, self.p.device(0, 0, 1)).wait_recv()

    def start(self, b):
        self.keep(b).start()
        for copy in self.first(b):
            copy.start()

    def forward(self, b):
        self.arrived(S_X, b, (0, 1, 0))
        self.arrived(S_Y, b, (1, 0, 0))
        for copy in self.second(b):
            copy.start()

    def forward_last(self, b):
        self.arrived(S_DIAG_Y, b, (1, 1, 0), 0)
        self.arrived(S_DIAG_X, b, (1, 1, 0), 1)
        for copy in self.third(b):
            copy.start()

    def finish(self, b):
        self.arrived(S_CORE, b, (0, 0, 1))
        self.arrived(S_CORE_X, b, (0, 1, 1))
        self.arrived(S_CORE_Y, b, (1, 0, 1))
        self.arrived(S_CORE_D, b, (1, 1, 1))

    def drain(self, b):
        self.keep(b).wait()
        for copy in self.first(b) + self.second(b) + self.third(b):
            copy.wait_send()


def swap_pairs(place, parts, outs, send, recv, local):
    pairs = []
    for i, (part, out) in enumerate(zip(parts, outs)):
        pairs.append((pltpu.make_async_copy(part.at[place.me], out.at[place.me], local.at[i]), None))
        for k, flips in enumerate(FLIPS):
            there = out.at[place.rank(*flips)]
            pairs.append(tuple(
                pltpu.make_async_remote_copy(
                    src_ref=src, dst_ref=dst, send_sem=send.at[i, k], recv_sem=recv.at[i, k],
                    device_id=place.device(*flips), device_id_type=MESH,
                )
                for src, dst in ((part.at[place.rank(*flips)], out.at[place.me]), (there, there))
            ))
    return pairs


def swap_starts(place, parts, outs, send, recv, local):
    pairs = swap_pairs(place, parts, outs, send, recv, local)
    for copy, _ in pairs:
        copy.start()
    return pairs


def swap_waits(pairs):
    for copy, arrival in pairs:
        if arrival is None:
            copy.wait()
        else:
            copy.wait_send()
            arrival.wait_recv()


def greet_all(place):
    barrier = pltpu.get_barrier_semaphore()
    for flips in ((0, 0, 1), (0, 1, 0), (1, 0, 0), (0, 1, 1), (1, 0, 1), (1, 1, 0), (1, 1, 1)):
        pl.semaphore_signal(barrier, inc=1, device_id=place.device(*flips), device_id_type=MESH)
    pl.semaphore_wait(barrier, 7)


def fold(gain, w):
    return (gain * w.astype(F32)).astype(BF)


FLIPS = ((0, 0, 1), (0, 1, 0), (1, 0, 0), (0, 1, 1), (1, 0, 1), (1, 1, 0), (1, 1, 1))
ANY_SPEC = pl.BlockSpec(memory_space=pl.ANY)
VMEM_SPEC = pl.BlockSpec(memory_space=pltpu.VMEM)


def column_peers(place, planes):
    peers = []
    for hop in range(planes):
        for flip in (0, 1):
            if hop or flip:
                plane = lax.rem(place.plane + hop, planes)
                peers.append((plane, place.rank(0, 0, flip)))
    return peers


def column_spread(place, planes, src, dst, send, recv):
    waits = []
    for k, (plane, rank) in enumerate(column_peers(place, planes)):
        mine = dst.at[place.plane, place.core]
        copy = pltpu.make_async_remote_copy(
            src_ref=src, dst_ref=mine, send_sem=send.at[k], recv_sem=recv.at[k],
            device_id=(plane, rank), device_id_type=MESH,
        )
        copy.start()
        back = lax.rem(planes + 2 * place.plane - plane, planes)
        there = dst.at[back, lax.rem(rank, 2)]
        waits.append((copy, pltpu.make_async_remote_copy(
            src_ref=there, dst_ref=there, send_sem=send.at[k], recv_sem=recv.at[k],
            device_id=(plane, rank), device_id_type=MESH,
        )))
    return waits


def greet_column_and_plane(place, planes):
    barrier = pltpu.get_barrier_semaphore()
    devices = [place.device(*flips) for flips in FLIPS]
    devices += [p for p in column_peers(place, planes)[1:]]
    for device in devices:
        pl.semaphore_signal(barrier, inc=1, device_id=device, device_id_type=MESH)
    pl.semaphore_wait(barrier, len(devices))


class Line:
    def __init__(self, place, planes, full, sems):
        self.p, self.planes, self.full, self.sems = place, planes, full, sems

    def copy(self, way, plane, to, hop):
        send, recv = self.sems
        block = self.full.at[plane]
        return pltpu.make_async_remote_copy(
            src_ref=block, dst_ref=block, send_sem=send.at[way, hop], recv_sem=recv.at[way, hop],
            device_id=(to, self.p.me), device_id_type=MESH,
        )

    def each(self, hop, arriving, body):
        plane, last = self.p.plane, self.planes - 1
        if arriving:
            conditions = (plane - hop >= 0, plane + hop <= last)
        else:
            conditions = ((plane - hop >= 0) & (plane + 1 <= last), (plane + hop <= last) & (plane >= 1))
        for way, condition in enumerate(conditions):
            @pl.when(condition)
            def _():
                block = plane - hop if way == 0 else plane + hop
                to = lax.rem(plane + (1 if way == 0 else last), self.planes)
                body(self.copy(way, block, to, hop - 1 if arriving else hop))

    def start(self, hop):
        self.each(hop, False, lambda copy: copy.start())

    def arrive(self, hop):
        self.each(hop, True, lambda copy: copy.wait_recv())

    def drain(self):
        for hop in range(self.planes - 1):
            self.each(hop, False, lambda copy: copy.wait_send())


def enter_plane(weights, gain, x, unit_weights, unit_gain, ids, gap, per_rank, groups, planes, collective_id):
    rows, model = weights[0].shape
    head = model // (8 * per_rank)
    channels = per_rank * head
    span = 8 // groups
    tokens = x.shape[0]
    x_rows = tokens // PIECES
    every_unit = unit_weights[0].shape[1]
    units_in = every_unit // (8 * planes)
    units = units_in * planes
    x = x.reshape(PIECES, x_rows, model)
    blocks = tokens // BLOCK

    def kernel(q_ref, f_ref, i_ref, gain_ref, x_ref, gate_ref, up_ref, unit_gain_ref, ids_ref, gap_ref,
               qfi_out, full, unit_out, cut_out, gap_out,
               part, normed, unit_part, ids_in, gap_in, *sems):
        (swap_send, swap_recv, swap_local, send, recv, local, gap_send, gap_recv, z_send, z_recv) = sems
        place = Place()
        scale = gain_ref[...]
        for w, ref in enumerate((q_ref, f_ref, i_ref)):
            for rank, source, target in ((r, t, c) for v, r, c, t in head_moves(head, per_rank, groups, span) if v == w):
                part[rank, :, target] = fold(scale, ref[:, source])
        greet_column_and_plane(place, planes)
        first = swap_starts(
            place, [part], [qfi_out.at[place.plane]],
            swap_send.at[pl.ds(0, 1)], swap_recv.at[pl.ds(0, 1)], swap_local.at[pl.ds(0, 1)],
        )
        gaps = column_spread(place, planes, gap_ref, gap_in, gap_send, gap_recv)
        gap_in[place.plane, place.core] = gap_ref[...]
        ids_in[place.me] = ids_ref[...]
        id_pairs = []
        for k, flips in enumerate(FLIPS):
            there = ids_in.at[place.rank(*flips)]
            id_pairs.append(tuple(
                pltpu.make_async_remote_copy(
                    src_ref=src, dst_ref=dst, send_sem=swap_send.at[1, k], recv_sem=swap_recv.at[1, k],
                    device_id=place.device(*flips), device_id_type=MESH,
                )
                for src, dst in ((ids_ref, ids_in.at[place.me]), (there, there))
            ))
            id_pairs[-1][0].start()

        gather = Gather(place, normed, full, (send, recv), local)

        @pl.loop(0, PIECES)
        def _(b):
            value = x_ref[b].astype(F32)
            normed[b] = (value * inverse_rms(row_mean(value * value))).astype(BF)
            gather.start(b)

        line = Line(place, planes, qfi_out, (z_send, z_recv))
        swap_waits(first)
        line.start(0)
        unit_scale = unit_gain_ref[...]
        for side, ref in enumerate((gate_ref, up_ref)):
            for _, rank, target, source in (move for move in unit_moves(units, planes, 8) if move[0] == side):
                unit_part[rank, :, target] = fold(unit_scale, ref[:, source])
        unit_copies = swap_starts(
            place, [unit_part], [unit_out],
            swap_send.at[pl.ds(2, 1)], swap_recv.at[pl.ds(2, 1)], swap_local.at[pl.ds(1, 1)],
        )
        for copy, arrival in id_pairs + gaps:
            copy.wait_send()
            arrival.wait_recv()
        segment = ids_in[:, 0, :].astype(F32)
        live = jnp.sum(ids_in[:, 1, :tokens].astype(F32))
        lane = lax.broadcasted_iota(jnp.int32, (8, EXTRA), 1)
        parts = [segment[:, c * BLOCK : (c + 1) * BLOCK] for c in range(blocks)]
        ends = [jnp.max(p, axis=1, keepdims=True) for p in parts]
        begin = jnp.min(parts[0], axis=1, keepdims=True)
        before = jnp.concatenate([begin[:1], ends[-1][:-1]], axis=0)
        result = jnp.where(lane == blocks, live, 0.0)
        for c in range(blocks):
            stay = jnp.sum((parts[c] == before).astype(F32), axis=1, keepdims=True)
            result = jnp.where(lane == c, stay, result)
            before = ends[c]
        cut_out[...] = result.astype(jnp.int32)
        for j in range(per_rank):
            for c in range(span):
                at = (j * span + c) * rows
                gap_out[:, at : at + rows] = gap_in[place.core * per_rank + j, c, :1, :rows].astype(F32)
        stages = [lambda: pl.loop(0, 3)(gather.forward), lambda: pl.loop(3, PIECES)(gather.forward)]
        stages += [lambda: pl.loop(0, PIECES)(gather.forward_last)]
        for hop in range(1, planes):
            if hop <= len(stages):
                stages[hop - 1]()
            line.arrive(hop)
            if hop < planes - 1:
                line.start(hop)
        for stage in stages[planes - 1 :]:
            stage()
        pl.loop(0, PIECES)(gather.finish)
        swap_waits(unit_copies)
        line.drain()
        pl.loop(0, PIECES)(gather.drain)

    qfi, full, unit_rows, cut, gap = pl.pallas_call(
        kernel,
        in_specs=[VMEM_SPEC] * 10,
        out_specs=[ANY_SPEC] * 3 + [VMEM_SPEC] * 2,
        out_shape=[
            jax.ShapeDtypeStruct((planes, 8, rows, 3 * channels), BF),
            jax.ShapeDtypeStruct((8, PIECES, x_rows, model), BF),
            jax.ShapeDtypeStruct((8, rows, 2 * units), BF),
            jax.ShapeDtypeStruct((8, EXTRA), jnp.int32),
            jax.ShapeDtypeStruct((1, channels), F32),
        ],
        scratch_shapes=[
            pltpu.VMEM((8, rows, 3 * channels), BF),
            pltpu.VMEM((PIECES, x_rows, model), BF),
            pltpu.VMEM((8, rows, 2 * units), BF),
            pltpu.VMEM((8,) + ids.shape, ids.dtype),
            pltpu.VMEM((planes, 2) + gap.shape, gap.dtype),
            pltpu.SemaphoreType.DMA((3, 7)),
            pltpu.SemaphoreType.DMA((3, 7)),
            pltpu.SemaphoreType.DMA((2,)),
            pltpu.SemaphoreType.DMA((KINDS, PIECES)),
            pltpu.SemaphoreType.DMA((KINDS, PIECES)),
            pltpu.SemaphoreType.DMA((PIECES,)),
            pltpu.SemaphoreType.DMA((2 * planes - 1,)),
            pltpu.SemaphoreType.DMA((2 * planes - 1,)),
            pltpu.SemaphoreType.DMA((2, planes)),
            pltpu.SemaphoreType.DMA((2, planes)),
        ],
        compiler_params=pltpu.CompilerParams(
            collective_id=collective_id, has_side_effects=True, vmem_limit_bytes=VMEM_LIMIT
        ),
        cost_estimate=pl.CostEstimate(flops=0, bytes_accessed=200 * tokens * model, transcendentals=0),
        name="enter_plane",
    )(*weights, gain, x, *unit_weights, unit_gain, ids, gap)
    return (
        qfi.reshape(model, 3 * channels),
        full.reshape(8 * tokens, model),
        unit_rows,
        cut,
        gap,
    )


def exit_plane(summed, gap_grad, planes, collective_id):
    def kernel(sum_ref, gap_ref, landed, gap_out, *sems):
        send, recv, local, gap_send, gap_recv = sems
        place = Place()
        greet_column_and_plane(place, planes)
        copies = swap_starts(place, [sum_ref], [landed], send, recv, local)
        gaps = column_spread(place, planes, gap_ref, gap_out, gap_send, gap_recv)
        own_gap = pltpu.make_async_copy(gap_ref, gap_out.at[place.plane, place.core], local.at[1])
        own_gap.start()
        swap_waits(copies)
        for copy, arrival in gaps:
            copy.wait_send()
            arrival.wait_recv()
        own_gap.wait()

    return pl.pallas_call(
        kernel,
        in_specs=[ANY_SPEC] * 2,
        out_specs=[ANY_SPEC] * 2,
        out_shape=[
            jax.ShapeDtypeStruct(summed.shape, summed.dtype),
            jax.ShapeDtypeStruct((planes, 2) + gap_grad.shape, gap_grad.dtype),
        ],
        scratch_shapes=[
            pltpu.SemaphoreType.DMA((1, 7)),
            pltpu.SemaphoreType.DMA((1, 7)),
            pltpu.SemaphoreType.DMA((2,)),
            pltpu.SemaphoreType.DMA((2 * planes - 1,)),
            pltpu.SemaphoreType.DMA((2 * planes - 1,)),
        ],
        compiler_params=pltpu.CompilerParams(collective_id=collective_id, has_side_effects=True),
        name="exit_plane",
    )(summed, gap_grad)


def finish(weights, gain, swapped, moves):
    rows, width = weights[0].shape
    tile = 512

    def kernel(*refs):
        in_ref, gain_ref = refs[0], refs[1]
        w_refs = refs[2 : 2 + len(weights)]
        outs, gain_out = refs[2 + len(weights) : -1], refs[-1]
        for w, rank, source, target in moves:
            outs[w][:, target] = in_ref[rank, :, source].astype(F32)
        scale = gain_ref[...]
        total = jnp.zeros((rows, tile), F32)
        for ref, out in zip(w_refs, outs):
            for at in range(0, width, tile):
                grad = out[:, at : at + tile]
                total += grad * ref[:, at : at + tile].astype(F32)
                out[:, at : at + tile] = grad * scale
        column = jnp.sum(total, axis=1, keepdims=True)
        diagonal = lax.broadcasted_iota(jnp.int32, (rows, rows), 0) == lax.broadcasted_iota(jnp.int32, (rows, rows), 1)
        gain_out[...] = jnp.sum(jnp.where(diagonal, column, 0.0), axis=0, keepdims=True)

    results = pl.pallas_call(
        kernel,
        in_specs=[VMEM_SPEC] * (2 + len(weights)),
        out_specs=[VMEM_SPEC] * (len(weights) + 1),
        out_shape=[jax.ShapeDtypeStruct((rows, width), F32)] * len(weights) + [jax.ShapeDtypeStruct((1, rows), F32)],
        compiler_params=pltpu.CompilerParams(vmem_limit_bytes=VMEM_LIMIT),
        name="finish",
    )(swapped, gain, *weights)
    return results[:-1], results[-1].reshape(rows)


def unit_moves(units, planes, ranks):
    units_in = units // planes
    return [
        (
            side,
            s,
            slice(side * units + i * units_in, side * units + (i + 1) * units_in),
            slice((i * ranks + s) * units_in, (i * ranks + s + 1) * units_in),
        )
        for side in range(2)
        for i in range(planes)
        for s in range(ranks)
    ]


def head_moves(head, per_rank, groups, span):
    moves = []
    for w in range(3):
        for a in range(groups):
            for m in range(span):
                for j in range(per_rank):
                    h = (m * per_rank + j) * groups + a
                    at = (w * per_rank + j) * head
                    moves.append((w, a * span + m, slice(at, at + head), slice(h * head, (h + 1) * head)))
    return moves


class Scatter:
    def __init__(self, left, weight, transposed, stats):
        self.rows, self.columns = left[2], left[3]
        self.transposed, self.stats = transposed, stats
        self.weight = weight
        self.depth = weight[1] if transposed else weight[0]
        self.width = weight[0] if transposed else weight[1]
        self.half = self.width // 2
        self.extra = EXTRA if stats else 0

    def scratch(self):
        rows, half, full = self.rows, self.half, self.width + self.extra
        right = half + self.extra
        return [
            pltpu.VMEM((PIECES, 8, rows, self.columns), BF),
            pltpu.VMEM(self.weight, BF),
            pltpu.VMEM((PIECES, 4, rows, full), BF),
            pltpu.VMEM((PIECES, 4, rows, full), BF),
            pltpu.VMEM((4, rows, full), F32),
            pltpu.VMEM((PIECES, 2, rows, half), BF),
            pltpu.VMEM((PIECES, 2, rows, half), BF),
            pltpu.VMEM((PIECES, 2, rows, right), BF),
            pltpu.VMEM((PIECES, 2, rows, right), BF),
            pltpu.VMEM((PIECES, 2, rows, half), F32),
            pltpu.VMEM((PIECES, 2, rows, right), F32),
            pltpu.VMEM((PIECES, rows, half), BF),
            pltpu.VMEM((PIECES, rows, half), BF),
            pltpu.VMEM((PIECES, rows, right), BF),
            pltpu.VMEM((PIECES, rows, right), BF),
            pltpu.SemaphoreType.DMA((PIECES,)),
            pltpu.SemaphoreType.DMA((2,)),
        ]

    def bind(self, place, sems, left_ref, weight_ref, refs):
        self.place, self.sems, self.left_ref, self.weight_ref = place, sems, left_ref, weight_ref
        (self.x_buf, self.w_buf, self.core_out, self.core_in, self.total, self.x_out, self.x_in, self.y_out, self.y_in,
         self.keep_a, self.keep_b, self.last_y_out, self.last_y_in, self.last_x_out,
         self.last_x_in, self.load_sem, self.w_sem) = refs

    def weight_copy(self, t):
        tile = min(TILE, self.width)
        at = pl.ds(t * tile, tile)
        if self.transposed:
            return pltpu.make_async_copy(self.weight_ref.at[at], self.w_buf.at[at], self.w_sem.at[t])
        return pltpu.make_async_copy(self.weight_ref.at[:, at], self.w_buf.at[:, at], self.w_sem.at[t])

    def start_loads(self):
        core = self.place.core
        for b in range(PIECES):
            for j in range(4):
                for side, at in ((0, 2 * j + 1 - core), (4, 2 * j + core)):
                    pltpu.make_async_copy(
                        self.left_ref.at[at, b], self.x_buf.at[b, side + j], self.load_sem.at[b]
                    ).start()
            if b == 0:
                for t in range(self.width // min(TILE, self.width)):
                    self.weight_copy(t).start()

    def send_core(self, b):
        return remote(self.core_out.at[b], self.core_in.at[b], self.sems, R_CORE, b, self.place.device(0, 0, 1))

    def send_x(self, b):
        return remote(self.x_out.at[b], self.x_in.at[b], self.sems, R_X, b, self.place.device(0, 1, 0))

    def send_y(self, b):
        return remote(self.y_out.at[b], self.y_in.at[b], self.sems, R_Y, b, self.place.device(1, 0, 0))

    def send_last_y(self, b):
        return remote(self.last_y_out.at[b], self.last_y_in.at[b], self.sems, R_LAST_Y, b, self.place.device(1, 0, 0))

    def send_last_x(self, b):
        return remote(self.last_x_out.at[b], self.last_x_in.at[b], self.sems, R_LAST_X, b, self.place.device(0, 1, 0))

    def produce(self, b):
        rows, depth, width, tile = self.rows, self.depth, self.width, min(TILE, self.width)
        pltpu.make_async_copy(self.x_buf.at[b], self.x_buf.at[b], self.load_sem.at[b]).wait()

        def product(side, t):
            lhs = self.x_buf[b, 4 * side : 4 * side + 4, :, :depth].reshape(4 * rows, depth)
            at = slice(t * tile, (t + 1) * tile)
            out = nt(lhs, self.w_buf[at, :]) if self.transposed else nn(lhs, self.w_buf[:, at])
            return out.reshape(4, rows, tile), at

        for t in range(width // tile):
            @pl.when(b == 0)
            def _():
                self.weight_copy(t).wait()

            out, at = product(0, t)
            self.core_out[b, :, :, at] = out.astype(BF)
        if self.stats:
            self.core_out[b, :, :, width:] = self.x_buf[b, :4, :, depth:]
        self.send_core(b).start()
        for t in range(width // tile):
            out, at = product(1, t)
            self.total[:, :, at] = out
        if self.stats:
            self.total[:, :, width:] = self.x_buf[b, 4:, :, depth:].astype(F32)

    def by_chunks(self, body):
        @pl.loop(0, self.rows // CHUNK)
        def _(r):
            body(pl.ds(pl.multiple_of(r * CHUNK, CHUNK), CHUNK))

    def stage_one(self, b):
        place, half, total, core_in = self.place, self.half, self.total, self.core_in
        self.send_core(b).wait_recv()

        def for_x(r):
            for i in range(2):
                go, stay = 2 * i + 1 - place.x, 2 * i + place.x
                self.x_out[b, i, r] = (total[go, r, :half] + core_in[b, go, r, :half].astype(F32)).astype(BF)
                self.keep_a[b, i, r] = total[stay, r, :half] + core_in[b, stay, r, :half].astype(F32)

        def for_y(r):
            for i in range(2):
                go, stay = 2 * (1 - place.y) + i, 2 * place.y + i
                self.y_out[b, i, r] = (total[go, r, half:] + core_in[b, go, r, half:].astype(F32)).astype(BF)
                self.keep_b[b, i, r] = total[stay, r, half:] + core_in[b, stay, r, half:].astype(F32)

        self.by_chunks(for_x)
        self.send_x(b).start()
        self.by_chunks(for_y)
        self.send_y(b).start()

    def stage_two(self, b):
        go_y, go_x = 1 - self.place.y, 1 - self.place.x

        def low(r):
            self.last_y_out[b, r] = (self.keep_a[b, go_y, r] + self.x_in[b, go_y, r].astype(F32)).astype(BF)

        def high(r):
            self.last_x_out[b, r] = (self.keep_b[b, go_x, r] + self.y_in[b, go_x, r].astype(F32)).astype(BF)

        self.send_x(b).wait_recv()
        self.by_chunks(low)
        self.send_last_y(b).start()
        self.send_y(b).wait_recv()
        self.by_chunks(high)
        self.send_last_x(b).start()

    def stage_three(self, b, body):
        self.send_last_y(b).wait_recv()
        self.send_last_x(b).wait_recv()
        y, x = self.place.y, self.place.x

        def end(r):
            low = self.keep_a[b, y, r] + self.x_in[b, y, r].astype(F32) + self.last_y_in[b, r].astype(F32)
            high = self.keep_b[b, x, r] + self.y_in[b, x, r].astype(F32) + self.last_x_in[b, r].astype(F32)
            result = jnp.concatenate([low, high[:, : self.half]], axis=1)
            body(r, result, high[:, self.half :] if self.stats else None)

        self.by_chunks(end)

    def drain(self, b):
        for copy in (self.send_core, self.send_x, self.send_y, self.send_last_y, self.send_last_x):
            copy(b).wait_send()


def guarded(body, b):
    @pl.when((b >= 0) & (b < PIECES))
    def _():
        body(b)


def plane_sems():
    return [pltpu.SemaphoreType.DMA((KINDS, PIECES)), pltpu.SemaphoreType.DMA((KINDS, PIECES))]


def product_scatter(left, weight, transposed, stats, epilogue, owned, outs, gathered, collective_id, fillers=()):
    tokens = left.shape[0] // 8
    rows = tokens // PIECES
    left = left.reshape(8, PIECES, rows, left.shape[1])
    scatter = Scatter(left.shape, weight.shape, transposed, stats)
    count = len(scatter.scratch())

    def kernel(*refs):
        refs = list(refs)
        left_ref, weight_ref = refs.pop(0), refs.pop(0)
        own_refs = [refs.pop(0) for _ in owned]
        extra_in = [[refs.pop(0) for _ in f.arrays] for f in fillers]
        out_refs = [refs.pop(0) for _ in outs]
        full_ref = refs.pop(0) if gathered else None
        extra_out = [refs.pop(0) for _ in fillers]
        place = Place()
        sems = (refs.pop(0), refs.pop(0))
        scatter.bind(place, sems, left_ref, weight_ref, refs[:count])
        refs = refs[count:]
        own_bufs = [refs.pop(0) for _ in owned]
        out_bufs = [refs.pop(0) for _ in outs]
        own_sem, out_sem = refs.pop(0), refs.pop(0)
        own_copies = [
            pltpu.make_async_copy(ref, buf, own_sem.at[i]) for i, (ref, buf) in enumerate(zip(own_refs, own_bufs))
        ]

        def out_copies(b):
            return [
                pltpu.make_async_copy(buf.at[b], ref.at[b], out_sem.at[i, b])
                for i, (buf, ref) in enumerate(zip(out_bufs, out_refs))
            ]

        scatter.start_loads()
        for copy in own_copies:
            copy.start()
        for f, ins, out in zip(fillers, extra_in, extra_out):
            f.bind(ins, out, refs[: len(f.scratch)])
            refs = refs[len(f.scratch) :]
            f.start()
        greet(place)
        if gathered:
            n_buf, keep_sem = refs
            gather = Gather(place, n_buf, full_ref, sems, keep_sem)

        def end(b):
            def rows_done(r, result, stat):
                written, sent = epilogue(result, stat, *[o[b, r] for o in own_bufs])
                for buf, value in zip(out_bufs, written):
                    buf[b, r] = value
                if gathered:
                    n_buf[b, r] = sent

            scatter.stage_three(b, rows_done)
            for copy in out_copies(b):
                copy.start()
            if gathered:
                gather.start(b)
        @pl.loop(0, PIECES + (9 if gathered else 5))
        def _(step):
            guarded(scatter.stage_one, step - 1)
            guarded(scatter.produce, step)
            guarded(scatter.stage_two, step - 3)
            for f in fillers:
                f.step(step)

            @pl.when(step == 5)
            def _():
                for copy in own_copies:
                    copy.wait()

            guarded(end, step - 5)
            if gathered:
                guarded(gather.forward, step - 7)
                guarded(gather.forward_last, step - 9)

        @pl.loop(0, PIECES)
        def _(b):
            if gathered:
                gather.finish(b)
                gather.drain(b)
            scatter.drain(b)
            for copy in out_copies(b):
                copy.wait()

        for f in fillers:
            f.end()

    any_spec = ANY_SPEC
    out_shape = [jax.ShapeDtypeStruct((PIECES, rows, c), d) for c, d in outs]
    out_specs = [any_spec] * len(outs)
    scratch = plane_sems() + scatter.scratch()
    scratch += [pltpu.VMEM((PIECES, rows, o.shape[1]), o.dtype) for o in owned]
    scratch += [pltpu.VMEM(o.shape, o.dtype) for o in out_shape]
    scratch += [pltpu.SemaphoreType.DMA((len(owned),)), pltpu.SemaphoreType.DMA((len(outs), PIECES))]
    if gathered:
        out_shape.append(jax.ShapeDtypeStruct((8, PIECES, rows, gathered), BF))
        out_specs.append(any_spec)
    args = [left, weight] + [o.reshape(PIECES, rows, o.shape[1]) for o in owned]
    in_specs = [any_spec, any_spec] + [any_spec] * len(owned)
    for f in fillers:
        args, in_specs = args + f.arrays, in_specs + [any_spec] * len(f.arrays)
        out_shape.append(f.out_shape)
        out_specs.append(any_spec)
        scratch += f.scratch
    if gathered:
        scratch += [pltpu.VMEM((PIECES, rows, gathered), BF), pltpu.SemaphoreType.DMA((PIECES,))]
    results = pl.pallas_call(
        kernel,
        in_specs=in_specs,
        out_specs=out_specs,
        out_shape=out_shape,
        scratch_shapes=scratch,
        compiler_params=pltpu.CompilerParams(
            collective_id=collective_id, has_side_effects=True, vmem_limit_bytes=VMEM_LIMIT
        ),
        cost_estimate=pl.CostEstimate(
            flops=16 * tokens * scatter.depth * scatter.width,
            bytes_accessed=(240 if gathered else 140) * tokens * scatter.width * 2,
            transcendentals=0,
        ),
        name="product_scatter",
    )(*args)
    flat = [r.reshape(tokens, r.shape[2]) for r in results[: len(outs)]]
    if gathered:
        flat.append(results[len(outs)].reshape(8 * tokens, gathered))
    return flat + list(results[len(outs) + (1 if gathered else 0) :])


class GradProduct:
    BLOCK = 256

    def __init__(self, left, right, by_right, first):
        self.left, self.right, self.by_right, self.first = left, right, by_right, first
        whole, streamed = (left, right) if by_right else (right, left)
        self.tokens, self.blocks = left.shape[0], streamed.shape[1] // self.BLOCK
        depth, width = left.shape[1], right.shape[1]
        block = (depth, self.BLOCK) if by_right else (self.BLOCK, width)
        self.arrays = [whole, streamed]
        self.out_shape = jax.ShapeDtypeStruct((depth, width), BF)
        self.scratch = [
            pltpu.VMEM(whole.shape, BF),
            pltpu.VMEM((2, self.tokens, self.BLOCK), BF),
            pltpu.VMEM((2,) + block, BF),
            pltpu.SemaphoreType.DMA((1,)),
            pltpu.SemaphoreType.DMA((2,)),
            pltpu.SemaphoreType.DMA((2,)),
        ]

    def plain(self):
        return tn(self.left, self.right).astype(BF)

    def bind(self, ins, out, refs):
        self.whole_ref, self.streamed_ref = ins
        self.out = out
        self.w_buf, self.s_buf, self.o_buf, self.w_sem, self.s_sem, self.o_sem = refs

    def columns(self, b):
        return pl.ds(pl.multiple_of(b * self.BLOCK, self.BLOCK), self.BLOCK)

    def load(self, b):
        return pltpu.make_async_copy(self.streamed_ref.at[:, self.columns(b)], self.s_buf.at[b % 2], self.s_sem.at[b % 2])

    def store(self, b):
        to = self.out.at[:, self.columns(b)] if self.by_right else self.out.at[self.columns(b)]
        return pltpu.make_async_copy(self.o_buf.at[b % 2], to, self.o_sem.at[b % 2])

    def whole_copy(self):
        return pltpu.make_async_copy(self.whole_ref, self.w_buf, self.w_sem.at[0])

    def start(self):
        self.whole_copy().start(priority=1)
        self.load(0).start(priority=1)
        self.load(1).start(priority=1)

    def step(self, step):
        b = step - self.first

        @pl.when(b == 0)
        def _():
            self.whole_copy().wait()

        @pl.when((b >= 0) & (b < self.blocks))
        def _():
            self.load(b).wait()

            @pl.when(b >= 2)
            def _():
                self.store(b - 2).wait()

            streamed, whole = self.s_buf[b % 2], self.w_buf[...]
            product = tn(whole, streamed) if self.by_right else tn(streamed, whole)
            self.o_buf[b % 2] = product.astype(BF)
            self.store(b).start(priority=1)

        @pl.when((b >= 0) & (b + 2 < self.blocks))
        def _():
            self.load(b + 2).start(priority=1)

    def end(self):
        self.store(self.blocks - 2).wait()
        self.store(self.blocks - 1).wait()


def mixer_specs(tokens, heads, reverse):
    width, span = heads * 128, UNROLL * BLOCK
    steps = tokens // span

    def at(i):
        return steps - 1 - i if reverse else i

    return (
        steps,
        pl.BlockSpec((span, 3 * width), lambda i, *_: (at(i), 0)),
        pl.BlockSpec((1, width), lambda i, *_: (0, 0)),
        pl.BlockSpec((UNROLL, heads, 128, 128), lambda i, *_: (at(i), 0, 0, 0)),
        lambda columns: pl.BlockSpec((span, columns), lambda i, *_: (at(i), 0)),
    )


def mixer_forward(cut, n1, weight, gap, own, out_pieces, per_rank, collective_id):
    tokens, heads = n1.shape[0], gap.shape[1] // 128
    width = heads * 128
    blocks = tokens // BLOCK // lax.axis_size("seq")
    steps, qfi_spec, gap_spec, kept_spec, block = mixer_specs(tokens, heads, False)
    together = lax.axis_size("seq") == 8

    def kernel(cut_ref, n_ref, w_ref, gap_ref, *refs):
        if not together:
            return mixer_forward_kernel(heads, blocks, cut_ref, n_ref, w_ref, gap_ref, *refs)
        (own_ref, pieces_ref, mixed_ref, kept_ref, qfi_ref, full_ref, rows_ref, state, own_buf, pieces_buf, send, recv, local,
         w_send, w_recv, w_local) = refs
        place = Place()
        gather = Gather(place, own_buf, full_ref, (send, recv), local)
        loads = [
            pltpu.make_async_copy(own_ref, own_buf, local.at[0]),
            pltpu.make_async_copy(pieces_ref, pieces_buf, w_local.at[0]),
        ]

        def exchange(j):
            core = place.core
            here = pltpu.make_async_copy(
                pieces_buf.at[core * per_rank + j], rows_ref.at[j, core], w_local.at[j]
            )
            there = pltpu.make_async_remote_copy(
                src_ref=pieces_buf.at[(1 - core) * per_rank + j], dst_ref=rows_ref.at[j, core],
                send_sem=w_send.at[j], recv_sem=w_recv.at[j], device_id=place.device(0, 0, 1), device_id_type=MESH,
            )
            back = rows_ref.at[j, 1 - core]
            arrival = pltpu.make_async_remote_copy(
                src_ref=back, dst_ref=back, send_sem=w_send.at[j], recv_sem=w_recv.at[j],
                device_id=place.device(0, 0, 1), device_id_type=MESH,
            )
            return here, there, arrival

        @pl.when(pl.program_id(0) == 0)
        def _():
            for load in loads:
                load.start()
            greet(place)
            for load in loads:
                load.wait()
            pl.loop(0, EARLY)(gather.start)
            for j in range(per_rank):
                here, there, _ = exchange(j)
                here.start()
                there.start()

        @pl.when(pl.program_id(0) == steps - 1)
        def _():
            pl.loop(0, EARLY)(gather.forward_last)

        mixer_forward_kernel(
            heads, blocks, cut_ref, n_ref, w_ref, gap_ref, mixed_ref, kept_ref, qfi_ref, state
        )

        for b in range(EARLY):
            @pl.when(pl.program_id(0) == min(steps - 1, (8 + 7 * b) // 4))
            def _():
                gather.forward(b)

        @pl.when(pl.program_id(0) == steps - 1)
        def _():
            for stage in (gather.finish, gather.drain):
                pl.loop(0, EARLY)(stage)
            for j in range(per_rank):
                here, there, arrival = exchange(j)
                here.wait()
                there.wait_send()
                arrival.wait_recv()

    fixed = pl.BlockSpec(weight.shape, lambda i, *_: (0, 0), pipeline_mode=pl.Buffered(1))
    in_specs, args = [block(n1.shape[1]), fixed, gap_spec], [n1, weight, gap]
    out_specs = [block(width + EXTRA), kept_spec, qfi_spec]
    out_shape = [
        jax.ShapeDtypeStruct((tokens, width + EXTRA), BF),
        jax.ShapeDtypeStruct((tokens // BLOCK, heads, 128, 128), BF),
        jax.ShapeDtypeStruct((tokens, 3 * width), F32),
    ]
    scratch = [pltpu.VMEM((heads, 128, 128), F32)]
    params = pltpu.CompilerParams(vmem_limit_bytes=VMEM_LIMIT)
    if together:
        rows = own.shape[0] // PIECES
        own = own.reshape(PIECES, rows, own.shape[1])
        w_rows, model = out_pieces.shape[1:]
        in_specs, args = in_specs + [ANY_SPEC] * 2, args + [own, out_pieces]
        out_specs = out_specs + [ANY_SPEC] * 2
        out_shape = out_shape + [
            jax.ShapeDtypeStruct((8,) + own.shape, own.dtype),
            jax.ShapeDtypeStruct((per_rank, 2, w_rows, model), BF),
        ]
        scratch = scratch + [pltpu.VMEM(own.shape, BF), pltpu.VMEM(out_pieces.shape, BF)]
        scratch = scratch + plane_sems() + [pltpu.SemaphoreType.DMA((PIECES,))]
        scratch = scratch + [pltpu.SemaphoreType.DMA((per_rank,))] * 3
        params = pltpu.CompilerParams(
            vmem_limit_bytes=VMEM_LIMIT, collective_id=collective_id, has_side_effects=True
        )
    results = pl.pallas_call(
        kernel,
        grid_spec=pltpu.PrefetchScalarGridSpec(
            num_scalar_prefetch=1, grid=(steps,), in_specs=in_specs, out_specs=out_specs, scratch_shapes=scratch
        ),
        out_shape=out_shape,
        compiler_params=params,
        cost_estimate=pl.CostEstimate(
            flops=tokens * width * (128 * 10 + 6 * n1.shape[1]),
            bytes_accessed=60 * tokens * n1.shape[1],
            transcendentals=tokens * width * 6,
        ),
        name="mixer_forward",
    )(cut, *args)
    mixed, kept, qfi = results[:3]
    if together:
        return mixed, kept, qfi, results[3], results[4].reshape(width, model)
    return mixed, kept, qfi, lax.all_gather(own, "seq", axis=0, tiled=True), None


def mixer_backward(cut, qfi, gap, kept, grad, parts, grad_out, per_rank, collective_id):
    tokens, heads = qfi.shape[0], gap.shape[1] // 128
    width = heads * 128
    blocks = tokens // BLOCK // lax.axis_size("seq")
    steps, qfi_spec, gap_spec, kept_spec, block = mixer_specs(tokens, heads, True)
    together = lax.axis_size("seq") == 8
    planes = lax.axis_size("dp")

    def kernel(cut_ref, qfi_ref, gap_ref, kept_ref, grad_ref, *refs):
        if not together:
            return mixer_backward_kernel(heads, blocks, cut_ref, qfi_ref, gap_ref, kept_ref, grad_ref, *refs)
        (parts_ref, og_ref, out_ref, gap_out_ref, swapped_ref, sum_ref, state, parts_buf, og_buf, by_plane, landed,
         send, recv, local, c_send, c_recv, z_send, z_recv, load_sem) = refs
        place, step = Place(), pl.program_id(0)
        core = place.core
        loads = [
            pltpu.make_async_copy(parts_ref, parts_buf, load_sem.at[0]),
            pltpu.make_async_copy(og_ref, og_buf, load_sem.at[1]),
        ]

        def over_core(j):
            there = by_plane.at[core * per_rank + j]
            back = by_plane.at[(1 - core) * per_rank + j]
            return [
                pltpu.make_async_remote_copy(
                    src_ref=src, dst_ref=dst, send_sem=c_send.at[j], recv_sem=c_recv.at[j],
                    device_id=place.device(0, 0, 1), device_id_type=MESH,
                )
                for src, dst in ((og_buf.at[j, 1 - core], there), (back, back))
            ]

        def over_planes(hop):
            plane = lax.rem(place.plane + hop, planes)
            back = landed.at[planes - hop - 1]
            return [
                pltpu.make_async_remote_copy(
                    src_ref=src, dst_ref=dst, send_sem=z_send.at[hop - 1], recv_sem=z_recv.at[hop - 1],
                    device_id=(plane, place.me), device_id_type=MESH,
                )
                for src, dst in ((by_plane.at[plane], landed.at[planes - hop - 1]), (back, back))
            ]

        swaps = functools.partial(swap_pairs, place, [parts_buf], [swapped_ref], send, recv, local)

        @pl.when(step == 0)
        def _():
            for load in loads:
                load.start()
            greet_column_and_plane(place, planes)
            for load in loads:
                load.wait()
            for j in range(per_rank):
                over_core(j)[0].start()
                by_plane[core * per_rank + j] = og_buf[j, core]
            for copy, _ in swaps():
                copy.start()

        @pl.when(step == 1)
        def _():
            for j in range(per_rank):
                there, arrival = over_core(j)
                there.wait_send()
                arrival.wait_recv()
            for hop in range(1, planes):
                over_planes(hop)[0].start()

        mixer_backward_kernel(
            heads, blocks, cut_ref, qfi_ref, gap_ref, kept_ref, grad_ref, out_ref, gap_out_ref, state
        )

        @pl.when(step == steps - 1)
        def _():
            swap_waits(swaps())
            total = by_plane[place.plane].astype(F32)
            for hop in range(1, planes):
                there, arrival = over_planes(hop)
                there.wait_send()
                arrival.wait_recv()
                total += landed[planes - hop - 1].astype(F32)
            sum_ref[...] = total

    in_specs = [qfi_spec, gap_spec, kept_spec, block(width)]
    out_specs = [block(3 * width), gap_spec]
    out_shape = [jax.ShapeDtypeStruct((tokens, 3 * width), BF), jax.ShapeDtypeStruct((1, width), F32)]
    scratch = [pltpu.VMEM((heads, 128, 128), F32)]
    args = [qfi, gap, kept, grad]
    params = pltpu.CompilerParams(vmem_limit_bytes=VMEM_LIMIT)
    if together:
        rows, model = grad_out.shape[2:]
        in_specs, args = in_specs + [ANY_SPEC] * 2, args + [parts, grad_out]
        out_specs = out_specs + [ANY_SPEC, pl.BlockSpec((rows, model), lambda i, *_: (0, 0))]
        out_shape = out_shape + [
            jax.ShapeDtypeStruct(parts.shape, BF),
            jax.ShapeDtypeStruct((rows, model), F32),
        ]
        scratch = scratch + [
            pltpu.VMEM(parts.shape, BF),
            pltpu.VMEM(grad_out.shape, BF),
            pltpu.VMEM((planes, rows, model), BF),
            pltpu.VMEM((planes - 1, rows, model), BF),
            pltpu.SemaphoreType.DMA((1, 7)),
            pltpu.SemaphoreType.DMA((1, 7)),
            pltpu.SemaphoreType.DMA((1,)),
            pltpu.SemaphoreType.DMA((per_rank,)),
            pltpu.SemaphoreType.DMA((per_rank,)),
            pltpu.SemaphoreType.DMA((planes - 1,)),
            pltpu.SemaphoreType.DMA((planes - 1,)),
            pltpu.SemaphoreType.DMA((2,)),
        ]
        params = pltpu.CompilerParams(
            vmem_limit_bytes=VMEM_LIMIT, collective_id=collective_id, has_side_effects=True
        )
    return pl.pallas_call(
        kernel,
        grid_spec=pltpu.PrefetchScalarGridSpec(
            num_scalar_prefetch=1, grid=(steps,), in_specs=in_specs, out_specs=out_specs, scratch_shapes=scratch
        ),
        out_shape=out_shape,
        compiler_params=params,
        cost_estimate=pl.CostEstimate(
            flops=tokens * width * 128 * 24, bytes_accessed=tokens * width * 28, transcendentals=tokens * width * 6
        ),
        name="mixer_backward",
    )(cut, *args)


def feed_forward_kernel(units, n_ref, gu_ref, units_ref, act_ref, slope_ref, gate_w, up_w):
    @pl.when(pl.program_id(0) == 0)
    def _():
        gate_w[...] = gu_ref[:, :units]
        up_w[...] = gu_ref[:, units:]

    n = n_ref[...]
    gate, up = nn(n, gate_w[...]), nn(n, up_w[...])
    sig = jax.nn.sigmoid(gate)
    act = gate * sig
    units_ref[...] = (act * up).astype(BF)
    act_ref[...] = act.astype(BF)
    slope_ref[...] = (up * sig * (1.0 + gate * (1.0 - sig))).astype(BF)


def add_up(total, product, out_ref):
    step = pl.program_id(0)

    @pl.when(step == 0)
    def _():
        total[...] = product

    @pl.when(step > 0)
    def _():
        total[...] += product

    @pl.when(step == pl.num_programs(0) - 1)
    def _():
        out_ref[...] = total[...].astype(BF)


def feed_backward_kernel(units, g_ref, down_ref, units_ref, act_ref, slope_ref, grad_ref, down_grad_ref, total):
    grad = g_ref[...]
    d_units = nt(grad, down_ref[...])
    grad_ref[:, :units] = (d_units * slope_ref[...].astype(F32)).astype(BF)
    grad_ref[:, units:] = (d_units * act_ref[...].astype(F32)).astype(BF)
    add_up(total, tn(units_ref[...], grad), down_grad_ref)


def output_backward_kernel(model, width, d_ref, mixed_ref, out_ref, d_mixed_ref, grad_ref, total):
    d_attn = d_ref[:, :model]
    mixed = mixed_ref[:, :width]
    beta = jnp.sum(d_ref[:, model:].astype(F32), axis=1, keepdims=True)
    d_mixed_ref[...] = (nt(d_attn, out_ref[...]) - beta * mixed.astype(F32)).astype(BF)
    add_up(total, tn(mixed, d_attn), grad_ref)


def fixed_block(shape):
    return pl.BlockSpec(shape, lambda i: (0, 0), pipeline_mode=pl.Buffered(1))


def row_block(columns):
    return pl.BlockSpec((512, columns), lambda i: (i, 0))


def feed_forward(n2, gu, own, full, collective_id):
    tokens, model = n2.shape
    units = gu.shape[1] // 2
    steps = tokens // 512
    together = lax.axis_size("seq") == 8

    def kernel(n_ref, gu_ref, *refs):
        if not together:
            return feed_forward_kernel(units, n_ref, gu_ref, *refs)
        own_ref, _, units_ref, act_ref, slope_ref, full_ref, gate_w, up_w, own_buf, send, recv, local = refs
        place, step = Place(), pl.program_id(0)
        gather = Gather(place, own_buf, full_ref, (send, recv), local)

        @pl.when(step == 0)
        def _():
            load = pltpu.make_async_copy(own_ref, own_buf, local.at[0])
            load.start()
            greet(place)
            load.wait()
            pl.loop(EARLY, PIECES)(gather.start)

        @pl.when(step == min(2, steps - 1))
        def _():
            pl.loop(EARLY, PIECES)(gather.forward)

        @pl.when(step == steps - 1)
        def _():
            pl.loop(EARLY, PIECES)(gather.forward_last)

        feed_forward_kernel(units, n_ref, gu_ref, units_ref, act_ref, slope_ref, gate_w, up_w)

        @pl.when(step == steps - 1)
        def _():
            for stage in (gather.finish, gather.drain):
                pl.loop(EARLY, PIECES)(stage)

    in_specs, args = [row_block(model), fixed_block(gu.shape)], [n2, gu]
    out_specs = [row_block(units)] * 3
    out_shape = [jax.ShapeDtypeStruct((tokens, units), d) for d in (BF, BF, BF)]
    scratch = [pltpu.VMEM((model, units), BF), pltpu.VMEM((model, units), BF)]
    params, aliases = pltpu.CompilerParams(vmem_limit_bytes=VMEM_LIMIT), {}
    if together:
        own = own.reshape(PIECES, own.shape[0] // PIECES, own.shape[1])
        in_specs, args = in_specs + [ANY_SPEC] * 2, args + [own, full]
        out_specs = out_specs + [ANY_SPEC]
        out_shape = out_shape + [jax.ShapeDtypeStruct(full.shape, full.dtype)]
        scratch = scratch + [pltpu.VMEM(own.shape, BF)] + plane_sems() + [pltpu.SemaphoreType.DMA((PIECES,))]
        params = pltpu.CompilerParams(
            vmem_limit_bytes=VMEM_LIMIT, collective_id=collective_id, has_side_effects=True
        )
        aliases = {3: 3}
    results = pl.pallas_call(
        kernel,
        grid=(steps,),
        in_specs=in_specs,
        out_specs=out_specs,
        out_shape=out_shape,
        scratch_shapes=scratch,
        compiler_params=params,
        input_output_aliases=aliases,
        cost_estimate=pl.CostEstimate(
            flops=4 * tokens * model * units, bytes_accessed=4 * tokens * model, transcendentals=tokens * units
        ),
        name="feed_forward",
    )(*args)
    if together:
        return results[0], results[1], results[2], results[3].reshape(tokens, model)
    return results[0], results[1], results[2], full


def feed_backward(grad, down, hidden_units, act, slope):
    tokens, model = grad.shape
    units = down.shape[0]
    return pl.pallas_call(
        functools.partial(feed_backward_kernel, units),
        grid=(tokens // 512,),
        in_specs=[row_block(model), fixed_block(down.shape)] + [row_block(units)] * 3,
        out_specs=[row_block(2 * units), fixed_block(down.shape)],
        out_shape=[jax.ShapeDtypeStruct((tokens, 2 * units), BF), jax.ShapeDtypeStruct(down.shape, BF)],
        scratch_shapes=[pltpu.VMEM(down.shape, F32)],
        compiler_params=pltpu.CompilerParams(vmem_limit_bytes=VMEM_LIMIT),
        cost_estimate=pl.CostEstimate(
            flops=4 * tokens * model * units, bytes_accessed=8 * tokens * model, transcendentals=0
        ),
        name="feed_backward",
    )(grad, down, hidden_units, act, slope)


def output_backward(d_attn, mixed, weight):
    tokens, (width, model) = mixed.shape[0], weight.shape
    return pl.pallas_call(
        functools.partial(output_backward_kernel, model, width),
        grid=(tokens // 512,),
        in_specs=[row_block(d_attn.shape[1]), row_block(mixed.shape[1]), fixed_block(weight.shape)],
        out_specs=[row_block(width), fixed_block(weight.shape)],
        out_shape=[jax.ShapeDtypeStruct((tokens, width), BF), jax.ShapeDtypeStruct(weight.shape, BF)],
        scratch_shapes=[pltpu.VMEM(weight.shape, F32)],
        compiler_params=pltpu.CompilerParams(vmem_limit_bytes=VMEM_LIMIT),
        cost_estimate=pl.CostEstimate(
            flops=4 * tokens * model * width, bytes_accessed=3 * tokens * model, transcendentals=0
        ),
        name="output_backward",
    )(d_attn, mixed, weight)


def gather_dp(v):
    return lax.all_gather(v, "dp", axis=0, tiled=True)


def scatter_dp(v):
    return lax.psum_scatter(v, "dp", scatter_dimension=0, tiled=True)


def swap_seq(v):
    return lax.all_to_all(v, "seq", split_axis=0, concat_axis=0, tiled=True)


def product_all(left, weight, transposed, stats, epilogue, owned, outs, gathered, collective_id, fillers=()):
    if lax.axis_size("seq") == 8:
        return product_scatter(left, weight, transposed, stats, epilogue, owned, outs, gathered, collective_id, fillers)
    depth = left.shape[1] - (EXTRA if stats else 0)
    product = (nt if transposed else nn)(left[:, :depth], weight).astype(BF)
    result = lax.psum_scatter(product, "seq", scatter_dimension=0, tiled=True).astype(F32)
    stat = None
    if stats:
        stat = lax.psum_scatter(left[:, depth:].astype(F32), "seq", scatter_dimension=0, tiled=True)
    written, sent = epilogue(result, stat, *owned)
    written = [w.astype(d) for w, (_, d) in zip(written, outs)]
    written += [lax.all_gather(sent, "seq", axis=0, tiled=True)] if gathered else []
    return written + [f.plain() for f in fillers]


def split_lanes(v):
    lane = lax.broadcasted_iota(jnp.int32, (v.shape[0], EXTRA), 1)
    high = v.astype(BF).astype(F32)
    return jnp.where(lane == 0, high, jnp.where(lane == 1, v - high, 0.0)).astype(BF)


def on_device(
    hidden,
    seg_ids,
    pad_mask,
    attn_gain,
    gate_gap,
    out_gain,
    w_query,
    w_forget,
    w_input,
    w_output,
    ffn_gain,
    w_gate,
    w_up,
    w_down,
    out_grad,
):
    planes, ranks = lax.axis_size("dp"), lax.axis_size("seq")
    row_tokens, model = hidden.shape[1:]
    rows = w_query.shape[0]
    units_in = w_down.shape[0]
    head = model // HEADS
    span = head // rows
    per_rank, groups = planes // span, ranks // span
    channels = per_rank * head
    units = planes * units_in
    tokens = ranks * row_tokens
    members = [[a * span + m for m in range(span)] for a in range(groups)]

    def to_heads(w):
        parts = w.reshape(rows, span, per_rank, groups, head)
        return parts.transpose(3, 1, 0, 2, 4).reshape(ranks, rows, channels)

    def from_heads(parts):
        parts = parts.reshape(groups, span, rows, per_rank, head)
        return parts.transpose(2, 1, 3, 0, 4).reshape(rows, model)

    def to_units(w):
        parts = w.reshape(rows, planes, ranks, units_in)
        return parts.transpose(2, 0, 1, 3).reshape(ranks, rows, units)

    def from_units(parts):
        parts = parts.reshape(ranks, rows, planes, units_in)
        return parts.transpose(1, 2, 0, 3).reshape(rows, planes * ranks * units_in)

    def own_rows(v):
        return v.reshape((span, per_rank) + v.shape[1:])

    def swap_group(v):
        return lax.all_to_all(v, "seq", split_axis=0, concat_axis=0, axis_index_groups=members)

    gain_a, gain_o, gain_f = (g.astype(F32)[:, None] for g in (attn_gain, out_gain, ffn_gain))

    plain = ranks != 8

    def order(first, *rest):
        return lax.optimization_barrier((first,) + rest)

    x16 = hidden[0]
    ids = jnp.concatenate([seg_ids, pad_mask], axis=0)
    mixer_weights = (w_query, w_forget, w_input)
    out_pieces = lax.all_gather(fold(gain_o, w_output), "dp", axis=0)
    if plain:
        qfi_part = jnp.concatenate([to_heads(fold(gain_a, w)) for w in mixer_weights], axis=2)
        qfi_full = gather_dp(swap_seq(qfi_part).reshape(ranks * rows, 3 * channels))
        gu_part = jnp.concatenate([to_units(fold(gain_f, w)) for w in (w_gate, w_up)], axis=2)
        gu_swapped = swap_seq(gu_part)
        x = x16.astype(F32)
        normed = (x * inverse_rms(row_mean(x * x))).astype(BF)
        n1 = lax.all_gather(normed, "seq", axis=0, tiled=True)
        gap_pieces = lax.all_gather(gate_gap, "dp", axis=0)
        gap_own = swap_group(own_rows(gap_pieces)).transpose(1, 0, 2).reshape(1, channels).astype(F32)
        ids = lax.all_gather(ids, "seq", axis=0)
        segment = ids[:, 0].reshape(tokens // BLOCK, BLOCK)
        live = jnp.sum(ids[:, 1]).reshape(1)
        ends = segment[:, -1]
        before = jnp.concatenate([segment[:1, 0], ends[:-1]])
        cut = jnp.sum((segment == before[:, None]).astype(jnp.int32), axis=1).reshape(ranks, -1)
        cut = jnp.concatenate([cut, jnp.broadcast_to(live, (ranks, 1))], axis=1)
        cut = jnp.pad(cut, ((0, 0), (0, EXTRA - cut.shape[1])))
    else:
        wide = -(-row_tokens // 128) * 128
        ids = jnp.pad(ids, ((0, 6), (0, wide - row_tokens)))
        gap_tile = jnp.pad(gate_gap[None], ((0, 15), (0, 128 - rows)))
        qfi_full, n1, gu_swapped, cut, gap_own = enter_plane(
            mixer_weights, gain_a, x16, (w_gate, w_up), gain_f, ids, gap_tile, per_rank, groups, planes, 1
        )
    gu_full = gather_dp(gu_swapped.reshape(ranks * rows, 2 * units))

    og16 = out_grad[0]
    mixed, kept, qfi, grad_all, out_own = mixer_forward(
        cut, n1, qfi_full, gap_own, og16, out_pieces, per_rank, 3
    )
    if plain:
        out_own = swap_group(own_rows(out_pieces)).transpose(1, 0, 2, 3).reshape(channels, model)

    def after_output(result, stat, x16):
        x = x16.astype(F32)
        factor_o = inverse_rms(jnp.sum(stat, axis=1, keepdims=True) / model)
        middle = x + factor_o * result
        normed = middle * inverse_rms(row_mean(middle * middle))
        return [middle, jnp.broadcast_to(factor_o, (x.shape[0], EXTRA))], normed.astype(BF)

    mixed, w_down_late = order(mixed, w_down)
    down_own = gather_dp(w_down_late)
    middle, factor_o, n2 = product_all(
        mixed, out_own, False, True, after_output, [x16], [(model, F32), (EXTRA, F32)], model, 4
    )
    hidden_units, act, slope, grad_all = feed_forward(n2, gu_full, og16, grad_all, 10)
    def after_down(result, stat, middle):
        return [(middle + result).astype(BF)], None

    d_gu, grad_down = feed_backward(grad_all, down_own, hidden_units, act, slope)
    down_sum = scatter_dp(grad_down)
    block_out, grad_gu = product_all(
        hidden_units, down_own, False, False, after_down, [middle], [(model, BF)], 0, 6,
        (GradProduct(n2, d_gu, False, 0),),
    )
    gu_sum = scatter_dp(grad_gu)
    d_gu, grad_gu = order(d_gu, grad_gu)

    def after_ffn(result, stat, middle, og16, x16, factor_o):
        factor_o = factor_o[:, :1]
        factor_m = inverse_rms(row_mean(middle * middle))
        normed = middle * factor_m
        d_middle = og16.astype(F32) + factor_m * (result - normed * row_mean(result * normed))
        mean_o = row_mean(d_middle * (middle - x16.astype(F32)))
        beta = split_lanes(factor_o * factor_o * mean_o)
        return [d_middle], jnp.concatenate([(factor_o * d_middle).astype(BF), beta], axis=1)

    d_middle, d_attn = product_all(
        d_gu, gu_full, True, False, after_ffn, [middle, og16, x16, factor_o], [(model, F32)], model + EXTRA, 5
    )
    d_attn, down_sum = order(d_attn, down_sum)
    d_mixed, grad_out = output_backward(d_attn, mixed, out_own)
    grad_out, d_mixed = order(grad_out, d_mixed)
    if plain:
        d_qfi, gap_grad = mixer_backward(cut, qfi, gap_own, kept, d_mixed, None, None, per_rank, 6)
        out_back = grad_out.reshape(per_rank, span, rows, model).transpose(1, 0, 2, 3)
        out_rows = scatter_dp(swap_group(out_back).reshape(planes * rows, model)).astype(F32)
        gu_rows = swap_seq(gu_sum).reshape(ranks, rows, 2 * units)
    else:
        d_qfi, gap_grad, gu_rows, out_rows = mixer_backward(
            cut, qfi, gap_own, kept, d_mixed, gu_sum.reshape(ranks, rows, 2 * units),
            grad_out.reshape(per_rank, span, rows, model), per_rank, 9,
        )
    grad_qfi = tn(n1, d_qfi).astype(BF)
    grad_qfi, d_qfi = order(grad_qfi, d_qfi)
    qfi_sum = scatter_dp(grad_qfi)

    def after_mixer(result, stat, x16, d_middle):
        x = x16.astype(F32)
        factor_x = inverse_rms(row_mean(x * x))
        normed = x * factor_x
        return [(d_middle + factor_x * (result - normed * row_mean(result * normed))).astype(BF)], None

    (hidden_grad,) = product_all(d_qfi, qfi_full, True, False, after_mixer, [x16, d_middle], [(model, BF)], 0, 7)

    hidden_grad, gu_rows, down_sum, out_rows, gap_grad = order(hidden_grad, gu_rows, down_sum, out_rows, gap_grad)

    def rowdot(w, g):
        return jnp.sum(w.astype(F32) * g, axis=1)

    g_out_gain = rowdot(w_output, out_rows)
    if plain:
        gu_rows = gu_rows.astype(F32)
        gate_rows, up_rows = from_units(gu_rows[:, :, :units]), from_units(gu_rows[:, :, units:])
        g_ffn_gain = rowdot(w_gate, gate_rows) + rowdot(w_up, up_rows)
        g_gate, g_up = gain_f * gate_rows, gain_f * up_rows
        gap_back = swap_group(gap_grad.reshape(per_rank, span, rows).transpose(1, 0, 2)).reshape(planes * rows)
        g_gap = scatter_dp(gap_back)
        qfi_rows = swap_seq(qfi_sum).reshape(ranks, rows, 3 * channels).astype(F32)
        parts = [from_heads(qfi_rows[:, :, j * channels : (j + 1) * channels]) for j in range(3)]
        g_attn_gain = sum(rowdot(w, g) for w, g in zip(mixer_weights, parts))
        g_query, g_forget, g_input = [gain_a * g for g in parts]
    else:
        (g_gate, g_up), g_ffn_gain = finish((w_gate, w_up), gain_f, gu_rows, unit_moves(units, planes, ranks))
        gap_tile = jnp.broadcast_to(gap_grad, (8, channels))
        qfi_rows, gap_all = exit_plane(qfi_sum.reshape(ranks, rows, 3 * channels), gap_tile, planes, 8)
        (g_query, g_forget, g_input), g_attn_gain = finish(
            mixer_weights, gain_a, qfi_rows, head_moves(head, per_rank, groups, span)
        )
        plane, me = lax.axis_index("dp"), lax.axis_index("seq")
        at = lax.rem(plane, per_rank) * head + lax.rem(me, 2) * rows
        from_core = jnp.sum(gap_all[:, :, 0], axis=0)
        g_gap = lax.dynamic_slice(from_core, (plane // per_rank, at), (1, rows))[0]
    return (
        block_out[None],
        hidden_grad[None],
        g_attn_gain,
        g_gap,
        g_out_gain,
        g_query,
        g_forget,
        g_input,
        gain_o * out_rows,
        g_ffn_gain,
        g_gate,
        g_up,
        down_sum.astype(F32),
    )


def solution(mesh):
    tok, row, both = P("dp", "seq", None), P("dp", "seq"), P(("dp", "seq"))
    mat = P(("dp", "seq"), None)
    return jax.shard_map(
        on_device,
        mesh=mesh,
        in_specs=(tok, row, row, both, both, both, mat, mat, mat, mat, both, mat, mat, mat, tok),
        out_specs=(tok, tok, both, both, both, mat, mat, mat, mat, both, mat, mat, mat),
        check_vma=False,
    )
```
